32 devices in a mesh: rows: 4 (over y, x), seq: 8 (over z, core).
Axes of the slice: x: 2, y: 2, z: 4, core: 2. Of those that a mesh axis runs over, the one named last changes fastest.
Arguments:
- inputs: bfloat16 [4, 1024, 768], P('rows', 'seq'), may hold values from -6 to 6
- doc_lengths: int32 [4, 12], P('rows'), may hold values from 1 to 640, 960 in all within a row
- ln1_gain: float32 [768], replicated, may hold values from 0.1 to 1.9
- ln1_bias: float32 [768], replicated, may hold values from -3 to 3
- w_query: bfloat16 [768, 768], replicated, may hold values from -0.21875 to 0.21875
- w_key: bfloat16 [768, 768], replicated, may hold values from -0.21875 to 0.21875
- w_value: bfloat16 [768, 768], replicated, may hold values from -0.21875 to 0.21875
- ln2_gain: float32 [768], replicated, may hold values from 0.1 to 1.9
- ln2_bias: float32 [768], replicated, may hold values from -3 to 3
- w_out: bfloat16 [768, 768], replicated, may hold values from -0.21875 to 0.21875
- ln3_gain: float32 [768], replicated, may hold values from 0.1 to 1.9
- ln3_bias: float32 [768], replicated, may hold values from -3 to 3
- w_up: bfloat16 [768, 3072], replicated, may hold values from -0.21875 to 0.21875
- w_down: bfloat16 [3072, 768], replicated, may hold values from -0.109375 to 0.109375
- out_grad: bfloat16 [4, 1024, 768], P('rows', 'seq'), may hold values from -6 to 6
Outputs:
- output: bfloat16 [4, 1024, 768], P('rows', 'seq')
- grad_inputs: bfloat16 [4, 1024, 768], P('rows', 'seq')
- grad_ln1_gain: float32 [768], P(('rows', 'seq'))
- grad_ln1_bias: float32 [768], P(('rows', 'seq'))
- grad_w_query: float32 [768, 768], P(('rows', 'seq'))
- grad_w_key: float32 [768, 768], P(('rows', 'seq'))
- grad_w_value: float32 [768, 768], P(('rows', 'seq'))
- grad_ln2_gain: float32 [768], P(('rows', 'seq'))
- grad_ln2_bias: float32 [768], P(('rows', 'seq'))
- grad_w_out: float32 [768, 768], P(('rows', 'seq'))
- grad_ln3_gain: float32 [768], P(('rows', 'seq'))
- grad_ln3_bias: float32 [768], P(('rows', 'seq'))
- grad_w_up: float32 [768, 3072], P(('rows', 'seq'))
- grad_w_down: float32 [3072, 768], P(('rows', 'seq'))
The draws below stay inside these ranges and needn't reach their ends.
Inputs may be any that keep to these rules, and one draw needn't show every extreme that they name: `doc_lengths`: each row's 12 document lengths sum to 960; the last 64 positions of a row are padding; in every row one document has exactly 640 tokens.
All inputs are finite; a program needn't handle non-finite values.
Results may differ from the reference program's by a relative error of at most 0.019.
Values may be sent and summed in bfloat16 or wider, within the bound.
No kernel may reach another device: no remote copies, remote signals or barrier semaphores. Data moves between devices by JAX's collectives and lax.ppermute only.
A program may use at most 192 MiB of HBM per device.

```python
import math
import jax
import jax.numpy as jnp
import numpy as np
from jax import lax

D = 768
HEADS = 12
HEAD_DIM = 64
FF = 3072
DOCS = 12
SEQ_LEN = 1024
ROWS = 4
PAD = 64
MOST_DOC = 640


def block_levels(stream_key, extent, cuts, smallest, high):
    factor_of, own = 1.0, jax.random.fold_in(stream_key, 6)
    for axis_at, parts in cuts:
        heights = jnp.exp(jax.random.uniform(jax.random.fold_in(own, axis_at), (parts,), jnp.float32, smallest / len(cuts), high / len(cuts)))
        factor_of = factor_of * jnp.repeat(heights, extent[axis_at] // parts).reshape([-1 if axis == axis_at else 1 for axis in range(len(extent))])
    return factor_of


def profile(amount, total, limit, slope):
    weights = [(1 << 20) // math.isqrt(rank ** slope) + 1 for rank in range(2, amount + 1)]
    rest, counts = total - limit - (amount - 1), [1] * (amount - 1)
    while rest > 0:
        movable = [i for i in range(amount - 1) if counts[i] < limit]
        whole, budget = sum([weights[i] for i in movable]), rest
        for i in movable:
            extra = min(limit - counts[i], max(1, budget * weights[i] // whole), rest)
            counts[i] = counts[i] + extra
            rest = rest - extra
    return np.array([limit] + counts)


def ragged_sizes(key, count, total, most, slope):
    if count == 2:
        one = jax.random.randint(key, (), max(1, total - most), min(most, total - 1) + 1)
        return jnp.stack([one, total - one])
    tallies = jnp.asarray(profile(count, total, most, slope), jnp.int32)
    twos = (count - 1) // 2
    donor, receiver = tallies[1:1 + 2 * twos:2], tallies[2:2 + 2 * twos:2]
    margin = jnp.minimum(donor - 1, most - receiver)
    shifted = jax.random.randint(jax.random.fold_in(key, 1), (twos,), 0, 1 << 20) % (margin + 1)
    tallies = tallies.at[1:1 + 2 * twos:2].set(donor - shifted).at[2:2 + 2 * twos:2].set(receiver + shifted)
    return tallies[jax.random.permutation(jax.random.fold_in(key, 2), count)]


def bell_draw(key, shape, deviation, reach, pieces=(), kind=jnp.bfloat16):
    result = jax.random.normal(key, shape, jnp.float32) * deviation
    if len(pieces) > 0:
        result = block_levels(key, shape, pieces, -0.22, 0.18) * result
    return jnp.clip(result, min=-reach, max=reach).astype(kind)


def setup_inputs(seed: int = 0) -> dict:
    splits = jax.random.split(jax.random.key(seed), 16)
    return {
        "inputs": bell_draw(splits[0], (ROWS, SEQ_LEN, D), 1.0, 6.0, ((0, 4), (1, 8))),
        "doc_lengths": jax.vmap(lambda own: ragged_sizes(own, DOCS, SEQ_LEN - PAD, MOST_DOC, 2))(jax.random.split(splits[1], ROWS)).reshape((ROWS, DOCS)).astype(jnp.int32),
        "ln1_gain": jnp.clip(1.0 + 0.18 * jax.random.normal(splits[2], (D,), jnp.float32), 0.1, 1.9),
        "ln1_bias": bell_draw(splits[3], (D,), 0.5, 3.0, (), jnp.float32),
        "w_query": bell_draw(splits[4], (D, D), D ** -0.5, 0.21875),
        "w_key": bell_draw(splits[5], (D, D), D ** -0.5, 0.21875),
        "w_value": bell_draw(splits[6], (D, D), D ** -0.5, 0.21875),
        "ln2_gain": jnp.clip(1.0 + 0.18 * jax.random.normal(splits[7], (D,), jnp.float32), 0.1, 1.9),
        "ln2_bias": bell_draw(splits[8], (D,), 0.5, 3.0, (), jnp.float32),
        "w_out": bell_draw(splits[9], (D, D), D ** -0.5, 0.21875),
        "ln3_gain": jnp.clip(1.0 + 0.18 * jax.random.normal(splits[10], (D,), jnp.float32), 0.1, 1.9),
        "ln3_bias": bell_draw(splits[11], (D,), 0.5, 3.0, (), jnp.float32),
        "w_up": bell_draw(splits[12], (D, FF), D ** -0.5, 0.21875),
        "w_down": bell_draw(splits[13], (FF, D), FF ** -0.5, 0.109375),
        "out_grad": bell_draw(splits[14], (ROWS, SEQ_LEN, D), 1.0, 6.0, ((0, 4), (1, 8))),
    }


segment_pairs = ((2048, 1), (4096, 2), (8192, 4), (16384, 6))
masked_value = -1e+30
highest = lax.Precision.HIGHEST

@jax.custom_vjp
def low(v):
    return lax.optimization_barrier(v.astype(jnp.bfloat16)).astype(jnp.float32)

@jax.custom_vjp
def low_back(v):
    return v

def low_keep(v):
    return (low(v), None)

def low_pass(kept, grad):
    return (grad,)

def back_keep(v):
    return (v, None)

def back_low(kept, grad):
    return (low(grad),)
low.defvjp(low_keep, low_pass)
low_back.defvjp(back_keep, back_low)

def layer_norm(vector, gain_vec, bias_vec):
    row_mean = lax.optimization_barrier(jnp.mean(vector, axis=-1, keepdims=True))
    centered = vector - row_mean
    row_var = lax.optimization_barrier(jnp.mean(centered * centered, axis=-1, keepdims=True))
    return centered * lax.rsqrt(row_var + 1e-05) * gain_vec + bias_vec

def doc_of(positions, doc_ends):
    return lax.optimization_barrier(jnp.sum((positions[:, None] >= doc_ends[None, :]).astype(jnp.int32), axis=1)).astype(jnp.int32)

def pair_terms(query_pos, key_pos, query_doc, key_doc, head_count):
    head_ids = jnp.arange(head_count, dtype=jnp.int32)
    multiplicity = jnp.zeros((head_count, query_pos.shape[0], key_pos.shape[0]), jnp.float32)
    for seg_width, dilation in segment_pairs:
        same_seg = query_pos[:, None] // seg_width == key_pos[None, :] // seg_width
        query_pick = (query_pos % seg_width % dilation)[None, :] == (head_ids % dilation)[:, None]
        key_pick = (key_pos % seg_width % dilation)[None, :] == (head_ids % dilation)[:, None]
        joined = same_seg[None] & query_pick[:, :, None] & key_pick[:, None, :]
        multiplicity = multiplicity + joined.astype(jnp.float32)
    allowed = (key_pos[None, :] <= query_pos[:, None]) & (query_doc[:, None] == key_doc[None, :])
    allowed = allowed[None] & (multiplicity > 0.0)
    return (jnp.log(jnp.maximum(multiplicity, 1.0)), allowed)

def matmul(left, right):
    return jnp.dot(left, right, precision=highest, preferred_element_type=jnp.float32)

def attend_block(query_blk, query_pos, query_doc, keys_all, values_all, key_pos, key_doc):
    scores = low_back(0.125 * jnp.einsum('qhd,khd->hqk', query_blk, keys_all, precision=highest))
    log_mult, allowed = pair_terms(query_pos, key_pos, query_doc, key_doc, query_blk.shape[1])
    logits = jnp.where(allowed, scores + log_mult, masked_value)
    log_total = jax.nn.logsumexp(logits, axis=-1, keepdims=True)
    weights = jnp.exp(logits - log_total)
    return jnp.einsum('hqk,khd->qhd', low(weights), values_all, precision=highest)

def row_forward(params, row_input, row_lengths):
    ln1_gain, ln1_bias, w_query, w_key, w_value, ln2_gain, ln2_bias, w_out, ln3_gain, ln3_bias, w_up, w_down = params
    seq_len = row_input.shape[0]
    model_width = row_input.shape[1]
    head_count = HEADS
    head_size = HEAD_DIM
    doc_ends = jnp.cumsum(row_lengths).astype(jnp.int32)
    positions = jnp.arange(seq_len, dtype=jnp.int32)
    docs = doc_of(positions, doc_ends)
    normed_one = low(layer_norm(row_input, ln1_gain, ln1_bias))
    queries = low_back(low(matmul(normed_one, w_query))).reshape(seq_len, head_count, head_size)
    keys_all = low_back(low(matmul(normed_one, w_key))).reshape(seq_len, head_count, head_size)
    values_all = low_back(low(matmul(normed_one, w_value))).reshape(seq_len, head_count, head_size)
    block_rows = min(512, seq_len)
    block_total = seq_len // block_rows
    checked = jax.checkpoint(attend_block)

    def one_block(block_item):
        return checked(block_item[0], block_item[1], block_item[2], keys_all, values_all, positions, docs)
    attn = lax.map(one_block, (queries.reshape(block_total, block_rows, head_count, head_size), positions.reshape(block_total, block_rows), docs.reshape(block_total, block_rows)))
    attn = low_back(attn.reshape(seq_len, model_width))
    normed_two = low(layer_norm(attn, ln2_gain, ln2_bias))
    middle = row_input + low_back(matmul(normed_two, w_out))
    normed_three = low(layer_norm(middle, ln3_gain, ln3_bias))
    upper = low_back(matmul(normed_three, w_up))
    activated = low(jax.nn.gelu(upper, approximate=False))
    return middle + low_back(matmul(activated, w_down))

def reference(inputs, doc_lengths, ln1_gain, ln1_bias, w_query, w_key, w_value, ln2_gain, ln2_bias, w_out, ln3_gain, ln3_bias, w_up, w_down, out_grad):
    floats = (inputs.astype(jnp.float32), ln1_gain, ln1_bias, w_query.astype(jnp.float32), w_key.astype(jnp.float32), w_value.astype(jnp.float32), ln2_gain, ln2_bias, w_out.astype(jnp.float32), ln3_gain, ln3_bias, w_up.astype(jnp.float32), w_down.astype(jnp.float32))

    def whole_layer(layer_in, *params):

        def per_row(row_item):
            return row_forward(params, row_item[0], row_item[1])
        return lax.map(per_row, (layer_in, doc_lengths))
    layer_out, pullback = jax.vjp(whole_layer, *floats)
    positions = jnp.arange(SEQ_LEN, dtype=jnp.int32)
    doc_ends = jnp.cumsum(doc_lengths, axis=1).astype(jnp.int32)
    docs = lax.optimization_barrier(jnp.sum((positions[None, :, None] >= doc_ends[:, None, :]).astype(jnp.int32), axis=2))
    valid = (docs < DOCS).astype(jnp.float32)
    grads = pullback(out_grad.astype(jnp.float32) * valid[:, :, None])
    return (layer_out.astype(jnp.bfloat16), grads[0].astype(jnp.bfloat16), grads[1], grads[2], grads[3], grads[4], grads[5], grads[6], grads[7], grads[8], grads[9], grads[10], grads[11], grads[12])
```

```python
import math

import jax
import jax.numpy as jnp
from jax import lax
from jax.experimental import pallas as pl
from jax.experimental.pallas import tpu as pltpu
from jax.sharding import PartitionSpec as P

HEADS = 12
HEAD_DIM = 64


segment_pairs = ((2048, 1), (4096, 2), (8192, 4), (16384, 6))
masked_value = -1e30


def layer_norm(vector, gain_vec, bias_vec):
    row_mean = jnp.mean(vector, axis=-1, keepdims=True)
    centered = vector - row_mean
    row_var = jnp.mean(centered * centered, axis=-1, keepdims=True)
    return centered * lax.rsqrt(row_var + 1e-05) * gain_vec + bias_vec


def doc_of(positions, doc_ends):
    return jnp.sum((positions[:, None] >= doc_ends[None, :]).astype(jnp.int32), axis=1)


def pair_terms(query_pos, key_pos, query_doc, key_doc, head_count):
    head_ids = jnp.arange(head_count, dtype=jnp.int32)
    multiplicity = jnp.zeros((head_count, query_pos.shape[0], key_pos.shape[0]), jnp.float32)
    for seg_width, dilation in segment_pairs:
        same_seg = query_pos[:, None] // seg_width == key_pos[None, :] // seg_width
        query_pick = (query_pos % seg_width % dilation)[None, :] == (head_ids % dilation)[:, None]
        key_pick = (key_pos % seg_width % dilation)[None, :] == (head_ids % dilation)[:, None]
        joined = same_seg[None] & query_pick[:, :, None] & key_pick[:, None, :]
        multiplicity = multiplicity + joined.astype(jnp.float32)
    allowed = (key_pos[None, :] <= query_pos[:, None]) & (query_doc[:, None] == key_doc[None, :])
    allowed = allowed[None] & (multiplicity > 0.0)
    return (jnp.log(jnp.maximum(multiplicity, 1.0)), allowed)


def rows_inner(left, right):
    return lax.dot_general(
        left, right, (((0,), (0,)), ((), ())), preferred_element_type=jnp.float32
    )


def cols_inner(left, right):
    return lax.dot_general(
        left, right, (((1,), (1,)), ((), ())), preferred_element_type=jnp.float32
    )


def over_blocks(state, piece, step_fn):
    total_rows = piece[0].shape[0]
    block_rows = math.gcd(total_rows, 512)
    block_total = total_rows // block_rows
    split = tuple((part.reshape((block_total, block_rows) + part.shape[1:]) for part in piece))

    def inner(carried, block_item):
        return (step_fn(carried, block_item[1], block_item[0] * block_rows), None)

    result, unused = lax.scan(inner, state, (jnp.arange(block_total, dtype=jnp.int32), split))
    return result


def add_rows(buffer, start_pos, addend):
    current = lax.dynamic_slice_in_dim(buffer, start_pos, addend.shape[0], 0)
    return lax.dynamic_update_slice_in_dim(buffer, current + addend, start_pos, 0)


def shards(
    inputs,
    doc_lengths,
    ln1_gain,
    ln1_bias,
    w_query,
    w_key,
    w_value,
    ln2_gain,
    ln2_bias,
    w_out,
    ln3_gain,
    ln3_bias,
    w_up,
    w_down,
    out_grad,
):
    tok_rows = inputs.shape[1]
    head_count = HEADS
    head_size = HEAD_DIM
    model_width = inputs.shape[2]
    row_total = tok_rows * lax.axis_size("seq")
    layer_in = inputs[0].astype(jnp.float32)
    doc_ends = jnp.cumsum(doc_lengths[0])
    first_pos = lax.axis_index("seq") * tok_rows
    query_pos = first_pos + jnp.arange(tok_rows, dtype=jnp.int32)
    query_doc = doc_of(query_pos, doc_ends)
    valid = (query_doc < doc_lengths.shape[1]).astype(jnp.float32)
    first_norm, first_back = jax.vjp(layer_norm, layer_in, ln1_gain, ln1_bias)
    normed_one = first_norm.astype(jnp.bfloat16)
    queries = jnp.dot(normed_one, w_query, preferred_element_type=jnp.float32).astype(jnp.bfloat16)
    keys_local = jnp.dot(normed_one, w_key, preferred_element_type=jnp.float32).astype(jnp.bfloat16)
    values_local = jnp.dot(normed_one, w_value, preferred_element_type=jnp.float32).astype(
        jnp.bfloat16
    )
    query_heads = queries.reshape(tok_rows, head_count, head_size)

    def key_block_terms(key_start, key_count):
        key_pos = key_start + jnp.arange(key_count, dtype=jnp.int32)
        key_doc = doc_of(key_pos, doc_ends)
        return pair_terms(query_pos, key_pos, query_doc, key_doc, head_count)

    def with_pruning(step_fn):

        def wrapped(state, parts, start_pos):
            return step_fn(state, parts, start_pos)

        return wrapped

    def forward_step(state, parts, key_start):
        run_max, run_total, run_acc = state
        key_blk = parts[0].reshape(-1, head_count, head_size)
        value_blk = parts[1].reshape(-1, head_count, head_size)
        log_mult, allowed = key_block_terms(key_start, key_blk.shape[0])
        scores = 0.125 * jnp.einsum(
            "qhd,khd->hqk", query_heads, key_blk, preferred_element_type=jnp.float32
        )
        logits = jnp.where(allowed, scores + log_mult, masked_value)
        new_max = jnp.maximum(run_max, jnp.max(logits, axis=-1))
        weights = jnp.where(allowed, jnp.exp(logits - new_max[..., None]), 0.0)
        factor = jnp.exp(run_max - new_max)
        run_total = run_total * factor + jnp.sum(weights, axis=-1)
        run_acc = run_acc * factor[..., None] + jnp.einsum(
            "hqk,khd->hqd",
            weights.astype(jnp.bfloat16),
            value_blk,
            preferred_element_type=jnp.float32,
        )
        return (new_max, run_total, run_acc)

    forward_pruned = with_pruning(forward_step)
    start_state = (
        jnp.full((head_count, tok_rows), masked_value, jnp.float32),
        jnp.zeros((head_count, tok_rows), jnp.float32),
        jnp.zeros((head_count, tok_rows, head_size), jnp.float32),
    )
    final_state = over_blocks(
        start_state,
        (
            lax.all_gather(keys_local, "seq", axis=0, tiled=True),
            lax.all_gather(values_local, "seq", axis=0, tiled=True),
        ),
        forward_pruned,
    )
    run_max, run_total, run_acc = final_state
    row_lse = run_max + jnp.log(run_total)
    attn = (run_acc / run_total[..., None]).transpose(1, 0, 2).reshape(tok_rows, model_width)
    second_norm, second_back = jax.vjp(layer_norm, attn, ln2_gain, ln2_bias)
    normed_two = second_norm.astype(jnp.bfloat16)
    middle = layer_in + jnp.dot(normed_two, w_out, preferred_element_type=jnp.float32)
    third_norm, third_back = jax.vjp(layer_norm, middle, ln3_gain, ln3_bias)
    normed_three = third_norm.astype(jnp.bfloat16)
    upper = jnp.dot(normed_three, w_up, preferred_element_type=jnp.float32)
    activated_f, gelu_back = jax.vjp(
        lambda upper_in: jax.nn.gelu(upper_in, approximate=False), upper
    )
    activated = activated_f.astype(jnp.bfloat16)
    layer_out = middle + jnp.dot(activated, w_down, preferred_element_type=jnp.float32)
    grad_out = out_grad[0].astype(jnp.float32) * valid[:, None]
    grad_branch = grad_out.astype(jnp.bfloat16)
    grad_w_down = rows_inner(activated, grad_branch)
    grad_act = cols_inner(grad_branch, w_down)
    grad_upper = gelu_back(grad_act)[0].astype(jnp.bfloat16)
    grad_w_up = rows_inner(normed_three, grad_upper)
    grad_n3 = cols_inner(grad_upper, w_up)
    grad_mid_norm, grad_ln3_gain, grad_ln3_bias = third_back(grad_n3)
    grad_middle = grad_out + grad_mid_norm
    grad_proj = grad_middle.astype(jnp.bfloat16)
    grad_w_out = rows_inner(normed_two, grad_proj)
    grad_n2 = cols_inner(grad_proj, w_out)
    grad_attn_f, grad_ln2_gain, grad_ln2_bias = second_back(grad_n2)
    grad_attn = grad_attn_f.astype(jnp.bfloat16)
    grad_heads = grad_attn.reshape(tok_rows, head_count, head_size)
    row_delta = jnp.sum(
        (grad_attn.astype(jnp.float32) * attn).reshape(tok_rows, head_count, head_size), axis=-1
    )

    def backward_step(state, parts, key_start):
        grad_q_acc, grad_k_rows, grad_v_rows = state
        key_blk = parts[0].reshape(-1, head_count, head_size)
        value_blk = parts[1].reshape(-1, head_count, head_size)
        key_count = key_blk.shape[0]
        log_mult, allowed = key_block_terms(key_start, key_count)
        scores = 0.125 * jnp.einsum(
            "qhd,khd->hqk", query_heads, key_blk, preferred_element_type=jnp.float32
        )
        logits = jnp.where(allowed, scores + log_mult, masked_value)
        weights = jnp.where(allowed, jnp.exp(logits - row_lse[..., None]), 0.0)
        grad_weights = jnp.einsum(
            "qhd,khd->hqk", grad_heads, value_blk, preferred_element_type=jnp.float32
        )
        grad_scores = (weights * (grad_weights - row_delta.T[..., None])).astype(jnp.bfloat16)
        grad_q_acc = grad_q_acc + 0.125 * jnp.einsum(
            "hqk,khd->qhd", grad_scores, key_blk, preferred_element_type=jnp.float32
        )
        value_part = jnp.einsum(
            "hqk,qhd->khd",
            weights.astype(jnp.bfloat16),
            grad_heads,
            preferred_element_type=jnp.float32,
        ).reshape(key_count, model_width)
        key_part = 0.125 * jnp.einsum(
            "hqk,qhd->khd", grad_scores, query_heads, preferred_element_type=jnp.float32
        ).reshape(key_count, model_width)
        grad_k_rows = add_rows(grad_k_rows, key_start, key_part)
        grad_v_rows = add_rows(grad_v_rows, key_start, value_part)
        return (grad_q_acc, grad_k_rows, grad_v_rows)

    backward_pruned = with_pruning(backward_step)
    zero_state = (
        jnp.zeros((tok_rows, head_count, head_size), jnp.float32),
        jnp.zeros((row_total, model_width), jnp.float32),
        jnp.zeros((row_total, model_width), jnp.float32),
    )
    back_state = over_blocks(
        zero_state,
        (
            lax.all_gather(keys_local, "seq", axis=0, tiled=True),
            lax.all_gather(values_local, "seq", axis=0, tiled=True),
        ),
        backward_pruned,
    )
    grad_q_acc, grad_k_rows, grad_v_rows = back_state
    grad_k_acc, grad_v_acc = (
        lax.psum_scatter(
            grad_k_rows.astype(jnp.bfloat16), "seq", scatter_dimension=0, tiled=True
        ).astype(jnp.float32),
        lax.psum_scatter(
            grad_v_rows.astype(jnp.bfloat16), "seq", scatter_dimension=0, tiled=True
        ).astype(jnp.float32),
    )
    grad_queries = grad_q_acc.reshape(tok_rows, model_width).astype(jnp.bfloat16)
    grad_keys = grad_k_acc.astype(jnp.bfloat16)
    grad_values = grad_v_acc.astype(jnp.bfloat16)
    grad_w_query = rows_inner(normed_one, grad_queries)
    grad_w_key = rows_inner(normed_one, grad_keys)
    grad_w_value = rows_inner(normed_one, grad_values)
    grad_n1 = (
        cols_inner(grad_queries, w_query)
        + cols_inner(grad_keys, w_key)
        + cols_inner(grad_values, w_value)
    )
    grad_in_norm, grad_ln1_gain, grad_ln1_bias = first_back(grad_n1)
    grad_inputs = (grad_middle + grad_in_norm).astype(jnp.bfloat16)
    summed = (
        lax.psum_scatter(grad_ln1_gain, ("rows", "seq"), scatter_dimension=0, tiled=True),
        lax.psum_scatter(grad_ln1_bias, ("rows", "seq"), scatter_dimension=0, tiled=True),
        lax.psum_scatter(grad_w_query, ("rows", "seq"), scatter_dimension=0, tiled=True),
        lax.psum_scatter(grad_w_key, ("rows", "seq"), scatter_dimension=0, tiled=True),
        lax.psum_scatter(grad_w_value, ("rows", "seq"), scatter_dimension=0, tiled=True),
        lax.psum_scatter(grad_ln2_gain, ("rows", "seq"), scatter_dimension=0, tiled=True),
        lax.psum_scatter(grad_ln2_bias, ("rows", "seq"), scatter_dimension=0, tiled=True),
        lax.psum_scatter(grad_w_out, ("rows", "seq"), scatter_dimension=0, tiled=True),
        lax.psum_scatter(grad_ln3_gain, ("rows", "seq"), scatter_dimension=0, tiled=True),
        lax.psum_scatter(grad_ln3_bias, ("rows", "seq"), scatter_dimension=0, tiled=True),
        lax.psum_scatter(grad_w_up, ("rows", "seq"), scatter_dimension=0, tiled=True),
        lax.psum_scatter(grad_w_down, ("rows", "seq"), scatter_dimension=0, tiled=True),
    )
    return (
        layer_out.astype(jnp.bfloat16)[None],
        grad_inputs[None],
        summed[0],
        summed[1],
        summed[2],
        summed[3],
        summed[4],
        summed[5],
        summed[6],
        summed[7],
        summed[8],
        summed[9],
        summed[10],
        summed[11],
    )


def mapped(step, mesh, seq):
    spread = P(("rows",) + (seq if isinstance(seq, tuple) else (seq,)))
    tokens, plain = P("rows", seq, None), P()
    weights = P(spread[0], None)
    return jax.shard_map(
        step,
        mesh=mesh,
        in_specs=(tokens, P("rows", None)) + (plain,) * 12 + (tokens,),
        out_specs=(tokens, tokens, spread, spread, weights, weights, weights, spread, spread, weights)
        + (spread, spread, weights, weights),
        check_vma=False,
    )


F32 = jnp.float32
BF16 = jnp.bfloat16
NT = (((1,), (1,)), ((), ()))
TN = (((0,), (0,)), ((), ()))
NN = (((1,), (0,)), ((), ()))


def mm(left, right, dims):
    return lax.dot_general(left, right, dims, preferred_element_type=F32)


def unit_norm(vector):
    centered = vector - jnp.mean(vector, axis=-1, keepdims=True)
    scale = lax.rsqrt(jnp.mean(centered * centered, axis=-1, keepdims=True) + 1e-05)
    return centered * scale, scale


def norm_back(grad, gain, unit, scale):
    weighted = grad * gain
    mean_w = jnp.mean(weighted, axis=-1, keepdims=True)
    mean_wu = jnp.mean(weighted * unit, axis=-1, keepdims=True)
    return scale * (weighted - mean_w - unit * mean_wu)


def cost(flops, nbytes, trans=0):
    return pl.CostEstimate(flops=int(flops), bytes_accessed=int(nbytes), transcendentals=int(trans))


def vmem_specs(count):
    return [pl.BlockSpec(memory_space=pltpu.VMEM)] * count


def smem_spec():
    return pl.BlockSpec(memory_space=pltpu.SMEM)


def qkv_call(blocks, place, gain, bias, weight, width):
    count = len(blocks)
    rows, model = blocks[0].shape

    def body(place_ref, *refs):
        xs, (gain_ref, bias_ref, weight_ref, q_ref, kv_ref, unit_ref) = refs[:count], refs[count:]
        z_index = place_ref[0]
        for k in range(count):
            unit, _ = unit_norm(xs[k][...].astype(F32))
            normed = (unit * gain_ref[...] + bias_ref[...]).astype(BF16)
            made = mm(normed, weight_ref[...], NN)
            at = z_index ^ k
            q_ref[at] = (made[:, :width].astype(BF16).astype(F32) * 0.125).astype(BF16)
            kv_ref[at] = made[:, width:].astype(BF16)
            unit_ref[at] = unit.astype(BF16)

    return pl.pallas_call(
        body,
        out_shape=(
            jax.ShapeDtypeStruct((count, rows, width), BF16),
            jax.ShapeDtypeStruct((count, rows, 2 * width), BF16),
            jax.ShapeDtypeStruct((count, rows, model), BF16),
        ),
        in_specs=[smem_spec()] + vmem_specs(count + 3),
        out_specs=tuple(vmem_specs(3)),
        cost_estimate=cost(2 * count * rows * model * 3 * width, 4 * count * rows * model + 6 * model * width),
        name="qkv_heads",
    )(place, *blocks, gain, bias, weight)


def lane_head(lanes, heads_here):
    return lax.broadcasted_iota(jnp.int32, (1, lanes), 1) // HEAD_DIM


def residue(pos_f, modulus):
    return pos_f - modulus * jnp.floor((pos_f + 0.5) * (1.0 / modulus))


def stack_heads(block, heads_here):
    head_of = lane_head(block.shape[1], heads_here)
    return jnp.concatenate(
        [jnp.where(head_of == h, block, jnp.zeros_like(block)) for h in range(heads_here)], axis=0
    )


def fold_heads(stacked, rows, heads_here):
    head_of = lane_head(stacked.shape[1], heads_here)
    total = jnp.zeros((rows, stacked.shape[1]), stacked.dtype)
    for h in range(heads_here):
        total = jnp.where(head_of == h, stacked[h * rows : (h + 1) * rows], total)
    return total


def attend_call(place, lengths, queries, kv_own, kv_other, heads_here):
    count, rows, width = queries.shape
    tall, wide = heads_here * rows, count * rows
    docs = lengths.shape[1]
    step = 16

    def body(place_ref, len_ref, q_ref, own_ref, oth_ref, send_ref, out_ref, prob_ref, s_scr, m_scr, hot_scr):
        z_index, core = place_ref[0], place_ref[1]
        sides = (own_ref, oth_ref)
        cores = (core, 1 - core)
        lane = lax.broadcasted_iota(jnp.int32, (rows, 128), 1).astype(F32)
        for side in range(2):
            for b in range(count):
                pos = lax.broadcasted_iota(jnp.int32, (rows, 1), 0) + (2 * b + cores[side]) * rows
                hot = (residue(pos.astype(F32), 12.0) == lane).astype(F32)
                hot_scr[side, b * rows : (b + 1) * rows, :] = hot.astype(BF16)
        for i in range(count):
            keys = (i + 1) * rows
            pos = lax.broadcasted_iota(jnp.int32, (rows, 1), 0) + (2 * i + core) * rows
            pos_f = pos.astype(F32)
            begin = jnp.zeros_like(pos)
            run = jnp.int32(0)
            for d in range(docs):
                run = run + len_ref[0, d]
                begin = jnp.where(pos >= run, run, begin)
            tables = []
            for h in range(heads_here):
                head = (z_index * heads_here + h).astype(F32)
                table = jnp.ones((rows, 128), F32)
                for r in (2.0, 4.0, 6.0):
                    mine = residue(head, r)
                    pick_q = (residue(pos_f, r) == mine).astype(F32)
                    pick_k = (residue(lane, r) == mine).astype(F32)
                    table = table + pick_q * pick_k
                tables.append(jnp.where(lane < 12.0, table, 0.0))
            table = jnp.concatenate(tables, axis=0).astype(BF16)
            stacked = stack_heads(q_ref[i], heads_here)
            for side in range(2):
                key = sides[side][:, :, :width].reshape(wide, width)[:keys]
                s_scr[side, :, :keys] = mm(stacked, key, NT)
                m_scr[side, :, :keys] = mm(table, hot_scr[side, :keys], NT)
            key_pos = [
                jnp.concatenate(
                    [
                        lax.broadcasted_iota(jnp.int32, (1, rows), 1) + (2 * b + cores[side]) * rows
                        for b in range(i + 1)
                    ],
                    axis=1,
                )
                for side in range(2)
            ]
            for h in range(heads_here):
                for at in range(0, rows, step):
                    lo = h * rows + at
                    pos_c, begin_c = pos[at : at + step], begin[at : at + step]
                    masked = []
                    for side in range(2):
                        ok = (key_pos[side] <= pos_c) & (key_pos[side] >= begin_c)
                        masked.append(jnp.where(ok, s_scr[side, lo : lo + step, :keys], masked_value))
                    top = jnp.maximum(
                        jnp.max(masked[0], axis=1, keepdims=True), jnp.max(masked[1], axis=1, keepdims=True)
                    )
                    parts = [
                        jnp.exp(masked[side] - top) * m_scr[side, lo : lo + step, :keys] for side in range(2)
                    ]
                    total = jnp.sum(parts[0], axis=1, keepdims=True) + jnp.sum(parts[1], axis=1, keepdims=True)
                    inverse = 1.0 / total
                    for side in range(2):
                        prob_ref[i, side, lo : lo + step, :keys] = (parts[side] * inverse).astype(BF16)
            mixed = jnp.zeros((tall, width), F32)
            for side in range(2):
                value = sides[side][:, :, width:].reshape(wide, width)[:keys]
                mixed = mixed + mm(prob_ref[i, side, :, :keys], value, NN)
            result = fold_heads(mixed, rows, heads_here)
            out_ref[i] = result
            send_ref[i] = result.astype(BF16)

    return pl.pallas_call(
        body,
        out_shape=(
            jax.ShapeDtypeStruct((count, rows, width), BF16),
            jax.ShapeDtypeStruct((count, rows, width), F32),
            jax.ShapeDtypeStruct((count, 2, tall, wide), BF16),
        ),
        in_specs=[smem_spec(), smem_spec()] + vmem_specs(3),
        out_specs=tuple(vmem_specs(3)),
        scratch_shapes=[
            pltpu.VMEM((2, tall, wide), F32),
            pltpu.VMEM((2, tall, wide), F32),
            pltpu.VMEM((2, wide, 128), BF16),
        ],
        cost_estimate=cost(4 * tall * wide * count * width, 8 * count * tall * wide, count * tall * wide),
        name="attend",
    )(place, lengths, queries, kv_own, kv_other)


def attend_back_call(queries, kv_own, kv_other, prob, attn, grad_attn, heads_here):
    count, rows, width = queries.shape
    tall, wide = heads_here * rows, count * rows
    step = 16

    def body(q_ref, own_ref, oth_ref, prob_ref, attn_ref, grad_ref, dq_ref, down_ref, doth_ref, p_scr, d_scr, acc):
        sides = (own_ref, oth_ref)
        acc[...] = jnp.zeros_like(acc)
        for i in range(count):
            keys = (i + 1) * rows
            grad = grad_ref[i]
            stacked_q = stack_heads(q_ref[i], heads_here)
            stacked_g = stack_heads(grad, heads_here)
            product = grad.astype(F32) * attn_ref[i]
            head_of = lane_head(width, heads_here)
            delta = [
                jnp.sum(jnp.where(head_of == h, product, 0.0), axis=1, keepdims=True) for h in range(heads_here)
            ]
            for side in range(2):
                value = sides[side][:, :, width:].reshape(wide, width)[:keys]
                p_scr[side, :, :keys] = mm(stacked_g, value, NT)
            for h in range(heads_here):
                for at in range(0, rows, step):
                    lo = h * rows + at
                    for side in range(2):
                        weights = prob_ref[i, side, lo : lo + step, :keys].astype(F32)
                        shifted = p_scr[side, lo : lo + step, :keys] - delta[h][at : at + step]
                        d_scr[side, lo : lo + step, :keys] = (weights * shifted).astype(BF16)
            grad_q = jnp.zeros((tall, width), F32)
            for side in range(2):
                key = sides[side][:, :, :width].reshape(wide, width)[:keys]
                moved = d_scr[side, :, :keys]
                grad_q = grad_q + mm(moved, key, NN)
                acc[side, :keys, :width] += mm(moved, stacked_q, TN)
                acc[side, :keys, width:] += mm(prob_ref[i, side, :, :keys], stacked_g, TN)
            dq_ref[i] = (0.125 * fold_heads(grad_q, rows, heads_here)).astype(BF16)
        down_ref[...] = acc[0].reshape(count, rows, 2 * width)
        doth_ref[...] = acc[1].reshape(count, rows, 2 * width).astype(BF16)

    return pl.pallas_call(
        body,
        out_shape=(
            jax.ShapeDtypeStruct((count, rows, width), BF16),
            jax.ShapeDtypeStruct((count, rows, 2 * width), F32),
            jax.ShapeDtypeStruct((count, rows, 2 * width), BF16),
        ),
        in_specs=vmem_specs(6),
        out_specs=tuple(vmem_specs(3)),
        scratch_shapes=[
            pltpu.VMEM((2, tall, wide), F32),
            pltpu.VMEM((2, tall, wide), BF16),
            pltpu.VMEM((2, wide, 2 * width), F32),
        ],
        cost_estimate=cost(8 * tall * wide * count * width, 8 * count * tall * wide),
        name="attend_back",
    )(queries, kv_own, kv_other, prob, attn, grad_attn)


def gather_heads(pieces, live):
    return jnp.concatenate([pieces[k][:, :live] for k in range(pieces.shape[0])], axis=1)


def forward_call(pieces, layer_in, vectors, w_out, w_up, parts, live):
    count, rows, width = pieces.shape
    model, hidden = w_up.shape
    part = hidden // parts
    quarter = model // parts
    pad_q = -(-quarter // 128) * 128

    def body(piece_ref, in_ref, g2, b2, g3, b3, wo_ref, wu_ref, msg_ref, mid_ref, act_ref, slope_ref, n3_scr, n2_scr):
        @pl.when(pl.program_id(0) == 0)
        def _():
            unit2, _ = unit_norm(gather_heads(piece_ref, live).astype(F32))
            normed2 = (unit2 * g2[...] + b2[...]).astype(BF16)
            middle = in_ref[...].astype(F32) + mm(normed2, wo_ref[...], NN)
            mid_ref[...] = middle
            unit3, _ = unit_norm(middle)
            n3_scr[...] = (unit3 * g3[...] + b3[...]).astype(BF16)
            for r in range(parts):
                n2_scr[r, :, :quarter] = normed2[:, r * quarter : (r + 1) * quarter]
                if pad_q > quarter:
                    n2_scr[r, :, quarter:] = jnp.zeros((rows, pad_q - quarter), BF16)

        normed3 = n3_scr[...]
        upper = mm(normed3, wu_ref[...], NN)
        cumulative = 0.5 * (1.0 + lax.erf(upper * 0.7071067811865476))
        density = jnp.exp(-0.5 * upper * upper) * 0.3989422804014327
        act = (upper * cumulative).astype(BF16)
        act_ref[...] = act
        slope_ref[...] = (cumulative + upper * density).astype(BF16)
        msg_ref[0, :, :part] = act
        msg_ref[0, :, part : part + model] = normed3
        msg_ref[0, :, part + model :] = n2_scr[pl.program_id(0)]

    fixed = lambda *shape: pl.BlockSpec(shape, lambda r: (0,) * len(shape))
    return pl.pallas_call(
        body,
        grid=(parts,),
        out_shape=(
            jax.ShapeDtypeStruct((parts, rows, part + model + pad_q), BF16),
            jax.ShapeDtypeStruct((rows, model), F32),
            jax.ShapeDtypeStruct((rows, hidden), BF16),
            jax.ShapeDtypeStruct((rows, hidden), BF16),
        ),
        in_specs=[fixed(count, rows, width), fixed(rows, model)]
        + [fixed(1, model)] * 4
        + [fixed(model, model), pl.BlockSpec((model, part), lambda r: (0, r))],
        out_specs=(
            pl.BlockSpec((1, rows, part + model + pad_q), lambda r: (r, 0, 0)),
            fixed(rows, model),
            pl.BlockSpec((rows, part), lambda r: (0, r)),
            pl.BlockSpec((rows, part), lambda r: (0, r)),
        ),
        scratch_shapes=[pltpu.VMEM((rows, model), BF16), pltpu.VMEM((parts, rows, pad_q), BF16)],
        cost_estimate=cost(2 * rows * model * (model + hidden), 2 * model * (model + hidden) + 8 * rows * hidden, 2 * rows * hidden),
        name="token_forward",
    )(pieces, layer_in, *vectors, w_out, w_up)


def backward_call(pieces, middle, act, slope, grad_out, vectors, w_out, w_up, w_down, parts, live):
    count, rows, width = pieces.shape
    model, hidden = w_up.shape
    part = hidden // parts
    quarter = model // parts

    def body(
        piece_ref, mid_ref, act_ref, slope_ref, go_ref, g2, b2, g3, b3, wo_ref, wu_ref, wd_ref,
        out_ref, msg_ref, gmid_ref, gattn_ref, down_scr, n3_scr,
    ):
        r = pl.program_id(0)

        @pl.when(r == 0)
        def _():
            down_scr[...] = mid_ref[...]
            n3_scr[...] = jnp.zeros_like(n3_scr)

        go = go_ref[...]
        down_scr[...] += mm(act_ref[...], wd_ref[...], NN)
        grad_up = (mm(go, wd_ref[...], NT) * slope_ref[...].astype(F32)).astype(BF16)
        msg_ref[r, :rows, :part] = grad_up
        n3_scr[...] += mm(grad_up, wu_ref[...], NT)

        @pl.when(r == parts - 1)
        def _():
            out_ref[...] = down_scr[...].astype(BF16)
            grad3 = n3_scr[...]
            unit3, scale3 = unit_norm(mid_ref[...])
            grad_mid = go.astype(F32) + norm_back(grad3, g3[...], unit3, scale3)
            gmid_ref[...] = grad_mid
            proj = grad_mid.astype(BF16)
            grad2 = mm(proj, wo_ref[...], NT)
            unit2, scale2 = unit_norm(gather_heads(piece_ref, live).astype(F32))
            grad_attn = norm_back(grad2, g2[...], unit2, scale2).astype(BF16)
            for k in range(count):
                gattn_ref[k, :, :live] = grad_attn[:, k * live : (k + 1) * live]
                if width > live:
                    gattn_ref[k, :, live:] = jnp.zeros((rows, width - live), BF16)
            sums = [
                jnp.sum(grad2 * unit2, axis=0, keepdims=True),
                jnp.sum(grad2, axis=0, keepdims=True),
                jnp.sum(grad3 * unit3, axis=0, keepdims=True),
                jnp.sum(grad3, axis=0, keepdims=True),
            ]
            table = jnp.concatenate(sums + [jnp.zeros((12, model), F32)], axis=0).astype(BF16)
            for k in range(parts):
                msg_ref[k, :rows, part:] = proj
                msg_ref[k, rows:, part : part + quarter] = table[:, k * quarter : (k + 1) * quarter]

    fixed = lambda *shape: pl.BlockSpec(shape, lambda r: (0,) * len(shape))
    return pl.pallas_call(
        body,
        grid=(parts,),
        out_shape=(
            jax.ShapeDtypeStruct((rows, model), BF16),
            jax.ShapeDtypeStruct((parts, rows + 16, part + model), BF16),
            jax.ShapeDtypeStruct((rows, model), F32),
            jax.ShapeDtypeStruct((count, rows, width), BF16),
        ),
        in_specs=[
            fixed(count, rows, width),
            fixed(rows, model),
            pl.BlockSpec((rows, part), lambda r: (0, r)),
            pl.BlockSpec((rows, part), lambda r: (0, r)),
            fixed(rows, model),
        ]
        + [fixed(1, model)] * 4
        + [
            fixed(model, model),
            pl.BlockSpec((model, part), lambda r: (0, r)),
            pl.BlockSpec((part, model), lambda r: (r, 0)),
        ],
        out_specs=(
            fixed(rows, model),
            fixed(parts, rows + 16, part + model),
            fixed(rows, model),
            fixed(count, rows, width),
        ),
        scratch_shapes=[pltpu.VMEM((rows, model), F32), pltpu.VMEM((rows, model), F32)],
        cost_estimate=cost(2 * rows * model * (model + 3 * hidden), 2 * model * (model + 2 * hidden) + 8 * rows * hidden),
        name="token_backward",
    )(pieces, middle, act, slope, grad_out, *vectors, w_out, w_up, w_down)


def down_grad_call(place, sent, grads, parts, chips, part, model):
    rows = sent.shape[1]
    own = part // (2 * chips)

    def body(place_ref, sent_ref, grad_ref, keep_ref, send_ref, scr):
        core = place_ref[1]
        act = sent_ref[:, :, :part].reshape(parts * rows, part)
        scr[...] = mm(act, grad_ref[...].reshape(parts * rows, model), TN).reshape(chips, 2, own, model)
        for k in range(chips):
            keep_ref[k] = scr[k, core]
            send_ref[k] = scr[k, 1 - core].astype(BF16)

    return pl.pallas_call(
        body,
        out_shape=(
            jax.ShapeDtypeStruct((chips, own, model), F32),
            jax.ShapeDtypeStruct((chips, own, model), BF16),
        ),
        in_specs=[smem_spec()] + vmem_specs(2),
        out_specs=tuple(vmem_specs(2)),
        scratch_shapes=[pltpu.VMEM((chips, 2, own, model), F32)],
        cost_estimate=cost(2 * parts * rows * part * model, 2 * parts * rows * (part + model) + 4 * part * model),
        name="grad_down",
    )(place, sent, grads)


def up_grad_call(place, sent, back, parts, chips, part, model):
    rows = sent.shape[1]
    quarter = model // parts
    own = model // (parts * chips * 2)
    tall = (parts + 1) * own + 8

    def body(place_ref, sent_ref, back_ref, keep_ref, send_ref, up_scr, out_scr):
        core = place_ref[1]
        normed3 = sent_ref[:, :, part : part + model].reshape(parts * rows, model)
        normed2 = sent_ref[:, :, part + model :].reshape(parts * rows, sent.shape[2] - part - model)
        grad_up = back_ref[:, :rows, :part].reshape(parts * rows, part)
        proj = back_ref[:, :rows, part:].reshape(parts * rows, model)
        up_scr[...] = mm(normed3, grad_up, TN).reshape(parts, chips, 2, own, part)
        out_scr[...] = mm(normed2, proj, TN)[:quarter].reshape(chips, 2, own, model)
        table = jnp.zeros((8, quarter), F32)
        for r in range(parts):
            table = table + back_ref[r, rows : rows + 8, part : part + quarter].astype(F32)
        for k in range(chips):
            for side in range(2):
                at = (2 * k + side) * own
                piece = jnp.concatenate([table[:, at : at + own], jnp.zeros((8, model - own), F32)], axis=1)

                @pl.when(core == side)
                def _(piece=piece):
                    keep_ref[k, tall - 8 :, :] = piece

                @pl.when(core != side)
                def _(piece=piece):
                    send_ref[k, tall - 8 :, :] = piece.astype(BF16)

            kept = [up_scr[r, k, core] for r in range(parts)] + [out_scr[k, core]]
            keep_ref[k, : tall - 8, :] = jnp.concatenate(kept, axis=0)
            passed = [up_scr[r, k, 1 - core] for r in range(parts)] + [out_scr[k, 1 - core]]
            send_ref[k, : tall - 8, :] = jnp.concatenate(passed, axis=0).astype(BF16)

    return pl.pallas_call(
        body,
        out_shape=(
            jax.ShapeDtypeStruct((chips, tall, model), F32),
            jax.ShapeDtypeStruct((chips, tall, model), BF16),
        ),
        in_specs=[smem_spec()] + vmem_specs(2),
        out_specs=tuple(vmem_specs(2)),
        scratch_shapes=[
            pltpu.VMEM((parts, chips, 2, own, part), F32),
            pltpu.VMEM((chips, 2, own, model), F32),
        ],
        cost_estimate=cost(2 * parts * rows * (part + quarter) * model, 2 * parts * rows * (part + 2 * model) + 6 * part * model),
        name="grad_up_out",
    )(place, sent, back)


def qkv_grad_call(place, unit, grads, gain_col, bias_col, weight, parts, chips, live, width):
    count, rows, model = unit.shape
    own = model // (parts * chips * 2)

    def body(place_ref, unit_ref, grad_ref, gain_ref, bias_ref, weight_ref, keep_ref, send_ref, scr):
        core = place_ref[1]
        grad = grad_ref[...].reshape(count * rows, 3 * width)
        cross = mm(unit_ref[...].reshape(count * rows, model), grad, TN)
        total = jnp.sum(grad.astype(F32), axis=0, keepdims=True)
        weight_f = weight_ref[...].astype(F32)
        grad_gain = jnp.sum(weight_f * cross, axis=1, keepdims=True)
        grad_bias = jnp.sum(weight_f * total, axis=1, keepdims=True)
        lane = lax.broadcasted_iota(jnp.int32, (1, 3 * width), 1)
        made = gain_ref[...] * cross + bias_ref[...] * total
        made = jnp.where(lane == live, grad_gain, jnp.where(lane == live + 1, grad_bias, made))
        scr[...] = made.reshape(parts, chips, 2, own, 3 * width)
        for r in range(parts):
            keep_ref[r] = jnp.concatenate([scr[r, k, core] for k in range(chips)], axis=0)
            send_ref[r] = jnp.concatenate([scr[r, k, 1 - core] for k in range(chips)], axis=0).astype(BF16)

    return pl.pallas_call(
        body,
        out_shape=(
            jax.ShapeDtypeStruct((parts, chips * own, 3 * width), F32),
            jax.ShapeDtypeStruct((parts, chips * own, 3 * width), BF16),
        ),
        in_specs=[smem_spec()] + vmem_specs(5),
        out_specs=tuple(vmem_specs(2)),
        scratch_shapes=[pltpu.VMEM((parts, chips, 2, own, 3 * width), F32)],
        cost_estimate=cost(2 * count * rows * model * 3 * width, 20 * model * width),
        name="grad_qkv",
    )(place, unit, grads, gain_col, bias_col, weight)


def input_grad_call(pieces, layer_in, grad_mid, gain, w_query, w_key, w_value, live, width):
    count, rows, _ = pieces.shape
    model = layer_in.shape[1]

    def body(piece_ref, in_ref, gmid_ref, gain_ref, wq_ref, wk_ref, wv_ref, out_ref):
        grad = jnp.zeros((rows, model), F32)
        for at, w_ref in enumerate((wq_ref, wk_ref, wv_ref)):
            part = jnp.concatenate(
                [piece_ref[k, :, at * width : at * width + live] for k in range(count)], axis=1
            )
            grad = grad + mm(part, w_ref[...], NT)
        unit, scale = unit_norm(in_ref[...].astype(F32))
        out_ref[...] = (gmid_ref[...] + norm_back(grad, gain_ref[...], unit, scale)).astype(BF16)

    return pl.pallas_call(
        body,
        out_shape=jax.ShapeDtypeStruct((rows, model), BF16),
        in_specs=vmem_specs(7),
        out_specs=pl.BlockSpec(memory_space=pltpu.VMEM),
        cost_estimate=cost(6 * rows * model * model, 6 * model * model),
        name="grad_inputs",
    )(pieces, layer_in, grad_mid, gain, w_query, w_key, w_value)


def swap_core(value):
    return lax.ppermute(value, "core", [(0, 1), (1, 0)])


def swap_chip(value, bit, chips):
    return lax.ppermute(value, "chip", [(k, k ^ bit) for k in range(chips)])


def exchange(value, axis):
    return lax.all_to_all(value, axis, 0, 0, tiled=True)


def gather_chips(block, chips):
    found = {0: block}
    bit = chips // 2
    while bit >= 1:
        for k in sorted(found):
            found[k | bit] = swap_chip(found[k], bit, chips)
        bit //= 2
    return [found[k] for k in range(chips)]


def scatter_chips(value, z_index, chips):
    bit = 1
    while bit < chips:
        pairs = value.reshape((value.shape[0] // 2, 2) + value.shape[1:])
        mine = (z_index // bit) % 2
        away = lax.dynamic_index_in_dim(pairs, 1 - mine, 1, keepdims=False).astype(BF16)
        stay = lax.dynamic_index_in_dim(pairs, mine, 1, keepdims=False)
        value = stay + swap_chip(away, bit, chips).astype(F32)
        bit *= 2
    return value[0]


def fast_shards(
    inputs, doc_lengths, ln1_gain, ln1_bias, w_query, w_key, w_value, ln2_gain, ln2_bias, w_out,
    ln3_gain, ln3_bias, w_up, w_down, out_grad,
):
    rows, model = inputs.shape[1:]
    chips, parts = lax.axis_size("chip"), lax.axis_size("rows")
    z_index, core = lax.axis_index("chip"), lax.axis_index("core")
    heads_here = HEADS // chips
    live = heads_here * HEAD_DIM
    width = -(-live // 128) * 128
    hidden = w_up.shape[1]
    part = hidden // parts
    own = model // (parts * chips * 2)
    place = jnp.stack([z_index, core]).astype(jnp.int32)
    layer_in = inputs[0]
    as_row = lambda v: v.reshape(1, model)

    blocks = gather_chips(layer_in, chips)
    pos = (2 * z_index + core) * rows + jnp.arange(rows, dtype=jnp.int32)
    valid = pos < jnp.sum(doc_lengths[0])
    grad_out = jnp.where(valid[:, None], out_grad[0], jnp.zeros_like(out_grad[0]))
    grads_plane = exchange(jnp.broadcast_to(grad_out[None], (parts, rows, model)), "rows")

    def columns(weight):
        mine = lax.dynamic_slice_in_dim(weight, z_index * live, live, 1)
        return jnp.pad(mine, ((0, 0), (0, width - live)))

    w_heads = jnp.concatenate([columns(w_query), columns(w_key), columns(w_value)], axis=1)

    queries, kv_own, unit_one = qkv_call(blocks, place, as_row(ln1_gain), as_row(ln1_bias), w_heads, width)
    kv_other = swap_core(kv_own)
    attn_send, attn_heads, prob = attend_call(place, doc_lengths, queries, kv_own, kv_other, heads_here)
    pieces = exchange(attn_send, "chip")

    vectors = tuple(as_row(v) for v in (ln2_gain, ln2_bias, ln3_gain, ln3_bias))
    sent, middle, act, slope = forward_call(pieces, layer_in, vectors, w_out, w_up, parts, live)
    sent = exchange(sent, "rows")
    output, back, grad_mid, grad_attn = backward_call(
        pieces, middle, act, slope, grad_out, vectors, w_out, w_up, w_down, parts, live
    )
    grad_heads = exchange(grad_attn, "chip")
    back = exchange(back, "rows")
    down_keep, down_send = down_grad_call(place, sent, grads_plane, parts, chips, part, model)
    grad_w_down = scatter_chips(down_keep + swap_core(down_send).astype(F32), z_index, chips)

    grad_q, grad_kv, grad_kv_other = attend_back_call(
        queries, kv_own, kv_other, prob, attn_heads, grad_heads, heads_here
    )
    grad_kv = (grad_kv + swap_core(grad_kv_other).astype(F32)).astype(BF16)
    grad_qkv = jnp.concatenate([grad_q, grad_kv], axis=2)
    grad_pieces = exchange(grad_qkv, "chip")

    qkv_keep, qkv_send = qkv_grad_call(
        place, unit_one, grad_qkv, ln1_gain.reshape(model, 1), ln1_bias.reshape(model, 1), w_heads,
        parts, chips, live, width,
    )
    qkv_sum = (qkv_keep + swap_core(qkv_send).astype(F32)).astype(BF16)
    qkv_sum = jnp.sum(exchange(qkv_sum, "rows").astype(F32), axis=0).astype(BF16)
    qkv_all = exchange(qkv_sum.reshape(chips, own, 3 * width), "chip")

    up_keep, up_send = up_grad_call(place, sent, back, parts, chips, part, model)
    up_sum = scatter_chips(up_keep + swap_core(up_send).astype(F32), z_index, chips)
    up_all = exchange(up_sum[: parts * own].astype(BF16).reshape(parts, own, part), "rows")
    grad_w_up = up_all.astype(F32).transpose(1, 0, 2).reshape(own, hidden)
    grad_w_out = up_sum[parts * own : (parts + 1) * own]
    norm_sums = up_sum[(parts + 1) * own :, :own]

    grad_inputs = input_grad_call(
        grad_pieces, layer_in, grad_mid, as_row(ln1_gain), w_query, w_key, w_value, live, width
    )
    qkv_f = qkv_all.astype(F32)

    def final_columns(at):
        return qkv_f[:, :, at * width : at * width + live].transpose(1, 0, 2).reshape(own, model)

    norm_one = jnp.sum(qkv_f[:, :, live : live + 2], axis=0)
    return (
        output[None],
        grad_inputs[None],
        norm_one[:, 0],
        norm_one[:, 1],
        final_columns(0),
        final_columns(1),
        final_columns(2),
        norm_sums[0],
        norm_sums[1],
        grad_w_out,
        norm_sums[2],
        norm_sums[3],
        grad_w_up,
        grad_w_down,
    )


def takes_fast(mesh):
    seq = mesh.shape["seq"]
    chips = seq // 2
    return seq % 2 == 0 and chips & (chips - 1) == 0 and HEADS % max(chips, 1) == 0


def solution(mesh):
    if takes_fast(mesh):
        parts, seq = mesh.shape["rows"], mesh.shape["seq"]
        split = jax.sharding.Mesh(mesh.devices.reshape(parts, seq // 2, 2), ("rows", "chip", "core"))
        return mapped(fast_shards, split, ("chip", "core"))
    return mapped(shards, mesh, "seq")
```

```python
import math

import jax
import jax.numpy as jnp
from jax import lax
from jax.experimental import pallas as pl
from jax.experimental.pallas import tpu as pltpu
from jax.sharding import PartitionSpec as P

HEADS = 12
HEAD_DIM = 64


segment_pairs = ((2048, 1), (4096, 2), (8192, 4), (16384, 6))
masked_value = -1e30


def layer_norm(vector, gain_vec, bias_vec):
    row_mean = jnp.mean(vector, axis=-1, keepdims=True)
    centered = vector - row_mean
    row_var = jnp.mean(centered * centered, axis=-1, keepdims=True)
    return centered * lax.rsqrt(row_var + 1e-05) * gain_vec + bias_vec


def doc_of(positions, doc_ends):
    return jnp.sum((positions[:, None] >= doc_ends[None, :]).astype(jnp.int32), axis=1)


def pair_terms(query_pos, key_pos, query_doc, key_doc, head_count):
    head_ids = jnp.arange(head_count, dtype=jnp.int32)
    multiplicity = jnp.zeros((head_count, query_pos.shape[0], key_pos.shape[0]), jnp.float32)
    for seg_width, dilation in segment_pairs:
        same_seg = query_pos[:, None] // seg_width == key_pos[None, :] // seg_width
        query_pick = (query_pos % seg_width % dilation)[None, :] == (head_ids % dilation)[:, None]
        key_pick = (key_pos % seg_width % dilation)[None, :] == (head_ids % dilation)[:, None]
        joined = same_seg[None] & query_pick[:, :, None] & key_pick[:, None, :]
        multiplicity = multiplicity + joined.astype(jnp.float32)
    allowed = (key_pos[None, :] <= query_pos[:, None]) & (query_doc[:, None] == key_doc[None, :])
    allowed = allowed[None] & (multiplicity > 0.0)
    return (jnp.log(jnp.maximum(multiplicity, 1.0)), allowed)


def rows_inner(left, right):
    return lax.dot_general(
        left, right, (((0,), (0,)), ((), ())), preferred_element_type=jnp.float32
    )


def cols_inner(left, right):
    return lax.dot_general(
        left, right, (((1,), (1,)), ((), ())), preferred_element_type=jnp.float32
    )


def over_blocks(state, piece, step_fn):
    total_rows = piece[0].shape[0]
    block_rows = math.gcd(total_rows, 512)
    block_total = total_rows // block_rows
    split = tuple((part.reshape((block_total, block_rows) + part.shape[1:]) for part in piece))

    def inner(carried, block_item):
        return (step_fn(carried, block_item[1], block_item[0] * block_rows), None)

    result, unused = lax.scan(inner, state, (jnp.arange(block_total, dtype=jnp.int32), split))
    return result


def add_rows(buffer, start_pos, addend):
    current = lax.dynamic_slice_in_dim(buffer, start_pos, addend.shape[0], 0)
    return lax.dynamic_update_slice_in_dim(buffer, current + addend, start_pos, 0)


def shards(
    inputs,
    doc_lengths,
    ln1_gain,
    ln1_bias,
    w_query,
    w_key,
    w_value,
    ln2_gain,
    ln2_bias,
    w_out,
    ln3_gain,
    ln3_bias,
    w_up,
    w_down,
    out_grad,
):
    tok_rows = inputs.shape[1]
    head_count = HEADS
    head_size = HEAD_DIM
    model_width = inputs.shape[2]
    row_total = tok_rows * lax.axis_size("seq")
    layer_in = inputs[0].astype(jnp.float32)
    doc_ends = jnp.cumsum(doc_lengths[0])
    first_pos = lax.axis_index("seq") * tok_rows
    query_pos = first_pos + jnp.arange(tok_rows, dtype=jnp.int32)
    query_doc = doc_of(query_pos, doc_ends)
    valid = (query_doc < doc_lengths.shape[1]).astype(jnp.float32)
    first_norm, first_back = jax.vjp(layer_norm, layer_in, ln1_gain, ln1_bias)
    normed_one = first_norm.astype(jnp.bfloat16)
    queries = jnp.dot(normed_one, w_query, preferred_element_type=jnp.float32).astype(jnp.bfloat16)
    keys_local = jnp.dot(normed_one, w_key, preferred_element_type=jnp.float32).astype(jnp.bfloat16)
    values_local = jnp.dot(normed_one, w_value, preferred_element_type=jnp.float32).astype(
        jnp.bfloat16
    )
    query_heads = queries.reshape(tok_rows, head_count, head_size)

    def key_block_terms(key_start, key_count):
        key_pos = key_start + jnp.arange(key_count, dtype=jnp.int32)
        key_doc = doc_of(key_pos, doc_ends)
        return pair_terms(query_pos, key_pos, query_doc, key_doc, head_count)

    def with_pruning(step_fn):

        def wrapped(state, parts, start_pos):
            return step_fn(state, parts, start_pos)

        return wrapped

    def forward_step(state, parts, key_start):
        run_max, run_total, run_acc = state
        key_blk = parts[0].reshape(-1, head_count, head_size)
        value_blk = parts[1].reshape(-1, head_count, head_size)
        log_mult, allowed = key_block_terms(key_start, key_blk.shape[0])
        scores = 0.125 * jnp.einsum(
            "qhd,khd->hqk", query_heads, key_blk, preferred_element_type=jnp.float32
        )
        logits = jnp.where(allowed, scores + log_mult, masked_value)
        new_max = jnp.maximum(run_max, jnp.max(logits, axis=-1))
        weights = jnp.where(allowed, jnp.exp(logits - new_max[..., None]), 0.0)
        factor = jnp.exp(run_max - new_max)
        run_total = run_total * factor + jnp.sum(weights, axis=-1)
        run_acc = run_acc * factor[..., None] + jnp.einsum(
            "hqk,khd->hqd",
            weights.astype(jnp.bfloat16),
            value_blk,
            preferred_element_type=jnp.float32,
        )
        return (new_max, run_total, run_acc)

    forward_pruned = with_pruning(forward_step)
    start_state = (
        jnp.full((head_count, tok_rows), masked_value, jnp.float32),
        jnp.zeros((head_count, tok_rows), jnp.float32),
        jnp.zeros((head_count, tok_rows, head_size), jnp.float32),
    )
    final_state = over_blocks(
        start_state,
        (
            lax.all_gather(keys_local, "seq", axis=0, tiled=True),
            lax.all_gather(values_local, "seq", axis=0, tiled=True),
        ),
        forward_pruned,
    )
    run_max, run_total, run_acc = final_state
    row_lse = run_max + jnp.log(run_total)
    attn = (run_acc / run_total[..., None]).transpose(1, 0, 2).reshape(tok_rows, model_width)
    second_norm, second_back = jax.vjp(layer_norm, attn, ln2_gain, ln2_bias)
    normed_two = second_norm.astype(jnp.bfloat16)
    middle = layer_in + jnp.dot(normed_two, w_out, preferred_element_type=jnp.float32)
    third_norm, third_back = jax.vjp(layer_norm, middle, ln3_gain, ln3_bias)
    normed_three = third_norm.astype(jnp.bfloat16)
    upper = jnp.dot(normed_three, w_up, preferred_element_type=jnp.float32)
    activated_f, gelu_back = jax.vjp(
        lambda upper_in: jax.nn.gelu(upper_in, approximate=False), upper
    )
    activated = activated_f.astype(jnp.bfloat16)
    layer_out = middle + jnp.dot(activated, w_down, preferred_element_type=jnp.float32)
    grad_out = out_grad[0].astype(jnp.float32) * valid[:, None]
    grad_branch = grad_out.astype(jnp.bfloat16)
    grad_w_down = rows_inner(activated, grad_branch)
    grad_act = cols_inner(grad_branch, w_down)
    grad_upper = gelu_back(grad_act)[0].astype(jnp.bfloat16)
    grad_w_up = rows_inner(normed_three, grad_upper)
    grad_n3 = cols_inner(grad_upper, w_up)
    grad_mid_norm, grad_ln3_gain, grad_ln3_bias = third_back(grad_n3)
    grad_middle = grad_out + grad_mid_norm
    grad_proj = grad_middle.astype(jnp.bfloat16)
    grad_w_out = rows_inner(normed_two, grad_proj)
    grad_n2 = cols_inner(grad_proj, w_out)
    grad_attn_f, grad_ln2_gain, grad_ln2_bias = second_back(grad_n2)
    grad_attn = grad_attn_f.astype(jnp.bfloat16)
    grad_heads = grad_attn.reshape(tok_rows, head_count, head_size)
    row_delta = jnp.sum(
        (grad_attn.astype(jnp.float32) * attn).reshape(tok_rows, head_count, head_size), axis=-1
    )

    def backward_step(state, parts, key_start):
        grad_q_acc, grad_k_rows, grad_v_rows = state
        key_blk = parts[0].reshape(-1, head_count, head_size)
        value_blk = parts[1].reshape(-1, head_count, head_size)
        key_count = key_blk.shape[0]
        log_mult, allowed = key_block_terms(key_start, key_count)
        scores = 0.125 * jnp.einsum(
            "qhd,khd->hqk", query_heads, key_blk, preferred_element_type=jnp.float32
        )
        logits = jnp.where(allowed, scores + log_mult, masked_value)
        weights = jnp.where(allowed, jnp.exp(logits - row_lse[..., None]), 0.0)
        grad_weights = jnp.einsum(
            "qhd,khd->hqk", grad_heads, value_blk, preferred_element_type=jnp.float32
        )
        grad_scores = (weights * (grad_weights - row_delta.T[..., None])).astype(jnp.bfloat16)
        grad_q_acc = grad_q_acc + 0.125 * jnp.einsum(
            "hqk,khd->qhd", grad_scores, key_blk, preferred_element_type=jnp.float32
        )
        value_part = jnp.einsum(
            "hqk,qhd->khd",
            weights.astype(jnp.bfloat16),
            grad_heads,
            preferred_element_type=jnp.float32,
        ).reshape(key_count, model_width)
        key_part = 0.125 * jnp.einsum(
            "hqk,qhd->khd", grad_scores, query_heads, preferred_element_type=jnp.float32
        ).reshape(key_count, model_width)
        grad_k_rows = add_rows(grad_k_rows, key_start, key_part)
        grad_v_rows = add_rows(grad_v_rows, key_start, value_part)
        return (grad_q_acc, grad_k_rows, grad_v_rows)

    backward_pruned = with_pruning(backward_step)
    zero_state = (
        jnp.zeros((tok_rows, head_count, head_size), jnp.float32),
        jnp.zeros((row_total, model_width), jnp.float32),
        jnp.zeros((row_total, model_width), jnp.float32),
    )
    back_state = over_blocks(
        zero_state,
        (
            lax.all_gather(keys_local, "seq", axis=0, tiled=True),
            lax.all_gather(values_local, "seq", axis=0, tiled=True),
        ),
        backward_pruned,
    )
    grad_q_acc, grad_k_rows, grad_v_rows = back_state
    grad_k_acc, grad_v_acc = (
        lax.psum_scatter(
            grad_k_rows.astype(jnp.bfloat16), "seq", scatter_dimension=0, tiled=True
        ).astype(jnp.float32),
        lax.psum_scatter(
            grad_v_rows.astype(jnp.bfloat16), "seq", scatter_dimension=0, tiled=True
        ).astype(jnp.float32),
    )
    grad_queries = grad_q_acc.reshape(tok_rows, model_width).astype(jnp.bfloat16)
    grad_keys = grad_k_acc.astype(jnp.bfloat16)
    grad_values = grad_v_acc.astype(jnp.bfloat16)
    grad_w_query = rows_inner(normed_one, grad_queries)
    grad_w_key = rows_inner(normed_one, grad_keys)
    grad_w_value = rows_inner(normed_one, grad_values)
    grad_n1 = (
        cols_inner(grad_queries, w_query)
        + cols_inner(grad_keys, w_key)
        + cols_inner(grad_values, w_value)
    )
    grad_in_norm, grad_ln1_gain, grad_ln1_bias = first_back(grad_n1)
    grad_inputs = (grad_middle + grad_in_norm).astype(jnp.bfloat16)
    summed = (
        lax.psum_scatter(grad_ln1_gain, ("rows", "seq"), scatter_dimension=0, tiled=True),
        lax.psum_scatter(grad_ln1_bias, ("rows", "seq"), scatter_dimension=0, tiled=True),
        lax.psum_scatter(grad_w_query, ("rows", "seq"), scatter_dimension=0, tiled=True),
        lax.psum_scatter(grad_w_key, ("rows", "seq"), scatter_dimension=0, tiled=True),
        lax.psum_scatter(grad_w_value, ("rows", "seq"), scatter_dimension=0, tiled=True),
        lax.psum_scatter(grad_ln2_gain, ("rows", "seq"), scatter_dimension=0, tiled=True),
        lax.psum_scatter(grad_ln2_bias, ("rows", "seq"), scatter_dimension=0, tiled=True),
        lax.psum_scatter(grad_w_out, ("rows", "seq"), scatter_dimension=0, tiled=True),
        lax.psum_scatter(grad_ln3_gain, ("rows", "seq"), scatter_dimension=0, tiled=True),
        lax.psum_scatter(grad_ln3_bias, ("rows", "seq"), scatter_dimension=0, tiled=True),
        lax.psum_scatter(grad_w_up, ("rows", "seq"), scatter_dimension=0, tiled=True),
        lax.psum_scatter(grad_w_down, ("rows", "seq"), scatter_dimension=0, tiled=True),
    )
    return (
        layer_out.astype(jnp.bfloat16)[None],
        grad_inputs[None],
        summed[0],
        summed[1],
        summed[2],
        summed[3],
        summed[4],
        summed[5],
        summed[6],
        summed[7],
        summed[8],
        summed[9],
        summed[10],
        summed[11],
    )


def mapped(step, mesh, seq):
    spread = P(("rows",) + (seq if isinstance(seq, tuple) else (seq,)))
    tokens, plain = P("rows", seq, None), P()
    weights = P(spread[0], None)
    return jax.shard_map(
        step,
        mesh=mesh,
        in_specs=(tokens, P("rows", None)) + (plain,) * 12 + (tokens,),
        out_specs=(tokens, tokens, spread, spread, weights, weights, weights, spread, spread, weights)
        + (spread, spread, weights, weights),
        check_vma=False,
    )


F32 = jnp.float32
PACE = 1e6
BF16 = jnp.bfloat16
NT = (((1,), (1,)), ((), ()))
TN = (((0,), (0,)), ((), ()))
NN = (((1,), (0,)), ((), ()))


def mm(left, right, dims):
    return lax.dot_general(left, right, dims, preferred_element_type=F32)


def unit_norm(vector):
    centered = vector - jnp.mean(vector, axis=-1, keepdims=True)
    scale = lax.rsqrt(jnp.mean(centered * centered, axis=-1, keepdims=True) + 1e-05)
    return centered * scale, scale


def norm_back(grad, gain, unit, scale):
    weighted = grad * gain
    mean_w = jnp.mean(weighted, axis=-1, keepdims=True)
    mean_wu = jnp.mean(weighted * unit, axis=-1, keepdims=True)
    return scale * (weighted - mean_w - unit * mean_wu)


def shape(dtype, *dims):
    return jax.ShapeDtypeStruct(dims, dtype)


def row(ref):
    return ref[...].reshape(1, ref.shape[0])


def size_of(item):
    total = jnp.dtype(item.dtype).itemsize
    for dim in item.shape:
        total *= dim
    return total


def kernel(body, outs, scalars, operands, scratch=(), micros=2.0, name=None):
    single = not isinstance(outs, (tuple, list))
    listed = (outs,) if single else tuple(outs)
    vmem = pl.BlockSpec(memory_space=pltpu.VMEM)
    smem = pl.BlockSpec(memory_space=pltpu.SMEM)
    moved = sum(size_of(v) for v in (*operands, *listed))
    held = sum(size_of(v) for v in scratch)
    return pl.pallas_call(
        body,
        out_shape=outs if single else listed,
        in_specs=[smem] * len(scalars) + [vmem] * len(operands),
        out_specs=vmem if single else (vmem,) * len(listed),
        scratch_shapes=[pltpu.VMEM(v.shape, v.dtype) for v in scratch],
        compiler_params=pltpu.CompilerParams(vmem_limit_bytes=min(60 << 20, (moved + held) * 5 // 4 + (6 << 20))),
        cost_estimate=pl.CostEstimate(flops=int(micros * PACE), bytes_accessed=int(micros * PACE / 1e3), transcendentals=0),
        name=name,
    )(*scalars, *operands)


def packed_rows(rows, live):
    return rows * live // 128


def pack(block):
    rows, live = block.shape
    whole = live // 128
    pieces = [block[:, 128 * j : 128 * (j + 1)] for j in range(whole)]
    if live % 128:
        rest = block[:, 128 * whole :]
        pieces.append(jnp.concatenate([rest[: rows // 2], rest[rows // 2 :]], axis=1))
    return jnp.concatenate(pieces, axis=0)


def unpack(block, rows, live):
    whole = live // 128
    pieces = [block[rows * j : rows * (j + 1)] for j in range(whole)]
    if live % 128:
        rest = block[rows * whole :]
        pieces.append(jnp.concatenate([rest[:, :64], rest[:, 64:]], axis=0))
    return jnp.concatenate(pieces, axis=1)


def mask_call(place, lengths, out_grad):
    rows, model = out_grad.shape

    def body(place_ref, len_ref, in_ref, out_ref):
        last = jnp.int32(0)
        for d in range(lengths.shape[1]):
            last = last + len_ref[0, d]
        pos = lax.broadcasted_iota(jnp.int32, (rows, 1), 0) + (2 * place_ref[0] + place_ref[1]) * rows
        out_ref[...] = jnp.where(pos < last, in_ref[...].astype(F32), 0.0).astype(BF16)

    return kernel(body, shape(BF16, rows, model), (place, lengths), (out_grad,), micros=0.7, name="mask_grad")


def qkv_call(blocks, gain, bias, weight, width):
    count = len(blocks)
    rows, model = blocks[0].shape

    def body(*refs):
        xs, (gain_ref, bias_ref, weight_ref, q_ref, kv_ref, unit_ref) = refs[:count], refs[count:]
        for k in range(count):
            unit, _ = unit_norm(xs[k][...].astype(F32))
            normed = (unit * row(gain_ref) + row(bias_ref)).astype(BF16)
            made = mm(normed, weight_ref[...], NN)
            q_ref[k] = (made[:, :width].astype(BF16).astype(F32) * 0.125).astype(BF16)
            kv_ref[k] = made[:, width:].astype(BF16)
            unit_ref[k] = unit.astype(BF16)

    outs = (
        shape(BF16, count, rows, width),
        shape(BF16, count, rows, 2 * width),
        shape(BF16, count, rows, model),
    )
    return kernel(body, outs, (), (*blocks, gain, bias, weight), micros=1.2 * count, name="qkv_heads")


def lane_head(lanes):
    return lax.broadcasted_iota(jnp.int32, (1, lanes), 1) // HEAD_DIM


def residue(pos_f, modulus):
    return pos_f - modulus * jnp.floor((pos_f + 0.5) * (1.0 / modulus))


def stack_heads(block, heads_here):
    head_of = lane_head(block.shape[1])
    return jnp.concatenate(
        [jnp.where(head_of == h, block, jnp.zeros_like(block)) for h in range(heads_here)], axis=0
    )


def fold_heads(stacked, rows, heads_here):
    head_of = lane_head(stacked.shape[1])
    total = jnp.zeros((rows, stacked.shape[1]), stacked.dtype)
    for h in range(heads_here):
        total = jnp.where(head_of == h, stacked[h * rows : (h + 1) * rows], total)
    return total


def attend_call(place, lengths, groups, queries, kv_own, kv_other, heads_here):
    count = sum(len(g) for g in groups)
    rows, width = queries[0].shape[1:]
    tall, wide = heads_here * rows, count * rows
    docs = lengths.shape[1]
    step = 16
    n = len(groups)

    def body(place_ref, len_ref, *refs):
        q_in, own_in, oth_in = refs[:n], refs[n : 2 * n], refs[2 * n : 3 * n]
        out_ref, prob_ref, q_ref, own_ref, oth_ref = refs[3 * n : 3 * n + 5]
        msgs, (s_scr, m_scr, hot_scr, send_scr) = refs[3 * n + 5 : 3 * n + 5 + count], refs[3 * n + 5 + count :]
        z_index, core = place_ref[0], place_ref[1]
        for g, ks in enumerate(groups):
            for j, k in enumerate(ks):
                q_ref[z_index ^ k] = q_in[g][j]
                own_ref[z_index ^ k] = own_in[g][j]
                oth_ref[z_index ^ k] = oth_in[g][j]
        sides = (own_ref, oth_ref)
        cores = (core, 1 - core)
        lane = lax.broadcasted_iota(jnp.int32, (rows, 128), 1).astype(F32)
        for side in range(2):
            for b in range(count):
                pos = lax.broadcasted_iota(jnp.int32, (rows, 1), 0) + (2 * b + cores[side]) * rows
                hot = (residue(pos.astype(F32), 12.0) == lane).astype(F32)
                hot_scr[side, b * rows : (b + 1) * rows, :] = hot.astype(BF16)
        for i in range(count):
            keys = (i + 1) * rows
            pos = lax.broadcasted_iota(jnp.int32, (rows, 1), 0) + (2 * i + core) * rows
            pos_f = pos.astype(F32)
            begin = jnp.zeros_like(pos)
            run = jnp.int32(0)
            for d in range(docs):
                run = run + len_ref[0, d]
                begin = jnp.where(pos >= run, run, begin)
            tables = []
            for h in range(heads_here):
                head = (z_index * heads_here + h).astype(F32)
                table = jnp.ones((rows, 128), F32)
                for r in (2.0, 4.0, 6.0):
                    mine = residue(head, r)
                    pick_q = (residue(pos_f, r) == mine).astype(F32)
                    pick_k = (residue(lane, r) == mine).astype(F32)
                    table = table + pick_q * pick_k
                tables.append(jnp.where(lane < 12.0, table, 0.0))
            table = jnp.concatenate(tables, axis=0).astype(BF16)
            stacked = stack_heads(q_ref[i], heads_here)
            for side in range(2):
                key = sides[side][:, :, :width].reshape(wide, width)[:keys]
                s_scr[side, :, :keys] = mm(stacked, key, NT)
                m_scr[side, :, :keys] = mm(table, hot_scr[side, :keys], NT)
            key_pos = [
                jnp.concatenate(
                    [
                        lax.broadcasted_iota(jnp.int32, (1, rows), 1) + (2 * b + cores[side]) * rows
                        for b in range(i + 1)
                    ],
                    axis=1,
                )
                for side in range(2)
            ]
            for h in range(heads_here):
                for at in range(0, rows, step):
                    lo = h * rows + at
                    pos_c, begin_c = pos[at : at + step], begin[at : at + step]
                    masked = []
                    for side in range(2):
                        ok = (key_pos[side] <= pos_c) & (key_pos[side] >= begin_c)
                        masked.append(jnp.where(ok, s_scr[side, lo : lo + step, :keys], masked_value))
                    top = jnp.maximum(
                        jnp.max(masked[0], axis=1, keepdims=True), jnp.max(masked[1], axis=1, keepdims=True)
                    )
                    parts = [
                        jnp.exp(masked[side] - top) * m_scr[side, lo : lo + step, :keys] for side in range(2)
                    ]
                    total = jnp.sum(parts[0], axis=1, keepdims=True) + jnp.sum(parts[1], axis=1, keepdims=True)
                    inverse = 1.0 / total
                    for side in range(2):
                        prob_ref[i, side, lo : lo + step, :keys] = (parts[side] * inverse).astype(BF16)
            mixed = jnp.zeros((tall, width), F32)
            for side in range(2):
                value = sides[side][:, :, width:].reshape(wide, width)[:keys]
                mixed = mixed + mm(prob_ref[i, side, :, :keys], value, NN)
            result = fold_heads(mixed, rows, heads_here)
            out_ref[i] = result
            send_scr[i] = pack(result.astype(BF16)[:, :live])
        for k in range(count):
            msgs[k][...] = send_scr[z_index ^ k]

    live = heads_here * HEAD_DIM
    outs = (
        shape(F32, count, rows, width),
        shape(BF16, count, 2, tall, wide),
        shape(BF16, count, rows, width),
        shape(BF16, count, rows, 2 * width),
        shape(BF16, count, rows, 2 * width),
    ) + (shape(BF16, packed_rows(rows, live), 128),) * count
    scratch = (
        shape(F32, 2, tall, wide),
        shape(F32, 2, tall, wide),
        shape(BF16, 2, wide, 128),
        shape(BF16, count, packed_rows(rows, live), 128),
    )
    operands = (*queries, *kv_own, *kv_other)
    found = kernel(
        body, outs, (place, lengths), operands, scratch, micros=6.0, name="attend"
    )
    return found[0], found[1:5], list(found[5:])


def attend_back_call(place, queries, kv_own, kv_other, prob, attn, grads, heads_here):
    count, rows, width = queries.shape
    tall, wide = heads_here * rows, count * rows
    step = 16

    live = heads_here * HEAD_DIM

    def body(place_ref, q_ref, own_ref, oth_ref, prob_ref, attn_ref, *refs):
        grad_refs, (dq_ref, down_ref, doth_ref, p_scr, d_scr, acc, grad_ref) = refs[:count], refs[count:]
        sides = (own_ref, oth_ref)
        acc[...] = jnp.zeros_like(acc)
        grad_ref[...] = jnp.zeros_like(grad_ref)
        for k in range(count):
            grad_ref[place_ref[0] ^ k, :, :live] = unpack(grad_refs[k][...], rows, live)
        for i in range(count):
            keys = (i + 1) * rows
            grad = grad_ref[i]
            stacked_q = stack_heads(q_ref[i], heads_here)
            stacked_g = stack_heads(grad, heads_here)
            product = grad.astype(F32) * attn_ref[i]
            head_of = lane_head(width)
            delta = [
                jnp.sum(jnp.where(head_of == h, product, 0.0), axis=1, keepdims=True) for h in range(heads_here)
            ]
            for side in range(2):
                value = sides[side][:, :, width:].reshape(wide, width)[:keys]
                p_scr[side, :, :keys] = mm(stacked_g, value, NT)
            for h in range(heads_here):
                for at in range(0, rows, step):
                    lo = h * rows + at
                    for side in range(2):
                        weights = prob_ref[i, side, lo : lo + step, :keys].astype(F32)
                        shifted = p_scr[side, lo : lo + step, :keys] - delta[h][at : at + step]
                        d_scr[side, lo : lo + step, :keys] = (weights * shifted).astype(BF16)
            grad_q = jnp.zeros((tall, width), F32)
            for side in range(2):
                key = sides[side][:, :, :width].reshape(wide, width)[:keys]
                moved = d_scr[side, :, :keys]
                grad_q = grad_q + mm(moved, key, NN)
                acc[side, :keys, :width] += mm(moved, stacked_q, TN)
                acc[side, :keys, width:] += mm(prob_ref[i, side, :, :keys], stacked_g, TN)
            dq_ref[i] = (0.125 * fold_heads(grad_q, rows, heads_here)).astype(BF16)
        down_ref[...] = acc[0].reshape(count, rows, 2 * width)
        doth_ref[...] = acc[1].reshape(count, rows, 2 * width).astype(BF16)

    outs = (
        shape(BF16, count, rows, width),
        shape(F32, count, rows, 2 * width),
        shape(BF16, count, rows, 2 * width),
    )
    scratch = (
        shape(F32, 2, tall, wide),
        shape(BF16, 2, tall, wide),
        shape(F32, 2, wide, 2 * width),
        shape(BF16, count, rows, width),
    )
    operands = (queries, kv_own, kv_other, prob, attn, *grads)
    return kernel(body, outs, (place,), operands, scratch, micros=6.0, name="attend_back")


def join_call(place, grad_q, grad_kv, arrived, live):
    count, rows, width = grad_q.shape

    def body(place_ref, q_ref, kv_ref, in_ref, out_ref, *rest):
        msgs, scr = rest[:count], rest[count]
        for b in range(count):
            both = (kv_ref[b] + in_ref[b].astype(F32)).astype(BF16)
            out_ref[b, :, :width] = q_ref[b]
            out_ref[b, :, width:] = both
            dense = [q_ref[b][:, :live], both[:, :live], both[:, width : width + live]]
            scr[b] = pack(jnp.concatenate(dense, axis=1))
        for k in range(count):
            msgs[k][...] = scr[place_ref[0] ^ k]

    message = shape(BF16, packed_rows(rows, 3 * live), 128)
    outs = (shape(BF16, count, rows, 3 * width),) + (message,) * count
    scratch = (shape(BF16, count, *message.shape),)
    joined, *msgs = kernel(body, outs, (place,), (grad_q, grad_kv, arrived), scratch, micros=0.7, name="join_grads")
    return joined, msgs


def gather_heads(place_ref, pieces, scr, rows, live):
    for k, ref in enumerate(pieces):
        scr[place_ref[0] ^ k] = ref[...]
    return jnp.concatenate([unpack(scr[k], rows, live) for k in range(len(pieces))], axis=1)


def norms_call(place, pieces, layer_in, vectors, w_out, parts, live):
    count, rows = len(pieces), layer_in.shape[0]
    model = w_out.shape[0]
    quarter = model // parts
    pad_q = -(-quarter // 128) * 128

    def body(place_ref, *refs):
        in_ref, g2, b2, g3, b3, wo_ref, mid_ref, attn_ref = refs[count : count + 8]
        msgs, (n2_scr, piece_scr) = refs[count + 8 : count + 8 + parts], refs[count + 8 + parts :]
        attn = gather_heads(place_ref, refs[:count], piece_scr, rows, live)
        attn_ref[...] = attn
        unit2, _ = unit_norm(attn.astype(F32))
        normed2 = (unit2 * row(g2) + row(b2)).astype(BF16)
        for r in range(parts):
            n2_scr[r, :, :quarter] = normed2[:, r * quarter : (r + 1) * quarter]
            if pad_q > quarter:
                n2_scr[r, :, quarter:] = jnp.zeros((rows, pad_q - quarter), BF16)
        middle = in_ref[...].astype(F32) + mm(normed2, wo_ref[...], NN)
        mid_ref[...] = middle
        unit3, _ = unit_norm(middle)
        normed3 = (unit3 * row(g3) + row(b3)).astype(BF16)
        for k in range(parts):
            msgs[k][:, :model] = normed3
            msgs[k][:, model:] = n2_scr[place_ref[2] ^ k]

    outs = (shape(F32, rows, model), shape(BF16, rows, model)) + (shape(BF16, rows, model + pad_q),) * parts
    operands = (*pieces, layer_in, *vectors, w_out)
    scratch = (shape(BF16, parts, rows, pad_q), shape(BF16, count, *pieces[0].shape))
    mid, attn, *msgs = kernel(body, outs, (place,), operands, scratch, micros=1.5, name="norms")
    return mid, attn, msgs


def up_call(place, normed3, w_up, parts):
    rows, (model, hidden) = normed3.shape[0], w_up.shape
    part = hidden // parts

    def body(place_ref, n3_ref, wu_ref, act_ref, slope_ref, *msgs):
        normed = n3_ref[:, :model]
        for r in range(parts):
            upper = mm(normed, wu_ref[:, r * part : (r + 1) * part], NN)
            cumulative = 0.5 * (1.0 + lax.erf(upper * 0.7071067811865476))
            density = jnp.exp(-0.5 * upper * upper) * 0.3989422804014327
            act_ref[r] = (upper * cumulative).astype(BF16)
            slope_ref[r] = (cumulative + upper * density).astype(BF16)
        for k in range(parts):
            msgs[k][...] = act_ref[place_ref[2] ^ k]

    outs = (shape(BF16, parts, rows, part),) * 2 + (shape(BF16, rows, part),) * parts
    act, slope, *msgs = kernel(body, outs, (place,), (normed3, w_up), micros=2.0, name="up_gelu")
    return act, slope, msgs


def backward_call(place, attn, middle, act, slope, grad_out, vectors, w_out, w_up, w_down, parts, count, live):
    rows = attn.shape[0]
    model, hidden = w_up.shape
    part, quarter = hidden // parts, model // parts
    message = shape(BF16, packed_rows(rows, live), 128)

    def body(
        place_ref, attn_ref, mid_ref, act_ref, slope_ref, go_ref, g2, b2, g3, b3, wo_ref, wu_ref, wd_ref,
        out_ref, gmid_ref, *rest,
    ):
        msgs, heads = rest[:parts], rest[parts : parts + count]
        up_scr, table_scr, head_scr = rest[parts + count :]
        here = place_ref[2]
        go = go_ref[...]
        middle = mid_ref[...]
        out = middle
        grad3 = jnp.zeros((rows, model), F32)
        for r in range(parts):
            w_d = wd_ref[r * part : (r + 1) * part, :]
            out = out + mm(act_ref[r], w_d, NN)
            grad_up = (mm(go, w_d, NT) * slope_ref[r].astype(F32)).astype(BF16)
            up_scr[r] = grad_up
            grad3 = grad3 + mm(grad_up, wu_ref[:, r * part : (r + 1) * part], NT)
        out_ref[...] = out.astype(BF16)
        unit3, scale3 = unit_norm(middle)
        grad_mid = go.astype(F32) + norm_back(grad3, row(g3), unit3, scale3)
        gmid_ref[...] = grad_mid
        proj = grad_mid.astype(BF16)
        grad2 = mm(proj, wo_ref[...], NT)
        unit2, scale2 = unit_norm(attn_ref[...].astype(F32))
        grad_attn = norm_back(grad2, row(g2), unit2, scale2).astype(BF16)
        for k in range(count):
            head_scr[k] = pack(grad_attn[:, k * live : (k + 1) * live])
        for k in range(count):
            heads[k][...] = head_scr[place_ref[0] ^ k]
        sums = [
            jnp.sum(grad2 * unit2, axis=0, keepdims=True),
            jnp.sum(grad2, axis=0, keepdims=True),
            jnp.sum(grad3 * unit3, axis=0, keepdims=True),
            jnp.sum(grad3, axis=0, keepdims=True),
        ]
        table = jnp.concatenate(sums + [jnp.zeros((12, model), F32)], axis=0).astype(BF16)
        for r in range(parts):
            table_scr[r, :, :quarter] = table[:, r * quarter : (r + 1) * quarter]
        for k in range(parts):
            msgs[k][:rows, :part] = up_scr[here ^ k]
            msgs[k][:rows, part:] = proj
            msgs[k][rows:, :] = jnp.zeros((16, part + model), BF16)
            msgs[k][rows:, part : part + quarter] = table_scr[here ^ k, :, :quarter]

    outs = (
        shape(BF16, rows, model),
        shape(F32, rows, model),
    )
    outs += (shape(BF16, rows + 16, part + model),) * parts + (message,) * count
    operands = (attn, middle, act, slope, grad_out, *vectors, w_out, w_up, w_down)
    scratch = (
        shape(BF16, parts, rows, part),
        shape(BF16, parts, 16, -(-quarter // 128) * 128),
        shape(BF16, count, *message.shape),
    )
    found = kernel(body, outs, (place,), operands, scratch, micros=9.0, name="token_backward")
    found = list(found)
    return found[0], found[1], found[2 : 2 + parts], found[2 + parts :]


def down_grad_call(place, acts, grads, chips):
    parts = len(acts)
    part, model = acts[0].shape[1], grads[0].shape[1]
    own = part // (2 * chips)

    def body(place_ref, *refs):
        act_refs, grad_refs, (keep_ref, send_ref, scr) = refs[:parts], refs[parts : 2 * parts], refs[2 * parts :]
        core = place_ref[1]
        act = jnp.concatenate([ref[...] for ref in act_refs], axis=0)
        grad = jnp.concatenate([ref[...] for ref in grad_refs], axis=0)
        scr[...] = mm(act, grad, TN).reshape(chips, 2, own, model)
        for k in range(chips):
            keep_ref[k] = scr[k, core]
            send_ref[k] = scr[k, 1 - core].astype(BF16)

    outs = (shape(F32, chips, own, model), shape(BF16, chips, own, model))
    scratch = (shape(F32, chips, 2, own, model),)
    return kernel(body, outs, (place,), (*acts, *grads), scratch, micros=3.0, name="grad_down")


def up_grad_call(place, sent, back, chips, part, model):
    parts = len(sent)
    rows = sent[0].shape[0]
    quarter = model // parts
    own = model // (parts * chips * 2)
    tall = (parts + 1) * own + 8

    def body(place_ref, *refs):
        sent_refs, back_refs = refs[:parts], refs[parts : 2 * parts]
        keep_ref, send_ref, up_scr, out_scr, vec_scr = refs[2 * parts :]
        core = place_ref[1]
        normed3 = jnp.concatenate([ref[:, :model] for ref in sent_refs], axis=0)
        normed2 = jnp.concatenate([ref[:, model:] for ref in sent_refs], axis=0)
        grad_up = jnp.concatenate([ref[:rows, :part] for ref in back_refs], axis=0)
        proj = jnp.concatenate([ref[:rows, part:] for ref in back_refs], axis=0)
        up_scr[...] = mm(normed3, grad_up, TN).reshape(parts, chips, 2, own, part)
        out_scr[...] = mm(normed2, proj, TN)[:quarter].reshape(chips, 2, own, model)
        table = jnp.zeros((8, quarter), F32)
        for ref in back_refs:
            table = table + ref[rows:, part : part + quarter].astype(F32)[:8]
        vec_scr[...] = jnp.zeros_like(vec_scr)
        for k in range(chips):
            for side in range(2):
                at = (2 * k + side) * own
                vec_scr[k, side, :, :own] = table[:, at : at + own]
        for k in range(chips):
            for side, ref in ((core, keep_ref), (1 - core, send_ref)):
                pieces = [up_scr[r, k, side] for r in range(parts)] + [out_scr[k, side], vec_scr[k, side]]
                ref[k] = jnp.concatenate(pieces, axis=0).astype(ref.dtype)

    outs = (shape(F32, chips, tall, model), shape(BF16, chips, tall, model))
    scratch = (
        shape(F32, parts, chips, 2, own, part),
        shape(F32, chips, 2, own, model),
        shape(F32, chips, 2, 8, model),
    )
    return kernel(body, outs, (place,), (*sent, *back), scratch, micros=4.0, name="grad_up_out")


def qkv_grad_call(place, groups, units, grads, gain, bias, weight, parts, live, width):
    count, rows = grads.shape[:2]
    model = weight.shape[0]
    own = model // (parts * count * 2)
    n = len(units)

    def body(place_ref, *refs):
        unit_refs = refs[:n]
        grad_ref, gain_ref, bias_ref, weight_ref, keep_ref, send_ref, unit_scr, scr = refs[n:]
        z_index, core = place_ref[0], place_ref[1]
        for g, ks in enumerate(groups):
            for j, k in enumerate(ks):
                unit_scr[z_index ^ k] = unit_refs[g][j]
        grad = grad_ref[...].reshape(count * rows, 3 * width)
        cross = mm(unit_scr[...].reshape(count * rows, model), grad, TN)
        total = jnp.sum(grad.astype(F32), axis=0, keepdims=True)
        columns = jnp.concatenate([row(gain_ref), row(bias_ref), jnp.zeros((6, model), F32)], axis=0).T
        weight_f = weight_ref[...].astype(F32)
        grad_gain = jnp.sum(weight_f * cross, axis=1, keepdims=True)
        grad_bias = jnp.sum(weight_f * total, axis=1, keepdims=True)
        lane = lax.broadcasted_iota(jnp.int32, (1, 3 * width), 1)
        made = columns[:, 0:1] * cross + columns[:, 1:2] * total
        made = jnp.where(lane == live, grad_gain, jnp.where(lane == live + 1, grad_bias, made))
        scr[...] = made.reshape(parts, count, 2, own, 3 * width)
        for r in range(parts):
            keep_ref[r] = jnp.concatenate([scr[r, k, core] for k in range(count)], axis=0)
            send_ref[r] = jnp.concatenate([scr[r, k, 1 - core] for k in range(count)], axis=0).astype(BF16)

    outs = (shape(F32, parts, count * own, 3 * width), shape(BF16, parts, count * own, 3 * width))
    scratch = (shape(BF16, count, rows, model), shape(F32, parts, count, 2, own, 3 * width))
    operands = (*units, grads, gain, bias, weight)
    return kernel(body, outs, (place,), operands, scratch, micros=4.0, name="grad_qkv")


def spread_call(place, keep, arrived):
    parts = keep.shape[0]

    def body(place_ref, keep_ref, in_ref, *outs):
        for k in range(parts):
            at = place_ref[2] ^ k
            outs[k][...] = (keep_ref[at] + in_ref[at].astype(F32)).astype(BF16)

    return kernel(body, (shape(BF16, *keep.shape[1:]),) * parts, (place,), (keep, arrived), micros=0.8, name="spread")


def halve_call(place, keep, arrived, bit):
    half = keep.shape[0] // 2

    def body(place_ref, keep_ref, in_ref, stay_ref, away_ref):
        mine = (place_ref[0] // bit) % 2
        for j in range(half):
            here, there = 2 * j + mine, 2 * j + 1 - mine
            stay_ref[j] = keep_ref[here] + in_ref[here].astype(F32)
            away_ref[j] = (keep_ref[there] + in_ref[there].astype(F32)).astype(BF16)

    rest = keep.shape[1:]
    return kernel(body, (shape(F32, half, *rest), shape(BF16, half, *rest)), (place,), (keep, arrived), micros=0.8, name="halve")


def finish_down_call(keep, arrived):
    def body(keep_ref, in_ref, out_ref):
        out_ref[...] = keep_ref[0] + in_ref[0].astype(F32)

    return kernel(body, shape(F32, *keep.shape[1:]), (), (keep, arrived), micros=0.6, name="finish_down")


def finish_up_call(place, keep, arrived, parts, own, part):
    model = keep.shape[2]

    def body(place_ref, keep_ref, in_ref, out_ref, g2, b2, g3, b3, *rest):
        msgs, scr = rest[:parts], rest[parts]
        value = keep_ref[0] + in_ref[0].astype(F32)
        out_ref[...] = value[parts * own : (parts + 1) * own]
        for at, ref in enumerate((g2, b2, g3, b3)):
            line = (parts + 1) * own + at
            ref[...] = value[line : line + 1, :own].reshape(own)
        scr[...] = value[: parts * own].reshape(parts, own, part)
        for k in range(parts):
            msgs[k][...] = scr[place_ref[2] ^ k].astype(BF16)

    outs = (shape(F32, own, model),) + (shape(F32, own),) * 4 + (shape(BF16, own, part),) * parts
    scratch = (shape(F32, parts, own, part),)
    return kernel(body, outs, (place,), (keep, arrived), scratch, micros=0.8, name="finish_up")


def place_up_call(place, pieces):
    parts = len(pieces)
    own, part = pieces[0].shape

    def body(place_ref, *refs):
        for k in range(parts):
            at = pl.multiple_of((place_ref[2] ^ k) * part, 128)
            refs[parts][:, pl.ds(at, part)] = refs[k][...].astype(F32)

    return kernel(body, shape(F32, own, parts * part), (place,), tuple(pieces), micros=0.5, name="place_up")


def share_call(place, pieces, chips):
    own = pieces[0].shape[0] // chips

    def body(place_ref, *refs):
        ins, outs, scr = refs[: len(pieces)], refs[len(pieces) : -1], refs[-1]
        total = ins[0][...].astype(F32)
        for ref in ins[1:]:
            total = total + ref[...].astype(F32)
        scr[...] = total.reshape(chips, own, total.shape[1])
        for k in range(chips):
            outs[k][...] = scr[place_ref[0] ^ k].astype(BF16)

    lanes = pieces[0].shape[1]
    outs = (shape(BF16, own, lanes),) * chips
    return kernel(body, outs, (place,), tuple(pieces), (shape(F32, chips, own, lanes),), micros=0.7, name="share")


def finish_qkv_call(place, pieces, model, live, width):
    count, own = len(pieces), pieces[0].shape[0]

    def body(place_ref, *refs):
        q_ref, k_ref, v_ref, gain_ref, bias_ref, in_ref = refs[count:]
        for k in range(count):
            in_ref[place_ref[0] ^ k] = refs[k][...].astype(F32)
        for at, ref in enumerate((q_ref, k_ref, v_ref)):
            ref[...] = jnp.concatenate(
                [in_ref[k, :, at * width : at * width + live] for k in range(count)], axis=1
            )
        total = jnp.sum(in_ref[:, :, live : live + 2], axis=0).T
        gain_ref[...] = total[0:1].reshape(own)
        bias_ref[...] = total[1:2].reshape(own)

    outs = (shape(F32, own, model),) * 3 + (shape(F32, own),) * 2
    scratch = (shape(F32, count, *pieces[0].shape),)
    return kernel(body, outs, (place,), tuple(pieces), scratch, micros=0.8, name="finish_qkv")


def input_grad_call(place, pieces, layer_in, grad_mid, gain, w_query, w_key, w_value, live):
    count = len(pieces)
    rows, model = layer_in.shape

    def body(place_ref, *refs):
        in_ref, gmid_ref, gain_ref, wq_ref, wk_ref, wv_ref, out_ref, scr = refs[count:]
        for k in range(count):
            scr[place_ref[0] ^ k] = refs[k][...]
        blocks = [unpack(scr[k], rows, 3 * live) for k in range(count)]
        grad = jnp.zeros((rows, model), F32)
        for at, w_ref in enumerate((wq_ref, wk_ref, wv_ref)):
            part = jnp.concatenate([block[:, at * live : (at + 1) * live] for block in blocks], axis=1)
            grad = grad + mm(part, w_ref[...], NT)
        unit, scale = unit_norm(in_ref[...].astype(F32))
        out_ref[...] = (gmid_ref[...] + norm_back(grad, row(gain_ref), unit, scale)).astype(BF16)

    operands = (*pieces, layer_in, grad_mid, gain, w_query, w_key, w_value)
    scratch = (shape(BF16, count, *pieces[0].shape),)
    return kernel(body, shape(BF16, rows, model), (place,), operands, scratch, micros=3.0, name="grad_inputs")


def swap_core(value):
    return lax.ppermute(value, "core", [(0, 1), (1, 0)])


def swap(value, axis, bit):
    return lax.ppermute(value, axis, [(k, k ^ bit) for k in range(lax.axis_size(axis))])


def trade(messages, axis):
    return [messages[0]] + [swap(messages[k], axis, k) for k in range(1, len(messages))]


def gather_chips(block, chips):
    found = {0: block}
    bit = chips // 2
    while bit >= 1:
        for k in sorted(found):
            found[k | bit] = swap(found[k], "chip", bit)
        bit //= 2
    return [found[k] for k in range(chips)]


def scatter_chips(place, keep, arrived, chips, bit):
    while bit < chips:
        keep, away = halve_call(place, keep, arrived, bit)
        arrived = swap(away, "chip", bit)
        bit *= 2
    return keep, arrived


def fast_shards(
    inputs, doc_lengths, ln1_gain, ln1_bias, w_query, w_key, w_value, ln2_gain, ln2_bias, w_out,
    ln3_gain, ln3_bias, w_up, w_down, out_grad,
):
    rows, model = inputs.shape[1:]
    chips, parts = lax.axis_size("chip"), lax.axis_size("rows")
    z_index = lax.axis_index("chip")
    heads_here = HEADS // chips
    live = heads_here * HEAD_DIM
    width = -(-live // 128) * 128
    hidden = w_up.shape[1]
    part = hidden // parts
    own = model // (parts * chips * 2)
    place = jnp.stack([z_index, lax.axis_index("core"), lax.axis_index("rows")]).astype(jnp.int32)
    scope = jax.named_scope

    def columns(weight):
        mine = lax.dynamic_slice_in_dim(weight, z_index * live, live, 1)
        return jnp.pad(mine, ((0, 0), (0, width - live)))

    place, layer_in, out_grad = lax.optimization_barrier((place, inputs[0], out_grad[0]))
    with scope("gather_in"):
        blocks = gather_chips(layer_in, chips)
    grad_out = mask_call(place, doc_lengths, out_grad)
    w_heads = jnp.concatenate([columns(w_query), columns(w_key), columns(w_value)], axis=1)
    groups = [g for g in ([0], list(range(1, chips - 1)), [chips - 1]) if g] if chips > 1 else [[0]]
    made = [qkv_call([blocks[k] for k in g], ln1_gain, ln1_bias, w_heads, width) for g in groups]
    queries, kv_own, units = ([m[at] for m in made] for at in range(3))
    with scope("core_kv"):
        kv_other = [swap_core(v) for v in kv_own]
    attn_heads, (prob, queries, kv_own, kv_other), messages = attend_call(
        place, doc_lengths, groups, queries, kv_own, kv_other, heads_here
    )
    fence = lax.optimization_barrier
    messages, grad_out = fence((messages, grad_out))
    with scope("chip_attn"):
        pieces = trade(messages, "chip")
    with scope("plane_out"):
        grads_plane = trade([grad_out] * parts, "rows")
    pieces, grads_plane = fence((pieces, grads_plane))

    vectors = (ln2_gain, ln2_bias, ln3_gain, ln3_bias)
    middle, attn, sent = norms_call(place, pieces, layer_in, vectors, w_out, parts, live)
    act, slope, acts = up_call(place, sent[0], w_up, parts)
    with scope("plane_norms"):
        sent = trade(sent, "rows")
    with scope("plane_act"):
        acts = trade(acts, "rows")
    output, grad_mid, back, messages = backward_call(
        place, attn, middle, act, slope, grad_out, vectors, w_out, w_up, w_down, parts, chips, live
    )
    with scope("chip_grad"):
        grad_heads = trade(messages, "chip")
    grad_heads, sent = fence((grad_heads, sent))
    grad_q, grad_kv, grad_kv_other = attend_back_call(
        place, queries, kv_own, kv_other, prob, attn_heads, grad_heads, heads_here
    )
    grad_kv_other, acts = fence((grad_kv_other, acts))
    down_keep, down_send = down_grad_call(place, acts, grads_plane, chips)
    with scope("core_grad"):
        grad_kv_other = swap_core(grad_kv_other)
    with scope("core_down"):
        down_recv = swap_core(down_send)
    grad_qkv, messages = join_call(place, grad_q, grad_kv, grad_kv_other, live)
    down_keep, down_away = halve_call(place, down_keep, down_recv, 1)
    messages, down_away, back, grad_qkv = fence((messages, down_away, back, grad_qkv))
    with scope("chip_qkv"):
        grad_pieces = trade(messages, "chip")
    with scope("plane_back"):
        back = trade(back, "rows")
    with scope("down_one"):
        down_recv = swap(down_away, "chip", 1)
    qkv_keep, qkv_send = qkv_grad_call(
        place, groups, units, grad_qkv, ln1_gain, ln1_bias, w_heads, parts, live, width
    )
    qkv_send, down_recv, grad_pieces, back = fence((qkv_send, down_recv, grad_pieces, back))
    up_keep, up_send = up_grad_call(place, sent, back, chips, part, model)
    with scope("core_w"):
        qkv_send = swap_core(qkv_send)
    with scope("core_up"):
        up_recv = swap_core(up_send)
    with scope("down_two"):
        down_keep, down_last = scatter_chips(place, down_keep, down_recv, chips, 2)
    with scope("plane_w"):
        qkv_sums = trade(spread_call(place, qkv_keep, qkv_send), "rows")
    with scope("up_sum"):
        up_keep, up_last = scatter_chips(place, up_keep, up_recv, chips, 1)
    with scope("chip_w"):
        qkv_all = trade(share_call(place, qkv_sums, chips), "chip")
    gwo, g2, b2, g3, b3, *up_rows = finish_up_call(place, up_keep, up_last, parts, own, part)
    with scope("plane_rows"):
        up_rows = trade(up_rows, "rows")
    gwq, gwk, gwv, g1, b1 = finish_qkv_call(place, qkv_all, model, live, width)
    gwu = place_up_call(place, up_rows)
    gwd = finish_down_call(down_keep, down_last)
    grad_inputs = input_grad_call(
        place, grad_pieces, layer_in, grad_mid, ln1_gain, w_query, w_key, w_value, live
    )
    return (
        output[None], grad_inputs[None], g1, b1, gwq, gwk, gwv, g2, b2, gwo, g3, b3, gwu, gwd,
    )


def takes_fast(mesh):
    seq, parts = mesh.shape["seq"], mesh.shape["rows"]
    chips = seq // 2
    return seq % 2 == 0 and chips & (chips - 1) == 0 and parts & (parts - 1) == 0 and HEADS % max(chips, 1) == 0


def solution(mesh):
    if takes_fast(mesh):
        parts, seq = mesh.shape["rows"], mesh.shape["seq"]
        split = jax.sharding.Mesh(mesh.devices.reshape(parts, seq // 2, 2), ("rows", "chip", "core"))
        return mapped(fast_shards, split, ("chip", "core"))
    return mapped(shards, mesh, "seq")
```

```python
import math

import jax
import jax.numpy as jnp
from jax import lax
from jax.experimental import pallas as pl
from jax.experimental.pallas import tpu as pltpu
from jax.sharding import PartitionSpec as P

HEADS = 12
HEAD_DIM = 64


segment_pairs = ((2048, 1), (4096, 2), (8192, 4), (16384, 6))
masked_value = -1e30


def layer_norm(vector, gain_vec, bias_vec):
    row_mean = jnp.mean(vector, axis=-1, keepdims=True)
    centered = vector - row_mean
    row_var = jnp.mean(centered * centered, axis=-1, keepdims=True)
    return centered * lax.rsqrt(row_var + 1e-05) * gain_vec + bias_vec


def doc_of(positions, doc_ends):
    return jnp.sum((positions[:, None] >= doc_ends[None, :]).astype(jnp.int32), axis=1)


def pair_terms(query_pos, key_pos, query_doc, key_doc, head_count):
    head_ids = jnp.arange(head_count, dtype=jnp.int32)
    multiplicity = jnp.zeros((head_count, query_pos.shape[0], key_pos.shape[0]), jnp.float32)
    for seg_width, dilation in segment_pairs:
        same_seg = query_pos[:, None] // seg_width == key_pos[None, :] // seg_width
        query_pick = (query_pos % seg_width % dilation)[None, :] == (head_ids % dilation)[:, None]
        key_pick = (key_pos % seg_width % dilation)[None, :] == (head_ids % dilation)[:, None]
        joined = same_seg[None] & query_pick[:, :, None] & key_pick[:, None, :]
        multiplicity = multiplicity + joined.astype(jnp.float32)
    allowed = (key_pos[None, :] <= query_pos[:, None]) & (query_doc[:, None] == key_doc[None, :])
    allowed = allowed[None] & (multiplicity > 0.0)
    return (jnp.log(jnp.maximum(multiplicity, 1.0)), allowed)


def rows_inner(left, right):
    return lax.dot_general(
        left, right, (((0,), (0,)), ((), ())), preferred_element_type=jnp.float32
    )


def cols_inner(left, right):
    return lax.dot_general(
        left, right, (((1,), (1,)), ((), ())), preferred_element_type=jnp.float32
    )


def over_blocks(state, piece, step_fn):
    total_rows = piece[0].shape[0]
    block_rows = math.gcd(total_rows, 512)
    block_total = total_rows // block_rows
    split = tuple((part.reshape((block_total, block_rows) + part.shape[1:]) for part in piece))

    def inner(carried, block_item):
        return (step_fn(carried, block_item[1], block_item[0] * block_rows), None)

    result, unused = lax.scan(inner, state, (jnp.arange(block_total, dtype=jnp.int32), split))
    return result


def add_rows(buffer, start_pos, addend):
    current = lax.dynamic_slice_in_dim(buffer, start_pos, addend.shape[0], 0)
    return lax.dynamic_update_slice_in_dim(buffer, current + addend, start_pos, 0)


def shards(
    inputs,
    doc_lengths,
    ln1_gain,
    ln1_bias,
    w_query,
    w_key,
    w_value,
    ln2_gain,
    ln2_bias,
    w_out,
    ln3_gain,
    ln3_bias,
    w_up,
    w_down,
    out_grad,
):
    tok_rows = inputs.shape[1]
    head_count = HEADS
    head_size = HEAD_DIM
    model_width = inputs.shape[2]
    row_total = tok_rows * lax.axis_size("seq")
    layer_in = inputs[0].astype(jnp.float32)
    doc_ends = jnp.cumsum(doc_lengths[0])
    first_pos = lax.axis_index("seq") * tok_rows
    query_pos = first_pos + jnp.arange(tok_rows, dtype=jnp.int32)
    query_doc = doc_of(query_pos, doc_ends)
    valid = (query_doc < doc_lengths.shape[1]).astype(jnp.float32)
    first_norm, first_back = jax.vjp(layer_norm, layer_in, ln1_gain, ln1_bias)
    normed_one = first_norm.astype(jnp.bfloat16)
    queries = jnp.dot(normed_one, w_query, preferred_element_type=jnp.float32).astype(jnp.bfloat16)
    keys_local = jnp.dot(normed_one, w_key, preferred_element_type=jnp.float32).astype(jnp.bfloat16)
    values_local = jnp.dot(normed_one, w_value, preferred_element_type=jnp.float32).astype(
        jnp.bfloat16
    )
    query_heads = queries.reshape(tok_rows, head_count, head_size)

    def key_block_terms(key_start, key_count):
        key_pos = key_start + jnp.arange(key_count, dtype=jnp.int32)
        key_doc = doc_of(key_pos, doc_ends)
        return pair_terms(query_pos, key_pos, query_doc, key_doc, head_count)

    def with_pruning(step_fn):

        def wrapped(state, parts, start_pos):
            return step_fn(state, parts, start_pos)

        return wrapped

    def forward_step(state, parts, key_start):
        run_max, run_total, run_acc = state
        key_blk = parts[0].reshape(-1, head_count, head_size)
        value_blk = parts[1].reshape(-1, head_count, head_size)
        log_mult, allowed = key_block_terms(key_start, key_blk.shape[0])
        scores = 0.125 * jnp.einsum(
            "qhd,khd->hqk", query_heads, key_blk, preferred_element_type=jnp.float32
        )
        logits = jnp.where(allowed, scores + log_mult, masked_value)
        new_max = jnp.maximum(run_max, jnp.max(logits, axis=-1))
        weights = jnp.where(allowed, jnp.exp(logits - new_max[..., None]), 0.0)
        factor = jnp.exp(run_max - new_max)
        run_total = run_total * factor + jnp.sum(weights, axis=-1)
        run_acc = run_acc * factor[..., None] + jnp.einsum(
            "hqk,khd->hqd",
            weights.astype(jnp.bfloat16),
            value_blk,
            preferred_element_type=jnp.float32,
        )
        return (new_max, run_total, run_acc)

    forward_pruned = with_pruning(forward_step)
    start_state = (
        jnp.full((head_count, tok_rows), masked_value, jnp.float32),
        jnp.zeros((head_count, tok_rows), jnp.float32),
        jnp.zeros((head_count, tok_rows, head_size), jnp.float32),
    )
    final_state = over_blocks(
        start_state,
        (
            lax.all_gather(keys_local, "seq", axis=0, tiled=True),
            lax.all_gather(values_local, "seq", axis=0, tiled=True),
        ),
        forward_pruned,
    )
    run_max, run_total, run_acc = final_state
    row_lse = run_max + jnp.log(run_total)
    attn = (run_acc / run_total[..., None]).transpose(1, 0, 2).reshape(tok_rows, model_width)
    second_norm, second_back = jax.vjp(layer_norm, attn, ln2_gain, ln2_bias)
    normed_two = second_norm.astype(jnp.bfloat16)
    middle = layer_in + jnp.dot(normed_two, w_out, preferred_element_type=jnp.float32)
    third_norm, third_back = jax.vjp(layer_norm, middle, ln3_gain, ln3_bias)
    normed_three = third_norm.astype(jnp.bfloat16)
    upper = jnp.dot(normed_three, w_up, preferred_element_type=jnp.float32)
    activated_f, gelu_back = jax.vjp(
        lambda upper_in: jax.nn.gelu(upper_in, approximate=False), upper
    )
    activated = activated_f.astype(jnp.bfloat16)
    layer_out = middle + jnp.dot(activated, w_down, preferred_element_type=jnp.float32)
    grad_out = out_grad[0].astype(jnp.float32) * valid[:, None]
    grad_branch = grad_out.astype(jnp.bfloat16)
    grad_w_down = rows_inner(activated, grad_branch)
    grad_act = cols_inner(grad_branch, w_down)
    grad_upper = gelu_back(grad_act)[0].astype(jnp.bfloat16)
    grad_w_up = rows_inner(normed_three, grad_upper)
    grad_n3 = cols_inner(grad_upper, w_up)
    grad_mid_norm, grad_ln3_gain, grad_ln3_bias = third_back(grad_n3)
    grad_middle = grad_out + grad_mid_norm
    grad_proj = grad_middle.astype(jnp.bfloat16)
    grad_w_out = rows_inner(normed_two, grad_proj)
    grad_n2 = cols_inner(grad_proj, w_out)
    grad_attn_f, grad_ln2_gain, grad_ln2_bias = second_back(grad_n2)
    grad_attn = grad_attn_f.astype(jnp.bfloat16)
    grad_heads = grad_attn.reshape(tok_rows, head_count, head_size)
    row_delta = jnp.sum(
        (grad_attn.astype(jnp.float32) * attn).reshape(tok_rows, head_count, head_size), axis=-1
    )

    def backward_step(state, parts, key_start):
        grad_q_acc, grad_k_rows, grad_v_rows = state
        key_blk = parts[0].reshape(-1, head_count, head_size)
        value_blk = parts[1].reshape(-1, head_count, head_size)
        key_count = key_blk.shape[0]
        log_mult, allowed = key_block_terms(key_start, key_count)
        scores = 0.125 * jnp.einsum(
            "qhd,khd->hqk", query_heads, key_blk, preferred_element_type=jnp.float32
        )
        logits = jnp.where(allowed, scores + log_mult, masked_value)
        weights = jnp.where(allowed, jnp.exp(logits - row_lse[..., None]), 0.0)
        grad_weights = jnp.einsum(
            "qhd,khd->hqk", grad_heads, value_blk, preferred_element_type=jnp.float32
        )
        grad_scores = (weights * (grad_weights - row_delta.T[..., None])).astype(jnp.bfloat16)
        grad_q_acc = grad_q_acc + 0.125 * jnp.einsum(
            "hqk,khd->qhd", grad_scores, key_blk, preferred_element_type=jnp.float32
        )
        value_part = jnp.einsum(
            "hqk,qhd->khd",
            weights.astype(jnp.bfloat16),
            grad_heads,
            preferred_element_type=jnp.float32,
        ).reshape(key_count, model_width)
        key_part = 0.125 * jnp.einsum(
            "hqk,qhd->khd", grad_scores, query_heads, preferred_element_type=jnp.float32
        ).reshape(key_count, model_width)
        grad_k_rows = add_rows(grad_k_rows, key_start, key_part)
        grad_v_rows = add_rows(grad_v_rows, key_start, value_part)
        return (grad_q_acc, grad_k_rows, grad_v_rows)

    backward_pruned = with_pruning(backward_step)
    zero_state = (
        jnp.zeros((tok_rows, head_count, head_size), jnp.float32),
        jnp.zeros((row_total, model_width), jnp.float32),
        jnp.zeros((row_total, model_width), jnp.float32),
    )
    back_state = over_blocks(
        zero_state,
        (
            lax.all_gather(keys_local, "seq", axis=0, tiled=True),
            lax.all_gather(values_local, "seq", axis=0, tiled=True),
        ),
        backward_pruned,
    )
    grad_q_acc, grad_k_rows, grad_v_rows = back_state
    grad_k_acc, grad_v_acc = (
        lax.psum_scatter(
            grad_k_rows.astype(jnp.bfloat16), "seq", scatter_dimension=0, tiled=True
        ).astype(jnp.float32),
        lax.psum_scatter(
            grad_v_rows.astype(jnp.bfloat16), "seq", scatter_dimension=0, tiled=True
        ).astype(jnp.float32),
    )
    grad_queries = grad_q_acc.reshape(tok_rows, model_width).astype(jnp.bfloat16)
    grad_keys = grad_k_acc.astype(jnp.bfloat16)
    grad_values = grad_v_acc.astype(jnp.bfloat16)
    grad_w_query = rows_inner(normed_one, grad_queries)
    grad_w_key = rows_inner(normed_one, grad_keys)
    grad_w_value = rows_inner(normed_one, grad_values)
    grad_n1 = (
        cols_inner(grad_queries, w_query)
        + cols_inner(grad_keys, w_key)
        + cols_inner(grad_values, w_value)
    )
    grad_in_norm, grad_ln1_gain, grad_ln1_bias = first_back(grad_n1)
    grad_inputs = (grad_middle + grad_in_norm).astype(jnp.bfloat16)
    summed = (
        lax.psum_scatter(grad_ln1_gain, ("rows", "seq"), scatter_dimension=0, tiled=True),
        lax.psum_scatter(grad_ln1_bias, ("rows", "seq"), scatter_dimension=0, tiled=True),
        lax.psum_scatter(grad_w_query, ("rows", "seq"), scatter_dimension=0, tiled=True),
        lax.psum_scatter(grad_w_key, ("rows", "seq"), scatter_dimension=0, tiled=True),
        lax.psum_scatter(grad_w_value, ("rows", "seq"), scatter_dimension=0, tiled=True),
        lax.psum_scatter(grad_ln2_gain, ("rows", "seq"), scatter_dimension=0, tiled=True),
        lax.psum_scatter(grad_ln2_bias, ("rows", "seq"), scatter_dimension=0, tiled=True),
        lax.psum_scatter(grad_w_out, ("rows", "seq"), scatter_dimension=0, tiled=True),
        lax.psum_scatter(grad_ln3_gain, ("rows", "seq"), scatter_dimension=0, tiled=True),
        lax.psum_scatter(grad_ln3_bias, ("rows", "seq"), scatter_dimension=0, tiled=True),
        lax.psum_scatter(grad_w_up, ("rows", "seq"), scatter_dimension=0, tiled=True),
        lax.psum_scatter(grad_w_down, ("rows", "seq"), scatter_dimension=0, tiled=True),
    )
    return (
        layer_out.astype(jnp.bfloat16)[None],
        grad_inputs[None],
        summed[0],
        summed[1],
        summed[2],
        summed[3],
        summed[4],
        summed[5],
        summed[6],
        summed[7],
        summed[8],
        summed[9],
        summed[10],
        summed[11],
    )


def mapped(step, mesh, seq):
    spread = P(("rows",) + (seq if isinstance(seq, tuple) else (seq,)))
    tokens, plain = P("rows", seq, None), P()
    weights = P(spread[0], None)
    return jax.shard_map(
        step,
        mesh=mesh,
        in_specs=(tokens, P("rows", None)) + (plain,) * 12 + (tokens,),
        out_specs=(tokens, tokens, spread, spread, weights, weights, weights, spread, spread, weights)
        + (spread, spread, weights, weights),
        check_vma=False,
    )


F32 = jnp.float32
PACE = 1e6
BF16 = jnp.bfloat16
NT = (((1,), (1,)), ((), ()))
TN = (((0,), (0,)), ((), ()))
NN = (((1,), (0,)), ((), ()))


def mm(left, right, dims):
    return lax.dot_general(left, right, dims, preferred_element_type=F32)


def unit_norm(vector):
    centered = vector - jnp.mean(vector, axis=-1, keepdims=True)
    scale = lax.rsqrt(jnp.mean(centered * centered, axis=-1, keepdims=True) + 1e-05)
    return centered * scale, scale


def norm_back(grad, gain, unit, scale):
    weighted = grad * gain
    mean_w = jnp.mean(weighted, axis=-1, keepdims=True)
    mean_wu = jnp.mean(weighted * unit, axis=-1, keepdims=True)
    return scale * (weighted - mean_w - unit * mean_wu)


def shape(dtype, *dims):
    return jax.ShapeDtypeStruct(dims, dtype)


def row(ref):
    return ref[...].reshape(1, ref.shape[0])


def size_of(item):
    total = jnp.dtype(item.dtype).itemsize
    for dim in item.shape:
        total *= dim
    return total


def kernel(body, outs, scalars, operands, scratch=(), micros=2.0, name=None):
    single = not isinstance(outs, (tuple, list))
    listed = (outs,) if single else tuple(outs)
    vmem = pl.BlockSpec(memory_space=pltpu.VMEM)
    smem = pl.BlockSpec(memory_space=pltpu.SMEM)
    moved = sum(size_of(v) for v in (*operands, *listed))
    held = sum(size_of(v) for v in scratch)
    return pl.pallas_call(
        body,
        out_shape=outs if single else listed,
        in_specs=[smem] * len(scalars) + [vmem] * len(operands),
        out_specs=vmem if single else (vmem,) * len(listed),
        scratch_shapes=[pltpu.VMEM(v.shape, v.dtype) for v in scratch],
        compiler_params=pltpu.CompilerParams(vmem_limit_bytes=min(60 << 20, (moved + held) * 5 // 4 + (6 << 20))),
        cost_estimate=pl.CostEstimate(flops=int(micros * PACE), bytes_accessed=int(micros * PACE / 1e3), transcendentals=0),
        name=name,
    )(*scalars, *operands)


def packed_rows(rows, live):
    return rows * live // 128


def pack(block):
    rows, live = block.shape
    whole = live // 128
    pieces = [block[:, 128 * j : 128 * (j + 1)] for j in range(whole)]
    if live % 128:
        rest = block[:, 128 * whole :]
        pieces.append(jnp.concatenate([rest[: rows // 2], rest[rows // 2 :]], axis=1))
    return jnp.concatenate(pieces, axis=0)


def unpack(block, rows, live):
    whole = live // 128
    pieces = [block[rows * j : rows * (j + 1)] for j in range(whole)]
    if live % 128:
        rest = block[rows * whole :]
        pieces.append(jnp.concatenate([rest[:, :64], rest[:, 64:]], axis=0))
    return jnp.concatenate(pieces, axis=1)


def mask_call(place, lengths, out_grad, parts):
    rows, model = out_grad.shape

    def body(place_ref, len_ref, in_ref, out_ref, msg_ref):
        last = jnp.int32(0)
        for d in range(lengths.shape[1]):
            last = last + len_ref[0, d]
        pos = lax.broadcasted_iota(jnp.int32, (rows, 1), 0) + (2 * place_ref[0] + place_ref[1]) * rows
        masked = jnp.where(pos < last, in_ref[...].astype(F32), 0.0).astype(BF16)
        out_ref[...] = masked
        for r in range(parts):
            msg_ref[r] = masked

    outs = (shape(BF16, rows, model), shape(BF16, parts, rows, model))
    return kernel(body, outs, (place, lengths), (out_grad,), micros=0.7, name="mask_grad")


def qkv_call(blocks, gain, bias, weight, width):
    count = len(blocks)
    rows, model = blocks[0].shape

    def body(*refs):
        xs, (gain_ref, bias_ref, weight_ref, q_ref, kv_ref, unit_ref) = refs[:count], refs[count:]
        for k in range(count):
            unit, _ = unit_norm(xs[k][...].astype(F32))
            normed = (unit * row(gain_ref) + row(bias_ref)).astype(BF16)
            made = mm(normed, weight_ref[...], NN)
            q_ref[k] = (made[:, :width].astype(BF16).astype(F32) * 0.125).astype(BF16)
            kv_ref[k] = made[:, width:].astype(BF16)
            unit_ref[k] = unit.astype(BF16)

    outs = (
        shape(BF16, count, rows, width),
        shape(BF16, count, rows, 2 * width),
        shape(BF16, count, rows, model),
    )
    return kernel(body, outs, (), (*blocks, gain, bias, weight), micros=1.2 * count, name="qkv_heads")


def lane_head(lanes):
    return lax.broadcasted_iota(jnp.int32, (1, lanes), 1) // HEAD_DIM


def residue(pos_f, modulus):
    return pos_f - modulus * jnp.floor((pos_f + 0.5) * (1.0 / modulus))


def stack_heads(block, heads_here):
    head_of = lane_head(block.shape[1])
    return jnp.concatenate(
        [jnp.where(head_of == h, block, jnp.zeros_like(block)) for h in range(heads_here)], axis=0
    )


def fold_heads(stacked, rows, heads_here):
    head_of = lane_head(stacked.shape[1])
    total = jnp.zeros((rows, stacked.shape[1]), stacked.dtype)
    for h in range(heads_here):
        total = jnp.where(head_of == h, stacked[h * rows : (h + 1) * rows], total)
    return total


def attend_call(place, lengths, groups, queries, kv_own, kv_other, heads_here):
    count = sum(len(g) for g in groups)
    rows, width = queries[0].shape[1:]
    tall, wide = heads_here * rows, count * rows
    docs = lengths.shape[1]
    step = 16
    n = len(groups)

    def body(place_ref, len_ref, *refs):
        q_in, own_in, oth_in = refs[:n], refs[n : 2 * n], refs[2 * n : 3 * n]
        out_ref, prob_ref, q_ref, own_ref, oth_ref = refs[3 * n : 3 * n + 5]
        msgs, (s_scr, m_scr, hot_scr, send_scr) = refs[3 * n + 5 : 3 * n + 5 + count], refs[3 * n + 5 + count :]
        z_index, core = place_ref[0], place_ref[1]
        for g, ks in enumerate(groups):
            for j, k in enumerate(ks):
                q_ref[z_index ^ k] = q_in[g][j]
                own_ref[z_index ^ k] = own_in[g][j]
                oth_ref[z_index ^ k] = oth_in[g][j]
        sides = (own_ref, oth_ref)
        cores = (core, 1 - core)
        lane = lax.broadcasted_iota(jnp.int32, (rows, 128), 1).astype(F32)
        for side in range(2):
            for b in range(count):
                pos = lax.broadcasted_iota(jnp.int32, (rows, 1), 0) + (2 * b + cores[side]) * rows
                hot = (residue(pos.astype(F32), 12.0) == lane).astype(F32)
                hot_scr[side, b * rows : (b + 1) * rows, :] = hot.astype(BF16)
        for i in range(count):
            keys = (i + 1) * rows
            pos = lax.broadcasted_iota(jnp.int32, (rows, 1), 0) + (2 * i + core) * rows
            pos_f = pos.astype(F32)
            begin = jnp.zeros_like(pos)
            run = jnp.int32(0)
            for d in range(docs):
                run = run + len_ref[0, d]
                begin = jnp.where(pos >= run, run, begin)
            tables = []
            for h in range(heads_here):
                head = (z_index * heads_here + h).astype(F32)
                table = jnp.ones((rows, 128), F32)
                for r in (2.0, 4.0, 6.0):
                    mine = residue(head, r)
                    pick_q = (residue(pos_f, r) == mine).astype(F32)
                    pick_k = (residue(lane, r) == mine).astype(F32)
                    table = table + pick_q * pick_k
                tables.append(jnp.where(lane < 12.0, table, 0.0))
            table = jnp.concatenate(tables, axis=0).astype(BF16)
            stacked = stack_heads(q_ref[i], heads_here)
            for side in range(2):
                key = sides[side][:, :, :width].reshape(wide, width)[:keys]
                s_scr[side, :, :keys] = mm(stacked, key, NT)
                m_scr[side, :, :keys] = mm(table, hot_scr[side, :keys], NT)
            key_pos = [
                jnp.concatenate(
                    [
                        lax.broadcasted_iota(jnp.int32, (1, rows), 1) + (2 * b + cores[side]) * rows
                        for b in range(i + 1)
                    ],
                    axis=1,
                )
                for side in range(2)
            ]
            for h in range(heads_here):
                for at in range(0, rows, step):
                    lo = h * rows + at
                    pos_c, begin_c = pos[at : at + step], begin[at : at + step]
                    masked = []
                    for side in range(2):
                        ok = (key_pos[side] <= pos_c) & (key_pos[side] >= begin_c)
                        masked.append(jnp.where(ok, s_scr[side, lo : lo + step, :keys], masked_value))
                    top = jnp.maximum(
                        jnp.max(masked[0], axis=1, keepdims=True), jnp.max(masked[1], axis=1, keepdims=True)
                    )
                    parts = [
                        jnp.exp(masked[side] - top) * m_scr[side, lo : lo + step, :keys] for side in range(2)
                    ]
                    total = jnp.sum(parts[0], axis=1, keepdims=True) + jnp.sum(parts[1], axis=1, keepdims=True)
                    inverse = 1.0 / total
                    for side in range(2):
                        prob_ref[i, side, lo : lo + step, :keys] = (parts[side] * inverse).astype(BF16)
            mixed = jnp.zeros((tall, width), F32)
            for side in range(2):
                value = sides[side][:, :, width:].reshape(wide, width)[:keys]
                mixed = mixed + mm(prob_ref[i, side, :, :keys], value, NN)
            result = fold_heads(mixed, rows, heads_here)
            out_ref[i] = result
            send_scr[i] = pack(result.astype(BF16)[:, :live])
        for k in range(count):
            msgs[k][...] = send_scr[z_index ^ k]

    live = heads_here * HEAD_DIM
    outs = (
        shape(F32, count, rows, width),
        shape(BF16, count, 2, tall, wide),
        shape(BF16, count, rows, width),
        shape(BF16, count, rows, 2 * width),
        shape(BF16, count, rows, 2 * width),
    ) + (shape(BF16, packed_rows(rows, live), 128),) * count
    scratch = (
        shape(F32, 2, tall, wide),
        shape(F32, 2, tall, wide),
        shape(BF16, 2, wide, 128),
        shape(BF16, count, packed_rows(rows, live), 128),
    )
    operands = (*queries, *kv_own, *kv_other)
    found = kernel(
        body, outs, (place, lengths), operands, scratch, micros=6.0, name="attend"
    )
    return found[0], found[1:5], list(found[5:])


def attend_back_call(place, queries, kv_own, kv_other, prob, attn, grads, heads_here):
    count, rows, width = queries.shape
    tall, wide = heads_here * rows, count * rows
    step = 16

    live = heads_here * HEAD_DIM

    def body(place_ref, q_ref, own_ref, oth_ref, prob_ref, attn_ref, *refs):
        grad_refs, (dq_ref, down_ref, doth_ref, p_scr, d_scr, acc, grad_ref) = refs[:count], refs[count:]
        sides = (own_ref, oth_ref)
        acc[...] = jnp.zeros_like(acc)
        grad_ref[...] = jnp.zeros_like(grad_ref)
        for k in range(count):
            grad_ref[place_ref[0] ^ k, :, :live] = unpack(grad_refs[k][...], rows, live)
        for i in range(count):
            keys = (i + 1) * rows
            grad = grad_ref[i]
            stacked_q = stack_heads(q_ref[i], heads_here)
            stacked_g = stack_heads(grad, heads_here)
            product = grad.astype(F32) * attn_ref[i]
            head_of = lane_head(width)
            delta = [
                jnp.sum(jnp.where(head_of == h, product, 0.0), axis=1, keepdims=True) for h in range(heads_here)
            ]
            for side in range(2):
                value = sides[side][:, :, width:].reshape(wide, width)[:keys]
                p_scr[side, :, :keys] = mm(stacked_g, value, NT)
            for h in range(heads_here):
                for at in range(0, rows, step):
                    lo = h * rows + at
                    for side in range(2):
                        weights = prob_ref[i, side, lo : lo + step, :keys].astype(F32)
                        shifted = p_scr[side, lo : lo + step, :keys] - delta[h][at : at + step]
                        d_scr[side, lo : lo + step, :keys] = (weights * shifted).astype(BF16)
            grad_q = jnp.zeros((tall, width), F32)
            for side in range(2):
                key = sides[side][:, :, :width].reshape(wide, width)[:keys]
                moved = d_scr[side, :, :keys]
                grad_q = grad_q + mm(moved, key, NN)
                acc[side, :keys, :width] += mm(moved, stacked_q, TN)
                acc[side, :keys, width:] += mm(prob_ref[i, side, :, :keys], stacked_g, TN)
            dq_ref[i] = (0.125 * fold_heads(grad_q, rows, heads_here)).astype(BF16)
        down_ref[...] = acc[0].reshape(count, rows, 2 * width)
        doth_ref[...] = acc[1].reshape(count, rows, 2 * width).astype(BF16)

    outs = (
        shape(BF16, count, rows, width),
        shape(F32, count, rows, 2 * width),
        shape(BF16, count, rows, 2 * width),
    )
    scratch = (
        shape(F32, 2, tall, wide),
        shape(BF16, 2, tall, wide),
        shape(F32, 2, wide, 2 * width),
        shape(BF16, count, rows, width),
    )
    operands = (queries, kv_own, kv_other, prob, attn, *grads)
    return kernel(body, outs, (place,), operands, scratch, micros=6.0, name="attend_back")


def join_call(place, grad_q, grad_kv, arrived, live):
    count, rows, width = grad_q.shape

    def body(place_ref, q_ref, kv_ref, in_ref, out_ref, *rest):
        msgs, scr = rest[:count], rest[count]
        for b in range(count):
            both = (kv_ref[b] + in_ref[b].astype(F32)).astype(BF16)
            out_ref[b, :, :width] = q_ref[b]
            out_ref[b, :, width:] = both
            dense = [q_ref[b][:, :live], both[:, :live], both[:, width : width + live]]
            scr[b] = pack(jnp.concatenate(dense, axis=1))
        for k in range(count):
            msgs[k][...] = scr[place_ref[0] ^ k]

    message = shape(BF16, packed_rows(rows, 3 * live), 128)
    outs = (shape(BF16, count, rows, 3 * width),) + (message,) * count
    scratch = (shape(BF16, count, *message.shape),)
    joined, *msgs = kernel(body, outs, (place,), (grad_q, grad_kv, arrived), scratch, micros=0.7, name="join_grads")
    return joined, msgs


def gather_heads(place_ref, pieces, scr, rows, live):
    for k, ref in enumerate(pieces):
        scr[place_ref[0] ^ k] = ref[...]
    return jnp.concatenate([unpack(scr[k], rows, live) for k in range(len(pieces))], axis=1)


def norms_call(place, pieces, layer_in, vectors, w_out, live):
    count, rows = len(pieces), layer_in.shape[0]
    model = w_out.shape[0]

    def body(place_ref, *refs):
        in_ref, g2, b2, g3, b3, wo_ref, mid_ref, attn_ref, n3_ref, piece_scr = refs[count:]
        attn = gather_heads(place_ref, refs[:count], piece_scr, rows, live)
        attn_ref[...] = attn
        unit2, _ = unit_norm(attn.astype(F32))
        normed2 = (unit2 * row(g2) + row(b2)).astype(BF16)
        middle = in_ref[...].astype(F32) + mm(normed2, wo_ref[...], NN)
        mid_ref[...] = middle
        unit3, _ = unit_norm(middle)
        n3_ref[...] = (unit3 * row(g3) + row(b3)).astype(BF16)

    outs = (shape(F32, rows, model), shape(BF16, rows, model), shape(BF16, rows, model))
    operands = (*pieces, layer_in, *vectors, w_out)
    scratch = (shape(BF16, count, *pieces[0].shape),)
    return kernel(body, outs, (place,), operands, scratch, micros=1.5, name="norms")


def up_call(place, normed3, w_up, parts):
    rows, (model, hidden) = normed3.shape[0], w_up.shape
    part = hidden // parts

    def body(place_ref, n3_ref, wu_ref, act_ref, slope_ref, *msgs):
        normed = n3_ref[...]
        for r in range(parts):
            upper = mm(normed, wu_ref[:, r * part : (r + 1) * part], NN)
            cumulative = 0.5 * (1.0 + lax.erf(upper * 0.7071067811865476))
            density = jnp.exp(-0.5 * upper * upper) * 0.3989422804014327
            act_ref[r] = (upper * cumulative).astype(BF16)
            slope_ref[r] = (cumulative + upper * density).astype(BF16)
        for k in range(parts):
            msgs[k][...] = act_ref[place_ref[2] ^ k]

    outs = (shape(BF16, parts, rows, part),) * 2 + (shape(BF16, rows, part),) * parts
    act, slope, *msgs = kernel(body, outs, (place,), (normed3, w_up), micros=2.0, name="up_gelu")
    return act, slope, msgs


def padded_quarter(quarter):
    return -(-(quarter + 64) // 128) * 128


def backward_call(place, attn, middle, act, slope, grad_out, vectors, w_out, w_up, w_down, parts, count, live):
    rows = attn.shape[0]
    model, hidden = w_up.shape
    part, quarter = hidden // parts, model // parts
    pad_q = padded_quarter(quarter)
    message = shape(BF16, packed_rows(rows, live), 128)

    def body(
        place_ref, attn_ref, mid_ref, act_ref, slope_ref, go_ref, g2, b2, g3, b3, wo_ref, wu_ref, wd_ref,
        out_ref, gmid_ref, *rest,
    ):
        msg_ref, heads, head_scr = rest[0], rest[1 : 1 + count], rest[1 + count]
        go = go_ref[...]
        middle = mid_ref[...]
        out = middle
        grad3 = jnp.zeros((rows, model), F32)
        for r in range(parts):
            w_d = wd_ref[r * part : (r + 1) * part, :]
            out = out + mm(act_ref[r], w_d, NN)
            grad_up = (mm(go, w_d, NT) * slope_ref[r].astype(F32)).astype(BF16)
            msg_ref[r, :, :part] = grad_up
            grad3 = grad3 + mm(grad_up, wu_ref[:, r * part : (r + 1) * part], NT)
        out_ref[...] = out.astype(BF16)
        unit3, scale3 = unit_norm(middle)
        grad_mid = go.astype(F32) + norm_back(grad3, row(g3), unit3, scale3)
        gmid_ref[...] = grad_mid
        proj = grad_mid.astype(BF16)
        grad2 = mm(proj, wo_ref[...], NT)
        unit2, scale2 = unit_norm(attn_ref[...].astype(F32))
        grad_attn = norm_back(grad2, row(g2), unit2, scale2).astype(BF16)
        for k in range(count):
            head_scr[k] = pack(grad_attn[:, k * live : (k + 1) * live])
        for k in range(count):
            heads[k][...] = head_scr[place_ref[0] ^ k]
        sums = [
            jnp.sum(grad2 * unit2, axis=0, keepdims=True),
            jnp.sum(grad2, axis=0, keepdims=True),
            jnp.sum(grad3 * unit3, axis=0, keepdims=True),
            jnp.sum(grad3, axis=0, keepdims=True),
        ]
        table = jnp.concatenate(sums + [jnp.zeros((4, model), F32)], axis=0)
        normed2 = (unit2 * row(g2) + row(b2)).astype(BF16)
        normed3 = (unit3 * row(g3) + row(b3)).astype(BF16)
        spare, lines = pad_q - quarter, quarter // 64
        for r in range(parts):
            chunks = [table[:, r * quarter + 64 * j : r * quarter + 64 * (j + 1)] for j in range(lines)]
            side = jnp.concatenate(chunks + [jnp.zeros((rows - 8 * lines, 64), F32)], axis=0).astype(BF16)
            pieces = [normed2[:, r * quarter : (r + 1) * quarter], side]
            if spare > 64:
                pieces.append(jnp.zeros((rows, spare - 64), BF16))
            msg_ref[r, :, part : part + model] = proj
            msg_ref[r, :, part + model : part + 2 * model] = normed3
            msg_ref[r, :, part + 2 * model :] = jnp.concatenate(pieces, axis=1)

    outs = (
        shape(BF16, rows, model),
        shape(F32, rows, model),
    )
    outs += (shape(BF16, parts, rows, part + 2 * model + pad_q),) + (message,) * count
    operands = (attn, middle, act, slope, grad_out, *vectors, w_out, w_up, w_down)
    scratch = (shape(BF16, count, *message.shape),)
    found = kernel(body, outs, (place,), operands, scratch, micros=9.0, name="token_backward")
    found = list(found)
    return found[0], found[1], found[2], found[3:]


def down_grad_call(place, acts, grads, chips):
    parts = len(acts)
    part, model = acts[0].shape[1], grads.shape[2]
    own = part // (2 * chips)

    def body(place_ref, *refs):
        act_refs, (grads_ref, keep_ref, send_ref, scr) = refs[:parts], refs[parts:]
        core = place_ref[1]
        act = jnp.concatenate([ref[...] for ref in act_refs], axis=0)
        grad = jnp.concatenate([grads_ref[place_ref[2] ^ k] for k in range(parts)], axis=0)
        scr[...] = mm(act, grad, TN).reshape(chips, 2, own, model)
        for k in range(chips):
            keep_ref[k] = scr[k, core]
            send_ref[k] = scr[k, 1 - core].astype(BF16)

    outs = (shape(F32, chips, own, model), shape(BF16, chips, own, model))
    scratch = (shape(F32, chips, 2, own, model),)
    return kernel(body, outs, (place,), (*acts, grads), scratch, micros=3.0, name="grad_down")


def up_grad_call(place, back, chips, part, model):
    parts, rows = back.shape[:2]
    quarter = model // parts
    own = model // (parts * chips * 2)
    tall = (parts + 1) * own + 8

    def body(place_ref, back_ref, keep_ref, send_ref, up_scr, out_scr, vec_scr):
        core = place_ref[1]
        ends = (0, part, part + model, part + 2 * model, back.shape[2])
        grad_up, proj, normed3, normed2 = (
            back_ref[:, :, lo:hi].reshape(parts * rows, hi - lo) for lo, hi in zip(ends, ends[1:])
        )
        up_scr[...] = mm(normed3, grad_up, TN).reshape(parts, chips, 2, own, part)
        out_scr[...] = mm(normed2, proj, TN)[:quarter].reshape(chips, 2, own, model)
        lines = quarter // 64
        side = jnp.zeros((8 * lines, 64), F32)
        for r in range(parts):
            block = back_ref[r, :, ends[3] :].astype(F32)
            side = side + block[: 8 * lines, quarter : quarter + 64]
        table = jnp.concatenate([side[8 * j : 8 * (j + 1)] for j in range(lines)], axis=1)
        vec_scr[...] = jnp.zeros_like(vec_scr)
        for k in range(chips):
            for side in range(2):
                at = (2 * k + side) * own
                vec_scr[k, side, :, :own] = table[:, at : at + own]
        for k in range(chips):
            for side, ref in ((core, keep_ref), (1 - core, send_ref)):
                pieces = [up_scr[r, k, side] for r in range(parts)] + [out_scr[k, side], vec_scr[k, side]]
                ref[k] = jnp.concatenate(pieces, axis=0).astype(ref.dtype)

    outs = (shape(F32, chips, tall, model), shape(BF16, chips, tall, model))
    scratch = (
        shape(F32, parts, chips, 2, own, part),
        shape(F32, chips, 2, own, model),
        shape(F32, chips, 2, 8, model),
    )
    return kernel(body, outs, (place,), (back,), scratch, micros=4.0, name="grad_up_out")


def qkv_grad_call(place, groups, units, grads, gain, bias, weight, parts, live, width):
    count, rows = grads.shape[:2]
    model = weight.shape[0]
    own = model // (parts * count * 2)
    n = len(units)

    def body(place_ref, *refs):
        unit_refs = refs[:n]
        grad_ref, gain_ref, bias_ref, weight_ref, keep_ref, send_ref, unit_scr, scr = refs[n:]
        z_index, core = place_ref[0], place_ref[1]
        for g, ks in enumerate(groups):
            for j, k in enumerate(ks):
                unit_scr[z_index ^ k] = unit_refs[g][j]
        grad = grad_ref[...].reshape(count * rows, 3 * width)
        cross = mm(unit_scr[...].reshape(count * rows, model), grad, TN)
        total = jnp.sum(grad.astype(F32), axis=0, keepdims=True)
        columns = jnp.concatenate([row(gain_ref), row(bias_ref), jnp.zeros((6, model), F32)], axis=0).T
        weight_f = weight_ref[...].astype(F32)
        grad_gain = jnp.sum(weight_f * cross, axis=1, keepdims=True)
        grad_bias = jnp.sum(weight_f * total, axis=1, keepdims=True)
        lane = lax.broadcasted_iota(jnp.int32, (1, 3 * width), 1)
        made = columns[:, 0:1] * cross + columns[:, 1:2] * total
        made = jnp.where(lane == live, grad_gain, jnp.where(lane == live + 1, grad_bias, made))
        scr[...] = made.reshape(parts, count, 2, own, 3 * width)
        for r in range(parts):
            keep_ref[r] = jnp.concatenate([scr[r, k, core] for k in range(count)], axis=0)
            send_ref[r] = jnp.concatenate([scr[r, k, 1 - core] for k in range(count)], axis=0).astype(BF16)

    outs = (shape(F32, parts, count * own, 3 * width), shape(BF16, parts, count * own, 3 * width))
    scratch = (shape(BF16, count, rows, model), shape(F32, parts, count, 2, own, 3 * width))
    operands = (*units, grads, gain, bias, weight)
    return kernel(body, outs, (place,), operands, scratch, micros=4.0, name="grad_qkv")


def spread_call(keep, arrived):
    def body(keep_ref, in_ref, out_ref):
        out_ref[...] = (keep_ref[...] + in_ref[...].astype(F32)).astype(BF16)

    return kernel(body, shape(BF16, *keep.shape), (), (keep, arrived), micros=0.8, name="spread")


def halve_call(place, keep, arrived, bit):
    half = keep.shape[0] // 2

    def body(place_ref, keep_ref, in_ref, stay_ref, away_ref):
        mine = (place_ref[0] // bit) % 2
        for j in range(half):
            here, there = 2 * j + mine, 2 * j + 1 - mine
            stay_ref[j] = keep_ref[here] + in_ref[here].astype(F32)
            away_ref[j] = (keep_ref[there] + in_ref[there].astype(F32)).astype(BF16)

    rest = keep.shape[1:]
    return kernel(body, (shape(F32, half, *rest), shape(BF16, half, *rest)), (place,), (keep, arrived), micros=0.8, name="halve")


def finish_down_call(keep, arrived):
    def body(keep_ref, in_ref, out_ref):
        out_ref[...] = keep_ref[0] + in_ref[0].astype(F32)

    return kernel(body, shape(F32, *keep.shape[1:]), (), (keep, arrived), micros=0.6, name="finish_down")


def finish_up_call(keep, arrived, parts, own, part):
    model = keep.shape[2]

    def body(keep_ref, in_ref, out_ref, g2, b2, g3, b3, rows_ref):
        value = keep_ref[0] + in_ref[0].astype(F32)
        out_ref[...] = value[parts * own : (parts + 1) * own]
        for at, ref in enumerate((g2, b2, g3, b3)):
            line = (parts + 1) * own + at
            ref[...] = value[line : line + 1, :own].reshape(own)
        rows_ref[...] = value[: parts * own].reshape(parts, own, part).astype(BF16)

    outs = (shape(F32, own, model),) + (shape(F32, own),) * 4 + (shape(BF16, parts, own, part),)
    return kernel(body, outs, (), (keep, arrived), micros=0.8, name="finish_up")


def place_up_call(pieces):
    parts, own, part = pieces.shape

    def body(in_ref, out_ref):
        for r in range(parts):
            out_ref[:, r * part : (r + 1) * part] = in_ref[r].astype(F32)

    return kernel(body, shape(F32, own, parts * part), (), (pieces,), micros=0.5, name="place_up")


def share_call(place, pieces, chips):
    parts, tall, lanes = pieces.shape
    own = tall // chips

    def body(place_ref, in_ref, *refs):
        outs, scr = refs[:-1], refs[-1]
        total = in_ref[0].astype(F32)
        for r in range(1, parts):
            total = total + in_ref[r].astype(F32)
        scr[...] = total.reshape(chips, own, lanes)
        for k in range(chips):
            outs[k][...] = scr[place_ref[0] ^ k].astype(BF16)

    outs = (shape(BF16, own, lanes),) * chips
    return kernel(body, outs, (place,), (pieces,), (shape(F32, chips, own, lanes),), micros=0.7, name="share")


def finish_qkv_call(place, pieces, model, live, width):
    count, own = len(pieces), pieces[0].shape[0]

    def body(place_ref, *refs):
        q_ref, k_ref, v_ref, gain_ref, bias_ref, in_ref = refs[count:]
        for k in range(count):
            in_ref[place_ref[0] ^ k] = refs[k][...].astype(F32)
        for at, ref in enumerate((q_ref, k_ref, v_ref)):
            ref[...] = jnp.concatenate(
                [in_ref[k, :, at * width : at * width + live] for k in range(count)], axis=1
            )
        total = jnp.sum(in_ref[:, :, live : live + 2], axis=0).T
        gain_ref[...] = total[0:1].reshape(own)
        bias_ref[...] = total[1:2].reshape(own)

    outs = (shape(F32, own, model),) * 3 + (shape(F32, own),) * 2
    scratch = (shape(F32, count, *pieces[0].shape),)
    return kernel(body, outs, (place,), tuple(pieces), scratch, micros=0.8, name="finish_qkv")


def input_grad_call(place, pieces, layer_in, grad_mid, gain, w_query, w_key, w_value, live):
    count = len(pieces)
    rows, model = layer_in.shape

    def body(place_ref, *refs):
        in_ref, gmid_ref, gain_ref, wq_ref, wk_ref, wv_ref, out_ref, scr = refs[count:]
        for k in range(count):
            scr[place_ref[0] ^ k] = refs[k][...]
        blocks = [unpack(scr[k], rows, 3 * live) for k in range(count)]
        grad = jnp.zeros((rows, model), F32)
        for at, w_ref in enumerate((wq_ref, wk_ref, wv_ref)):
            part = jnp.concatenate([block[:, at * live : (at + 1) * live] for block in blocks], axis=1)
            grad = grad + mm(part, w_ref[...], NT)
        unit, scale = unit_norm(in_ref[...].astype(F32))
        out_ref[...] = (gmid_ref[...] + norm_back(grad, row(gain_ref), unit, scale)).astype(BF16)

    operands = (*pieces, layer_in, grad_mid, gain, w_query, w_key, w_value)
    scratch = (shape(BF16, count, *pieces[0].shape),)
    return kernel(body, shape(BF16, rows, model), (place,), operands, scratch, micros=3.0, name="grad_inputs")


def swap_core(value):
    return lax.ppermute(value, "core", [(0, 1), (1, 0)])


def swap(value, axis, bit):
    return lax.ppermute(value, axis, [(k, k ^ bit) for k in range(lax.axis_size(axis))])


def trade(messages, axis):
    return [messages[0]] + [swap(messages[k], axis, k) for k in range(1, len(messages))]


def plane_trade(messages):
    return lax.all_to_all(messages, "rows", 0, 0)


def gather_chips(block, chips):
    found = {0: block}
    bit = chips // 2
    while bit >= 1:
        for k in sorted(found):
            found[k | bit] = swap(found[k], "chip", bit)
        bit //= 2
    return [found[k] for k in range(chips)]


def scatter_chips(place, keep, arrived, chips, bit):
    while bit < chips:
        keep, away = halve_call(place, keep, arrived, bit)
        arrived = swap(away, "chip", bit)
        bit *= 2
    return keep, arrived


def after(values, *others):
    return lax.optimization_barrier((values, others))[0]


def fast_shards(
    inputs, doc_lengths, ln1_gain, ln1_bias, w_query, w_key, w_value, ln2_gain, ln2_bias, w_out,
    ln3_gain, ln3_bias, w_up, w_down, out_grad,
):
    rows, model = inputs.shape[1:]
    chips, parts = lax.axis_size("chip"), lax.axis_size("rows")
    z_index = lax.axis_index("chip")
    heads_here = HEADS // chips
    live = heads_here * HEAD_DIM
    width = -(-live // 128) * 128
    hidden = w_up.shape[1]
    part = hidden // parts
    own = model // (parts * chips * 2)
    place = jnp.stack([z_index, lax.axis_index("core"), lax.axis_index("rows")]).astype(jnp.int32)
    scope = jax.named_scope

    def columns(weight):
        mine = lax.dynamic_slice_in_dim(weight, z_index * live, live, 1)
        return jnp.pad(mine, ((0, 0), (0, width - live)))

    place, layer_in, out_grad = lax.optimization_barrier((place, inputs[0], out_grad[0]))
    with scope("gather_in"):
        blocks = gather_chips(layer_in, chips)
    grad_out, grads_plane = mask_call(place, doc_lengths, out_grad, parts)
    w_heads = jnp.concatenate([columns(w_query), columns(w_key), columns(w_value)], axis=1)
    groups = [g for g in ([0], list(range(1, chips - 1)), [chips - 1]) if g] if chips > 1 else [[0]]
    made = [qkv_call([blocks[k] for k in g], ln1_gain, ln1_bias, w_heads, width) for g in groups]
    queries, kv_own, units = ([m[at] for m in made] for at in range(3))
    with scope("core_kv"):
        kv_other = [swap_core(v) for v in kv_own]
    attn_heads, (prob, queries, kv_own, kv_other), messages = attend_call(
        place, doc_lengths, groups, queries, kv_own, kv_other, heads_here
    )
    fence = lax.optimization_barrier
    with scope("chip_attn"):
        pieces = trade(messages, "chip")
    with scope("plane_out"):
        grads_plane = plane_trade(grads_plane)
    pieces = after(pieces, grads_plane)

    vectors = (ln2_gain, ln2_bias, ln3_gain, ln3_bias)
    middle, attn, normed3 = norms_call(place, pieces, layer_in, vectors, w_out, live)
    act, slope, acts = up_call(place, normed3, w_up, parts)
    with scope("plane_act"):
        acts = trade(acts, "rows")
    output, grad_mid, back, messages = backward_call(
        place, attn, middle, act, slope, grad_out, vectors, w_out, w_up, w_down, parts, chips, live
    )
    acts[:3], messages, back = fence((acts[:3], messages, back))
    with scope("chip_grad"):
        grad_heads = trade(messages, "chip")
    with scope("plane_back"):
        back = plane_trade(after(back, grad_heads[1:2]))
    acts = after(acts, grad_heads[1:])
    down_keep, down_send = down_grad_call(place, acts, grads_plane, chips)
    with scope("core_down"):
        down_recv = swap_core(down_send)
    grad_q, grad_kv, grad_kv_other = attend_back_call(
        place, queries, kv_own, kv_other, prob, attn_heads, grad_heads, heads_here
    )
    with scope("core_grad"):
        grad_kv_other = swap_core(grad_kv_other)
    down_recv = after(down_recv, grad_q)
    with scope("down_sum"):
        down_keep, down_away = halve_call(place, down_keep, down_recv, 1)
        grad_kv_other, down_away = fence((grad_kv_other, down_away))
        down_recv = swap(down_away, "chip", 1)
    grad_qkv, messages = join_call(place, grad_q, grad_kv, grad_kv_other, live)
    with scope("chip_qkv"):
        grad_pieces = trade(messages, "chip")
    qkv_keep, qkv_send = qkv_grad_call(
        place, groups, units, grad_qkv, ln1_gain, ln1_bias, w_heads, parts, live, width
    )
    with scope("core_w"):
        qkv_send = swap_core(qkv_send)
    qkv_send = after(qkv_send, (grad_pieces, down_recv))
    qkv_sums = spread_call(qkv_keep, qkv_send)
    with scope("down_sum"):
        down_keep, down_last = scatter_chips(place, down_keep, down_recv, chips, 2)
    back = after(back, (down_keep, qkv_sums))
    up_keep, up_send = up_grad_call(place, back, chips, part, model)
    with scope("plane_w"):
        traded = plane_trade(qkv_sums)
    with scope("core_up"):
        up_recv = swap_core(up_send)
    up_keep, up_away = halve_call(place, up_keep, up_recv, 1)
    with scope("up_sum"):
        up_recv = swap(up_away, "chip", 1)
    traded = after(traded, up_away)
    with scope("chip_w"):
        shared = share_call(place, traded, chips)
        qkv_all = trade(shared, "chip")
    grad_inputs = input_grad_call(
        place, grad_pieces, layer_in, grad_mid, ln1_gain, w_query, w_key, w_value, live
    )
    gwd = finish_down_call(down_keep, down_last)
    up_recv = after(up_recv, down_last)
    with scope("up_sum"):
        up_keep, up_last = scatter_chips(place, up_keep, up_recv, chips, 2)
    up_last = after(up_last, (qkv_all, gwd, grad_inputs))
    gwo, g2, b2, g3, b3, up_rows = finish_up_call(up_keep, up_last, parts, own, part)
    with scope("plane_rows"):
        up_rows = plane_trade(up_rows)
    gwq, gwk, gwv, g1, b1 = finish_qkv_call(place, qkv_all, model, live, width)
    gwu = place_up_call(up_rows)
    return (
        output[None], grad_inputs[None], g1, b1, gwq, gwk, gwv, g2, b2, gwo, g3, b3, gwu, gwd,
    )


def takes_fast(mesh):
    seq, parts = mesh.shape["seq"], mesh.shape["rows"]
    chips = seq // 2
    return seq % 2 == 0 and chips & (chips - 1) == 0 and parts in (1, 2, 4) and HEADS % max(chips, 1) == 0


def solution(mesh):
    if takes_fast(mesh):
        parts, seq = mesh.shape["rows"], mesh.shape["seq"]
        split = jax.sharding.Mesh(mesh.devices.reshape(parts, seq // 2, 2), ("rows", "chip", "core"))
        return mapped(fast_shards, split, ("chip", "core"))
    return mapped(shards, mesh, "seq")
```

```python
import math

import jax
import jax.numpy as jnp
from jax import lax
from jax.experimental import pallas as pl
from jax.experimental.pallas import tpu as pltpu
from jax.sharding import PartitionSpec as P

HEADS = 12
HEAD_DIM = 64


segment_pairs = ((2048, 1), (4096, 2), (8192, 4), (16384, 6))
masked_value = -1e30


def layer_norm(vector, gain_vec, bias_vec):
    row_mean = jnp.mean(vector, axis=-1, keepdims=True)
    centered = vector - row_mean
    row_var = jnp.mean(centered * centered, axis=-1, keepdims=True)
    return centered * lax.rsqrt(row_var + 1e-05) * gain_vec + bias_vec


def doc_of(positions, doc_ends):
    return jnp.sum((positions[:, None] >= doc_ends[None, :]).astype(jnp.int32), axis=1)


def pair_terms(query_pos, key_pos, query_doc, key_doc, head_count):
    head_ids = jnp.arange(head_count, dtype=jnp.int32)
    multiplicity = jnp.zeros((head_count, query_pos.shape[0], key_pos.shape[0]), jnp.float32)
    for seg_width, dilation in segment_pairs:
        same_seg = query_pos[:, None] // seg_width == key_pos[None, :] // seg_width
        query_pick = (query_pos % seg_width % dilation)[None, :] == (head_ids % dilation)[:, None]
        key_pick = (key_pos % seg_width % dilation)[None, :] == (head_ids % dilation)[:, None]
        joined = same_seg[None] & query_pick[:, :, None] & key_pick[:, None, :]
        multiplicity = multiplicity + joined.astype(jnp.float32)
    allowed = (key_pos[None, :] <= query_pos[:, None]) & (query_doc[:, None] == key_doc[None, :])
    allowed = allowed[None] & (multiplicity > 0.0)
    return (jnp.log(jnp.maximum(multiplicity, 1.0)), allowed)


def rows_inner(left, right):
    return lax.dot_general(
        left, right, (((0,), (0,)), ((), ())), preferred_element_type=jnp.float32
    )


def cols_inner(left, right):
    return lax.dot_general(
        left, right, (((1,), (1,)), ((), ())), preferred_element_type=jnp.float32
    )


def over_blocks(state, piece, step_fn):
    total_rows = piece[0].shape[0]
    block_rows = math.gcd(total_rows, 512)
    block_total = total_rows // block_rows
    split = tuple((part.reshape((block_total, block_rows) + part.shape[1:]) for part in piece))

    def inner(carried, block_item):
        return (step_fn(carried, block_item[1], block_item[0] * block_rows), None)

    result, unused = lax.scan(inner, state, (jnp.arange(block_total, dtype=jnp.int32), split))
    return result


def add_rows(buffer, start_pos, addend):
    current = lax.dynamic_slice_in_dim(buffer, start_pos, addend.shape[0], 0)
    return lax.dynamic_update_slice_in_dim(buffer, current + addend, start_pos, 0)


def shards(
    inputs,
    doc_lengths,
    ln1_gain,
    ln1_bias,
    w_query,
    w_key,
    w_value,
    ln2_gain,
    ln2_bias,
    w_out,
    ln3_gain,
    ln3_bias,
    w_up,
    w_down,
    out_grad,
):
    tok_rows = inputs.shape[1]
    head_count = HEADS
    head_size = HEAD_DIM
    model_width = inputs.shape[2]
    row_total = tok_rows * lax.axis_size("seq")
    layer_in = inputs[0].astype(jnp.float32)
    doc_ends = jnp.cumsum(doc_lengths[0])
    first_pos = lax.axis_index("seq") * tok_rows
    query_pos = first_pos + jnp.arange(tok_rows, dtype=jnp.int32)
    query_doc = doc_of(query_pos, doc_ends)
    valid = (query_doc < doc_lengths.shape[1]).astype(jnp.float32)
    first_norm, first_back = jax.vjp(layer_norm, layer_in, ln1_gain, ln1_bias)
    normed_one = first_norm.astype(jnp.bfloat16)
    queries = jnp.dot(normed_one, w_query, preferred_element_type=jnp.float32).astype(jnp.bfloat16)
    keys_local = jnp.dot(normed_one, w_key, preferred_element_type=jnp.float32).astype(jnp.bfloat16)
    values_local = jnp.dot(normed_one, w_value, preferred_element_type=jnp.float32).astype(
        jnp.bfloat16
    )
    query_heads = queries.reshape(tok_rows, head_count, head_size)

    def key_block_terms(key_start, key_count):
        key_pos = key_start + jnp.arange(key_count, dtype=jnp.int32)
        key_doc = doc_of(key_pos, doc_ends)
        return pair_terms(query_pos, key_pos, query_doc, key_doc, head_count)

    def with_pruning(step_fn):

        def wrapped(state, parts, start_pos):
            return step_fn(state, parts, start_pos)

        return wrapped

    def forward_step(state, parts, key_start):
        run_max, run_total, run_acc = state
        key_blk = parts[0].reshape(-1, head_count, head_size)
        value_blk = parts[1].reshape(-1, head_count, head_size)
        log_mult, allowed = key_block_terms(key_start, key_blk.shape[0])
        scores = 0.125 * jnp.einsum(
            "qhd,khd->hqk", query_heads, key_blk, preferred_element_type=jnp.float32
        )
        logits = jnp.where(allowed, scores + log_mult, masked_value)
        new_max = jnp.maximum(run_max, jnp.max(logits, axis=-1))
        weights = jnp.where(allowed, jnp.exp(logits - new_max[..., None]), 0.0)
        factor = jnp.exp(run_max - new_max)
        run_total = run_total * factor + jnp.sum(weights, axis=-1)
        run_acc = run_acc * factor[..., None] + jnp.einsum(
            "hqk,khd->hqd",
            weights.astype(jnp.bfloat16),
            value_blk,
            preferred_element_type=jnp.float32,
        )
        return (new_max, run_total, run_acc)

    forward_pruned = with_pruning(forward_step)
    start_state = (
        jnp.full((head_count, tok_rows), masked_value, jnp.float32),
        jnp.zeros((head_count, tok_rows), jnp.float32),
        jnp.zeros((head_count, tok_rows, head_size), jnp.float32),
    )
    final_state = over_blocks(
        start_state,
        (
            lax.all_gather(keys_local, "seq", axis=0, tiled=True),
            lax.all_gather(values_local, "seq", axis=0, tiled=True),
        ),
        forward_pruned,
    )
    run_max, run_total, run_acc = final_state
    row_lse = run_max + jnp.log(run_total)
    attn = (run_acc / run_total[..., None]).transpose(1, 0, 2).reshape(tok_rows, model_width)
    second_norm, second_back = jax.vjp(layer_norm, attn, ln2_gain, ln2_bias)
    normed_two = second_norm.astype(jnp.bfloat16)
    middle = layer_in + jnp.dot(normed_two, w_out, preferred_element_type=jnp.float32)
    third_norm, third_back = jax.vjp(layer_norm, middle, ln3_gain, ln3_bias)
    normed_three = third_norm.astype(jnp.bfloat16)
    upper = jnp.dot(normed_three, w_up, preferred_element_type=jnp.float32)
    activated_f, gelu_back = jax.vjp(
        lambda upper_in: jax.nn.gelu(upper_in, approximate=False), upper
    )
    activated = activated_f.astype(jnp.bfloat16)
    layer_out = middle + jnp.dot(activated, w_down, preferred_element_type=jnp.float32)
    grad_out = out_grad[0].astype(jnp.float32) * valid[:, None]
    grad_branch = grad_out.astype(jnp.bfloat16)
    grad_w_down = rows_inner(activated, grad_branch)
    grad_act = cols_inner(grad_branch, w_down)
    grad_upper = gelu_back(grad_act)[0].astype(jnp.bfloat16)
    grad_w_up = rows_inner(normed_three, grad_upper)
    grad_n3 = cols_inner(grad_upper, w_up)
    grad_mid_norm, grad_ln3_gain, grad_ln3_bias = third_back(grad_n3)
    grad_middle = grad_out + grad_mid_norm
    grad_proj = grad_middle.astype(jnp.bfloat16)
    grad_w_out = rows_inner(normed_two, grad_proj)
    grad_n2 = cols_inner(grad_proj, w_out)
    grad_attn_f, grad_ln2_gain, grad_ln2_bias = second_back(grad_n2)
    grad_attn = grad_attn_f.astype(jnp.bfloat16)
    grad_heads = grad_attn.reshape(tok_rows, head_count, head_size)
    row_delta = jnp.sum(
        (grad_attn.astype(jnp.float32) * attn).reshape(tok_rows, head_count, head_size), axis=-1
    )

    def backward_step(state, parts, key_start):
        grad_q_acc, grad_k_rows, grad_v_rows = state
        key_blk = parts[0].reshape(-1, head_count, head_size)
        value_blk = parts[1].reshape(-1, head_count, head_size)
        key_count = key_blk.shape[0]
        log_mult, allowed = key_block_terms(key_start, key_count)
        scores = 0.125 * jnp.einsum(
            "qhd,khd->hqk", query_heads, key_blk, preferred_element_type=jnp.float32
        )
        logits = jnp.where(allowed, scores + log_mult, masked_value)
        weights = jnp.where(allowed, jnp.exp(logits - row_lse[..., None]), 0.0)
        grad_weights = jnp.einsum(
            "qhd,khd->hqk", grad_heads, value_blk, preferred_element_type=jnp.float32
        )
        grad_scores = (weights * (grad_weights - row_delta.T[..., None])).astype(jnp.bfloat16)
        grad_q_acc = grad_q_acc + 0.125 * jnp.einsum(
            "hqk,khd->qhd", grad_scores, key_blk, preferred_element_type=jnp.float32
        )
        value_part = jnp.einsum(
            "hqk,qhd->khd",
            weights.astype(jnp.bfloat16),
            grad_heads,
            preferred_element_type=jnp.float32,
        ).reshape(key_count, model_width)
        key_part = 0.125 * jnp.einsum(
            "hqk,qhd->khd", grad_scores, query_heads, preferred_element_type=jnp.float32
        ).reshape(key_count, model_width)
        grad_k_rows = add_rows(grad_k_rows, key_start, key_part)
        grad_v_rows = add_rows(grad_v_rows, key_start, value_part)
        return (grad_q_acc, grad_k_rows, grad_v_rows)

    backward_pruned = with_pruning(backward_step)
    zero_state = (
        jnp.zeros((tok_rows, head_count, head_size), jnp.float32),
        jnp.zeros((row_total, model_width), jnp.float32),
        jnp.zeros((row_total, model_width), jnp.float32),
    )
    back_state = over_blocks(
        zero_state,
        (
            lax.all_gather(keys_local, "seq", axis=0, tiled=True),
            lax.all_gather(values_local, "seq", axis=0, tiled=True),
        ),
        backward_pruned,
    )
    grad_q_acc, grad_k_rows, grad_v_rows = back_state
    grad_k_acc, grad_v_acc = (
        lax.psum_scatter(
            grad_k_rows.astype(jnp.bfloat16), "seq", scatter_dimension=0, tiled=True
        ).astype(jnp.float32),
        lax.psum_scatter(
            grad_v_rows.astype(jnp.bfloat16), "seq", scatter_dimension=0, tiled=True
        ).astype(jnp.float32),
    )
    grad_queries = grad_q_acc.reshape(tok_rows, model_width).astype(jnp.bfloat16)
    grad_keys = grad_k_acc.astype(jnp.bfloat16)
    grad_values = grad_v_acc.astype(jnp.bfloat16)
    grad_w_query = rows_inner(normed_one, grad_queries)
    grad_w_key = rows_inner(normed_one, grad_keys)
    grad_w_value = rows_inner(normed_one, grad_values)
    grad_n1 = (
        cols_inner(grad_queries, w_query)
        + cols_inner(grad_keys, w_key)
        + cols_inner(grad_values, w_value)
    )
    grad_in_norm, grad_ln1_gain, grad_ln1_bias = first_back(grad_n1)
    grad_inputs = (grad_middle + grad_in_norm).astype(jnp.bfloat16)
    summed = (
        lax.psum_scatter(grad_ln1_gain, ("rows", "seq"), scatter_dimension=0, tiled=True),
        lax.psum_scatter(grad_ln1_bias, ("rows", "seq"), scatter_dimension=0, tiled=True),
        lax.psum_scatter(grad_w_query, ("rows", "seq"), scatter_dimension=0, tiled=True),
        lax.psum_scatter(grad_w_key, ("rows", "seq"), scatter_dimension=0, tiled=True),
        lax.psum_scatter(grad_w_value, ("rows", "seq"), scatter_dimension=0, tiled=True),
        lax.psum_scatter(grad_ln2_gain, ("rows", "seq"), scatter_dimension=0, tiled=True),
        lax.psum_scatter(grad_ln2_bias, ("rows", "seq"), scatter_dimension=0, tiled=True),
        lax.psum_scatter(grad_w_out, ("rows", "seq"), scatter_dimension=0, tiled=True),
        lax.psum_scatter(grad_ln3_gain, ("rows", "seq"), scatter_dimension=0, tiled=True),
        lax.psum_scatter(grad_ln3_bias, ("rows", "seq"), scatter_dimension=0, tiled=True),
        lax.psum_scatter(grad_w_up, ("rows", "seq"), scatter_dimension=0, tiled=True),
        lax.psum_scatter(grad_w_down, ("rows", "seq"), scatter_dimension=0, tiled=True),
    )
    return (
        layer_out.astype(jnp.bfloat16)[None],
        grad_inputs[None],
        summed[0],
        summed[1],
        summed[2],
        summed[3],
        summed[4],
        summed[5],
        summed[6],
        summed[7],
        summed[8],
        summed[9],
        summed[10],
        summed[11],
    )


def mapped(step, mesh, seq):
    spread = P(("rows",) + (seq if isinstance(seq, tuple) else (seq,)))
    tokens, plain = P("rows", seq, None), P()
    weights = P(spread[0], None)
    return jax.shard_map(
        step,
        mesh=mesh,
        in_specs=(tokens, P("rows", None)) + (plain,) * 12 + (tokens,),
        out_specs=(tokens, tokens, spread, spread, weights, weights, weights, spread, spread, weights)
        + (spread, spread, weights, weights),
        check_vma=False,
    )


F32 = jnp.float32
PACE = 1e6
BF16 = jnp.bfloat16
NT = (((1,), (1,)), ((), ()))
TN = (((0,), (0,)), ((), ()))
NN = (((1,), (0,)), ((), ()))


def mm(left, right, dims):
    return lax.dot_general(left, right, dims, preferred_element_type=F32)


def unit_norm(vector):
    centered = vector - jnp.mean(vector, axis=-1, keepdims=True)
    scale = lax.rsqrt(jnp.mean(centered * centered, axis=-1, keepdims=True) + 1e-05)
    return centered * scale, scale


def norm_back(grad, gain, unit, scale):
    weighted = grad * gain
    mean_w = jnp.mean(weighted, axis=-1, keepdims=True)
    mean_wu = jnp.mean(weighted * unit, axis=-1, keepdims=True)
    return scale * (weighted - mean_w - unit * mean_wu)


def shape(dtype, *dims):
    return jax.ShapeDtypeStruct(dims, dtype)


def row(ref):
    return ref[...].reshape(1, ref.shape[0])


def size_of(item):
    total = jnp.dtype(item.dtype).itemsize
    for dim in item.shape:
        total *= dim
    return total


def kernel(body, outs, scalars, operands, scratch=(), micros=2.0, name=None):
    single = not isinstance(outs, (tuple, list))
    listed = (outs,) if single else tuple(outs)
    vmem = pl.BlockSpec(memory_space=pltpu.VMEM)
    smem = pl.BlockSpec(memory_space=pltpu.SMEM)
    moved = sum(size_of(v) for v in (*operands, *listed))
    held = sum(size_of(v) for v in scratch)
    return pl.pallas_call(
        body,
        out_shape=outs if single else listed,
        in_specs=[smem] * len(scalars) + [vmem] * len(operands),
        out_specs=vmem if single else (vmem,) * len(listed),
        scratch_shapes=[pltpu.VMEM(v.shape, v.dtype) for v in scratch],
        compiler_params=pltpu.CompilerParams(vmem_limit_bytes=min(60 << 20, (moved + held) * 5 // 4 + (6 << 20))),
        cost_estimate=pl.CostEstimate(flops=int(micros * PACE), bytes_accessed=int(micros * PACE / 1e3), transcendentals=0),
        name=name,
    )(*scalars, *operands)


def packed_rows(rows, live):
    return rows * live // 128


def pack(block):
    rows, live = block.shape
    whole = live // 128
    pieces = [block[:, 128 * j : 128 * (j + 1)] for j in range(whole)]
    if live % 128:
        rest = block[:, 128 * whole :]
        pieces.append(jnp.concatenate([rest[: rows // 2], rest[rows // 2 :]], axis=1))
    return jnp.concatenate(pieces, axis=0)


def unpack(block, rows, live):
    whole = live // 128
    pieces = [block[rows * j : rows * (j + 1)] for j in range(whole)]
    if live % 128:
        rest = block[rows * whole :]
        pieces.append(jnp.concatenate([rest[:, :64], rest[:, 64:]], axis=0))
    return jnp.concatenate(pieces, axis=1)


def mask_call(place, lengths, out_grad):
    rows, model = out_grad.shape

    def body(place_ref, len_ref, in_ref, out_ref):
        last = jnp.int32(0)
        for d in range(lengths.shape[1]):
            last = last + len_ref[0, d]
        pos = lax.broadcasted_iota(jnp.int32, (rows, 1), 0) + (2 * place_ref[0] + place_ref[1]) * rows
        out_ref[...] = jnp.where(pos < last, in_ref[...].astype(F32), 0.0).astype(BF16)

    return kernel(body, shape(BF16, rows, model), (place, lengths), (out_grad,), micros=0.7, name="mask_grad")


def qkv_call(blocks, gain, bias, weight, width):
    count = len(blocks)
    rows, model = blocks[0].shape

    def body(*refs):
        xs, (gain_ref, bias_ref, weight_ref, q_ref, kv_ref, unit_ref) = refs[:count], refs[count:]
        for k in range(count):
            unit, _ = unit_norm(xs[k][...].astype(F32))
            normed = (unit * row(gain_ref) + row(bias_ref)).astype(BF16)
            made = mm(normed, weight_ref[...], NN)
            q_ref[k] = (made[:, :width].astype(BF16).astype(F32) * 0.125).astype(BF16)
            kv_ref[k] = made[:, width:].astype(BF16)
            unit_ref[k] = unit.astype(BF16)

    outs = (
        shape(BF16, count, rows, width),
        shape(BF16, count, rows, 2 * width),
        shape(BF16, count, rows, model),
    )
    return kernel(body, outs, (), (*blocks, gain, bias, weight), micros=1.2 * count, name="qkv_heads")


def lane_head(lanes):
    return lax.broadcasted_iota(jnp.int32, (1, lanes), 1) // HEAD_DIM


def residue(pos_f, modulus):
    return pos_f - modulus * jnp.floor((pos_f + 0.5) * (1.0 / modulus))


def stack_heads(block, heads_here):
    head_of = lane_head(block.shape[1])
    return jnp.concatenate(
        [jnp.where(head_of == h, block, jnp.zeros_like(block)) for h in range(heads_here)], axis=0
    )


def fold_heads(stacked, rows, heads_here):
    head_of = lane_head(stacked.shape[1])
    total = jnp.zeros((rows, stacked.shape[1]), stacked.dtype)
    for h in range(heads_here):
        total = jnp.where(head_of == h, stacked[h * rows : (h + 1) * rows], total)
    return total


def attend_call(place, lengths, groups, queries, kv_own, kv_other, heads_here):
    count = sum(len(g) for g in groups)
    rows, width = queries[0].shape[1:]
    tall, wide = heads_here * rows, count * rows
    docs = lengths.shape[1]
    step = 16
    n = len(groups)

    def body(place_ref, len_ref, *refs):
        q_in, own_in, oth_in = refs[:n], refs[n : 2 * n], refs[2 * n : 3 * n]
        out_ref, prob_ref, q_ref, own_ref, oth_ref = refs[3 * n : 3 * n + 5]
        msgs, (s_scr, m_scr, hot_scr, send_scr) = refs[3 * n + 5 : 3 * n + 5 + count], refs[3 * n + 5 + count :]
        z_index, core = place_ref[0], place_ref[1]
        for g, ks in enumerate(groups):
            for j, k in enumerate(ks):
                q_ref[z_index ^ k] = q_in[g][j]
                own_ref[z_index ^ k] = own_in[g][j]
                oth_ref[z_index ^ k] = oth_in[g][j]
        sides = (own_ref, oth_ref)
        cores = (core, 1 - core)
        lane = lax.broadcasted_iota(jnp.int32, (rows, 128), 1).astype(F32)
        for side in range(2):
            for b in range(count):
                pos = lax.broadcasted_iota(jnp.int32, (rows, 1), 0) + (2 * b + cores[side]) * rows
                hot = (residue(pos.astype(F32), 12.0) == lane).astype(F32)
                hot_scr[side, b * rows : (b + 1) * rows, :] = hot.astype(BF16)
        for i in range(count):
            keys = (i + 1) * rows
            pos = lax.broadcasted_iota(jnp.int32, (rows, 1), 0) + (2 * i + core) * rows
            pos_f = pos.astype(F32)
            begin = jnp.zeros_like(pos)
            run = jnp.int32(0)
            for d in range(docs):
                run = run + len_ref[0, d]
                begin = jnp.where(pos >= run, run, begin)
            tables = []
            for h in range(heads_here):
                head = (z_index * heads_here + h).astype(F32)
                table = jnp.ones((rows, 128), F32)
                for r in (2.0, 4.0, 6.0):
                    mine = residue(head, r)
                    pick_q = (residue(pos_f, r) == mine).astype(F32)
                    pick_k = (residue(lane, r) == mine).astype(F32)
                    table = table + pick_q * pick_k
                tables.append(jnp.where(lane < 12.0, table, 0.0))
            table = jnp.concatenate(tables, axis=0).astype(BF16)
            stacked = stack_heads(q_ref[i], heads_here)
            for side in range(2):
                key = sides[side][:, :, :width].reshape(wide, width)[:keys]
                s_scr[side, :, :keys] = mm(stacked, key, NT)
                m_scr[side, :, :keys] = mm(table, hot_scr[side, :keys], NT)
            key_pos = [
                jnp.concatenate(
                    [
                        lax.broadcasted_iota(jnp.int32, (1, rows), 1) + (2 * b + cores[side]) * rows
                        for b in range(i + 1)
                    ],
                    axis=1,
                )
                for side in range(2)
            ]
            for h in range(heads_here):
                for at in range(0, rows, step):
                    lo = h * rows + at
                    pos_c, begin_c = pos[at : at + step], begin[at : at + step]
                    masked = []
                    for side in range(2):
                        ok = (key_pos[side] <= pos_c) & (key_pos[side] >= begin_c)
                        masked.append(jnp.where(ok, s_scr[side, lo : lo + step, :keys], masked_value))
                    top = jnp.maximum(
                        jnp.max(masked[0], axis=1, keepdims=True), jnp.max(masked[1], axis=1, keepdims=True)
                    )
                    parts = [
                        jnp.exp(masked[side] - top) * m_scr[side, lo : lo + step, :keys] for side in range(2)
                    ]
                    total = jnp.sum(parts[0], axis=1, keepdims=True) + jnp.sum(parts[1], axis=1, keepdims=True)
                    inverse = 1.0 / total
                    for side in range(2):
                        prob_ref[i, side, lo : lo + step, :keys] = (parts[side] * inverse).astype(BF16)
            mixed = jnp.zeros((tall, width), F32)
            for side in range(2):
                value = sides[side][:, :, width:].reshape(wide, width)[:keys]
                mixed = mixed + mm(prob_ref[i, side, :, :keys], value, NN)
            result = fold_heads(mixed, rows, heads_here)
            out_ref[i] = result
            send_scr[i] = pack(result.astype(BF16)[:, :live])
        for k in range(count):
            msgs[k][...] = send_scr[z_index ^ k]

    live = heads_here * HEAD_DIM
    outs = (
        shape(F32, count, rows, width),
        shape(BF16, count, 2, tall, wide),
        shape(BF16, count, rows, width),
        shape(BF16, count, rows, 2 * width),
        shape(BF16, count, rows, 2 * width),
    ) + (shape(BF16, packed_rows(rows, live), 128),) * count
    scratch = (
        shape(F32, 2, tall, wide),
        shape(F32, 2, tall, wide),
        shape(BF16, 2, wide, 128),
        shape(BF16, count, packed_rows(rows, live), 128),
    )
    operands = (*queries, *kv_own, *kv_other)
    found = kernel(
        body, outs, (place, lengths), operands, scratch, micros=6.0, name="attend"
    )
    return found[0], found[1:5], list(found[5:])


def attend_back_call(place, queries, kv_own, kv_other, prob, attn, grads, heads_here):
    count, rows, width = queries.shape
    tall, wide = heads_here * rows, count * rows
    step = 16

    live = heads_here * HEAD_DIM

    def body(place_ref, q_ref, own_ref, oth_ref, prob_ref, attn_ref, *refs):
        grad_refs, (dq_ref, down_ref, doth_ref, p_scr, d_scr, acc, grad_ref) = refs[:count], refs[count:]
        sides = (own_ref, oth_ref)
        acc[...] = jnp.zeros_like(acc)
        grad_ref[...] = jnp.zeros_like(grad_ref)
        for k in range(count):
            grad_ref[place_ref[0] ^ k, :, :live] = unpack(grad_refs[k][...], rows, live)
        for i in range(count):
            keys = (i + 1) * rows
            grad = grad_ref[i]
            stacked_q = stack_heads(q_ref[i], heads_here)
            stacked_g = stack_heads(grad, heads_here)
            product = grad.astype(F32) * attn_ref[i]
            head_of = lane_head(width)
            delta = [
                jnp.sum(jnp.where(head_of == h, product, 0.0), axis=1, keepdims=True) for h in range(heads_here)
            ]
            for side in range(2):
                value = sides[side][:, :, width:].reshape(wide, width)[:keys]
                p_scr[side, :, :keys] = mm(stacked_g, value, NT)
            for h in range(heads_here):
                for at in range(0, rows, step):
                    lo = h * rows + at
                    for side in range(2):
                        weights = prob_ref[i, side, lo : lo + step, :keys].astype(F32)
                        shifted = p_scr[side, lo : lo + step, :keys] - delta[h][at : at + step]
                        d_scr[side, lo : lo + step, :keys] = (weights * shifted).astype(BF16)
            grad_q = jnp.zeros((tall, width), F32)
            for side in range(2):
                key = sides[side][:, :, :width].reshape(wide, width)[:keys]
                moved = d_scr[side, :, :keys]
                grad_q = grad_q + mm(moved, key, NN)
                acc[side, :keys, :width] += mm(moved, stacked_q, TN)
                acc[side, :keys, width:] += mm(prob_ref[i, side, :, :keys], stacked_g, TN)
            dq_ref[i] = (0.125 * fold_heads(grad_q, rows, heads_here)).astype(BF16)
        down_ref[...] = acc[0].reshape(count, rows, 2 * width)
        doth_ref[...] = acc[1].reshape(count, rows, 2 * width).astype(BF16)

    outs = (
        shape(BF16, count, rows, width),
        shape(F32, count, rows, 2 * width),
        shape(BF16, count, rows, 2 * width),
    )
    scratch = (
        shape(F32, 2, tall, wide),
        shape(BF16, 2, tall, wide),
        shape(F32, 2, wide, 2 * width),
        shape(BF16, count, rows, width),
    )
    operands = (queries, kv_own, kv_other, prob, attn, *grads)
    return kernel(body, outs, (place,), operands, scratch, micros=6.0, name="attend_back")


def join_call(place, grad_q, grad_kv, arrived, live):
    count, rows, width = grad_q.shape

    def body(place_ref, q_ref, kv_ref, in_ref, out_ref, *rest):
        msgs, scr = rest[:count], rest[count]
        for b in range(count):
            both = (kv_ref[b] + in_ref[b].astype(F32)).astype(BF16)
            out_ref[b, :, :width] = q_ref[b]
            out_ref[b, :, width:] = both
            dense = [q_ref[b][:, :live], both[:, :live], both[:, width : width + live]]
            scr[b] = pack(jnp.concatenate(dense, axis=1))
        for k in range(count):
            msgs[k][...] = scr[place_ref[0] ^ k]

    message = shape(BF16, packed_rows(rows, 3 * live), 128)
    outs = (shape(BF16, count, rows, 3 * width),) + (message,) * count
    scratch = (shape(BF16, count, *message.shape),)
    joined, *msgs = kernel(body, outs, (place,), (grad_q, grad_kv, arrived), scratch, micros=0.7, name="join_grads")
    return joined, msgs


def gather_heads(place_ref, pieces, scr, rows, live):
    for k, ref in enumerate(pieces):
        scr[place_ref[0] ^ k] = ref[...]
    return jnp.concatenate([unpack(scr[k], rows, live) for k in range(len(pieces))], axis=1)


def norms_call(place, pieces, layer_in, vectors, w_out, live):
    count, rows = len(pieces), layer_in.shape[0]
    model = w_out.shape[0]

    def body(place_ref, *refs):
        in_ref, g2, b2, g3, b3, wo_ref, mid_ref, attn_ref, n3_ref, piece_scr = refs[count:]
        attn = gather_heads(place_ref, refs[:count], piece_scr, rows, live)
        attn_ref[...] = attn
        unit2, _ = unit_norm(attn.astype(F32))
        normed2 = (unit2 * row(g2) + row(b2)).astype(BF16)
        middle = in_ref[...].astype(F32) + mm(normed2, wo_ref[...], NN)
        mid_ref[...] = middle
        unit3, _ = unit_norm(middle)
        n3_ref[...] = (unit3 * row(g3) + row(b3)).astype(BF16)

    outs = (shape(F32, rows, model), shape(BF16, rows, model), shape(BF16, rows, model))
    operands = (*pieces, layer_in, *vectors, w_out)
    scratch = (shape(BF16, count, *pieces[0].shape),)
    return kernel(body, outs, (place,), operands, scratch, micros=1.5, name="norms")


def up_call(place, normed3, w_up, parts):
    rows, (model, hidden) = normed3.shape[0], w_up.shape
    part = hidden // parts

    def body(place_ref, n3_ref, wu_ref, act_ref, slope_ref, *msgs):
        normed = n3_ref[...]
        for r in range(parts):
            upper = mm(normed, wu_ref[:, r * part : (r + 1) * part], NN)
            cumulative = 0.5 * (1.0 + lax.erf(upper * 0.7071067811865476))
            density = jnp.exp(-0.5 * upper * upper) * 0.3989422804014327
            act_ref[r] = (upper * cumulative).astype(BF16)
            slope_ref[r] = (cumulative + upper * density).astype(BF16)
        for k in range(parts):
            msgs[k][...] = act_ref[place_ref[2] ^ k]

    outs = (shape(BF16, parts, rows, part),) * 2 + (shape(BF16, rows, part),) * parts
    act, slope, *msgs = kernel(body, outs, (place,), (normed3, w_up), micros=2.0, name="up_gelu")
    return act, slope, msgs


def padded_quarter(quarter):
    return -(-(quarter + 64) // 128) * 128


def backward_call(place, attn, middle, act, slope, grad_out, vectors, w_out, w_up, w_down, parts, count, live):
    rows = attn.shape[0]
    model, hidden = w_up.shape
    part, quarter = hidden // parts, model // parts
    pad_q = padded_quarter(quarter)
    message = shape(BF16, packed_rows(rows, live), 128)

    def body(
        place_ref, attn_ref, mid_ref, act_ref, slope_ref, go_ref, g2, b2, g3, b3, wo_ref, wu_ref, wd_ref,
        out_ref, gmid_ref, *rest,
    ):
        msgs, heads = rest[:parts], rest[parts : parts + count]
        up_scr, n2_scr, head_scr = rest[parts + count :]
        here = place_ref[2]
        go = go_ref[...]
        middle = mid_ref[...]
        out = middle
        grad3 = jnp.zeros((rows, model), F32)
        for r in range(parts):
            w_d = wd_ref[r * part : (r + 1) * part, :]
            out = out + mm(act_ref[r], w_d, NN)
            grad_up = (mm(go, w_d, NT) * slope_ref[r].astype(F32)).astype(BF16)
            up_scr[r] = grad_up
            grad3 = grad3 + mm(grad_up, wu_ref[:, r * part : (r + 1) * part], NT)
        out_ref[...] = out.astype(BF16)
        unit3, scale3 = unit_norm(middle)
        grad_mid = go.astype(F32) + norm_back(grad3, row(g3), unit3, scale3)
        gmid_ref[...] = grad_mid
        proj = grad_mid.astype(BF16)
        grad2 = mm(proj, wo_ref[...], NT)
        unit2, scale2 = unit_norm(attn_ref[...].astype(F32))
        grad_attn = norm_back(grad2, row(g2), unit2, scale2).astype(BF16)
        for k in range(count):
            head_scr[k] = pack(grad_attn[:, k * live : (k + 1) * live])
        for k in range(count):
            heads[k][...] = head_scr[place_ref[0] ^ k]
        sums = [
            jnp.sum(grad2 * unit2, axis=0, keepdims=True),
            jnp.sum(grad2, axis=0, keepdims=True),
            jnp.sum(grad3 * unit3, axis=0, keepdims=True),
            jnp.sum(grad3, axis=0, keepdims=True),
        ]
        table = jnp.concatenate(sums + [jnp.zeros((4, model), F32)], axis=0)
        normed2 = (unit2 * row(g2) + row(b2)).astype(BF16)
        normed3 = (unit3 * row(g3) + row(b3)).astype(BF16)
        spare, lines = pad_q - quarter, quarter // 64
        for r in range(parts):
            chunks = [table[:, r * quarter + 64 * j : r * quarter + 64 * (j + 1)] for j in range(lines)]
            side = jnp.concatenate(chunks + [jnp.zeros((rows - 8 * lines, 64), F32)], axis=0).astype(BF16)
            pieces = [normed2[:, r * quarter : (r + 1) * quarter], side]
            if spare > 64:
                pieces.append(jnp.zeros((rows, spare - 64), BF16))
            n2_scr[r] = jnp.concatenate(pieces, axis=1)
        for k in range(parts):
            msgs[k][:, :part] = up_scr[here ^ k]
            msgs[k][:, part : part + model] = proj
            msgs[k][:, part + model : part + 2 * model] = normed3
            msgs[k][:, part + 2 * model :] = n2_scr[here ^ k]

    outs = (
        shape(BF16, rows, model),
        shape(F32, rows, model),
    )
    outs += (shape(BF16, rows, part + 2 * model + pad_q),) * parts + (message,) * count
    operands = (attn, middle, act, slope, grad_out, *vectors, w_out, w_up, w_down)
    scratch = (
        shape(BF16, parts, rows, part),
        shape(BF16, parts, rows, pad_q),
        shape(BF16, count, *message.shape),
    )
    found = kernel(body, outs, (place,), operands, scratch, micros=9.0, name="token_backward")
    found = list(found)
    return found[0], found[1], found[2 : 2 + parts], found[2 + parts :]


def down_grad_call(place, acts, grads, chips):
    parts = len(acts)
    part, model = acts[0].shape[1], grads[0].shape[1]
    own = part // (2 * chips)

    def body(place_ref, *refs):
        act_refs, grad_refs, (keep_ref, send_ref, scr) = refs[:parts], refs[parts : 2 * parts], refs[2 * parts :]
        core = place_ref[1]
        act = jnp.concatenate([ref[...] for ref in act_refs], axis=0)
        grad = jnp.concatenate([ref[...] for ref in grad_refs], axis=0)
        scr[...] = mm(act, grad, TN).reshape(chips, 2, own, model)
        for k in range(chips):
            keep_ref[k] = scr[k, core]
            send_ref[k] = scr[k, 1 - core].astype(BF16)

    outs = (shape(F32, chips, own, model), shape(BF16, chips, own, model))
    scratch = (shape(F32, chips, 2, own, model),)
    return kernel(body, outs, (place,), (*acts, *grads), scratch, micros=3.0, name="grad_down")


def up_grad_call(place, back, chips, part, model):
    parts = len(back)
    quarter = model // parts
    own = model // (parts * chips * 2)
    tall = (parts + 1) * own + 8

    def body(place_ref, *refs):
        back_refs = refs[:parts]
        keep_ref, send_ref, up_scr, out_scr, vec_scr = refs[parts:]
        core = place_ref[1]
        ends = (0, part, part + model, part + 2 * model, back_refs[0].shape[1])
        grad_up, proj, normed3, normed2 = (
            jnp.concatenate([ref[:, lo:hi] for ref in back_refs], axis=0) for lo, hi in zip(ends, ends[1:])
        )
        up_scr[...] = mm(normed3, grad_up, TN).reshape(parts, chips, 2, own, part)
        out_scr[...] = mm(normed2, proj, TN)[:quarter].reshape(chips, 2, own, model)
        lines = quarter // 64
        side = jnp.zeros((8 * lines, 64), F32)
        for ref in back_refs:
            side = side + ref[:, ends[3] + quarter : ends[3] + quarter + 64].astype(F32)[: 8 * lines]
        table = jnp.concatenate([side[8 * j : 8 * (j + 1)] for j in range(lines)], axis=1)
        vec_scr[...] = jnp.zeros_like(vec_scr)
        for k in range(chips):
            for side in range(2):
                at = (2 * k + side) * own
                vec_scr[k, side, :, :own] = table[:, at : at + own]
        for k in range(chips):
            for side, ref in ((core, keep_ref), (1 - core, send_ref)):
                pieces = [up_scr[r, k, side] for r in range(parts)] + [out_scr[k, side], vec_scr[k, side]]
                ref[k] = jnp.concatenate(pieces, axis=0).astype(ref.dtype)

    outs = (shape(F32, chips, tall, model), shape(BF16, chips, tall, model))
    scratch = (
        shape(F32, parts, chips, 2, own, part),
        shape(F32, chips, 2, own, model),
        shape(F32, chips, 2, 8, model),
    )
    return kernel(body, outs, (place,), tuple(back), scratch, micros=4.0, name="grad_up_out")


def qkv_grad_call(place, groups, units, grads, gain, bias, weight, parts, live, width):
    count, rows = grads.shape[:2]
    model = weight.shape[0]
    own = model // (parts * count * 2)
    n = len(units)

    def body(place_ref, *refs):
        unit_refs = refs[:n]
        grad_ref, gain_ref, bias_ref, weight_ref, keep_ref, send_ref, unit_scr, scr = refs[n:]
        z_index, core = place_ref[0], place_ref[1]
        for g, ks in enumerate(groups):
            for j, k in enumerate(ks):
                unit_scr[z_index ^ k] = unit_refs[g][j]
        grad = grad_ref[...].reshape(count * rows, 3 * width)
        cross = mm(unit_scr[...].reshape(count * rows, model), grad, TN)
        total = jnp.sum(grad.astype(F32), axis=0, keepdims=True)
        columns = jnp.concatenate([row(gain_ref), row(bias_ref), jnp.zeros((6, model), F32)], axis=0).T
        weight_f = weight_ref[...].astype(F32)
        grad_gain = jnp.sum(weight_f * cross, axis=1, keepdims=True)
        grad_bias = jnp.sum(weight_f * total, axis=1, keepdims=True)
        lane = lax.broadcasted_iota(jnp.int32, (1, 3 * width), 1)
        made = columns[:, 0:1] * cross + columns[:, 1:2] * total
        made = jnp.where(lane == live, grad_gain, jnp.where(lane == live + 1, grad_bias, made))
        scr[...] = made.reshape(parts, count, 2, own, 3 * width)
        for r in range(parts):
            keep_ref[r] = jnp.concatenate([scr[r, k, core] for k in range(count)], axis=0)
            send_ref[r] = jnp.concatenate([scr[r, k, 1 - core] for k in range(count)], axis=0).astype(BF16)

    outs = (shape(F32, parts, count * own, 3 * width), shape(BF16, parts, count * own, 3 * width))
    scratch = (shape(BF16, count, rows, model), shape(F32, parts, count, 2, own, 3 * width))
    operands = (*units, grads, gain, bias, weight)
    return kernel(body, outs, (place,), operands, scratch, micros=4.0, name="grad_qkv")


def spread_call(place, keep, arrived):
    parts = keep.shape[0]

    def body(place_ref, keep_ref, in_ref, *outs):
        for k in range(parts):
            at = place_ref[2] ^ k
            outs[k][...] = (keep_ref[at] + in_ref[at].astype(F32)).astype(BF16)

    return kernel(body, (shape(BF16, *keep.shape[1:]),) * parts, (place,), (keep, arrived), micros=0.8, name="spread")


def halve_call(place, keep, arrived, bit):
    half = keep.shape[0] // 2

    def body(place_ref, keep_ref, in_ref, stay_ref, away_ref):
        mine = (place_ref[0] // bit) % 2
        for j in range(half):
            here, there = 2 * j + mine, 2 * j + 1 - mine
            stay_ref[j] = keep_ref[here] + in_ref[here].astype(F32)
            away_ref[j] = (keep_ref[there] + in_ref[there].astype(F32)).astype(BF16)

    rest = keep.shape[1:]
    return kernel(body, (shape(F32, half, *rest), shape(BF16, half, *rest)), (place,), (keep, arrived), micros=0.8, name="halve")


def finish_down_call(keep, arrived):
    def body(keep_ref, in_ref, out_ref):
        out_ref[...] = keep_ref[0] + in_ref[0].astype(F32)

    return kernel(body, shape(F32, *keep.shape[1:]), (), (keep, arrived), micros=0.6, name="finish_down")


def finish_up_call(place, keep, arrived, parts, own, part):
    model = keep.shape[2]

    def body(place_ref, keep_ref, in_ref, out_ref, g2, b2, g3, b3, *rest):
        msgs, scr = rest[:parts], rest[parts]
        value = keep_ref[0] + in_ref[0].astype(F32)
        out_ref[...] = value[parts * own : (parts + 1) * own]
        for at, ref in enumerate((g2, b2, g3, b3)):
            line = (parts + 1) * own + at
            ref[...] = value[line : line + 1, :own].reshape(own)
        scr[...] = value[: parts * own].reshape(parts, own, part)
        for k in range(parts):
            msgs[k][...] = scr[place_ref[2] ^ k].astype(BF16)

    outs = (shape(F32, own, model),) + (shape(F32, own),) * 4 + (shape(BF16, own, part),) * parts
    scratch = (shape(F32, parts, own, part),)
    return kernel(body, outs, (place,), (keep, arrived), scratch, micros=0.8, name="finish_up")


def place_up_call(place, pieces):
    parts = len(pieces)
    own, part = pieces[0].shape

    def body(place_ref, *refs):
        for k in range(parts):
            at = pl.multiple_of((place_ref[2] ^ k) * part, 128)
            refs[parts][:, pl.ds(at, part)] = refs[k][...].astype(F32)

    return kernel(body, shape(F32, own, parts * part), (place,), tuple(pieces), micros=0.5, name="place_up")


def share_call(place, pieces, chips):
    own = pieces[0].shape[0] // chips

    def body(place_ref, *refs):
        ins, outs, scr = refs[: len(pieces)], refs[len(pieces) : -1], refs[-1]
        total = ins[0][...].astype(F32)
        for ref in ins[1:]:
            total = total + ref[...].astype(F32)
        scr[...] = total.reshape(chips, own, total.shape[1])
        for k in range(chips):
            outs[k][...] = scr[place_ref[0] ^ k].astype(BF16)

    lanes = pieces[0].shape[1]
    outs = (shape(BF16, own, lanes),) * chips
    return kernel(body, outs, (place,), tuple(pieces), (shape(F32, chips, own, lanes),), micros=0.7, name="share")


def finish_qkv_call(place, pieces, model, live, width):
    count, own = len(pieces), pieces[0].shape[0]

    def body(place_ref, *refs):
        q_ref, k_ref, v_ref, gain_ref, bias_ref, in_ref = refs[count:]
        for k in range(count):
            in_ref[place_ref[0] ^ k] = refs[k][...].astype(F32)
        for at, ref in enumerate((q_ref, k_ref, v_ref)):
            ref[...] = jnp.concatenate(
                [in_ref[k, :, at * width : at * width + live] for k in range(count)], axis=1
            )
        total = jnp.sum(in_ref[:, :, live : live + 2], axis=0).T
        gain_ref[...] = total[0:1].reshape(own)
        bias_ref[...] = total[1:2].reshape(own)

    outs = (shape(F32, own, model),) * 3 + (shape(F32, own),) * 2
    scratch = (shape(F32, count, *pieces[0].shape),)
    return kernel(body, outs, (place,), tuple(pieces), scratch, micros=0.8, name="finish_qkv")


def input_grad_call(place, pieces, layer_in, grad_mid, gain, w_query, w_key, w_value, live):
    count = len(pieces)
    rows, model = layer_in.shape

    def body(place_ref, *refs):
        in_ref, gmid_ref, gain_ref, wq_ref, wk_ref, wv_ref, out_ref, scr = refs[count:]
        for k in range(count):
            scr[place_ref[0] ^ k] = refs[k][...]
        blocks = [unpack(scr[k], rows, 3 * live) for k in range(count)]
        grad = jnp.zeros((rows, model), F32)
        for at, w_ref in enumerate((wq_ref, wk_ref, wv_ref)):
            part = jnp.concatenate([block[:, at * live : (at + 1) * live] for block in blocks], axis=1)
            grad = grad + mm(part, w_ref[...], NT)
        unit, scale = unit_norm(in_ref[...].astype(F32))
        out_ref[...] = (gmid_ref[...] + norm_back(grad, row(gain_ref), unit, scale)).astype(BF16)

    operands = (*pieces, layer_in, grad_mid, gain, w_query, w_key, w_value)
    scratch = (shape(BF16, count, *pieces[0].shape),)
    return kernel(body, shape(BF16, rows, model), (place,), operands, scratch, micros=3.0, name="grad_inputs")


def swap_core(value):
    return lax.ppermute(value, "core", [(0, 1), (1, 0)])


def swap(value, axis, bit):
    return lax.ppermute(value, axis, [(k, k ^ bit) for k in range(lax.axis_size(axis))])


def trade(messages, axis):
    found = {k: swap(messages[k], axis, k) for k in range(len(messages) - 1, 0, -1)}
    return [messages[0]] + [found[k] for k in range(1, len(messages))]


def gather_chips(block, chips):
    found = {0: block}
    bit = chips // 2
    while bit >= 1:
        for k in sorted(found):
            found[k | bit] = swap(found[k], "chip", bit)
        bit //= 2
    return [found[k] for k in range(chips)]


def scatter_chips(place, keep, arrived, chips, bit):
    while bit < chips:
        keep, away = halve_call(place, keep, arrived, bit)
        arrived = swap(away, "chip", bit)
        bit *= 2
    return keep, arrived


def after(values, *others):
    return lax.optimization_barrier((values, others))[0]


def fast_shards(
    inputs, doc_lengths, ln1_gain, ln1_bias, w_query, w_key, w_value, ln2_gain, ln2_bias, w_out,
    ln3_gain, ln3_bias, w_up, w_down, out_grad,
):
    rows, model = inputs.shape[1:]
    chips, parts = lax.axis_size("chip"), lax.axis_size("rows")
    z_index = lax.axis_index("chip")
    heads_here = HEADS // chips
    live = heads_here * HEAD_DIM
    width = -(-live // 128) * 128
    hidden = w_up.shape[1]
    part = hidden // parts
    own = model // (parts * chips * 2)
    place = jnp.stack([z_index, lax.axis_index("core"), lax.axis_index("rows")]).astype(jnp.int32)
    scope = jax.named_scope

    def columns(weight):
        mine = lax.dynamic_slice_in_dim(weight, z_index * live, live, 1)
        return jnp.pad(mine, ((0, 0), (0, width - live)))

    place, layer_in, out_grad = lax.optimization_barrier((place, inputs[0], out_grad[0]))
    with scope("gather_in"):
        blocks = gather_chips(layer_in, chips)
    grad_out = mask_call(place, doc_lengths, out_grad)
    w_heads = jnp.concatenate([columns(w_query), columns(w_key), columns(w_value)], axis=1)
    groups = [g for g in ([0], list(range(1, chips - 1)), [chips - 1]) if g] if chips > 1 else [[0]]
    made = [qkv_call([blocks[k] for k in g], ln1_gain, ln1_bias, w_heads, width) for g in groups]
    queries, kv_own, units = ([m[at] for m in made] for at in range(3))
    with scope("core_kv"):
        kv_other = [swap_core(v) for v in kv_own]
    attn_heads, (prob, queries, kv_own, kv_other), messages = attend_call(
        place, doc_lengths, groups, queries, kv_own, kv_other, heads_here
    )
    fence = lax.optimization_barrier
    with scope("chip_attn"):
        pieces = trade(messages, "chip")
    with scope("plane_out"):
        grads_plane = trade([grad_out] * parts, "rows")
    pieces = after(pieces, grads_plane)

    vectors = (ln2_gain, ln2_bias, ln3_gain, ln3_bias)
    middle, attn, normed3 = norms_call(place, pieces, layer_in, vectors, w_out, live)
    act, slope, acts = up_call(place, normed3, w_up, parts)
    with scope("plane_act"):
        acts = trade(acts, "rows")
    output, grad_mid, back, messages = backward_call(
        place, attn, middle, act, slope, grad_out, vectors, w_out, w_up, w_down, parts, chips, live
    )
    back = after(back, acts[1:])
    with scope("chip_grad"):
        grad_heads = trade(messages, "chip")
    with scope("plane_back"):
        far = [swap(back[k], "rows", k) for k in range(3, parts)]
    grad_q, grad_kv, grad_kv_other = attend_back_call(
        place, queries, kv_own, kv_other, prob, attn_heads, grad_heads, heads_here
    )
    with scope("core_grad"):
        grad_kv_other = swap_core(grad_kv_other)
    down_keep, down_send = down_grad_call(place, after(acts, grad_q), grads_plane, chips)
    grad_kv_other, down_send, far = fence((grad_kv_other, down_send, far))
    with scope("core_down"):
        down_recv = swap_core(down_send)
    with scope("plane_back"):
        near = after(back[1:3], far)
        back = back[:1] + [swap(near[k], "rows", k + 1) for k in range(len(near))] + far
    grad_qkv, messages = join_call(place, grad_q, grad_kv, grad_kv_other, live)
    with scope("down_sum"):
        down_keep, down_away = halve_call(place, down_keep, after(down_recv, grad_qkv), 1)
        grad_qkv, down_away = fence((grad_qkv, down_away))
        down_recv = swap(down_away, "chip", 1)
    with scope("chip_qkv"):
        grad_pieces = trade(messages, "chip")
    qkv_keep, qkv_send = qkv_grad_call(
        place, groups, units, grad_qkv, ln1_gain, ln1_bias, w_heads, parts, live, width
    )
    with scope("core_w"):
        qkv_send = swap_core(qkv_send)
    qkv_send = after(qkv_send, (grad_pieces, down_recv))
    qkv_sums = spread_call(place, qkv_keep, qkv_send)
    with scope("down_sum"):
        down_keep, down_last = scatter_chips(place, down_keep, down_recv, chips, 2)
    back = after(back, (down_keep, qkv_sums))
    up_keep, up_send = up_grad_call(place, back, chips, part, model)
    with scope("plane_w"):
        traded = trade(qkv_sums, "rows")
    with scope("core_up"):
        up_recv = swap_core(up_send)
    up_keep, up_away = halve_call(place, up_keep, up_recv, 1)
    with scope("up_sum"):
        up_recv = swap(up_away, "chip", 1)
    traded = after(traded, up_away)
    with scope("chip_w"):
        shared = share_call(place, traded, chips)
        qkv_all = trade(shared, "chip")
    grad_inputs = input_grad_call(
        place, grad_pieces, layer_in, grad_mid, ln1_gain, w_query, w_key, w_value, live
    )
    gwd = finish_down_call(down_keep, down_last)
    up_recv = after(up_recv, (down_last, traded))
    with scope("up_sum"):
        up_keep, up_last = scatter_chips(place, up_keep, up_recv, chips, 2)
    up_last = after(up_last, (qkv_all, gwd, grad_inputs))
    gwo, g2, b2, g3, b3, *up_rows = finish_up_call(place, up_keep, up_last, parts, own, part)
    with scope("plane_rows"):
        up_rows = trade(up_rows, "rows")
    gwq, gwk, gwv, g1, b1 = finish_qkv_call(place, qkv_all, model, live, width)
    gwu = place_up_call(place, up_rows)
    return (
        output[None], grad_inputs[None], g1, b1, gwq, gwk, gwv, g2, b2, gwo, g3, b3, gwu, gwd,
    )


def takes_fast(mesh):
    seq, parts = mesh.shape["seq"], mesh.shape["rows"]
    chips = seq // 2
    return seq % 2 == 0 and chips & (chips - 1) == 0 and parts in (1, 2, 4) and HEADS % max(chips, 1) == 0


def solution(mesh):
    if takes_fast(mesh):
        parts, seq = mesh.shape["rows"], mesh.shape["seq"]
        split = jax.sharding.Mesh(mesh.devices.reshape(parts, seq // 2, 2), ("rows", "chip", "core"))
        return mapped(fast_shards, split, ("chip", "core"))
    return mapped(shards, mesh, "seq")
```

```python
import math

import jax
import jax.numpy as jnp
from jax import lax
from jax.experimental import pallas as pl
from jax.experimental.pallas import tpu as pltpu
from jax.sharding import PartitionSpec as P

HEADS = 12
HEAD_DIM = 64


segment_pairs = ((2048, 1), (4096, 2), (8192, 4), (16384, 6))
masked_value = -1e30


def layer_norm(vector, gain_vec, bias_vec):
    row_mean = jnp.mean(vector, axis=-1, keepdims=True)
    centered = vector - row_mean
    row_var = jnp.mean(centered * centered, axis=-1, keepdims=True)
    return centered * lax.rsqrt(row_var + 1e-05) * gain_vec + bias_vec


def doc_of(positions, doc_ends):
    return jnp.sum((positions[:, None] >= doc_ends[None, :]).astype(jnp.int32), axis=1)


def pair_terms(query_pos, key_pos, query_doc, key_doc, head_count):
    head_ids = jnp.arange(head_count, dtype=jnp.int32)
    multiplicity = jnp.zeros((head_count, query_pos.shape[0], key_pos.shape[0]), jnp.float32)
    for seg_width, dilation in segment_pairs:
        same_seg = query_pos[:, None] // seg_width == key_pos[None, :] // seg_width
        query_pick = (query_pos % seg_width % dilation)[None, :] == (head_ids % dilation)[:, None]
        key_pick = (key_pos % seg_width % dilation)[None, :] == (head_ids % dilation)[:, None]
        joined = same_seg[None] & query_pick[:, :, None] & key_pick[:, None, :]
        multiplicity = multiplicity + joined.astype(jnp.float32)
    allowed = (key_pos[None, :] <= query_pos[:, None]) & (query_doc[:, None] == key_doc[None, :])
    allowed = allowed[None] & (multiplicity > 0.0)
    return (jnp.log(jnp.maximum(multiplicity, 1.0)), allowed)


def rows_inner(left, right):
    return lax.dot_general(
        left, right, (((0,), (0,)), ((), ())), preferred_element_type=jnp.float32
    )


def cols_inner(left, right):
    return lax.dot_general(
        left, right, (((1,), (1,)), ((), ())), preferred_element_type=jnp.float32
    )


def over_blocks(state, piece, step_fn):
    total_rows = piece[0].shape[0]
    block_rows = math.gcd(total_rows, 512)
    block_total = total_rows // block_rows
    split = tuple((part.reshape((block_total, block_rows) + part.shape[1:]) for part in piece))

    def inner(carried, block_item):
        return (step_fn(carried, block_item[1], block_item[0] * block_rows), None)

    result, unused = lax.scan(inner, state, (jnp.arange(block_total, dtype=jnp.int32), split))
    return result


def add_rows(buffer, start_pos, addend):
    current = lax.dynamic_slice_in_dim(buffer, start_pos, addend.shape[0], 0)
    return lax.dynamic_update_slice_in_dim(buffer, current + addend, start_pos, 0)


def shards(
    inputs,
    doc_lengths,
    ln1_gain,
    ln1_bias,
    w_query,
    w_key,
    w_value,
    ln2_gain,
    ln2_bias,
    w_out,
    ln3_gain,
    ln3_bias,
    w_up,
    w_down,
    out_grad,
):
    tok_rows = inputs.shape[1]
    head_count = HEADS
    head_size = HEAD_DIM
    model_width = inputs.shape[2]
    row_total = tok_rows * lax.axis_size("seq")
    layer_in = inputs[0].astype(jnp.float32)
    doc_ends = jnp.cumsum(doc_lengths[0])
    first_pos = lax.axis_index("seq") * tok_rows
    query_pos = first_pos + jnp.arange(tok_rows, dtype=jnp.int32)
    query_doc = doc_of(query_pos, doc_ends)
    valid = (query_doc < doc_lengths.shape[1]).astype(jnp.float32)
    first_norm, first_back = jax.vjp(layer_norm, layer_in, ln1_gain, ln1_bias)
    normed_one = first_norm.astype(jnp.bfloat16)
    queries = jnp.dot(normed_one, w_query, preferred_element_type=jnp.float32).astype(jnp.bfloat16)
    keys_local = jnp.dot(normed_one, w_key, preferred_element_type=jnp.float32).astype(jnp.bfloat16)
    values_local = jnp.dot(normed_one, w_value, preferred_element_type=jnp.float32).astype(
        jnp.bfloat16
    )
    query_heads = queries.reshape(tok_rows, head_count, head_size)

    def key_block_terms(key_start, key_count):
        key_pos = key_start + jnp.arange(key_count, dtype=jnp.int32)
        key_doc = doc_of(key_pos, doc_ends)
        return pair_terms(query_pos, key_pos, query_doc, key_doc, head_count)

    def with_pruning(step_fn):

        def wrapped(state, parts, start_pos):
            return step_fn(state, parts, start_pos)

        return wrapped

    def forward_step(state, parts, key_start):
        run_max, run_total, run_acc = state
        key_blk = parts[0].reshape(-1, head_count, head_size)
        value_blk = parts[1].reshape(-1, head_count, head_size)
        log_mult, allowed = key_block_terms(key_start, key_blk.shape[0])
        scores = 0.125 * jnp.einsum(
            "qhd,khd->hqk", query_heads, key_blk, preferred_element_type=jnp.float32
        )
        logits = jnp.where(allowed, scores + log_mult, masked_value)
        new_max = jnp.maximum(run_max, jnp.max(logits, axis=-1))
        weights = jnp.where(allowed, jnp.exp(logits - new_max[..., None]), 0.0)
        factor = jnp.exp(run_max - new_max)
        run_total = run_total * factor + jnp.sum(weights, axis=-1)
        run_acc = run_acc * factor[..., None] + jnp.einsum(
            "hqk,khd->hqd",
            weights.astype(jnp.bfloat16),
            value_blk,
            preferred_element_type=jnp.float32,
        )
        return (new_max, run_total, run_acc)

    forward_pruned = with_pruning(forward_step)
    start_state = (
        jnp.full((head_count, tok_rows), masked_value, jnp.float32),
        jnp.zeros((head_count, tok_rows), jnp.float32),
        jnp.zeros((head_count, tok_rows, head_size), jnp.float32),
    )
    final_state = over_blocks(
        start_state,
        (
            lax.all_gather(keys_local, "seq", axis=0, tiled=True),
            lax.all_gather(values_local, "seq", axis=0, tiled=True),
        ),
        forward_pruned,
    )
    run_max, run_total, run_acc = final_state
    row_lse = run_max + jnp.log(run_total)
    attn = (run_acc / run_total[..., None]).transpose(1, 0, 2).reshape(tok_rows, model_width)
    second_norm, second_back = jax.vjp(layer_norm, attn, ln2_gain, ln2_bias)
    normed_two = second_norm.astype(jnp.bfloat16)
    middle = layer_in + jnp.dot(normed_two, w_out, preferred_element_type=jnp.float32)
    third_norm, third_back = jax.vjp(layer_norm, middle, ln3_gain, ln3_bias)
    normed_three = third_norm.astype(jnp.bfloat16)
    upper = jnp.dot(normed_three, w_up, preferred_element_type=jnp.float32)
    activated_f, gelu_back = jax.vjp(
        lambda upper_in: jax.nn.gelu(upper_in, approximate=False), upper
    )
    activated = activated_f.astype(jnp.bfloat16)
    layer_out = middle + jnp.dot(activated, w_down, preferred_element_type=jnp.float32)
    grad_out = out_grad[0].astype(jnp.float32) * valid[:, None]
    grad_branch = grad_out.astype(jnp.bfloat16)
    grad_w_down = rows_inner(activated, grad_branch)
    grad_act = cols_inner(grad_branch, w_down)
    grad_upper = gelu_back(grad_act)[0].astype(jnp.bfloat16)
    grad_w_up = rows_inner(normed_three, grad_upper)
    grad_n3 = cols_inner(grad_upper, w_up)
    grad_mid_norm, grad_ln3_gain, grad_ln3_bias = third_back(grad_n3)
    grad_middle = grad_out + grad_mid_norm
    grad_proj = grad_middle.astype(jnp.bfloat16)
    grad_w_out = rows_inner(normed_two, grad_proj)
    grad_n2 = cols_inner(grad_proj, w_out)
    grad_attn_f, grad_ln2_gain, grad_ln2_bias = second_back(grad_n2)
    grad_attn = grad_attn_f.astype(jnp.bfloat16)
    grad_heads = grad_attn.reshape(tok_rows, head_count, head_size)
    row_delta = jnp.sum(
        (grad_attn.astype(jnp.float32) * attn).reshape(tok_rows, head_count, head_size), axis=-1
    )

    def backward_step(state, parts, key_start):
        grad_q_acc, grad_k_rows, grad_v_rows = state
        key_blk = parts[0].reshape(-1, head_count, head_size)
        value_blk = parts[1].reshape(-1, head_count, head_size)
        key_count = key_blk.shape[0]
        log_mult, allowed = key_block_terms(key_start, key_count)
        scores = 0.125 * jnp.einsum(
            "qhd,khd->hqk", query_heads, key_blk, preferred_element_type=jnp.float32
        )
        logits = jnp.where(allowed, scores + log_mult, masked_value)
        weights = jnp.where(allowed, jnp.exp(logits - row_lse[..., None]), 0.0)
        grad_weights = jnp.einsum(
            "qhd,khd->hqk", grad_heads, value_blk, preferred_element_type=jnp.float32
        )
        grad_scores = (weights * (grad_weights - row_delta.T[..., None])).astype(jnp.bfloat16)
        grad_q_acc = grad_q_acc + 0.125 * jnp.einsum(
            "hqk,khd->qhd", grad_scores, key_blk, preferred_element_type=jnp.float32
        )
        value_part = jnp.einsum(
            "hqk,qhd->khd",
            weights.astype(jnp.bfloat16),
            grad_heads,
            preferred_element_type=jnp.float32,
        ).reshape(key_count, model_width)
        key_part = 0.125 * jnp.einsum(
            "hqk,qhd->khd", grad_scores, query_heads, preferred_element_type=jnp.float32
        ).reshape(key_count, model_width)
        grad_k_rows = add_rows(grad_k_rows, key_start, key_part)
        grad_v_rows = add_rows(grad_v_rows, key_start, value_part)
        return (grad_q_acc, grad_k_rows, grad_v_rows)

    backward_pruned = with_pruning(backward_step)
    zero_state = (
        jnp.zeros((tok_rows, head_count, head_size), jnp.float32),
        jnp.zeros((row_total, model_width), jnp.float32),
        jnp.zeros((row_total, model_width), jnp.float32),
    )
    back_state = over_blocks(
        zero_state,
        (
            lax.all_gather(keys_local, "seq", axis=0, tiled=True),
            lax.all_gather(values_local, "seq", axis=0, tiled=True),
        ),
        backward_pruned,
    )
    grad_q_acc, grad_k_rows, grad_v_rows = back_state
    grad_k_acc, grad_v_acc = (
        lax.psum_scatter(
            grad_k_rows.astype(jnp.bfloat16), "seq", scatter_dimension=0, tiled=True
        ).astype(jnp.float32),
        lax.psum_scatter(
            grad_v_rows.astype(jnp.bfloat16), "seq", scatter_dimension=0, tiled=True
        ).astype(jnp.float32),
    )
    grad_queries = grad_q_acc.reshape(tok_rows, model_width).astype(jnp.bfloat16)
    grad_keys = grad_k_acc.astype(jnp.bfloat16)
    grad_values = grad_v_acc.astype(jnp.bfloat16)
    grad_w_query = rows_inner(normed_one, grad_queries)
    grad_w_key = rows_inner(normed_one, grad_keys)
    grad_w_value = rows_inner(normed_one, grad_values)
    grad_n1 = (
        cols_inner(grad_queries, w_query)
        + cols_inner(grad_keys, w_key)
        + cols_inner(grad_values, w_value)
    )
    grad_in_norm, grad_ln1_gain, grad_ln1_bias = first_back(grad_n1)
    grad_inputs = (grad_middle + grad_in_norm).astype(jnp.bfloat16)
    summed = (
        lax.psum_scatter(grad_ln1_gain, ("rows", "seq"), scatter_dimension=0, tiled=True),
        lax.psum_scatter(grad_ln1_bias, ("rows", "seq"), scatter_dimension=0, tiled=True),
        lax.psum_scatter(grad_w_query, ("rows", "seq"), scatter_dimension=0, tiled=True),
        lax.psum_scatter(grad_w_key, ("rows", "seq"), scatter_dimension=0, tiled=True),
        lax.psum_scatter(grad_w_value, ("rows", "seq"), scatter_dimension=0, tiled=True),
        lax.psum_scatter(grad_ln2_gain, ("rows", "seq"), scatter_dimension=0, tiled=True),
        lax.psum_scatter(grad_ln2_bias, ("rows", "seq"), scatter_dimension=0, tiled=True),
        lax.psum_scatter(grad_w_out, ("rows", "seq"), scatter_dimension=0, tiled=True),
        lax.psum_scatter(grad_ln3_gain, ("rows", "seq"), scatter_dimension=0, tiled=True),
        lax.psum_scatter(grad_ln3_bias, ("rows", "seq"), scatter_dimension=0, tiled=True),
        lax.psum_scatter(grad_w_up, ("rows", "seq"), scatter_dimension=0, tiled=True),
        lax.psum_scatter(grad_w_down, ("rows", "seq"), scatter_dimension=0, tiled=True),
    )
    return (
        layer_out.astype(jnp.bfloat16)[None],
        grad_inputs[None],
        summed[0],
        summed[1],
        summed[2],
        summed[3],
        summed[4],
        summed[5],
        summed[6],
        summed[7],
        summed[8],
        summed[9],
        summed[10],
        summed[11],
    )


def mapped(step, mesh, seq):
    spread = P(("rows",) + (seq if isinstance(seq, tuple) else (seq,)))
    tokens, plain = P("rows", seq, None), P()
    weights = P(spread[0], None)
    return jax.shard_map(
        step,
        mesh=mesh,
        in_specs=(tokens, P("rows", None)) + (plain,) * 12 + (tokens,),
        out_specs=(tokens, tokens, spread, spread, weights, weights, weights, spread, spread, weights)
        + (spread, spread, weights, weights),
        check_vma=False,
    )


F32 = jnp.float32
PACE = 1e6
BF16 = jnp.bfloat16
NT = (((1,), (1,)), ((), ()))
TN = (((0,), (0,)), ((), ()))
NN = (((1,), (0,)), ((), ()))


def mm(left, right, dims):
    return lax.dot_general(left, right, dims, preferred_element_type=F32)


def unit_norm(vector):
    centered = vector - jnp.mean(vector, axis=-1, keepdims=True)
    scale = lax.rsqrt(jnp.mean(centered * centered, axis=-1, keepdims=True) + 1e-05)
    return centered * scale, scale


def norm_back(grad, gain, unit, scale):
    weighted = grad * gain
    mean_w = jnp.mean(weighted, axis=-1, keepdims=True)
    mean_wu = jnp.mean(weighted * unit, axis=-1, keepdims=True)
    return scale * (weighted - mean_w - unit * mean_wu)


def shape(dtype, *dims):
    return jax.ShapeDtypeStruct(dims, dtype)


def row(ref):
    return ref[...].reshape(1, ref.shape[0])


def size_of(item):
    total = jnp.dtype(item.dtype).itemsize
    for dim in item.shape:
        total *= dim
    return total


def kernel(body, outs, scalars, operands, scratch=(), micros=2.0, name=None):
    single = not isinstance(outs, (tuple, list))
    listed = (outs,) if single else tuple(outs)
    vmem = pl.BlockSpec(memory_space=pltpu.VMEM)
    smem = pl.BlockSpec(memory_space=pltpu.SMEM)
    moved = sum(size_of(v) for v in (*operands, *listed))
    held = sum(size_of(v) for v in scratch)
    return pl.pallas_call(
        body,
        out_shape=outs if single else listed,
        in_specs=[smem] * len(scalars) + [vmem] * len(operands),
        out_specs=vmem if single else (vmem,) * len(listed),
        scratch_shapes=[pltpu.VMEM(v.shape, v.dtype) for v in scratch],
        compiler_params=pltpu.CompilerParams(vmem_limit_bytes=min(60 << 20, (moved + held) * 5 // 4 + (6 << 20))),
        cost_estimate=pl.CostEstimate(flops=int(micros * PACE), bytes_accessed=int(micros * PACE / 1e3), transcendentals=0),
        name=name,
    )(*scalars, *operands)


def packed_rows(rows, live):
    return rows * live // 128


def pack(block):
    rows, live = block.shape
    whole = live // 128
    pieces = [block[:, 128 * j : 128 * (j + 1)] for j in range(whole)]
    if live % 128:
        rest = block[:, 128 * whole :]
        pieces.append(jnp.concatenate([rest[: rows // 2], rest[rows // 2 :]], axis=1))
    return jnp.concatenate(pieces, axis=0)


def unpack(block, rows, live):
    whole = live // 128
    pieces = [block[rows * j : rows * (j + 1)] for j in range(whole)]
    if live % 128:
        rest = block[rows * whole :]
        pieces.append(jnp.concatenate([rest[:, :64], rest[:, 64:]], axis=0))
    return jnp.concatenate(pieces, axis=1)


def mask_call(place, lengths, out_grad):
    rows, model = out_grad.shape

    def body(place_ref, len_ref, in_ref, out_ref):
        last = jnp.int32(0)
        for d in range(lengths.shape[1]):
            last = last + len_ref[0, d]
        pos = lax.broadcasted_iota(jnp.int32, (rows, 1), 0) + (2 * place_ref[0] + place_ref[1]) * rows
        out_ref[...] = jnp.where(pos < last, in_ref[...].astype(F32), 0.0).astype(BF16)

    return kernel(body, shape(BF16, rows, model), (place, lengths), (out_grad,), micros=0.7, name="mask_grad")


def qkv_call(blocks, gain, bias, weight, width):
    count = len(blocks)
    rows, model = blocks[0].shape

    def body(*refs):
        xs, (gain_ref, bias_ref, weight_ref, q_ref, kv_ref, unit_ref) = refs[:count], refs[count:]
        for k in range(count):
            unit, _ = unit_norm(xs[k][...].astype(F32))
            normed = (unit * row(gain_ref) + row(bias_ref)).astype(BF16)
            made = mm(normed, weight_ref[...], NN)
            q_ref[k] = (made[:, :width].astype(BF16).astype(F32) * 0.125).astype(BF16)
            kv_ref[k] = made[:, width:].astype(BF16)
            unit_ref[k] = unit.astype(BF16)

    outs = (
        shape(BF16, count, rows, width),
        shape(BF16, count, rows, 2 * width),
        shape(BF16, count, rows, model),
    )
    return kernel(body, outs, (), (*blocks, gain, bias, weight), micros=1.2 * count, name="qkv_heads")


def lane_head(lanes):
    return lax.broadcasted_iota(jnp.int32, (1, lanes), 1) // HEAD_DIM


def residue(pos_f, modulus):
    return pos_f - modulus * jnp.floor((pos_f + 0.5) * (1.0 / modulus))


def stack_heads(block, heads_here):
    head_of = lane_head(block.shape[1])
    return jnp.concatenate(
        [jnp.where(head_of == h, block, jnp.zeros_like(block)) for h in range(heads_here)], axis=0
    )


def fold_heads(stacked, rows, heads_here):
    head_of = lane_head(stacked.shape[1])
    total = jnp.zeros((rows, stacked.shape[1]), stacked.dtype)
    for h in range(heads_here):
        total = jnp.where(head_of == h, stacked[h * rows : (h + 1) * rows], total)
    return total


def attend_call(place, lengths, groups, queries, kv_own, kv_other, heads_here):
    count = sum(len(g) for g in groups)
    rows, width = queries[0].shape[1:]
    tall, wide = heads_here * rows, count * rows
    docs = lengths.shape[1]
    step = 16
    n = len(groups)

    def body(place_ref, len_ref, *refs):
        q_in, own_in, oth_in = refs[:n], refs[n : 2 * n], refs[2 * n : 3 * n]
        out_ref, prob_ref, q_ref, own_ref, oth_ref = refs[3 * n : 3 * n + 5]
        msgs, (s_scr, m_scr, hot_scr, send_scr) = refs[3 * n + 5 : 3 * n + 5 + count], refs[3 * n + 5 + count :]
        z_index, core = place_ref[0], place_ref[1]
        for g, ks in enumerate(groups):
            for j, k in enumerate(ks):
                q_ref[z_index ^ k] = q_in[g][j]
                own_ref[z_index ^ k] = own_in[g][j]
                oth_ref[z_index ^ k] = oth_in[g][j]
        sides = (own_ref, oth_ref)
        cores = (core, 1 - core)
        lane = lax.broadcasted_iota(jnp.int32, (rows, 128), 1).astype(F32)
        for side in range(2):
            for b in range(count):
                pos = lax.broadcasted_iota(jnp.int32, (rows, 1), 0) + (2 * b + cores[side]) * rows
                hot = (residue(pos.astype(F32), 12.0) == lane).astype(F32)
                hot_scr[side, b * rows : (b + 1) * rows, :] = hot.astype(BF16)
        for i in range(count):
            keys = (i + 1) * rows
            pos = lax.broadcasted_iota(jnp.int32, (rows, 1), 0) + (2 * i + core) * rows
            pos_f = pos.astype(F32)
            begin = jnp.zeros_like(pos)
            run = jnp.int32(0)
            for d in range(docs):
                run = run + len_ref[0, d]
                begin = jnp.where(pos >= run, run, begin)
            tables = []
            for h in range(heads_here):
                head = (z_index * heads_here + h).astype(F32)
                table = jnp.ones((rows, 128), F32)
                for r in (2.0, 4.0, 6.0):
                    mine = residue(head, r)
                    pick_q = (residue(pos_f, r) == mine).astype(F32)
                    pick_k = (residue(lane, r) == mine).astype(F32)
                    table = table + pick_q * pick_k
                tables.append(jnp.where(lane < 12.0, table, 0.0))
            table = jnp.concatenate(tables, axis=0).astype(BF16)
            stacked = stack_heads(q_ref[i], heads_here)
            for side in range(2):
                key = sides[side][:, :, :width].reshape(wide, width)[:keys]
                s_scr[side, :, :keys] = mm(stacked, key, NT)
                m_scr[side, :, :keys] = mm(table, hot_scr[side, :keys], NT)
            key_pos = [
                jnp.concatenate(
                    [
                        lax.broadcasted_iota(jnp.int32, (1, rows), 1) + (2 * b + cores[side]) * rows
                        for b in range(i + 1)
                    ],
                    axis=1,
                )
                for side in range(2)
            ]
            for h in range(heads_here):
                for at in range(0, rows, step):
                    lo = h * rows + at
                    pos_c, begin_c = pos[at : at + step], begin[at : at + step]
                    masked = []
                    for side in range(2):
                        ok = (key_pos[side] <= pos_c) & (key_pos[side] >= begin_c)
                        masked.append(jnp.where(ok, s_scr[side, lo : lo + step, :keys], masked_value))
                    top = jnp.maximum(
                        jnp.max(masked[0], axis=1, keepdims=True), jnp.max(masked[1], axis=1, keepdims=True)
                    )
                    parts = [
                        jnp.exp(masked[side] - top) * m_scr[side, lo : lo + step, :keys] for side in range(2)
                    ]
                    total = jnp.sum(parts[0], axis=1, keepdims=True) + jnp.sum(parts[1], axis=1, keepdims=True)
                    inverse = 1.0 / total
                    for side in range(2):
                        prob_ref[i, side, lo : lo + step, :keys] = (parts[side] * inverse).astype(BF16)
            mixed = jnp.zeros((tall, width), F32)
            for side in range(2):
                value = sides[side][:, :, width:].reshape(wide, width)[:keys]
                mixed = mixed + mm(prob_ref[i, side, :, :keys], value, NN)
            result = fold_heads(mixed, rows, heads_here)
            out_ref[i] = result
            send_scr[i] = pack(result.astype(BF16)[:, :live])
        for k in range(count):
            msgs[k][...] = send_scr[z_index ^ k]

    live = heads_here * HEAD_DIM
    outs = (
        shape(F32, count, rows, width),
        shape(BF16, count, 2, tall, wide),
        shape(BF16, count, rows, width),
        shape(BF16, count, rows, 2 * width),
        shape(BF16, count, rows, 2 * width),
    ) + (shape(BF16, packed_rows(rows, live), 128),) * count
    scratch = (
        shape(F32, 2, tall, wide),
        shape(F32, 2, tall, wide),
        shape(BF16, 2, wide, 128),
        shape(BF16, count, packed_rows(rows, live), 128),
    )
    operands = (*queries, *kv_own, *kv_other)
    found = kernel(
        body, outs, (place, lengths), operands, scratch, micros=6.0, name="attend"
    )
    return found[0], found[1:5], list(found[5:])


def attend_back_call(place, queries, kv_own, kv_other, prob, attn, grads, heads_here):
    count, rows, width = queries.shape
    tall, wide = heads_here * rows, count * rows
    step = 16

    live = heads_here * HEAD_DIM

    def body(place_ref, q_ref, own_ref, oth_ref, prob_ref, attn_ref, *refs):
        grad_refs, (dq_ref, down_ref, doth_ref, p_scr, d_scr, acc, grad_ref) = refs[:count], refs[count:]
        sides = (own_ref, oth_ref)
        acc[...] = jnp.zeros_like(acc)
        grad_ref[...] = jnp.zeros_like(grad_ref)
        for k in range(count):
            grad_ref[place_ref[0] ^ k, :, :live] = unpack(grad_refs[k][...], rows, live)
        for i in range(count):
            keys = (i + 1) * rows
            grad = grad_ref[i]
            stacked_q = stack_heads(q_ref[i], heads_here)
            stacked_g = stack_heads(grad, heads_here)
            product = grad.astype(F32) * attn_ref[i]
            head_of = lane_head(width)
            delta = [
                jnp.sum(jnp.where(head_of == h, product, 0.0), axis=1, keepdims=True) for h in range(heads_here)
            ]
            for side in range(2):
                value = sides[side][:, :, width:].reshape(wide, width)[:keys]
                p_scr[side, :, :keys] = mm(stacked_g, value, NT)
            for h in range(heads_here):
                for at in range(0, rows, step):
                    lo = h * rows + at
                    for side in range(2):
                        weights = prob_ref[i, side, lo : lo + step, :keys].astype(F32)
                        shifted = p_scr[side, lo : lo + step, :keys] - delta[h][at : at + step]
                        d_scr[side, lo : lo + step, :keys] = (weights * shifted).astype(BF16)
            grad_q = jnp.zeros((tall, width), F32)
            for side in range(2):
                key = sides[side][:, :, :width].reshape(wide, width)[:keys]
                moved = d_scr[side, :, :keys]
                grad_q = grad_q + mm(moved, key, NN)
                acc[side, :keys, :width] += mm(moved, stacked_q, TN)
                acc[side, :keys, width:] += mm(prob_ref[i, side, :, :keys], stacked_g, TN)
            dq_ref[i] = (0.125 * fold_heads(grad_q, rows, heads_here)).astype(BF16)
        down_ref[...] = acc[0].reshape(count, rows, 2 * width)
        doth_ref[...] = acc[1].reshape(count, rows, 2 * width).astype(BF16)

    outs = (
        shape(BF16, count, rows, width),
        shape(F32, count, rows, 2 * width),
        shape(BF16, count, rows, 2 * width),
    )
    scratch = (
        shape(F32, 2, tall, wide),
        shape(BF16, 2, tall, wide),
        shape(F32, 2, wide, 2 * width),
        shape(BF16, count, rows, width),
    )
    operands = (queries, kv_own, kv_other, prob, attn, *grads)
    return kernel(body, outs, (place,), operands, scratch, micros=6.0, name="attend_back")


def join_call(place, grad_q, grad_kv, arrived, live):
    count, rows, width = grad_q.shape

    def body(place_ref, q_ref, kv_ref, in_ref, out_ref, *rest):
        msgs, scr = rest[:count], rest[count]
        for b in range(count):
            both = (kv_ref[b] + in_ref[b].astype(F32)).astype(BF16)
            out_ref[b, :, :width] = q_ref[b]
            out_ref[b, :, width:] = both
            dense = [q_ref[b][:, :live], both[:, :live], both[:, width : width + live]]
            scr[b] = pack(jnp.concatenate(dense, axis=1))
        for k in range(count):
            msgs[k][...] = scr[place_ref[0] ^ k]

    message = shape(BF16, packed_rows(rows, 3 * live), 128)
    outs = (shape(BF16, count, rows, 3 * width),) + (message,) * count
    scratch = (shape(BF16, count, *message.shape),)
    joined, *msgs = kernel(body, outs, (place,), (grad_q, grad_kv, arrived), scratch, micros=0.7, name="join_grads")
    return joined, msgs


def gather_heads(place_ref, pieces, scr, rows, live):
    for k, ref in enumerate(pieces):
        scr[place_ref[0] ^ k] = ref[...]
    return jnp.concatenate([unpack(scr[k], rows, live) for k in range(len(pieces))], axis=1)


def norms_call(place, pieces, layer_in, vectors, w_out, live):
    count, rows = len(pieces), layer_in.shape[0]
    model = w_out.shape[0]

    def body(place_ref, *refs):
        in_ref, g2, b2, g3, b3, wo_ref, mid_ref, attn_ref, n3_ref, piece_scr = refs[count:]
        attn = gather_heads(place_ref, refs[:count], piece_scr, rows, live)
        attn_ref[...] = attn
        unit2, _ = unit_norm(attn.astype(F32))
        normed2 = (unit2 * row(g2) + row(b2)).astype(BF16)
        middle = in_ref[...].astype(F32) + mm(normed2, wo_ref[...], NN)
        mid_ref[...] = middle
        unit3, _ = unit_norm(middle)
        n3_ref[...] = (unit3 * row(g3) + row(b3)).astype(BF16)

    outs = (shape(F32, rows, model), shape(BF16, rows, model), shape(BF16, rows, model))
    operands = (*pieces, layer_in, *vectors, w_out)
    scratch = (shape(BF16, count, *pieces[0].shape),)
    return kernel(body, outs, (place,), operands, scratch, micros=1.5, name="norms")


def up_call(place, normed3, w_up, parts):
    rows, (model, hidden) = normed3.shape[0], w_up.shape
    part = hidden // parts

    def body(place_ref, n3_ref, wu_ref, act_ref, slope_ref, *msgs):
        normed = n3_ref[...]
        for r in range(parts):
            upper = mm(normed, wu_ref[:, r * part : (r + 1) * part], NN)
            cumulative = 0.5 * (1.0 + lax.erf(upper * 0.7071067811865476))
            density = jnp.exp(-0.5 * upper * upper) * 0.3989422804014327
            act_ref[r] = (upper * cumulative).astype(BF16)
            slope_ref[r] = (cumulative + upper * density).astype(BF16)
        for k in range(parts):
            msgs[k][...] = act_ref[place_ref[2] ^ k]

    outs = (shape(BF16, parts, rows, part),) * 2 + (shape(BF16, rows, part),) * parts
    act, slope, *msgs = kernel(body, outs, (place,), (normed3, w_up), micros=2.0, name="up_gelu")
    return act, slope, msgs


def padded_quarter(quarter):
    return -(-(quarter + 64) // 128) * 128


def backward_call(place, attn, middle, act, slope, grad_out, vectors, w_out, w_up, w_down, parts, count, live):
    rows = attn.shape[0]
    model, hidden = w_up.shape
    part, quarter = hidden // parts, model // parts
    pad_q = padded_quarter(quarter)
    message = shape(BF16, packed_rows(rows, live), 128)

    def body(
        place_ref, attn_ref, mid_ref, act_ref, slope_ref, go_ref, g2, b2, g3, b3, wo_ref, wu_ref, wd_ref,
        out_ref, gmid_ref, *rest,
    ):
        msgs, heads = rest[:parts], rest[parts : parts + count]
        up_scr, n2_scr, head_scr = rest[parts + count :]
        here = place_ref[2]
        go = go_ref[...]
        middle = mid_ref[...]
        out = middle
        grad3 = jnp.zeros((rows, model), F32)
        for r in range(parts):
            w_d = wd_ref[r * part : (r + 1) * part, :]
            out = out + mm(act_ref[r], w_d, NN)
            grad_up = (mm(go, w_d, NT) * slope_ref[r].astype(F32)).astype(BF16)
            up_scr[r] = grad_up
            grad3 = grad3 + mm(grad_up, wu_ref[:, r * part : (r + 1) * part], NT)
        out_ref[...] = out.astype(BF16)
        unit3, scale3 = unit_norm(middle)
        grad_mid = go.astype(F32) + norm_back(grad3, row(g3), unit3, scale3)
        gmid_ref[...] = grad_mid
        proj = grad_mid.astype(BF16)
        grad2 = mm(proj, wo_ref[...], NT)
        unit2, scale2 = unit_norm(attn_ref[...].astype(F32))
        grad_attn = norm_back(grad2, row(g2), unit2, scale2).astype(BF16)
        for k in range(count):
            head_scr[k] = pack(grad_attn[:, k * live : (k + 1) * live])
        for k in range(count):
            heads[k][...] = head_scr[place_ref[0] ^ k]
        sums = [
            jnp.sum(grad2 * unit2, axis=0, keepdims=True),
            jnp.sum(grad2, axis=0, keepdims=True),
            jnp.sum(grad3 * unit3, axis=0, keepdims=True),
            jnp.sum(grad3, axis=0, keepdims=True),
        ]
        table = jnp.concatenate(sums + [jnp.zeros((4, model), F32)], axis=0)
        normed2 = (unit2 * row(g2) + row(b2)).astype(BF16)
        normed3 = (unit3 * row(g3) + row(b3)).astype(BF16)
        spare, lines = pad_q - quarter, quarter // 64
        for r in range(parts):
            chunks = [table[:, r * quarter + 64 * j : r * quarter + 64 * (j + 1)] for j in range(lines)]
            side = jnp.concatenate(chunks + [jnp.zeros((rows - 8 * lines, 64), F32)], axis=0).astype(BF16)
            pieces = [normed2[:, r * quarter : (r + 1) * quarter], side]
            if spare > 64:
                pieces.append(jnp.zeros((rows, spare - 64), BF16))
            n2_scr[r] = jnp.concatenate(pieces, axis=1)
        for k in range(parts):
            msgs[k][:, :part] = up_scr[here ^ k]
            msgs[k][:, part : part + model] = proj
            msgs[k][:, part + model : part + 2 * model] = normed3
            msgs[k][:, part + 2 * model :] = n2_scr[here ^ k]

    outs = (
        shape(BF16, rows, model),
        shape(F32, rows, model),
    )
    outs += (shape(BF16, rows, part + 2 * model + pad_q),) * parts + (message,) * count
    operands = (attn, middle, act, slope, grad_out, *vectors, w_out, w_up, w_down)
    scratch = (
        shape(BF16, parts, rows, part),
        shape(BF16, parts, rows, pad_q),
        shape(BF16, count, *message.shape),
    )
    found = kernel(body, outs, (place,), operands, scratch, micros=9.0, name="token_backward")
    found = list(found)
    return found[0], found[1], found[2 : 2 + parts], found[2 + parts :]


def down_grad_call(place, acts, grads, chips):
    parts = len(acts)
    part, model = acts[0].shape[1], grads[0].shape[1]
    own = part // (2 * chips)

    def body(place_ref, *refs):
        act_refs, grad_refs, (keep_ref, send_ref, scr) = refs[:parts], refs[parts : 2 * parts], refs[2 * parts :]
        core = place_ref[1]
        act = jnp.concatenate([ref[...] for ref in act_refs], axis=0)
        grad = jnp.concatenate([ref[...] for ref in grad_refs], axis=0)
        scr[...] = mm(act, grad, TN).reshape(chips, 2, own, model)
        for k in range(chips):
            keep_ref[k] = scr[k, core]
            send_ref[k] = scr[k, 1 - core].astype(BF16)

    outs = (shape(F32, chips, own, model), shape(BF16, chips, own, model))
    scratch = (shape(F32, chips, 2, own, model),)
    return kernel(body, outs, (place,), (*acts, *grads), scratch, micros=3.0, name="grad_down")


def up_grad_call(place, back, chips, part, model):
    parts = len(back)
    quarter = model // parts
    own = model // (parts * chips * 2)
    tall = (parts + 1) * own + 8

    def body(place_ref, *refs):
        back_refs = refs[:parts]
        keep_ref, send_ref, up_scr, out_scr, vec_scr = refs[parts:]
        core = place_ref[1]
        ends = (0, part, part + model, part + 2 * model, back_refs[0].shape[1])
        grad_up, proj, normed3, normed2 = (
            jnp.concatenate([ref[:, lo:hi] for ref in back_refs], axis=0) for lo, hi in zip(ends, ends[1:])
        )
        up_scr[...] = mm(normed3, grad_up, TN).reshape(parts, chips, 2, own, part)
        out_scr[...] = mm(normed2, proj, TN)[:quarter].reshape(chips, 2, own, model)
        lines = quarter // 64
        side = jnp.zeros((8 * lines, 64), F32)
        for ref in back_refs:
            side = side + ref[:, ends[3] + quarter : ends[3] + quarter + 64].astype(F32)[: 8 * lines]
        table = jnp.concatenate([side[8 * j : 8 * (j + 1)] for j in range(lines)], axis=1)
        vec_scr[...] = jnp.zeros_like(vec_scr)
        for k in range(chips):
            for side in range(2):
                at = (2 * k + side) * own
                vec_scr[k, side, :, :own] = table[:, at : at + own]
        for k in range(chips):
            for side, ref in ((core, keep_ref), (1 - core, send_ref)):
                pieces = [up_scr[r, k, side] for r in range(parts)] + [out_scr[k, side], vec_scr[k, side]]
                ref[k] = jnp.concatenate(pieces, axis=0).astype(ref.dtype)

    outs = (shape(F32, chips, tall, model), shape(BF16, chips, tall, model))
    scratch = (
        shape(F32, parts, chips, 2, own, part),
        shape(F32, chips, 2, own, model),
        shape(F32, chips, 2, 8, model),
    )
    return kernel(body, outs, (place,), tuple(back), scratch, micros=4.0, name="grad_up_out")


def qkv_grad_call(place, groups, units, grads, gain, bias, weight, parts, live, width):
    count, rows = grads.shape[:2]
    model = weight.shape[0]
    own = model // (parts * count * 2)
    n = len(units)

    def body(place_ref, *refs):
        unit_refs = refs[:n]
        grad_ref, gain_ref, bias_ref, weight_ref, keep_ref, send_ref, unit_scr, scr = refs[n:]
        z_index, core = place_ref[0], place_ref[1]
        for g, ks in enumerate(groups):
            for j, k in enumerate(ks):
                unit_scr[z_index ^ k] = unit_refs[g][j]
        grad = grad_ref[...].reshape(count * rows, 3 * width)
        cross = mm(unit_scr[...].reshape(count * rows, model), grad, TN)
        total = jnp.sum(grad.astype(F32), axis=0, keepdims=True)
        columns = jnp.concatenate([row(gain_ref), row(bias_ref), jnp.zeros((6, model), F32)], axis=0).T
        weight_f = weight_ref[...].astype(F32)
        grad_gain = jnp.sum(weight_f * cross, axis=1, keepdims=True)
        grad_bias = jnp.sum(weight_f * total, axis=1, keepdims=True)
        lane = lax.broadcasted_iota(jnp.int32, (1, 3 * width), 1)
        made = columns[:, 0:1] * cross + columns[:, 1:2] * total
        made = jnp.where(lane == live, grad_gain, jnp.where(lane == live + 1, grad_bias, made))
        scr[...] = made.reshape(parts, count, 2, own, 3 * width)
        for r in range(parts):
            keep_ref[r] = jnp.concatenate([scr[r, k, core] for k in range(count)], axis=0)
            send_ref[r] = jnp.concatenate([scr[r, k, 1 - core] for k in range(count)], axis=0).astype(BF16)

    outs = (shape(F32, parts, count * own, 3 * width), shape(BF16, parts, count * own, 3 * width))
    scratch = (shape(BF16, count, rows, model), shape(F32, parts, count, 2, own, 3 * width))
    operands = (*units, grads, gain, bias, weight)
    return kernel(body, outs, (place,), operands, scratch, micros=4.0, name="grad_qkv")


def spread_call(place, keep, arrived):
    parts = keep.shape[0]

    def body(place_ref, keep_ref, in_ref, *outs):
        for k in range(parts):
            at = place_ref[2] ^ k
            outs[k][...] = (keep_ref[at] + in_ref[at].astype(F32)).astype(BF16)

    return kernel(body, (shape(BF16, *keep.shape[1:]),) * parts, (place,), (keep, arrived), micros=0.8, name="spread")


def halve_call(place, keep, arrived, bit):
    half = keep.shape[0] // 2

    def body(place_ref, keep_ref, in_ref, stay_ref, away_ref):
        mine = (place_ref[0] // bit) % 2
        for j in range(half):
            here, there = 2 * j + mine, 2 * j + 1 - mine
            stay_ref[j] = keep_ref[here] + in_ref[here].astype(F32)
            away_ref[j] = (keep_ref[there] + in_ref[there].astype(F32)).astype(BF16)

    rest = keep.shape[1:]
    return kernel(body, (shape(F32, half, *rest), shape(BF16, half, *rest)), (place,), (keep, arrived), micros=0.8, name="halve")


def finish_down_call(keep, arrived):
    def body(keep_ref, in_ref, out_ref):
        out_ref[...] = keep_ref[0] + in_ref[0].astype(F32)

    return kernel(body, shape(F32, *keep.shape[1:]), (), (keep, arrived), micros=0.6, name="finish_down")


def finish_up_call(place, keep, arrived, parts, own, part):
    model = keep.shape[2]

    def body(place_ref, keep_ref, in_ref, out_ref, g2, b2, g3, b3, *rest):
        msgs, scr = rest[:parts], rest[parts]
        value = keep_ref[0] + in_ref[0].astype(F32)
        out_ref[...] = value[parts * own : (parts + 1) * own]
        for at, ref in enumerate((g2, b2, g3, b3)):
            line = (parts + 1) * own + at
            ref[...] = value[line : line + 1, :own].reshape(own)
        scr[...] = value[: parts * own].reshape(parts, own, part)
        for k in range(parts):
            msgs[k][...] = scr[place_ref[2] ^ k].astype(BF16)

    outs = (shape(F32, own, model),) + (shape(F32, own),) * 4 + (shape(BF16, own, part),) * parts
    scratch = (shape(F32, parts, own, part),)
    return kernel(body, outs, (place,), (keep, arrived), scratch, micros=0.8, name="finish_up")


def place_up_call(place, pieces):
    parts = len(pieces)
    own, part = pieces[0].shape

    def body(place_ref, *refs):
        for k in range(parts):
            at = pl.multiple_of((place_ref[2] ^ k) * part, 128)
            refs[parts][:, pl.ds(at, part)] = refs[k][...].astype(F32)

    return kernel(body, shape(F32, own, parts * part), (place,), tuple(pieces), micros=0.5, name="place_up")


def share_call(place, pieces, chips):
    own = pieces[0].shape[0] // chips

    def body(place_ref, *refs):
        ins, outs, scr = refs[: len(pieces)], refs[len(pieces) : -1], refs[-1]
        total = ins[0][...].astype(F32)
        for ref in ins[1:]:
            total = total + ref[...].astype(F32)
        scr[...] = total.reshape(chips, own, total.shape[1])
        for k in range(chips):
            outs[k][...] = scr[place_ref[0] ^ k].astype(BF16)

    lanes = pieces[0].shape[1]
    outs = (shape(BF16, own, lanes),) * chips
    return kernel(body, outs, (place,), tuple(pieces), (shape(F32, chips, own, lanes),), micros=0.7, name="share")


def finish_qkv_call(place, pieces, model, live, width):
    count, own = len(pieces), pieces[0].shape[0]

    def body(place_ref, *refs):
        q_ref, k_ref, v_ref, gain_ref, bias_ref, in_ref = refs[count:]
        for k in range(count):
            in_ref[place_ref[0] ^ k] = refs[k][...].astype(F32)
        for at, ref in enumerate((q_ref, k_ref, v_ref)):
            ref[...] = jnp.concatenate(
                [in_ref[k, :, at * width : at * width + live] for k in range(count)], axis=1
            )
        total = jnp.sum(in_ref[:, :, live : live + 2], axis=0).T
        gain_ref[...] = total[0:1].reshape(own)
        bias_ref[...] = total[1:2].reshape(own)

    outs = (shape(F32, own, model),) * 3 + (shape(F32, own),) * 2
    scratch = (shape(F32, count, *pieces[0].shape),)
    return kernel(body, outs, (place,), tuple(pieces), scratch, micros=0.8, name="finish_qkv")


def input_grad_call(place, pieces, layer_in, grad_mid, gain, w_query, w_key, w_value, live):
    count = len(pieces)
    rows, model = layer_in.shape

    def body(place_ref, *refs):
        in_ref, gmid_ref, gain_ref, wq_ref, wk_ref, wv_ref, out_ref, scr = refs[count:]
        for k in range(count):
            scr[place_ref[0] ^ k] = refs[k][...]
        blocks = [unpack(scr[k], rows, 3 * live) for k in range(count)]
        grad = jnp.zeros((rows, model), F32)
        for at, w_ref in enumerate((wq_ref, wk_ref, wv_ref)):
            part = jnp.concatenate([block[:, at * live : (at + 1) * live] for block in blocks], axis=1)
            grad = grad + mm(part, w_ref[...], NT)
        unit, scale = unit_norm(in_ref[...].astype(F32))
        out_ref[...] = (gmid_ref[...] + norm_back(grad, row(gain_ref), unit, scale)).astype(BF16)

    operands = (*pieces, layer_in, grad_mid, gain, w_query, w_key, w_value)
    scratch = (shape(BF16, count, *pieces[0].shape),)
    return kernel(body, shape(BF16, rows, model), (place,), operands, scratch, micros=3.0, name="grad_inputs")


def swap_core(value):
    return lax.ppermute(value, "core", [(0, 1), (1, 0)])


def swap(value, axis, bit):
    return lax.ppermute(value, axis, [(k, k ^ bit) for k in range(lax.axis_size(axis))])


def trade(messages, axis):
    found = {k: swap(messages[k], axis, k) for k in range(len(messages) - 1, 0, -1)}
    return [messages[0]] + [found[k] for k in range(1, len(messages))]


def gather_chips(block, chips):
    found = {0: block}
    bit = chips // 2
    while bit >= 1:
        for k in sorted(found):
            found[k | bit] = swap(found[k], "chip", bit)
        bit //= 2
    return [found[k] for k in range(chips)]


def scatter_chips(place, keep, arrived, chips, bit):
    while bit < chips:
        keep, away = halve_call(place, keep, arrived, bit)
        arrived = swap(away, "chip", bit)
        bit *= 2
    return keep, arrived


def after(values, *others):
    return lax.optimization_barrier((values, others))[0]


def fast_shards(
    inputs, doc_lengths, ln1_gain, ln1_bias, w_query, w_key, w_value, ln2_gain, ln2_bias, w_out,
    ln3_gain, ln3_bias, w_up, w_down, out_grad,
):
    rows, model = inputs.shape[1:]
    chips, parts = lax.axis_size("chip"), lax.axis_size("rows")
    z_index = lax.axis_index("chip")
    heads_here = HEADS // chips
    live = heads_here * HEAD_DIM
    width = -(-live // 128) * 128
    hidden = w_up.shape[1]
    part = hidden // parts
    own = model // (parts * chips * 2)
    place = jnp.stack([z_index, lax.axis_index("core"), lax.axis_index("rows")]).astype(jnp.int32)
    scope = jax.named_scope

    def columns(weight):
        mine = lax.dynamic_slice_in_dim(weight, z_index * live, live, 1)
        return jnp.pad(mine, ((0, 0), (0, width - live)))

    place, layer_in, out_grad = lax.optimization_barrier((place, inputs[0], out_grad[0]))
    with scope("gather_in"):
        blocks = gather_chips(layer_in, chips)
    grad_out = mask_call(place, doc_lengths, out_grad)
    w_heads = jnp.concatenate([columns(w_query), columns(w_key), columns(w_value)], axis=1)
    groups = [g for g in ([0], list(range(1, chips - 1)), [chips - 1]) if g] if chips > 1 else [[0]]
    made = [qkv_call([blocks[k] for k in g], ln1_gain, ln1_bias, w_heads, width) for g in groups]
    queries, kv_own, units = ([m[at] for m in made] for at in range(3))
    with scope("core_kv"):
        kv_other = [swap_core(v) for v in kv_own]
    attn_heads, (prob, queries, kv_own, kv_other), messages = attend_call(
        place, doc_lengths, groups, queries, kv_own, kv_other, heads_here
    )
    fence = lax.optimization_barrier
    with scope("chip_attn"):
        pieces = trade(messages, "chip")
    with scope("plane_out"):
        grads_plane = trade([grad_out] * parts, "rows")
    pieces = after(pieces, grads_plane)

    vectors = (ln2_gain, ln2_bias, ln3_gain, ln3_bias)
    middle, attn, normed3 = norms_call(place, pieces, layer_in, vectors, w_out, live)
    act, slope, acts = up_call(place, normed3, w_up, parts)
    with scope("plane_act"):
        acts = trade(acts, "rows")
    output, grad_mid, back, messages = backward_call(
        place, attn, middle, act, slope, grad_out, vectors, w_out, w_up, w_down, parts, chips, live
    )
    back = after(back, acts[1:])
    with scope("chip_grad"):
        grad_heads = trade(messages, "chip")
    with scope("plane_back"):
        far = [swap(back[k], "rows", k) for k in range(3, parts)]
    grad_q, grad_kv, grad_kv_other = attend_back_call(
        place, queries, kv_own, kv_other, prob, attn_heads, grad_heads, heads_here
    )
    with scope("core_grad"):
        grad_kv_other = swap_core(grad_kv_other)
    down_keep, down_send = down_grad_call(place, after(acts, grad_q), grads_plane, chips)
    grad_kv_other, down_send, far = fence((grad_kv_other, down_send, far))
    with scope("core_down"):
        down_recv = swap_core(down_send)
    with scope("plane_back"):
        near = after(back[1:3], far)
        back = back[:1] + [swap(near[k], "rows", k + 1) for k in range(len(near))] + far
    grad_qkv, messages = join_call(place, grad_q, grad_kv, grad_kv_other, live)
    with scope("down_sum"):
        down_keep, down_away = halve_call(place, down_keep, after(down_recv, grad_qkv), 1)
        grad_qkv, down_away = fence((grad_qkv, down_away))
        down_recv = swap(down_away, "chip", 1)
    with scope("chip_qkv"):
        grad_pieces = trade(messages, "chip")
    qkv_keep, qkv_send = qkv_grad_call(
        place, groups, units, grad_qkv, ln1_gain, ln1_bias, w_heads, parts, live, width
    )
    down_recv = after(down_recv, qkv_send)
    with scope("core_w"):
        qkv_send = swap_core(qkv_send)
    qkv_sums = spread_call(place, qkv_keep, qkv_send)
    with scope("down_sum"):
        down_keep, down_last = scatter_chips(place, down_keep, down_recv, chips, 2)
    back = after(back, (down_keep, grad_pieces[2:]))
    up_keep, up_send = up_grad_call(place, back, chips, part, model)
    with scope("plane_w"):
        traded = trade(qkv_sums, "rows")
    with scope("core_up"):
        up_recv = swap_core(up_send)
    up_keep, up_away = halve_call(place, up_keep, up_recv, 1)
    with scope("up_sum"):
        up_recv = swap(up_away, "chip", 1)
    traded = after(traded, up_away)
    with scope("chip_w"):
        shared = share_call(place, traded, chips)
        qkv_all = trade(shared, "chip")
    grad_inputs = input_grad_call(
        place, grad_pieces, layer_in, grad_mid, ln1_gain, w_query, w_key, w_value, live
    )
    gwd = finish_down_call(down_keep, down_last)
    up_recv = after(up_recv, (grad_pieces, shared, down_last))
    with scope("up_sum"):
        up_keep, up_last = scatter_chips(place, up_keep, up_recv, chips, 2)
    up_last = after(up_last, (qkv_all, gwd, grad_inputs))
    gwo, g2, b2, g3, b3, *up_rows = finish_up_call(place, up_keep, up_last, parts, own, part)
    with scope("plane_rows"):
        up_rows = trade(up_rows, "rows")
    gwq, gwk, gwv, g1, b1 = finish_qkv_call(place, qkv_all, model, live, width)
    gwu = place_up_call(place, up_rows)
    return (
        output[None], grad_inputs[None], g1, b1, gwq, gwk, gwv, g2, b2, gwo, g3, b3, gwu, gwd,
    )


def takes_fast(mesh):
    seq, parts = mesh.shape["seq"], mesh.shape["rows"]
    chips = seq // 2
    return seq % 2 == 0 and chips & (chips - 1) == 0 and parts in (1, 2, 4) and HEADS % max(chips, 1) == 0


def solution(mesh):
    if takes_fast(mesh):
        parts, seq = mesh.shape["rows"], mesh.shape["seq"]
        split = jax.sharding.Mesh(mesh.devices.reshape(parts, seq // 2, 2), ("rows", "chip", "core"))
        return mapped(fast_shards, split, ("chip", "core"))
    return mapped(shards, mesh, "seq")
```

```python
import math

import jax
import jax.numpy as jnp
from jax import lax
from jax.experimental import pallas as pl
from jax.experimental.pallas import tpu as pltpu
from jax.sharding import PartitionSpec as P

HEADS = 12
HEAD_DIM = 64


segment_pairs = ((2048, 1), (4096, 2), (8192, 4), (16384, 6))
masked_value = -1e30


def layer_norm(vector, gain_vec, bias_vec):
    row_mean = jnp.mean(vector, axis=-1, keepdims=True)
    centered = vector - row_mean
    row_var = jnp.mean(centered * centered, axis=-1, keepdims=True)
    return centered * lax.rsqrt(row_var + 1e-05) * gain_vec + bias_vec


def doc_of(positions, doc_ends):
    return jnp.sum((positions[:, None] >= doc_ends[None, :]).astype(jnp.int32), axis=1)


def pair_terms(query_pos, key_pos, query_doc, key_doc, head_count):
    head_ids = jnp.arange(head_count, dtype=jnp.int32)
    multiplicity = jnp.zeros((head_count, query_pos.shape[0], key_pos.shape[0]), jnp.float32)
    for seg_width, dilation in segment_pairs:
        same_seg = query_pos[:, None] // seg_width == key_pos[None, :] // seg_width
        query_pick = (query_pos % seg_width % dilation)[None, :] == (head_ids % dilation)[:, None]
        key_pick = (key_pos % seg_width % dilation)[None, :] == (head_ids % dilation)[:, None]
        joined = same_seg[None] & query_pick[:, :, None] & key_pick[:, None, :]
        multiplicity = multiplicity + joined.astype(jnp.float32)
    allowed = (key_pos[None, :] <= query_pos[:, None]) & (query_doc[:, None] == key_doc[None, :])
    allowed = allowed[None] & (multiplicity > 0.0)
    return (jnp.log(jnp.maximum(multiplicity, 1.0)), allowed)


def rows_inner(left, right):
    return lax.dot_general(
        left, right, (((0,), (0,)), ((), ())), preferred_element_type=jnp.float32
    )


def cols_inner(left, right):
    return lax.dot_general(
        left, right, (((1,), (1,)), ((), ())), preferred_element_type=jnp.float32
    )


def over_blocks(state, piece, step_fn):
    total_rows = piece[0].shape[0]
    block_rows = math.gcd(total_rows, 512)
    block_total = total_rows // block_rows
    split = tuple((part.reshape((block_total, block_rows) + part.shape[1:]) for part in piece))

    def inner(carried, block_item):
        return (step_fn(carried, block_item[1], block_item[0] * block_rows), None)

    result, unused = lax.scan(inner, state, (jnp.arange(block_total, dtype=jnp.int32), split))
    return result


def add_rows(buffer, start_pos, addend):
    current = lax.dynamic_slice_in_dim(buffer, start_pos, addend.shape[0], 0)
    return lax.dynamic_update_slice_in_dim(buffer, current + addend, start_pos, 0)


def shards(
    inputs,
    doc_lengths,
    ln1_gain,
    ln1_bias,
    w_query,
    w_key,
    w_value,
    ln2_gain,
    ln2_bias,
    w_out,
    ln3_gain,
    ln3_bias,
    w_up,
    w_down,
    out_grad,
):
    tok_rows = inputs.shape[1]
    head_count = HEADS
    head_size = HEAD_DIM
    model_width = inputs.shape[2]
    row_total = tok_rows * lax.axis_size("seq")
    layer_in = inputs[0].astype(jnp.float32)
    doc_ends = jnp.cumsum(doc_lengths[0])
    first_pos = lax.axis_index("seq") * tok_rows
    query_pos = first_pos + jnp.arange(tok_rows, dtype=jnp.int32)
    query_doc = doc_of(query_pos, doc_ends)
    valid = (query_doc < doc_lengths.shape[1]).astype(jnp.float32)
    first_norm, first_back = jax.vjp(layer_norm, layer_in, ln1_gain, ln1_bias)
    normed_one = first_norm.astype(jnp.bfloat16)
    queries = jnp.dot(normed_one, w_query, preferred_element_type=jnp.float32).astype(jnp.bfloat16)
    keys_local = jnp.dot(normed_one, w_key, preferred_element_type=jnp.float32).astype(jnp.bfloat16)
    values_local = jnp.dot(normed_one, w_value, preferred_element_type=jnp.float32).astype(
        jnp.bfloat16
    )
    query_heads = queries.reshape(tok_rows, head_count, head_size)

    def key_block_terms(key_start, key_count):
        key_pos = key_start + jnp.arange(key_count, dtype=jnp.int32)
        key_doc = doc_of(key_pos, doc_ends)
        return pair_terms(query_pos, key_pos, query_doc, key_doc, head_count)

    def with_pruning(step_fn):

        def wrapped(state, parts, start_pos):
            return step_fn(state, parts, start_pos)

        return wrapped

    def forward_step(state, parts, key_start):
        run_max, run_total, run_acc = state
        key_blk = parts[0].reshape(-1, head_count, head_size)
        value_blk = parts[1].reshape(-1, head_count, head_size)
        log_mult, allowed = key_block_terms(key_start, key_blk.shape[0])
        scores = 0.125 * jnp.einsum(
            "qhd,khd->hqk", query_heads, key_blk, preferred_element_type=jnp.float32
        )
        logits = jnp.where(allowed, scores + log_mult, masked_value)
        new_max = jnp.maximum(run_max, jnp.max(logits, axis=-1))
        weights = jnp.where(allowed, jnp.exp(logits - new_max[..., None]), 0.0)
        factor = jnp.exp(run_max - new_max)
        run_total = run_total * factor + jnp.sum(weights, axis=-1)
        run_acc = run_acc * factor[..., None] + jnp.einsum(
            "hqk,khd->hqd",
            weights.astype(jnp.bfloat16),
            value_blk,
            preferred_element_type=jnp.float32,
        )
        return (new_max, run_total, run_acc)

    forward_pruned = with_pruning(forward_step)
    start_state = (
        jnp.full((head_count, tok_rows), masked_value, jnp.float32),
        jnp.zeros((head_count, tok_rows), jnp.float32),
        jnp.zeros((head_count, tok_rows, head_size), jnp.float32),
    )
    final_state = over_blocks(
        start_state,
        (
            lax.all_gather(keys_local, "seq", axis=0, tiled=True),
            lax.all_gather(values_local, "seq", axis=0, tiled=True),
        ),
        forward_pruned,
    )
    run_max, run_total, run_acc = final_state
    row_lse = run_max + jnp.log(run_total)
    attn = (run_acc / run_total[..., None]).transpose(1, 0, 2).reshape(tok_rows, model_width)
    second_norm, second_back = jax.vjp(layer_norm, attn, ln2_gain, ln2_bias)
    normed_two = second_norm.astype(jnp.bfloat16)
    middle = layer_in + jnp.dot(normed_two, w_out, preferred_element_type=jnp.float32)
    third_norm, third_back = jax.vjp(layer_norm, middle, ln3_gain, ln3_bias)
    normed_three = third_norm.astype(jnp.bfloat16)
    upper = jnp.dot(normed_three, w_up, preferred_element_type=jnp.float32)
    activated_f, gelu_back = jax.vjp(
        lambda upper_in: jax.nn.gelu(upper_in, approximate=False), upper
    )
    activated = activated_f.astype(jnp.bfloat16)
    layer_out = middle + jnp.dot(activated, w_down, preferred_element_type=jnp.float32)
    grad_out = out_grad[0].astype(jnp.float32) * valid[:, None]
    grad_branch = grad_out.astype(jnp.bfloat16)
    grad_w_down = rows_inner(activated, grad_branch)
    grad_act = cols_inner(grad_branch, w_down)
    grad_upper = gelu_back(grad_act)[0].astype(jnp.bfloat16)
    grad_w_up = rows_inner(normed_three, grad_upper)
    grad_n3 = cols_inner(grad_upper, w_up)
    grad_mid_norm, grad_ln3_gain, grad_ln3_bias = third_back(grad_n3)
    grad_middle = grad_out + grad_mid_norm
    grad_proj = grad_middle.astype(jnp.bfloat16)
    grad_w_out = rows_inner(normed_two, grad_proj)
    grad_n2 = cols_inner(grad_proj, w_out)
    grad_attn_f, grad_ln2_gain, grad_ln2_bias = second_back(grad_n2)
    grad_attn = grad_attn_f.astype(jnp.bfloat16)
    grad_heads = grad_attn.reshape(tok_rows, head_count, head_size)
    row_delta = jnp.sum(
        (grad_attn.astype(jnp.float32) * attn).reshape(tok_rows, head_count, head_size), axis=-1
    )

    def backward_step(state, parts, key_start):
        grad_q_acc, grad_k_rows, grad_v_rows = state
        key_blk = parts[0].reshape(-1, head_count, head_size)
        value_blk = parts[1].reshape(-1, head_count, head_size)
        key_count = key_blk.shape[0]
        log_mult, allowed = key_block_terms(key_start, key_count)
        scores = 0.125 * jnp.einsum(
            "qhd,khd->hqk", query_heads, key_blk, preferred_element_type=jnp.float32
        )
        logits = jnp.where(allowed, scores + log_mult, masked_value)
        weights = jnp.where(allowed, jnp.exp(logits - row_lse[..., None]), 0.0)
        grad_weights = jnp.einsum(
            "qhd,khd->hqk", grad_heads, value_blk, preferred_element_type=jnp.float32
        )
        grad_scores = (weights * (grad_weights - row_delta.T[..., None])).astype(jnp.bfloat16)
        grad_q_acc = grad_q_acc + 0.125 * jnp.einsum(
            "hqk,khd->qhd", grad_scores, key_blk, preferred_element_type=jnp.float32
        )
        value_part = jnp.einsum(
            "hqk,qhd->khd",
            weights.astype(jnp.bfloat16),
            grad_heads,
            preferred_element_type=jnp.float32,
        ).reshape(key_count, model_width)
        key_part = 0.125 * jnp.einsum(
            "hqk,qhd->khd", grad_scores, query_heads, preferred_element_type=jnp.float32
        ).reshape(key_count, model_width)
        grad_k_rows = add_rows(grad_k_rows, key_start, key_part)
        grad_v_rows = add_rows(grad_v_rows, key_start, value_part)
        return (grad_q_acc, grad_k_rows, grad_v_rows)

    backward_pruned = with_pruning(backward_step)
    zero_state = (
        jnp.zeros((tok_rows, head_count, head_size), jnp.float32),
        jnp.zeros((row_total, model_width), jnp.float32),
        jnp.zeros((row_total, model_width), jnp.float32),
    )
    back_state = over_blocks(
        zero_state,
        (
            lax.all_gather(keys_local, "seq", axis=0, tiled=True),
            lax.all_gather(values_local, "seq", axis=0, tiled=True),
        ),
        backward_pruned,
    )
    grad_q_acc, grad_k_rows, grad_v_rows = back_state
    grad_k_acc, grad_v_acc = (
        lax.psum_scatter(
            grad_k_rows.astype(jnp.bfloat16), "seq", scatter_dimension=0, tiled=True
        ).astype(jnp.float32),
        lax.psum_scatter(
            grad_v_rows.astype(jnp.bfloat16), "seq", scatter_dimension=0, tiled=True
        ).astype(jnp.float32),
    )
    grad_queries = grad_q_acc.reshape(tok_rows, model_width).astype(jnp.bfloat16)
    grad_keys = grad_k_acc.astype(jnp.bfloat16)
    grad_values = grad_v_acc.astype(jnp.bfloat16)
    grad_w_query = rows_inner(normed_one, grad_queries)
    grad_w_key = rows_inner(normed_one, grad_keys)
    grad_w_value = rows_inner(normed_one, grad_values)
    grad_n1 = (
        cols_inner(grad_queries, w_query)
        + cols_inner(grad_keys, w_key)
        + cols_inner(grad_values, w_value)
    )
    grad_in_norm, grad_ln1_gain, grad_ln1_bias = first_back(grad_n1)
    grad_inputs = (grad_middle + grad_in_norm).astype(jnp.bfloat16)
    summed = (
        lax.psum_scatter(grad_ln1_gain, ("rows", "seq"), scatter_dimension=0, tiled=True),
        lax.psum_scatter(grad_ln1_bias, ("rows", "seq"), scatter_dimension=0, tiled=True),
        lax.psum_scatter(grad_w_query, ("rows", "seq"), scatter_dimension=0, tiled=True),
        lax.psum_scatter(grad_w_key, ("rows", "seq"), scatter_dimension=0, tiled=True),
        lax.psum_scatter(grad_w_value, ("rows", "seq"), scatter_dimension=0, tiled=True),
        lax.psum_scatter(grad_ln2_gain, ("rows", "seq"), scatter_dimension=0, tiled=True),
        lax.psum_scatter(grad_ln2_bias, ("rows", "seq"), scatter_dimension=0, tiled=True),
        lax.psum_scatter(grad_w_out, ("rows", "seq"), scatter_dimension=0, tiled=True),
        lax.psum_scatter(grad_ln3_gain, ("rows", "seq"), scatter_dimension=0, tiled=True),
        lax.psum_scatter(grad_ln3_bias, ("rows", "seq"), scatter_dimension=0, tiled=True),
        lax.psum_scatter(grad_w_up, ("rows", "seq"), scatter_dimension=0, tiled=True),
        lax.psum_scatter(grad_w_down, ("rows", "seq"), scatter_dimension=0, tiled=True),
    )
    return (
        layer_out.astype(jnp.bfloat16)[None],
        grad_inputs[None],
        summed[0],
        summed[1],
        summed[2],
        summed[3],
        summed[4],
        summed[5],
        summed[6],
        summed[7],
        summed[8],
        summed[9],
        summed[10],
        summed[11],
    )


def mapped(step, mesh, seq):
    spread = P(("rows",) + (seq if isinstance(seq, tuple) else (seq,)))
    tokens, plain = P("rows", seq, None), P()
    weights = P(spread[0], None)
    return jax.shard_map(
        step,
        mesh=mesh,
        in_specs=(tokens, P("rows", None)) + (plain,) * 12 + (tokens,),
        out_specs=(tokens, tokens, spread, spread, weights, weights, weights, spread, spread, weights)
        + (spread, spread, weights, weights),
        check_vma=False,
    )


F32 = jnp.float32
PACE = 1e6
BF16 = jnp.bfloat16
NT = (((1,), (1,)), ((), ()))
TN = (((0,), (0,)), ((), ()))
NN = (((1,), (0,)), ((), ()))


def mm(left, right, dims):
    return lax.dot_general(left, right, dims, preferred_element_type=F32)


def unit_norm(vector):
    centered = vector - jnp.mean(vector, axis=-1, keepdims=True)
    scale = lax.rsqrt(jnp.mean(centered * centered, axis=-1, keepdims=True) + 1e-05)
    return centered * scale, scale


def norm_back(grad, gain, unit, scale):
    weighted = grad * gain
    mean_w = jnp.mean(weighted, axis=-1, keepdims=True)
    mean_wu = jnp.mean(weighted * unit, axis=-1, keepdims=True)
    return scale * (weighted - mean_w - unit * mean_wu)


def shape(dtype, *dims):
    return jax.ShapeDtypeStruct(dims, dtype)


def row(ref):
    return ref[...].reshape(1, ref.shape[0])


def size_of(item):
    total = jnp.dtype(item.dtype).itemsize
    for dim in item.shape:
        total *= dim
    return total


def kernel(body, outs, scalars, operands, scratch=(), micros=2.0, name=None):
    single = not isinstance(outs, (tuple, list))
    listed = (outs,) if single else tuple(outs)
    vmem = pl.BlockSpec(memory_space=pltpu.VMEM)
    smem = pl.BlockSpec(memory_space=pltpu.SMEM)
    moved = sum(size_of(v) for v in (*operands, *listed))
    held = sum(size_of(v) for v in scratch)
    return pl.pallas_call(
        body,
        out_shape=outs if single else listed,
        in_specs=[smem] * len(scalars) + [vmem] * len(operands),
        out_specs=vmem if single else (vmem,) * len(listed),
        scratch_shapes=[pltpu.VMEM(v.shape, v.dtype) for v in scratch],
        compiler_params=pltpu.CompilerParams(vmem_limit_bytes=min(60 << 20, (moved + held) * 5 // 4 + (6 << 20))),
        cost_estimate=pl.CostEstimate(flops=int(micros * PACE), bytes_accessed=int(micros * PACE / 1e3), transcendentals=0),
        name=name,
    )(*scalars, *operands)


def packed_rows(rows, live):
    return rows * live // 128


def pack(block):
    rows, live = block.shape
    whole = live // 128
    pieces = [block[:, 128 * j : 128 * (j + 1)] for j in range(whole)]
    if live % 128:
        rest = block[:, 128 * whole :]
        pieces.append(jnp.concatenate([rest[: rows // 2], rest[rows // 2 :]], axis=1))
    return jnp.concatenate(pieces, axis=0)


def unpack(block, rows, live):
    whole = live // 128
    pieces = [block[rows * j : rows * (j + 1)] for j in range(whole)]
    if live % 128:
        rest = block[rows * whole :]
        pieces.append(jnp.concatenate([rest[:, :64], rest[:, 64:]], axis=0))
    return jnp.concatenate(pieces, axis=1)


def mask_call(place, lengths, out_grad):
    rows, model = out_grad.shape

    def body(place_ref, len_ref, in_ref, out_ref):
        last = jnp.int32(0)
        for d in range(lengths.shape[1]):
            last = last + len_ref[0, d]
        pos = lax.broadcasted_iota(jnp.int32, (rows, 1), 0) + (2 * place_ref[0] + place_ref[1]) * rows
        out_ref[...] = jnp.where(pos < last, in_ref[...].astype(F32), 0.0).astype(BF16)

    return kernel(body, shape(BF16, rows, model), (place, lengths), (out_grad,), micros=0.7, name="mask_grad")


def qkv_call(blocks, gain, bias, weight, width):
    count = len(blocks)
    rows, model = blocks[0].shape

    def body(*refs):
        xs, (gain_ref, bias_ref, weight_ref, q_ref, kv_ref, unit_ref) = refs[:count], refs[count:]
        for k in range(count):
            unit, _ = unit_norm(xs[k][...].astype(F32))
            normed = (unit * row(gain_ref) + row(bias_ref)).astype(BF16)
            made = mm(normed, weight_ref[...], NN)
            q_ref[k] = (made[:, :width].astype(BF16).astype(F32) * 0.125).astype(BF16)
            kv_ref[k] = made[:, width:].astype(BF16)
            unit_ref[k] = unit.astype(BF16)

    outs = (
        shape(BF16, count, rows, width),
        shape(BF16, count, rows, 2 * width),
        shape(BF16, count, rows, model),
    )
    return kernel(body, outs, (), (*blocks, gain, bias, weight), micros=1.2 * count, name="qkv_heads")


def lane_head(lanes):
    return lax.broadcasted_iota(jnp.int32, (1, lanes), 1) // HEAD_DIM


def residue(pos_f, modulus):
    return pos_f - modulus * jnp.floor((pos_f + 0.5) * (1.0 / modulus))


def stack_heads(block, heads_here):
    head_of = lane_head(block.shape[1])
    return jnp.concatenate(
        [jnp.where(head_of == h, block, jnp.zeros_like(block)) for h in range(heads_here)], axis=0
    )


def fold_heads(stacked, rows, heads_here):
    head_of = lane_head(stacked.shape[1])
    total = jnp.zeros((rows, stacked.shape[1]), stacked.dtype)
    for h in range(heads_here):
        total = jnp.where(head_of == h, stacked[h * rows : (h + 1) * rows], total)
    return total


def attend_call(place, lengths, groups, queries, kv_own, kv_other, heads_here):
    count = sum(len(g) for g in groups)
    rows, width = queries[0].shape[1:]
    tall, wide = heads_here * rows, count * rows
    docs = lengths.shape[1]
    step = 16
    n = len(groups)

    def body(place_ref, len_ref, *refs):
        q_in, own_in, oth_in = refs[:n], refs[n : 2 * n], refs[2 * n : 3 * n]
        out_ref, prob_ref, q_ref, own_ref, oth_ref = refs[3 * n : 3 * n + 5]
        msgs, (s_scr, m_scr, hot_scr, send_scr) = refs[3 * n + 5 : 3 * n + 5 + count], refs[3 * n + 5 + count :]
        z_index, core = place_ref[0], place_ref[1]
        for g, ks in enumerate(groups):
            for j, k in enumerate(ks):
                q_ref[z_index ^ k] = q_in[g][j]
                own_ref[z_index ^ k] = own_in[g][j]
                oth_ref[z_index ^ k] = oth_in[g][j]
        sides = (own_ref, oth_ref)
        cores = (core, 1 - core)
        lane = lax.broadcasted_iota(jnp.int32, (rows, 128), 1).astype(F32)
        for side in range(2):
            for b in range(count):
                pos = lax.broadcasted_iota(jnp.int32, (rows, 1), 0) + (2 * b + cores[side]) * rows
                hot = (residue(pos.astype(F32), 12.0) == lane).astype(F32)
                hot_scr[side, b * rows : (b + 1) * rows, :] = hot.astype(BF16)
        for i in range(count):
            keys = (i + 1) * rows
            pos = lax.broadcasted_iota(jnp.int32, (rows, 1), 0) + (2 * i + core) * rows
            pos_f = pos.astype(F32)
            begin = jnp.zeros_like(pos)
            run = jnp.int32(0)
            for d in range(docs):
                run = run + len_ref[0, d]
                begin = jnp.where(pos >= run, run, begin)
            tables = []
            for h in range(heads_here):
                head = (z_index * heads_here + h).astype(F32)
                table = jnp.ones((rows, 128), F32)
                for r in (2.0, 4.0, 6.0):
                    mine = residue(head, r)
                    pick_q = (residue(pos_f, r) == mine).astype(F32)
                    pick_k = (residue(lane, r) == mine).astype(F32)
                    table = table + pick_q * pick_k
                tables.append(jnp.where(lane < 12.0, table, 0.0))
            table = jnp.concatenate(tables, axis=0).astype(BF16)
            stacked = stack_heads(q_ref[i], heads_here)
            for side in range(2):
                key = sides[side][:, :, :width].reshape(wide, width)[:keys]
                s_scr[side, :, :keys] = mm(stacked, key, NT)
                m_scr[side, :, :keys] = mm(table, hot_scr[side, :keys], NT)
            key_pos = [
                jnp.concatenate(
                    [
                        lax.broadcasted_iota(jnp.int32, (1, rows), 1) + (2 * b + cores[side]) * rows
                        for b in range(i + 1)
                    ],
                    axis=1,
                )
                for side in range(2)
            ]
            for h in range(heads_here):
                for at in range(0, rows, step):
                    lo = h * rows + at
                    pos_c, begin_c = pos[at : at + step], begin[at : at + step]
                    masked = []
                    for side in range(2):
                        ok = (key_pos[side] <= pos_c) & (key_pos[side] >= begin_c)
                        masked.append(jnp.where(ok, s_scr[side, lo : lo + step, :keys], masked_value))
                    top = jnp.maximum(
                        jnp.max(masked[0], axis=1, keepdims=True), jnp.max(masked[1], axis=1, keepdims=True)
                    )
                    parts = [
                        jnp.exp(masked[side] - top) * m_scr[side, lo : lo + step, :keys] for side in range(2)
                    ]
                    total = jnp.sum(parts[0], axis=1, keepdims=True) + jnp.sum(parts[1], axis=1, keepdims=True)
                    inverse = 1.0 / total
                    for side in range(2):
                        prob_ref[i, side, lo : lo + step, :keys] = (parts[side] * inverse).astype(BF16)
            mixed = jnp.zeros((tall, width), F32)
            for side in range(2):
                value = sides[side][:, :, width:].reshape(wide, width)[:keys]
                mixed = mixed + mm(prob_ref[i, side, :, :keys], value, NN)
            result = fold_heads(mixed, rows, heads_here)
            out_ref[i] = result
            send_scr[i] = pack(result.astype(BF16)[:, :live])
        for k in range(count):
            msgs[k][...] = send_scr[z_index ^ k]

    live = heads_here * HEAD_DIM
    outs = (
        shape(F32, count, rows, width),
        shape(BF16, count, 2, tall, wide),
        shape(BF16, count, rows, width),
        shape(BF16, count, rows, 2 * width),
        shape(BF16, count, rows, 2 * width),
    ) + (shape(BF16, packed_rows(rows, live), 128),) * count
    scratch = (
        shape(F32, 2, tall, wide),
        shape(F32, 2, tall, wide),
        shape(BF16, 2, wide, 128),
        shape(BF16, count, packed_rows(rows, live), 128),
    )
    operands = (*queries, *kv_own, *kv_other)
    found = kernel(
        body, outs, (place, lengths), operands, scratch, micros=6.0, name="attend"
    )
    return found[0], found[1:5], list(found[5:])


def attend_back_call(place, queries, kv_own, kv_other, prob, attn, grads, heads_here):
    count, rows, width = queries.shape
    tall, wide = heads_here * rows, count * rows
    step = 16

    live = heads_here * HEAD_DIM

    def body(place_ref, q_ref, own_ref, oth_ref, prob_ref, attn_ref, *refs):
        grad_refs, (dq_ref, down_ref, doth_ref, p_scr, d_scr, acc, grad_ref) = refs[:count], refs[count:]
        sides = (own_ref, oth_ref)
        acc[...] = jnp.zeros_like(acc)
        grad_ref[...] = jnp.zeros_like(grad_ref)
        for k in range(count):
            grad_ref[place_ref[0] ^ k, :, :live] = unpack(grad_refs[k][...], rows, live)
        for i in range(count):
            keys = (i + 1) * rows
            grad = grad_ref[i]
            stacked_q = stack_heads(q_ref[i], heads_here)
            stacked_g = stack_heads(grad, heads_here)
            product = grad.astype(F32) * attn_ref[i]
            head_of = lane_head(width)
            delta = [
                jnp.sum(jnp.where(head_of == h, product, 0.0), axis=1, keepdims=True) for h in range(heads_here)
            ]
            for side in range(2):
                value = sides[side][:, :, width:].reshape(wide, width)[:keys]
                p_scr[side, :, :keys] = mm(stacked_g, value, NT)
            for h in range(heads_here):
                for at in range(0, rows, step):
                    lo = h * rows + at
                    for side in range(2):
                        weights = prob_ref[i, side, lo : lo + step, :keys].astype(F32)
                        shifted = p_scr[side, lo : lo + step, :keys] - delta[h][at : at + step]
                        d_scr[side, lo : lo + step, :keys] = (weights * shifted).astype(BF16)
            grad_q = jnp.zeros((tall, width), F32)
            for side in range(2):
                key = sides[side][:, :, :width].reshape(wide, width)[:keys]
                moved = d_scr[side, :, :keys]
                grad_q = grad_q + mm(moved, key, NN)
                acc[side, :keys, :width] += mm(moved, stacked_q, TN)
                acc[side, :keys, width:] += mm(prob_ref[i, side, :, :keys], stacked_g, TN)
            dq_ref[i] = (0.125 * fold_heads(grad_q, rows, heads_here)).astype(BF16)
        down_ref[...] = acc[0].reshape(count, rows, 2 * width)
        doth_ref[...] = acc[1].reshape(count, rows, 2 * width).astype(BF16)

    outs = (
        shape(BF16, count, rows, width),
        shape(F32, count, rows, 2 * width),
        shape(BF16, count, rows, 2 * width),
    )
    scratch = (
        shape(F32, 2, tall, wide),
        shape(BF16, 2, tall, wide),
        shape(F32, 2, wide, 2 * width),
        shape(BF16, count, rows, width),
    )
    operands = (queries, kv_own, kv_other, prob, attn, *grads)
    return kernel(body, outs, (place,), operands, scratch, micros=6.0, name="attend_back")


def join_call(place, grad_q, grad_kv, arrived, live):
    count, rows, width = grad_q.shape

    def body(place_ref, q_ref, kv_ref, in_ref, out_ref, *rest):
        msgs, scr = rest[:count], rest[count]
        for b in range(count):
            both = (kv_ref[b] + in_ref[b].astype(F32)).astype(BF16)
            out_ref[b, :, :width] = q_ref[b]
            out_ref[b, :, width:] = both
            dense = [q_ref[b][:, :live], both[:, :live], both[:, width : width + live]]
            scr[b] = pack(jnp.concatenate(dense, axis=1))
        for k in range(count):
            msgs[k][...] = scr[place_ref[0] ^ k]

    message = shape(BF16, packed_rows(rows, 3 * live), 128)
    outs = (shape(BF16, count, rows, 3 * width),) + (message,) * count
    scratch = (shape(BF16, count, *message.shape),)
    joined, *msgs = kernel(body, outs, (place,), (grad_q, grad_kv, arrived), scratch, micros=0.7, name="join_grads")
    return joined, msgs


def gather_heads(place_ref, pieces, scr, rows, live):
    for k, ref in enumerate(pieces):
        scr[place_ref[0] ^ k] = ref[...]
    return jnp.concatenate([unpack(scr[k], rows, live) for k in range(len(pieces))], axis=1)


def norms_call(place, pieces, layer_in, vectors, w_out, live):
    count, rows = len(pieces), layer_in.shape[0]
    model = w_out.shape[0]

    def body(place_ref, *refs):
        in_ref, g2, b2, g3, b3, wo_ref, mid_ref, attn_ref, n3_ref, piece_scr = refs[count:]
        attn = gather_heads(place_ref, refs[:count], piece_scr, rows, live)
        attn_ref[...] = attn
        unit2, _ = unit_norm(attn.astype(F32))
        normed2 = (unit2 * row(g2) + row(b2)).astype(BF16)
        middle = in_ref[...].astype(F32) + mm(normed2, wo_ref[...], NN)
        mid_ref[...] = middle
        unit3, _ = unit_norm(middle)
        n3_ref[...] = (unit3 * row(g3) + row(b3)).astype(BF16)

    outs = (shape(F32, rows, model), shape(BF16, rows, model), shape(BF16, rows, model))
    operands = (*pieces, layer_in, *vectors, w_out)
    scratch = (shape(BF16, count, *pieces[0].shape),)
    return kernel(body, outs, (place,), operands, scratch, micros=1.5, name="norms")


def up_call(place, normed3, w_up, parts):
    rows, (model, hidden) = normed3.shape[0], w_up.shape
    part = hidden // parts

    def body(place_ref, n3_ref, wu_ref, act_ref, slope_ref, *msgs):
        normed = n3_ref[...]
        for r in range(parts):
            upper = mm(normed, wu_ref[:, r * part : (r + 1) * part], NN)
            cumulative = 0.5 * (1.0 + lax.erf(upper * 0.7071067811865476))
            density = jnp.exp(-0.5 * upper * upper) * 0.3989422804014327
            act_ref[r] = (upper * cumulative).astype(BF16)
            slope_ref[r] = (cumulative + upper * density).astype(BF16)
        for k in range(parts):
            msgs[k][...] = act_ref[place_ref[2] ^ k]

    outs = (shape(BF16, parts, rows, part),) * 2 + (shape(BF16, rows, part),) * parts
    act, slope, *msgs = kernel(body, outs, (place,), (normed3, w_up), micros=2.0, name="up_gelu")
    return act, slope, msgs


def padded_quarter(quarter):
    return -(-(quarter + 64) // 128) * 128


def backward_call(place, attn, middle, act, slope, grad_out, vectors, w_out, w_up, w_down, parts, count, live):
    rows = attn.shape[0]
    model, hidden = w_up.shape
    part, quarter = hidden // parts, model // parts
    pad_q = padded_quarter(quarter)
    message = shape(BF16, packed_rows(rows, live), 128)

    def body(
        place_ref, attn_ref, mid_ref, act_ref, slope_ref, go_ref, g2, b2, g3, b3, wo_ref, wu_ref, wd_ref,
        out_ref, gmid_ref, *rest,
    ):
        msgs, heads = rest[:parts], rest[parts : parts + count]
        up_scr, n2_scr, head_scr = rest[parts + count :]
        here = place_ref[2]
        go = go_ref[...]
        middle = mid_ref[...]
        out = middle
        grad3 = jnp.zeros((rows, model), F32)
        for r in range(parts):
            w_d = wd_ref[r * part : (r + 1) * part, :]
            out = out + mm(act_ref[r], w_d, NN)
            grad_up = (mm(go, w_d, NT) * slope_ref[r].astype(F32)).astype(BF16)
            up_scr[r] = grad_up
            grad3 = grad3 + mm(grad_up, wu_ref[:, r * part : (r + 1) * part], NT)
        out_ref[...] = out.astype(BF16)
        unit3, scale3 = unit_norm(middle)
        grad_mid = go.astype(F32) + norm_back(grad3, row(g3), unit3, scale3)
        gmid_ref[...] = grad_mid
        proj = grad_mid.astype(BF16)
        grad2 = mm(proj, wo_ref[...], NT)
        unit2, scale2 = unit_norm(attn_ref[...].astype(F32))
        grad_attn = norm_back(grad2, row(g2), unit2, scale2).astype(BF16)
        for k in range(count):
            head_scr[k] = pack(grad_attn[:, k * live : (k + 1) * live])
        for k in range(count):
            heads[k][...] = head_scr[place_ref[0] ^ k]
        sums = [
            jnp.sum(grad2 * unit2, axis=0, keepdims=True),
            jnp.sum(grad2, axis=0, keepdims=True),
            jnp.sum(grad3 * unit3, axis=0, keepdims=True),
            jnp.sum(grad3, axis=0, keepdims=True),
        ]
        table = jnp.concatenate(sums + [jnp.zeros((4, model), F32)], axis=0)
        normed2 = (unit2 * row(g2) + row(b2)).astype(BF16)
        normed3 = (unit3 * row(g3) + row(b3)).astype(BF16)
        spare, lines = pad_q - quarter, quarter // 64
        for r in range(parts):
            chunks = [table[:, r * quarter + 64 * j : r * quarter + 64 * (j + 1)] for j in range(lines)]
            side = jnp.concatenate(chunks + [jnp.zeros((rows - 8 * lines, 64), F32)], axis=0).astype(BF16)
            pieces = [normed2[:, r * quarter : (r + 1) * quarter], side]
            if spare > 64:
                pieces.append(jnp.zeros((rows, spare - 64), BF16))
            n2_scr[r] = jnp.concatenate(pieces, axis=1)
        for k in range(parts):
            msgs[k][:, :part] = up_scr[here ^ k]
            msgs[k][:, part : part + model] = proj
            msgs[k][:, part + model : part + 2 * model] = normed3
            msgs[k][:, part + 2 * model :] = n2_scr[here ^ k]

    outs = (
        shape(BF16, rows, model),
        shape(F32, rows, model),
    )
    outs += (shape(BF16, rows, part + 2 * model + pad_q),) * parts + (message,) * count
    operands = (attn, middle, act, slope, grad_out, *vectors, w_out, w_up, w_down)
    scratch = (
        shape(BF16, parts, rows, part),
        shape(BF16, parts, rows, pad_q),
        shape(BF16, count, *message.shape),
    )
    found = kernel(body, outs, (place,), operands, scratch, micros=9.0, name="token_backward")
    found = list(found)
    return found[0], found[1], found[2 : 2 + parts], found[2 + parts :]


def down_grad_call(place, acts, grads, chips):
    parts = len(acts)
    part, model = acts[0].shape[1], grads[0].shape[1]
    own = part // (2 * chips)

    def body(place_ref, *refs):
        act_refs, grad_refs, (keep_ref, send_ref, scr) = refs[:parts], refs[parts : 2 * parts], refs[2 * parts :]
        core = place_ref[1]
        act = jnp.concatenate([ref[...] for ref in act_refs], axis=0)
        grad = jnp.concatenate([ref[...] for ref in grad_refs], axis=0)
        scr[...] = mm(act, grad, TN).reshape(chips, 2, own, model)
        for k in range(chips):
            keep_ref[k] = scr[k, core]
            send_ref[k] = scr[k, 1 - core].astype(BF16)

    outs = (shape(F32, chips, own, model), shape(BF16, chips, own, model))
    scratch = (shape(F32, chips, 2, own, model),)
    return kernel(body, outs, (place,), (*acts, *grads), scratch, micros=3.0, name="grad_down")


def up_grad_call(place, back, chips, part, model):
    parts = len(back)
    quarter = model // parts
    own = model // (parts * chips * 2)
    tall = (parts + 1) * own + 8

    def body(place_ref, *refs):
        back_refs = refs[:parts]
        keep_ref, send_ref, up_scr, out_scr, vec_scr = refs[parts:]
        core = place_ref[1]
        ends = (0, part, part + model, part + 2 * model, back_refs[0].shape[1])
        grad_up, proj, normed3, normed2 = (
            jnp.concatenate([ref[:, lo:hi] for ref in back_refs], axis=0) for lo, hi in zip(ends, ends[1:])
        )
        up_scr[...] = mm(normed3, grad_up, TN).reshape(parts, chips, 2, own, part)
        out_scr[...] = mm(normed2, proj, TN)[:quarter].reshape(chips, 2, own, model)
        lines = quarter // 64
        side = jnp.zeros((8 * lines, 64), F32)
        for ref in back_refs:
            side = side + ref[:, ends[3] + quarter : ends[3] + quarter + 64].astype(F32)[: 8 * lines]
        table = jnp.concatenate([side[8 * j : 8 * (j + 1)] for j in range(lines)], axis=1)
        vec_scr[...] = jnp.zeros_like(vec_scr)
        for k in range(chips):
            for side in range(2):
                at = (2 * k + side) * own
                vec_scr[k, side, :, :own] = table[:, at : at + own]
        for k in range(chips):
            for side, ref in ((core, keep_ref), (1 - core, send_ref)):
                pieces = [up_scr[r, k, side] for r in range(parts)] + [out_scr[k, side], vec_scr[k, side]]
                ref[k] = jnp.concatenate(pieces, axis=0).astype(ref.dtype)

    outs = (shape(F32, chips, tall, model), shape(BF16, chips, tall, model))
    scratch = (
        shape(F32, parts, chips, 2, own, part),
        shape(F32, chips, 2, own, model),
        shape(F32, chips, 2, 8, model),
    )
    return kernel(body, outs, (place,), tuple(back), scratch, micros=4.0, name="grad_up_out")


def qkv_grad_call(place, groups, units, grads, gain, bias, weight, parts, live, width):
    count, rows = grads.shape[:2]
    model = weight.shape[0]
    own = model // (parts * count * 2)
    n = len(units)

    def body(place_ref, *refs):
        unit_refs = refs[:n]
        grad_ref, gain_ref, bias_ref, weight_ref, keep_ref, send_ref, unit_scr, scr = refs[n:]
        z_index, core = place_ref[0], place_ref[1]
        for g, ks in enumerate(groups):
            for j, k in enumerate(ks):
                unit_scr[z_index ^ k] = unit_refs[g][j]
        grad = grad_ref[...].reshape(count * rows, 3 * width)
        cross = mm(unit_scr[...].reshape(count * rows, model), grad, TN)
        total = jnp.sum(grad.astype(F32), axis=0, keepdims=True)
        columns = jnp.concatenate([row(gain_ref), row(bias_ref), jnp.zeros((6, model), F32)], axis=0).T
        weight_f = weight_ref[...].astype(F32)
        grad_gain = jnp.sum(weight_f * cross, axis=1, keepdims=True)
        grad_bias = jnp.sum(weight_f * total, axis=1, keepdims=True)
        lane = lax.broadcasted_iota(jnp.int32, (1, 3 * width), 1)
        made = columns[:, 0:1] * cross + columns[:, 1:2] * total
        made = jnp.where(lane == live, grad_gain, jnp.where(lane == live + 1, grad_bias, made))
        scr[...] = made.reshape(parts, count, 2, own, 3 * width)
        for r in range(parts):
            keep_ref[r] = jnp.concatenate([scr[r, k, core] for k in range(count)], axis=0)
            send_ref[r] = jnp.concatenate([scr[r, k, 1 - core] for k in range(count)], axis=0).astype(BF16)

    outs = (shape(F32, parts, count * own, 3 * width), shape(BF16, parts, count * own, 3 * width))
    scratch = (shape(BF16, count, rows, model), shape(F32, parts, count, 2, own, 3 * width))
    operands = (*units, grads, gain, bias, weight)
    return kernel(body, outs, (place,), operands, scratch, micros=4.0, name="grad_qkv")


def spread_call(place, keep, arrived):
    parts = keep.shape[0]

    def body(place_ref, keep_ref, in_ref, *outs):
        for k in range(parts):
            at = place_ref[2] ^ k
            outs[k][...] = (keep_ref[at] + in_ref[at].astype(F32)).astype(BF16)

    return kernel(body, (shape(BF16, *keep.shape[1:]),) * parts, (place,), (keep, arrived), micros=0.8, name="spread")


def halve_call(place, keep, arrived, bit):
    half = keep.shape[0] // 2

    def body(place_ref, keep_ref, in_ref, stay_ref, away_ref):
        mine = (place_ref[0] // bit) % 2
        for j in range(half):
            here, there = 2 * j + mine, 2 * j + 1 - mine
            stay_ref[j] = keep_ref[here] + in_ref[here].astype(F32)
            away_ref[j] = (keep_ref[there] + in_ref[there].astype(F32)).astype(BF16)

    rest = keep.shape[1:]
    return kernel(body, (shape(F32, half, *rest), shape(BF16, half, *rest)), (place,), (keep, arrived), micros=0.8, name="halve")


def finish_down_call(keep, arrived):
    def body(keep_ref, in_ref, out_ref):
        out_ref[...] = keep_ref[0] + in_ref[0].astype(F32)

    return kernel(body, shape(F32, *keep.shape[1:]), (), (keep, arrived), micros=0.6, name="finish_down")


def finish_up_call(place, keep, arrived, parts, own, part):
    model = keep.shape[2]

    def body(place_ref, keep_ref, in_ref, out_ref, g2, b2, g3, b3, *rest):
        msgs, scr = rest[:parts], rest[parts]
        value = keep_ref[0] + in_ref[0].astype(F32)
        out_ref[...] = value[parts * own : (parts + 1) * own]
        for at, ref in enumerate((g2, b2, g3, b3)):
            line = (parts + 1) * own + at
            ref[...] = value[line : line + 1, :own].reshape(own)
        scr[...] = value[: parts * own].reshape(parts, own, part)
        for k in range(parts):
            msgs[k][...] = scr[place_ref[2] ^ k].astype(BF16)

    outs = (shape(F32, own, model),) + (shape(F32, own),) * 4 + (shape(BF16, own, part),) * parts
    scratch = (shape(F32, parts, own, part),)
    return kernel(body, outs, (place,), (keep, arrived), scratch, micros=0.8, name="finish_up")


def place_up_call(place, pieces):
    parts = len(pieces)
    own, part = pieces[0].shape

    def body(place_ref, *refs):
        for k in range(parts):
            at = pl.multiple_of((place_ref[2] ^ k) * part, 128)
            refs[parts][:, pl.ds(at, part)] = refs[k][...].astype(F32)

    return kernel(body, shape(F32, own, parts * part), (place,), tuple(pieces), micros=0.5, name="place_up")


def share_call(place, pieces, chips):
    own = pieces[0].shape[0] // chips

    def body(place_ref, *refs):
        ins, outs, scr = refs[: len(pieces)], refs[len(pieces) : -1], refs[-1]
        total = ins[0][...].astype(F32)
        for ref in ins[1:]:
            total = total + ref[...].astype(F32)
        scr[...] = total.reshape(chips, own, total.shape[1])
        for k in range(chips):
            outs[k][...] = scr[place_ref[0] ^ k].astype(BF16)

    lanes = pieces[0].shape[1]
    outs = (shape(BF16, own, lanes),) * chips
    return kernel(body, outs, (place,), tuple(pieces), (shape(F32, chips, own, lanes),), micros=0.7, name="share")


def finish_qkv_call(place, pieces, model, live, width):
    count, own = len(pieces), pieces[0].shape[0]

    def body(place_ref, *refs):
        q_ref, k_ref, v_ref, gain_ref, bias_ref, in_ref = refs[count:]
        for k in range(count):
            in_ref[place_ref[0] ^ k] = refs[k][...].astype(F32)
        for at, ref in enumerate((q_ref, k_ref, v_ref)):
            ref[...] = jnp.concatenate(
                [in_ref[k, :, at * width : at * width + live] for k in range(count)], axis=1
            )
        total = jnp.sum(in_ref[:, :, live : live + 2], axis=0).T
        gain_ref[...] = total[0:1].reshape(own)
        bias_ref[...] = total[1:2].reshape(own)

    outs = (shape(F32, own, model),) * 3 + (shape(F32, own),) * 2
    scratch = (shape(F32, count, *pieces[0].shape),)
    return kernel(body, outs, (place,), tuple(pieces), scratch, micros=0.8, name="finish_qkv")


def input_grad_call(place, pieces, layer_in, grad_mid, gain, w_query, w_key, w_value, live):
    count = len(pieces)
    rows, model = layer_in.shape

    def body(place_ref, *refs):
        in_ref, gmid_ref, gain_ref, wq_ref, wk_ref, wv_ref, out_ref, scr = refs[count:]
        for k in range(count):
            scr[place_ref[0] ^ k] = refs[k][...]
        blocks = [unpack(scr[k], rows, 3 * live) for k in range(count)]
        grad = jnp.zeros((rows, model), F32)
        for at, w_ref in enumerate((wq_ref, wk_ref, wv_ref)):
            part = jnp.concatenate([block[:, at * live : (at + 1) * live] for block in blocks], axis=1)
            grad = grad + mm(part, w_ref[...], NT)
        unit, scale = unit_norm(in_ref[...].astype(F32))
        out_ref[...] = (gmid_ref[...] + norm_back(grad, row(gain_ref), unit, scale)).astype(BF16)

    operands = (*pieces, layer_in, grad_mid, gain, w_query, w_key, w_value)
    scratch = (shape(BF16, count, *pieces[0].shape),)
    return kernel(body, shape(BF16, rows, model), (place,), operands, scratch, micros=3.0, name="grad_inputs")


def swap_core(value):
    return lax.ppermute(value, "core", [(0, 1), (1, 0)])


def swap(value, axis, bit):
    return lax.ppermute(value, axis, [(k, k ^ bit) for k in range(lax.axis_size(axis))])


def trade(messages, axis):
    found = {k: swap(messages[k], axis, k) for k in range(len(messages) - 1, 0, -1)}
    return [messages[0]] + [found[k] for k in range(1, len(messages))]


def gather_chips(block, chips):
    found = {0: block}
    bit = chips // 2
    while bit >= 1:
        for k in sorted(found):
            found[k | bit] = swap(found[k], "chip", bit)
        bit //= 2
    return [found[k] for k in range(chips)]


def scatter_chips(place, keep, arrived, chips, bit):
    while bit < chips:
        keep, away = halve_call(place, keep, arrived, bit)
        arrived = swap(away, "chip", bit)
        bit *= 2
    return keep, arrived


def after(values, *others):
    return lax.optimization_barrier((values, others))[0]


def fast_shards(
    inputs, doc_lengths, ln1_gain, ln1_bias, w_query, w_key, w_value, ln2_gain, ln2_bias, w_out,
    ln3_gain, ln3_bias, w_up, w_down, out_grad,
):
    rows, model = inputs.shape[1:]
    chips, parts = lax.axis_size("chip"), lax.axis_size("rows")
    z_index = lax.axis_index("chip")
    heads_here = HEADS // chips
    live = heads_here * HEAD_DIM
    width = -(-live // 128) * 128
    hidden = w_up.shape[1]
    part = hidden // parts
    own = model // (parts * chips * 2)
    place = jnp.stack([z_index, lax.axis_index("core"), lax.axis_index("rows")]).astype(jnp.int32)
    scope = jax.named_scope

    def columns(weight):
        mine = lax.dynamic_slice_in_dim(weight, z_index * live, live, 1)
        return jnp.pad(mine, ((0, 0), (0, width - live)))

    place, layer_in, out_grad = lax.optimization_barrier((place, inputs[0], out_grad[0]))
    with scope("gather_in"):
        blocks = gather_chips(layer_in, chips)
    grad_out = mask_call(place, doc_lengths, out_grad)
    w_heads = jnp.concatenate([columns(w_query), columns(w_key), columns(w_value)], axis=1)
    groups = [g for g in ([0], list(range(1, chips - 1)), [chips - 1]) if g] if chips > 1 else [[0]]
    made = [qkv_call([blocks[k] for k in g], ln1_gain, ln1_bias, w_heads, width) for g in groups]
    queries, kv_own, units = ([m[at] for m in made] for at in range(3))
    with scope("core_kv"):
        kv_other = [swap_core(v) for v in kv_own]
    attn_heads, (prob, queries, kv_own, kv_other), messages = attend_call(
        place, doc_lengths, groups, queries, kv_own, kv_other, heads_here
    )
    fence = lax.optimization_barrier
    with scope("chip_attn"):
        pieces = trade(messages, "chip")
    with scope("plane_out"):
        grads_plane = trade([grad_out] * parts, "rows")
    pieces = after(pieces, grads_plane)

    vectors = (ln2_gain, ln2_bias, ln3_gain, ln3_bias)
    middle, attn, normed3 = norms_call(place, pieces, layer_in, vectors, w_out, live)
    act, slope, acts = up_call(place, normed3, w_up, parts)
    with scope("plane_act"):
        acts = trade(acts, "rows")
    output, grad_mid, back, messages = backward_call(
        place, attn, middle, act, slope, grad_out, vectors, w_out, w_up, w_down, parts, chips, live
    )
    back = after(back, acts[1:])
    with scope("chip_grad"):
        grad_heads = trade(messages, "chip")
    with scope("plane_back"):
        far = [swap(back[k], "rows", k) for k in range(3, parts)]
    grad_q, grad_kv, grad_kv_other = attend_back_call(
        place, queries, kv_own, kv_other, prob, attn_heads, grad_heads, heads_here
    )
    with scope("core_grad"):
        grad_kv_other = swap_core(grad_kv_other)
    down_keep, down_send = down_grad_call(place, after(acts, grad_q), grads_plane, chips)
    grad_kv_other, down_send, far = fence((grad_kv_other, down_send, far))
    with scope("core_down"):
        down_recv = swap_core(down_send)
    with scope("plane_back"):
        near = after(back[1:3], far)
        back = back[:1] + [swap(near[k], "rows", k + 1) for k in range(len(near))] + far
    grad_qkv, messages = join_call(place, grad_q, grad_kv, grad_kv_other, live)
    with scope("down_sum"):
        down_keep, down_away = halve_call(place, down_keep, after(down_recv, grad_qkv), 1)
        grad_qkv, down_away = fence((grad_qkv, down_away))
        down_recv = swap(down_away, "chip", 1)
    with scope("chip_qkv"):
        grad_pieces = trade(messages, "chip")
    qkv_keep, qkv_send = qkv_grad_call(
        place, groups, units, grad_qkv, ln1_gain, ln1_bias, w_heads, parts, live, width
    )
    down_recv = after(down_recv, qkv_send)
    with scope("core_w"):
        qkv_send = swap_core(qkv_send)
    qkv_sums = spread_call(place, qkv_keep, qkv_send)
    with scope("down_sum"):
        down_keep, down_last = scatter_chips(place, down_keep, down_recv, chips, 2)
    back = after(back, (down_keep, grad_pieces[2:]))
    up_keep, up_send = up_grad_call(place, back, chips, part, model)
    with scope("plane_w"):
        traded = trade(qkv_sums, "rows")
    up_send = after(up_send, (down_last, grad_pieces[1:2]))
    with scope("core_up"):
        up_recv = swap_core(up_send)
    up_keep, up_away = halve_call(place, up_keep, up_recv, 1)
    with scope("up_sum"):
        up_recv = swap(up_away, "chip", 1)
    traded = after(traded, up_away)
    with scope("chip_w"):
        shared = share_call(place, traded, chips)
        qkv_all = trade(shared, "chip")
    grad_inputs = input_grad_call(
        place, grad_pieces, layer_in, grad_mid, ln1_gain, w_query, w_key, w_value, live
    )
    gwd = finish_down_call(down_keep, down_last)
    up_recv = after(up_recv, (grad_pieces, shared, down_last))
    with scope("up_sum"):
        up_keep, up_last = scatter_chips(place, up_keep, up_recv, chips, 2)
    up_last = after(up_last, (qkv_all, gwd, grad_inputs))
    gwo, g2, b2, g3, b3, *up_rows = finish_up_call(place, up_keep, up_last, parts, own, part)
    with scope("plane_rows"):
        up_rows = trade(up_rows, "rows")
    gwq, gwk, gwv, g1, b1 = finish_qkv_call(place, qkv_all, model, live, width)
    gwu = place_up_call(place, up_rows)
    return (
        output[None], grad_inputs[None], g1, b1, gwq, gwk, gwv, g2, b2, gwo, g3, b3, gwu, gwd,
    )


def takes_fast(mesh):
    seq, parts = mesh.shape["seq"], mesh.shape["rows"]
    chips = seq // 2
    return seq % 2 == 0 and chips & (chips - 1) == 0 and parts in (1, 2, 4) and HEADS % max(chips, 1) == 0


def solution(mesh):
    if takes_fast(mesh):
        parts, seq = mesh.shape["rows"], mesh.shape["seq"]
        split = jax.sharding.Mesh(mesh.devices.reshape(parts, seq // 2, 2), ("rows", "chip", "core"))
        return mapped(fast_shards, split, ("chip", "core"))
    return mapped(shards, mesh, "seq")
```

```python
import math

import jax
import jax.numpy as jnp
from jax import lax
from jax.experimental import pallas as pl
from jax.experimental.pallas import tpu as pltpu
from jax.sharding import PartitionSpec as P

HEADS = 12
HEAD_DIM = 64


segment_pairs = ((2048, 1), (4096, 2), (8192, 4), (16384, 6))
masked_value = -1e30


def layer_norm(vector, gain_vec, bias_vec):
    row_mean = jnp.mean(vector, axis=-1, keepdims=True)
    centered = vector - row_mean
    row_var = jnp.mean(centered * centered, axis=-1, keepdims=True)
    return centered * lax.rsqrt(row_var + 1e-05) * gain_vec + bias_vec


def doc_of(positions, doc_ends):
    return jnp.sum((positions[:, None] >= doc_ends[None, :]).astype(jnp.int32), axis=1)


def pair_terms(query_pos, key_pos, query_doc, key_doc, head_count):
    head_ids = jnp.arange(head_count, dtype=jnp.int32)
    multiplicity = jnp.zeros((head_count, query_pos.shape[0], key_pos.shape[0]), jnp.float32)
    for seg_width, dilation in segment_pairs:
        same_seg = query_pos[:, None] // seg_width == key_pos[None, :] // seg_width
        query_pick = (query_pos % seg_width % dilation)[None, :] == (head_ids % dilation)[:, None]
        key_pick = (key_pos % seg_width % dilation)[None, :] == (head_ids % dilation)[:, None]
        joined = same_seg[None] & query_pick[:, :, None] & key_pick[:, None, :]
        multiplicity = multiplicity + joined.astype(jnp.float32)
    allowed = (key_pos[None, :] <= query_pos[:, None]) & (query_doc[:, None] == key_doc[None, :])
    allowed = allowed[None] & (multiplicity > 0.0)
    return (jnp.log(jnp.maximum(multiplicity, 1.0)), allowed)


def rows_inner(left, right):
    return lax.dot_general(
        left, right, (((0,), (0,)), ((), ())), preferred_element_type=jnp.float32
    )


def cols_inner(left, right):
    return lax.dot_general(
        left, right, (((1,), (1,)), ((), ())), preferred_element_type=jnp.float32
    )


def over_blocks(state, piece, step_fn):
    total_rows = piece[0].shape[0]
    block_rows = math.gcd(total_rows, 512)
    block_total = total_rows // block_rows
    split = tuple((part.reshape((block_total, block_rows) + part.shape[1:]) for part in piece))

    def inner(carried, block_item):
        return (step_fn(carried, block_item[1], block_item[0] * block_rows), None)

    result, unused = lax.scan(inner, state, (jnp.arange(block_total, dtype=jnp.int32), split))
    return result


def add_rows(buffer, start_pos, addend):
    current = lax.dynamic_slice_in_dim(buffer, start_pos, addend.shape[0], 0)
    return lax.dynamic_update_slice_in_dim(buffer, current + addend, start_pos, 0)


def shards(
    inputs,
    doc_lengths,
    ln1_gain,
    ln1_bias,
    w_query,
    w_key,
    w_value,
    ln2_gain,
    ln2_bias,
    w_out,
    ln3_gain,
    ln3_bias,
    w_up,
    w_down,
    out_grad,
):
    tok_rows = inputs.shape[1]
    head_count = HEADS
    head_size = HEAD_DIM
    model_width = inputs.shape[2]
    row_total = tok_rows * lax.axis_size("seq")
    layer_in = inputs[0].astype(jnp.float32)
    doc_ends = jnp.cumsum(doc_lengths[0])
    first_pos = lax.axis_index("seq") * tok_rows
    query_pos = first_pos + jnp.arange(tok_rows, dtype=jnp.int32)
    query_doc = doc_of(query_pos, doc_ends)
    valid = (query_doc < doc_lengths.shape[1]).astype(jnp.float32)
    first_norm, first_back = jax.vjp(layer_norm, layer_in, ln1_gain, ln1_bias)
    normed_one = first_norm.astype(jnp.bfloat16)
    queries = jnp.dot(normed_one, w_query, preferred_element_type=jnp.float32).astype(jnp.bfloat16)
    keys_local = jnp.dot(normed_one, w_key, preferred_element_type=jnp.float32).astype(jnp.bfloat16)
    values_local = jnp.dot(normed_one, w_value, preferred_element_type=jnp.float32).astype(
        jnp.bfloat16
    )
    query_heads = queries.reshape(tok_rows, head_count, head_size)

    def key_block_terms(key_start, key_count):
        key_pos = key_start + jnp.arange(key_count, dtype=jnp.int32)
        key_doc = doc_of(key_pos, doc_ends)
        return pair_terms(query_pos, key_pos, query_doc, key_doc, head_count)

    def with_pruning(step_fn):

        def wrapped(state, parts, start_pos):
            return step_fn(state, parts, start_pos)

        return wrapped

    def forward_step(state, parts, key_start):
        run_max, run_total, run_acc = state
        key_blk = parts[0].reshape(-1, head_count, head_size)
        value_blk = parts[1].reshape(-1, head_count, head_size)
        log_mult, allowed = key_block_terms(key_start, key_blk.shape[0])
        scores = 0.125 * jnp.einsum(
            "qhd,khd->hqk", query_heads, key_blk, preferred_element_type=jnp.float32
        )
        logits = jnp.where(allowed, scores + log_mult, masked_value)
        new_max = jnp.maximum(run_max, jnp.max(logits, axis=-1))
        weights = jnp.where(allowed, jnp.exp(logits - new_max[..., None]), 0.0)
        factor = jnp.exp(run_max - new_max)
        run_total = run_total * factor + jnp.sum(weights, axis=-1)
        run_acc = run_acc * factor[..., None] + jnp.einsum(
            "hqk,khd->hqd",
            weights.astype(jnp.bfloat16),
            value_blk,
            preferred_element_type=jnp.float32,
        )
        return (new_max, run_total, run_acc)

    forward_pruned = with_pruning(forward_step)
    start_state = (
        jnp.full((head_count, tok_rows), masked_value, jnp.float32),
        jnp.zeros((head_count, tok_rows), jnp.float32),
        jnp.zeros((head_count, tok_rows, head_size), jnp.float32),
    )
    final_state = over_blocks(
        start_state,
        (
            lax.all_gather(keys_local, "seq", axis=0, tiled=True),
            lax.all_gather(values_local, "seq", axis=0, tiled=True),
        ),
        forward_pruned,
    )
    run_max, run_total, run_acc = final_state
    row_lse = run_max + jnp.log(run_total)
    attn = (run_acc / run_total[..., None]).transpose(1, 0, 2).reshape(tok_rows, model_width)
    second_norm, second_back = jax.vjp(layer_norm, attn, ln2_gain, ln2_bias)
    normed_two = second_norm.astype(jnp.bfloat16)
    middle = layer_in + jnp.dot(normed_two, w_out, preferred_element_type=jnp.float32)
    third_norm, third_back = jax.vjp(layer_norm, middle, ln3_gain, ln3_bias)
    normed_three = third_norm.astype(jnp.bfloat16)
    upper = jnp.dot(normed_three, w_up, preferred_element_type=jnp.float32)
    activated_f, gelu_back = jax.vjp(
        lambda upper_in: jax.nn.gelu(upper_in, approximate=False), upper
    )
    activated = activated_f.astype(jnp.bfloat16)
    layer_out = middle + jnp.dot(activated, w_down, preferred_element_type=jnp.float32)
    grad_out = out_grad[0].astype(jnp.float32) * valid[:, None]
    grad_branch = grad_out.astype(jnp.bfloat16)
    grad_w_down = rows_inner(activated, grad_branch)
    grad_act = cols_inner(grad_branch, w_down)
    grad_upper = gelu_back(grad_act)[0].astype(jnp.bfloat16)
    grad_w_up = rows_inner(normed_three, grad_upper)
    grad_n3 = cols_inner(grad_upper, w_up)
    grad_mid_norm, grad_ln3_gain, grad_ln3_bias = third_back(grad_n3)
    grad_middle = grad_out + grad_mid_norm
    grad_proj = grad_middle.astype(jnp.bfloat16)
    grad_w_out = rows_inner(normed_two, grad_proj)
    grad_n2 = cols_inner(grad_proj, w_out)
    grad_attn_f, grad_ln2_gain, grad_ln2_bias = second_back(grad_n2)
    grad_attn = grad_attn_f.astype(jnp.bfloat16)
    grad_heads = grad_attn.reshape(tok_rows, head_count, head_size)
    row_delta = jnp.sum(
        (grad_attn.astype(jnp.float32) * attn).reshape(tok_rows, head_count, head_size), axis=-1
    )

    def backward_step(state, parts, key_start):
        grad_q_acc, grad_k_rows, grad_v_rows = state
        key_blk = parts[0].reshape(-1, head_count, head_size)
        value_blk = parts[1].reshape(-1, head_count, head_size)
        key_count = key_blk.shape[0]
        log_mult, allowed = key_block_terms(key_start, key_count)
        scores = 0.125 * jnp.einsum(
            "qhd,khd->hqk", query_heads, key_blk, preferred_element_type=jnp.float32
        )
        logits = jnp.where(allowed, scores + log_mult, masked_value)
        weights = jnp.where(allowed, jnp.exp(logits - row_lse[..., None]), 0.0)
        grad_weights = jnp.einsum(
            "qhd,khd->hqk", grad_heads, value_blk, preferred_element_type=jnp.float32
        )
        grad_scores = (weights * (grad_weights - row_delta.T[..., None])).astype(jnp.bfloat16)
        grad_q_acc = grad_q_acc + 0.125 * jnp.einsum(
            "hqk,khd->qhd", grad_scores, key_blk, preferred_element_type=jnp.float32
        )
        value_part = jnp.einsum(
            "hqk,qhd->khd",
            weights.astype(jnp.bfloat16),
            grad_heads,
            preferred_element_type=jnp.float32,
        ).reshape(key_count, model_width)
        key_part = 0.125 * jnp.einsum(
            "hqk,qhd->khd", grad_scores, query_heads, preferred_element_type=jnp.float32
        ).reshape(key_count, model_width)
        grad_k_rows = add_rows(grad_k_rows, key_start, key_part)
        grad_v_rows = add_rows(grad_v_rows, key_start, value_part)
        return (grad_q_acc, grad_k_rows, grad_v_rows)

    backward_pruned = with_pruning(backward_step)
    zero_state = (
        jnp.zeros((tok_rows, head_count, head_size), jnp.float32),
        jnp.zeros((row_total, model_width), jnp.float32),
        jnp.zeros((row_total, model_width), jnp.float32),
    )
    back_state = over_blocks(
        zero_state,
        (
            lax.all_gather(keys_local, "seq", axis=0, tiled=True),
            lax.all_gather(values_local, "seq", axis=0, tiled=True),
        ),
        backward_pruned,
    )
    grad_q_acc, grad_k_rows, grad_v_rows = back_state
    grad_k_acc, grad_v_acc = (
        lax.psum_scatter(
            grad_k_rows.astype(jnp.bfloat16), "seq", scatter_dimension=0, tiled=True
        ).astype(jnp.float32),
        lax.psum_scatter(
            grad_v_rows.astype(jnp.bfloat16), "seq", scatter_dimension=0, tiled=True
        ).astype(jnp.float32),
    )
    grad_queries = grad_q_acc.reshape(tok_rows, model_width).astype(jnp.bfloat16)
    grad_keys = grad_k_acc.astype(jnp.bfloat16)
    grad_values = grad_v_acc.astype(jnp.bfloat16)
    grad_w_query = rows_inner(normed_one, grad_queries)
    grad_w_key = rows_inner(normed_one, grad_keys)
    grad_w_value = rows_inner(normed_one, grad_values)
    grad_n1 = (
        cols_inner(grad_queries, w_query)
        + cols_inner(grad_keys, w_key)
        + cols_inner(grad_values, w_value)
    )
    grad_in_norm, grad_ln1_gain, grad_ln1_bias = first_back(grad_n1)
    grad_inputs = (grad_middle + grad_in_norm).astype(jnp.bfloat16)
    summed = (
        lax.psum_scatter(grad_ln1_gain, ("rows", "seq"), scatter_dimension=0, tiled=True),
        lax.psum_scatter(grad_ln1_bias, ("rows", "seq"), scatter_dimension=0, tiled=True),
        lax.psum_scatter(grad_w_query, ("rows", "seq"), scatter_dimension=0, tiled=True),
        lax.psum_scatter(grad_w_key, ("rows", "seq"), scatter_dimension=0, tiled=True),
        lax.psum_scatter(grad_w_value, ("rows", "seq"), scatter_dimension=0, tiled=True),
        lax.psum_scatter(grad_ln2_gain, ("rows", "seq"), scatter_dimension=0, tiled=True),
        lax.psum_scatter(grad_ln2_bias, ("rows", "seq"), scatter_dimension=0, tiled=True),
        lax.psum_scatter(grad_w_out, ("rows", "seq"), scatter_dimension=0, tiled=True),
        lax.psum_scatter(grad_ln3_gain, ("rows", "seq"), scatter_dimension=0, tiled=True),
        lax.psum_scatter(grad_ln3_bias, ("rows", "seq"), scatter_dimension=0, tiled=True),
        lax.psum_scatter(grad_w_up, ("rows", "seq"), scatter_dimension=0, tiled=True),
        lax.psum_scatter(grad_w_down, ("rows", "seq"), scatter_dimension=0, tiled=True),
    )
    return (
        layer_out.astype(jnp.bfloat16)[None],
        grad_inputs[None],
        summed[0],
        summed[1],
        summed[2],
        summed[3],
        summed[4],
        summed[5],
        summed[6],
        summed[7],
        summed[8],
        summed[9],
        summed[10],
        summed[11],
    )


def mapped(step, mesh, seq):
    spread = P(("rows",) + (seq if isinstance(seq, tuple) else (seq,)))
    tokens, plain = P("rows", seq, None), P()
    weights = P(spread[0], None)
    return jax.shard_map(
        step,
        mesh=mesh,
        in_specs=(tokens, P("rows", None)) + (plain,) * 12 + (tokens,),
        out_specs=(tokens, tokens, spread, spread, weights, weights, weights, spread, spread, weights)
        + (spread, spread, weights, weights),
        check_vma=False,
    )


F32 = jnp.float32
PACE = 1e6
BF16 = jnp.bfloat16
NT = (((1,), (1,)), ((), ()))
TN = (((0,), (0,)), ((), ()))
NN = (((1,), (0,)), ((), ()))


def mm(left, right, dims):
    return lax.dot_general(left, right, dims, preferred_element_type=F32)


def unit_norm(vector):
    centered = vector - jnp.mean(vector, axis=-1, keepdims=True)
    scale = lax.rsqrt(jnp.mean(centered * centered, axis=-1, keepdims=True) + 1e-05)
    return centered * scale, scale


def norm_back(grad, gain, unit, scale):
    weighted = grad * gain
    mean_w = jnp.mean(weighted, axis=-1, keepdims=True)
    mean_wu = jnp.mean(weighted * unit, axis=-1, keepdims=True)
    return scale * (weighted - mean_w - unit * mean_wu)


def shape(dtype, *dims):
    return jax.ShapeDtypeStruct(dims, dtype)


def row(ref):
    return ref[...].reshape(1, ref.shape[0])


def size_of(item):
    total = jnp.dtype(item.dtype).itemsize
    for dim in item.shape:
        total *= dim
    return total


def kernel(body, outs, scalars, operands, scratch=(), micros=2.0, name=None):
    single = not isinstance(outs, (tuple, list))
    listed = (outs,) if single else tuple(outs)
    vmem = pl.BlockSpec(memory_space=pltpu.VMEM)
    smem = pl.BlockSpec(memory_space=pltpu.SMEM)
    moved = sum(size_of(v) for v in (*operands, *listed))
    held = sum(size_of(v) for v in scratch)
    return pl.pallas_call(
        body,
        out_shape=outs if single else listed,
        in_specs=[smem] * len(scalars) + [vmem] * len(operands),
        out_specs=vmem if single else (vmem,) * len(listed),
        scratch_shapes=[pltpu.VMEM(v.shape, v.dtype) for v in scratch],
        compiler_params=pltpu.CompilerParams(vmem_limit_bytes=min(60 << 20, (moved + held) * 5 // 4 + (6 << 20))),
        cost_estimate=pl.CostEstimate(flops=int(micros * PACE), bytes_accessed=int(micros * PACE / 1e3), transcendentals=0),
        name=name,
    )(*scalars, *operands)


def packed_rows(rows, live):
    return rows * live // 128


def pack(block):
    rows, live = block.shape
    whole = live // 128
    pieces = [block[:, 128 * j : 128 * (j + 1)] for j in range(whole)]
    if live % 128:
        rest = block[:, 128 * whole :]
        pieces.append(jnp.concatenate([rest[: rows // 2], rest[rows // 2 :]], axis=1))
    return jnp.concatenate(pieces, axis=0)


def unpack(block, rows, live):
    whole = live // 128
    pieces = [block[rows * j : rows * (j + 1)] for j in range(whole)]
    if live % 128:
        rest = block[rows * whole :]
        pieces.append(jnp.concatenate([rest[:, :64], rest[:, 64:]], axis=0))
    return jnp.concatenate(pieces, axis=1)


def mask_call(place, lengths, out_grad):
    rows, model = out_grad.shape

    def body(place_ref, len_ref, in_ref, out_ref):
        last = jnp.int32(0)
        for d in range(lengths.shape[1]):
            last = last + len_ref[0, d]
        pos = lax.broadcasted_iota(jnp.int32, (rows, 1), 0) + (2 * place_ref[0] + place_ref[1]) * rows
        out_ref[...] = jnp.where(pos < last, in_ref[...].astype(F32), 0.0).astype(BF16)

    return kernel(body, shape(BF16, rows, model), (place, lengths), (out_grad,), micros=0.7, name="mask_grad")


def qkv_call(blocks, gain, bias, weight, width):
    count = len(blocks)
    rows, model = blocks[0].shape

    def body(*refs):
        xs, (gain_ref, bias_ref, weight_ref, q_ref, kv_ref, unit_ref) = refs[:count], refs[count:]
        for k in range(count):
            unit, _ = unit_norm(xs[k][...].astype(F32))
            normed = (unit * row(gain_ref) + row(bias_ref)).astype(BF16)
            made = mm(normed, weight_ref[...], NN)
            q_ref[k] = (made[:, :width].astype(BF16).astype(F32) * 0.125).astype(BF16)
            kv_ref[k] = made[:, width:].astype(BF16)
            unit_ref[k] = unit.astype(BF16)

    outs = (
        shape(BF16, count, rows, width),
        shape(BF16, count, rows, 2 * width),
        shape(BF16, count, rows, model),
    )
    return kernel(body, outs, (), (*blocks, gain, bias, weight), micros=1.2 * count, name="qkv_heads")


def lane_head(lanes):
    return lax.broadcasted_iota(jnp.int32, (1, lanes), 1) // HEAD_DIM


def residue(pos_f, modulus):
    return pos_f - modulus * jnp.floor((pos_f + 0.5) * (1.0 / modulus))


def stack_heads(block, heads_here):
    head_of = lane_head(block.shape[1])
    return jnp.concatenate(
        [jnp.where(head_of == h, block, jnp.zeros_like(block)) for h in range(heads_here)], axis=0
    )


def fold_heads(stacked, rows, heads_here):
    head_of = lane_head(stacked.shape[1])
    total = jnp.zeros((rows, stacked.shape[1]), stacked.dtype)
    for h in range(heads_here):
        total = jnp.where(head_of == h, stacked[h * rows : (h + 1) * rows], total)
    return total


def attend_call(place, lengths, groups, queries, kv_own, kv_other, heads_here):
    count = sum(len(g) for g in groups)
    rows, width = queries[0].shape[1:]
    tall, wide = heads_here * rows, count * rows
    docs = lengths.shape[1]
    step = 16
    n = len(groups)

    def body(place_ref, len_ref, *refs):
        q_in, own_in, oth_in = refs[:n], refs[n : 2 * n], refs[2 * n : 3 * n]
        out_ref, prob_ref, q_ref, own_ref, oth_ref = refs[3 * n : 3 * n + 5]
        msgs, (s_scr, m_scr, hot_scr, send_scr) = refs[3 * n + 5 : 3 * n + 5 + count], refs[3 * n + 5 + count :]
        z_index, core = place_ref[0], place_ref[1]
        for g, ks in enumerate(groups):
            for j, k in enumerate(ks):
                q_ref[z_index ^ k] = q_in[g][j]
                own_ref[z_index ^ k] = own_in[g][j]
                oth_ref[z_index ^ k] = oth_in[g][j]
        sides = (own_ref, oth_ref)
        cores = (core, 1 - core)
        lane = lax.broadcasted_iota(jnp.int32, (rows, 128), 1).astype(F32)
        for side in range(2):
            for b in range(count):
                pos = lax.broadcasted_iota(jnp.int32, (rows, 1), 0) + (2 * b + cores[side]) * rows
                hot = (residue(pos.astype(F32), 12.0) == lane).astype(F32)
                hot_scr[side, b * rows : (b + 1) * rows, :] = hot.astype(BF16)
        for i in range(count):
            keys = (i + 1) * rows
            pos = lax.broadcasted_iota(jnp.int32, (rows, 1), 0) + (2 * i + core) * rows
            pos_f = pos.astype(F32)
            begin = jnp.zeros_like(pos)
            run = jnp.int32(0)
            for d in range(docs):
                run = run + len_ref[0, d]
                begin = jnp.where(pos >= run, run, begin)
            tables = []
            for h in range(heads_here):
                head = (z_index * heads_here + h).astype(F32)
                table = jnp.ones((rows, 128), F32)
                for r in (2.0, 4.0, 6.0):
                    mine = residue(head, r)
                    pick_q = (residue(pos_f, r) == mine).astype(F32)
                    pick_k = (residue(lane, r) == mine).astype(F32)
                    table = table + pick_q * pick_k
                tables.append(jnp.where(lane < 12.0, table, 0.0))
            table = jnp.concatenate(tables, axis=0).astype(BF16)
            stacked = stack_heads(q_ref[i], heads_here)
            for side in range(2):
                key = sides[side][:, :, :width].reshape(wide, width)[:keys]
                s_scr[side, :, :keys] = mm(stacked, key, NT)
                m_scr[side, :, :keys] = mm(table, hot_scr[side, :keys], NT)
            key_pos = [
                jnp.concatenate(
                    [
                        lax.broadcasted_iota(jnp.int32, (1, rows), 1) + (2 * b + cores[side]) * rows
                        for b in range(i + 1)
                    ],
                    axis=1,
                )
                for side in range(2)
            ]
            for h in range(heads_here):
                for at in range(0, rows, step):
                    lo = h * rows + at
                    pos_c, begin_c = pos[at : at + step], begin[at : at + step]
                    masked = []
                    for side in range(2):
                        ok = (key_pos[side] <= pos_c) & (key_pos[side] >= begin_c)
                        masked.append(jnp.where(ok, s_scr[side, lo : lo + step, :keys], masked_value))
                    top = jnp.maximum(
                        jnp.max(masked[0], axis=1, keepdims=True), jnp.max(masked[1], axis=1, keepdims=True)
                    )
                    parts = [
                        jnp.exp(masked[side] - top) * m_scr[side, lo : lo + step, :keys] for side in range(2)
                    ]
                    total = jnp.sum(parts[0], axis=1, keepdims=True) + jnp.sum(parts[1], axis=1, keepdims=True)
                    inverse = 1.0 / total
                    for side in range(2):
                        prob_ref[i, side, lo : lo + step, :keys] = (parts[side] * inverse).astype(BF16)
            mixed = jnp.zeros((tall, width), F32)
            for side in range(2):
                value = sides[side][:, :, width:].reshape(wide, width)[:keys]
                mixed = mixed + mm(prob_ref[i, side, :, :keys], value, NN)
            result = fold_heads(mixed, rows, heads_here)
            out_ref[i] = result
            send_scr[i] = pack(result.astype(BF16)[:, :live])
        for k in range(count):
            msgs[k][...] = send_scr[z_index ^ k]

    live = heads_here * HEAD_DIM
    outs = (
        shape(F32, count, rows, width),
        shape(BF16, count, 2, tall, wide),
        shape(BF16, count, rows, width),
        shape(BF16, count, rows, 2 * width),
        shape(BF16, count, rows, 2 * width),
    ) + (shape(BF16, packed_rows(rows, live), 128),) * count
    scratch = (
        shape(F32, 2, tall, wide),
        shape(F32, 2, tall, wide),
        shape(BF16, 2, wide, 128),
        shape(BF16, count, packed_rows(rows, live), 128),
    )
    operands = (*queries, *kv_own, *kv_other)
    found = kernel(
        body, outs, (place, lengths), operands, scratch, micros=6.0, name="attend"
    )
    return found[0], found[1:5], list(found[5:])


def attend_back_call(place, queries, kv_own, kv_other, prob, attn, grads, heads_here):
    count, rows, width = queries.shape
    tall, wide = heads_here * rows, count * rows
    step = 16

    live = heads_here * HEAD_DIM

    def body(place_ref, q_ref, own_ref, oth_ref, prob_ref, attn_ref, *refs):
        grad_refs, (dq_ref, down_ref, doth_ref, p_scr, d_scr, acc, grad_ref) = refs[:count], refs[count:]
        sides = (own_ref, oth_ref)
        acc[...] = jnp.zeros_like(acc)
        grad_ref[...] = jnp.zeros_like(grad_ref)
        for k in range(count):
            grad_ref[place_ref[0] ^ k, :, :live] = unpack(grad_refs[k][...], rows, live)
        for i in range(count):
            keys = (i + 1) * rows
            grad = grad_ref[i]
            stacked_q = stack_heads(q_ref[i], heads_here)
            stacked_g = stack_heads(grad, heads_here)
            product = grad.astype(F32) * attn_ref[i]
            head_of = lane_head(width)
            delta = [
                jnp.sum(jnp.where(head_of == h, product, 0.0), axis=1, keepdims=True) for h in range(heads_here)
            ]
            for side in range(2):
                value = sides[side][:, :, width:].reshape(wide, width)[:keys]
                p_scr[side, :, :keys] = mm(stacked_g, value, NT)
            for h in range(heads_here):
                for at in range(0, rows, step):
                    lo = h * rows + at
                    for side in range(2):
                        weights = prob_ref[i, side, lo : lo + step, :keys].astype(F32)
                        shifted = p_scr[side, lo : lo + step, :keys] - delta[h][at : at + step]
                        d_scr[side, lo : lo + step, :keys] = (weights * shifted).astype(BF16)
            grad_q = jnp.zeros((tall, width), F32)
            for side in range(2):
                key = sides[side][:, :, :width].reshape(wide, width)[:keys]
                moved = d_scr[side, :, :keys]
                grad_q = grad_q + mm(moved, key, NN)
                acc[side, :keys, :width] += mm(moved, stacked_q, TN)
                acc[side, :keys, width:] += mm(prob_ref[i, side, :, :keys], stacked_g, TN)
            dq_ref[i] = (0.125 * fold_heads(grad_q, rows, heads_here)).astype(BF16)
        down_ref[...] = acc[0].reshape(count, rows, 2 * width)
        doth_ref[...] = acc[1].reshape(count, rows, 2 * width).astype(BF16)

    outs = (
        shape(BF16, count, rows, width),
        shape(F32, count, rows, 2 * width),
        shape(BF16, count, rows, 2 * width),
    )
    scratch = (
        shape(F32, 2, tall, wide),
        shape(BF16, 2, tall, wide),
        shape(F32, 2, wide, 2 * width),
        shape(BF16, count, rows, width),
    )
    operands = (queries, kv_own, kv_other, prob, attn, *grads)
    return kernel(body, outs, (place,), operands, scratch, micros=6.0, name="attend_back")


def join_call(place, grad_q, grad_kv, arrived, live):
    count, rows, width = grad_q.shape

    def body(place_ref, q_ref, kv_ref, in_ref, out_ref, *rest):
        msgs, scr = rest[:count], rest[count]
        for b in range(count):
            both = (kv_ref[b] + in_ref[b].astype(F32)).astype(BF16)
            out_ref[b, :, :width] = q_ref[b]
            out_ref[b, :, width:] = both
            dense = [q_ref[b][:, :live], both[:, :live], both[:, width : width + live]]
            scr[b] = pack(jnp.concatenate(dense, axis=1))
        for k in range(count):
            msgs[k][...] = scr[place_ref[0] ^ k]

    message = shape(BF16, packed_rows(rows, 3 * live), 128)
    outs = (shape(BF16, count, rows, 3 * width),) + (message,) * count
    scratch = (shape(BF16, count, *message.shape),)
    joined, *msgs = kernel(body, outs, (place,), (grad_q, grad_kv, arrived), scratch, micros=0.7, name="join_grads")
    return joined, msgs


def gather_heads(place_ref, pieces, scr, rows, live):
    for k, ref in enumerate(pieces):
        scr[place_ref[0] ^ k] = ref[...]
    return jnp.concatenate([unpack(scr[k], rows, live) for k in range(len(pieces))], axis=1)


def norms_call(place, pieces, layer_in, vectors, w_out, live):
    count, rows = len(pieces), layer_in.shape[0]
    model = w_out.shape[0]

    def body(place_ref, *refs):
        in_ref, g2, b2, g3, b3, wo_ref, mid_ref, attn_ref, n3_ref, piece_scr = refs[count:]
        attn = gather_heads(place_ref, refs[:count], piece_scr, rows, live)
        attn_ref[...] = attn
        unit2, _ = unit_norm(attn.astype(F32))
        normed2 = (unit2 * row(g2) + row(b2)).astype(BF16)
        middle = in_ref[...].astype(F32) + mm(normed2, wo_ref[...], NN)
        mid_ref[...] = middle
        unit3, _ = unit_norm(middle)
        n3_ref[...] = (unit3 * row(g3) + row(b3)).astype(BF16)

    outs = (shape(F32, rows, model), shape(BF16, rows, model), shape(BF16, rows, model))
    operands = (*pieces, layer_in, *vectors, w_out)
    scratch = (shape(BF16, count, *pieces[0].shape),)
    return kernel(body, outs, (place,), operands, scratch, micros=1.5, name="norms")


def up_call(place, normed3, w_up, parts):
    rows, (model, hidden) = normed3.shape[0], w_up.shape
    part = hidden // parts

    def body(place_ref, n3_ref, wu_ref, act_ref, slope_ref, *msgs):
        normed = n3_ref[...]
        for r in range(parts):
            upper = mm(normed, wu_ref[:, r * part : (r + 1) * part], NN)
            cumulative = 0.5 * (1.0 + lax.erf(upper * 0.7071067811865476))
            density = jnp.exp(-0.5 * upper * upper) * 0.3989422804014327
            act_ref[r] = (upper * cumulative).astype(BF16)
            slope_ref[r] = (cumulative + upper * density).astype(BF16)
        for k in range(parts):
            msgs[k][...] = act_ref[place_ref[2] ^ k]

    outs = (shape(BF16, parts, rows, part),) * 2 + (shape(BF16, rows, part),) * parts
    act, slope, *msgs = kernel(body, outs, (place,), (normed3, w_up), micros=2.0, name="up_gelu")
    return act, slope, msgs


def padded_quarter(quarter):
    return -(-(quarter + 64) // 128) * 128


def backward_call(place, attn, middle, act, slope, grad_out, vectors, w_out, w_up, w_down, parts, count, live):
    rows = attn.shape[0]
    model, hidden = w_up.shape
    part, quarter = hidden // parts, model // parts
    pad_q = padded_quarter(quarter)
    message = shape(BF16, packed_rows(rows, live), 128)

    def body(
        place_ref, attn_ref, mid_ref, act_ref, slope_ref, go_ref, g2, b2, g3, b3, wo_ref, wu_ref, wd_ref,
        out_ref, gmid_ref, *rest,
    ):
        msgs, heads = rest[:parts], rest[parts : parts + count]
        up_scr, n2_scr, head_scr = rest[parts + count :]
        here = place_ref[2]
        go = go_ref[...]
        middle = mid_ref[...]
        out = middle
        grad3 = jnp.zeros((rows, model), F32)
        for r in range(parts):
            w_d = wd_ref[r * part : (r + 1) * part, :]
            out = out + mm(act_ref[r], w_d, NN)
            grad_up = (mm(go, w_d, NT) * slope_ref[r].astype(F32)).astype(BF16)
            up_scr[r] = grad_up
            grad3 = grad3 + mm(grad_up, wu_ref[:, r * part : (r + 1) * part], NT)
        out_ref[...] = out.astype(BF16)
        unit3, scale3 = unit_norm(middle)
        grad_mid = go.astype(F32) + norm_back(grad3, row(g3), unit3, scale3)
        gmid_ref[...] = grad_mid
        proj = grad_mid.astype(BF16)
        grad2 = mm(proj, wo_ref[...], NT)
        unit2, scale2 = unit_norm(attn_ref[...].astype(F32))
        grad_attn = norm_back(grad2, row(g2), unit2, scale2).astype(BF16)
        for k in range(count):
            head_scr[k] = pack(grad_attn[:, k * live : (k + 1) * live])
        for k in range(count):
            heads[k][...] = head_scr[place_ref[0] ^ k]
        sums = [
            jnp.sum(grad2 * unit2, axis=0, keepdims=True),
            jnp.sum(grad2, axis=0, keepdims=True),
            jnp.sum(grad3 * unit3, axis=0, keepdims=True),
            jnp.sum(grad3, axis=0, keepdims=True),
        ]
        table = jnp.concatenate(sums + [jnp.zeros((4, model), F32)], axis=0)
        normed2 = (unit2 * row(g2) + row(b2)).astype(BF16)
        normed3 = (unit3 * row(g3) + row(b3)).astype(BF16)
        spare, lines = pad_q - quarter, quarter // 64
        for r in range(parts):
            chunks = [table[:, r * quarter + 64 * j : r * quarter + 64 * (j + 1)] for j in range(lines)]
            side = jnp.concatenate(chunks + [jnp.zeros((rows - 8 * lines, 64), F32)], axis=0).astype(BF16)
            pieces = [normed2[:, r * quarter : (r + 1) * quarter], side]
            if spare > 64:
                pieces.append(jnp.zeros((rows, spare - 64), BF16))
            n2_scr[r] = jnp.concatenate(pieces, axis=1)
        for k in range(parts):
            msgs[k][:, :part] = up_scr[here ^ k]
            msgs[k][:, part : part + model] = proj
            msgs[k][:, part + model : part + 2 * model] = normed3
            msgs[k][:, part + 2 * model :] = n2_scr[here ^ k]

    outs = (
        shape(BF16, rows, model),
        shape(F32, rows, model),
    )
    outs += (shape(BF16, rows, part + 2 * model + pad_q),) * parts + (message,) * count
    operands = (attn, middle, act, slope, grad_out, *vectors, w_out, w_up, w_down)
    scratch = (
        shape(BF16, parts, rows, part),
        shape(BF16, parts, rows, pad_q),
        shape(BF16, count, *message.shape),
    )
    found = kernel(body, outs, (place,), operands, scratch, micros=9.0, name="token_backward")
    found = list(found)
    return found[0], found[1], found[2 : 2 + parts], found[2 + parts :]


def down_grad_call(place, acts, grads, chips):
    parts = len(acts)
    part, model = acts[0].shape[1], grads[0].shape[1]
    own = part // (2 * chips)

    def body(place_ref, *refs):
        act_refs, grad_refs, (keep_ref, send_ref, scr) = refs[:parts], refs[parts : 2 * parts], refs[2 * parts :]
        core = place_ref[1]
        act = jnp.concatenate([ref[...] for ref in act_refs], axis=0)
        grad = jnp.concatenate([ref[...] for ref in grad_refs], axis=0)
        scr[...] = mm(act, grad, TN).reshape(chips, 2, own, model)
        for k in range(chips):
            keep_ref[k] = scr[k, core]
            send_ref[k] = scr[k, 1 - core].astype(BF16)

    outs = (shape(F32, chips, own, model), shape(BF16, chips, own, model))
    scratch = (shape(F32, chips, 2, own, model),)
    return kernel(body, outs, (place,), (*acts, *grads), scratch, micros=3.0, name="grad_down")


def up_grad_call(place, back, chips, part, model):
    parts = len(back)
    quarter = model // parts
    own = model // (parts * chips * 2)
    tall = (parts + 1) * own + 8

    def body(place_ref, *refs):
        back_refs = refs[:parts]
        keep_ref, send_ref, up_scr, out_scr, vec_scr = refs[parts:]
        core = place_ref[1]
        ends = (0, part, part + model, part + 2 * model, back_refs[0].shape[1])
        grad_up, proj, normed3, normed2 = (
            jnp.concatenate([ref[:, lo:hi] for ref in back_refs], axis=0) for lo, hi in zip(ends, ends[1:])
        )
        up_scr[...] = mm(normed3, grad_up, TN).reshape(parts, chips, 2, own, part)
        out_scr[...] = mm(normed2, proj, TN)[:quarter].reshape(chips, 2, own, model)
        lines = quarter // 64
        side = jnp.zeros((8 * lines, 64), F32)
        for ref in back_refs:
            side = side + ref[:, ends[3] + quarter : ends[3] + quarter + 64].astype(F32)[: 8 * lines]
        table = jnp.concatenate([side[8 * j : 8 * (j + 1)] for j in range(lines)], axis=1)
        vec_scr[...] = jnp.zeros_like(vec_scr)
        for k in range(chips):
            for side in range(2):
                at = (2 * k + side) * own
                vec_scr[k, side, :, :own] = table[:, at : at + own]
        for k in range(chips):
            for side, ref in ((core, keep_ref), (1 - core, send_ref)):
                pieces = [up_scr[r, k, side] for r in range(parts)] + [out_scr[k, side], vec_scr[k, side]]
                ref[k] = jnp.concatenate(pieces, axis=0).astype(ref.dtype)

    outs = (shape(F32, chips, tall, model), shape(BF16, chips, tall, model))
    scratch = (
        shape(F32, parts, chips, 2, own, part),
        shape(F32, chips, 2, own, model),
        shape(F32, chips, 2, 8, model),
    )
    return kernel(body, outs, (place,), tuple(back), scratch, micros=4.0, name="grad_up_out")


def qkv_grad_call(place, groups, units, grads, gain, bias, weight, parts, live, width):
    count, rows = grads.shape[:2]
    model = weight.shape[0]
    own = model // (parts * count * 2)
    n = len(units)

    def body(place_ref, *refs):
        unit_refs = refs[:n]
        grad_ref, gain_ref, bias_ref, weight_ref, keep_ref, send_ref, unit_scr, scr = refs[n:]
        z_index, core = place_ref[0], place_ref[1]
        for g, ks in enumerate(groups):
            for j, k in enumerate(ks):
                unit_scr[z_index ^ k] = unit_refs[g][j]
        grad = grad_ref[...].reshape(count * rows, 3 * width)
        cross = mm(unit_scr[...].reshape(count * rows, model), grad, TN)
        total = jnp.sum(grad.astype(F32), axis=0, keepdims=True)
        columns = jnp.concatenate([row(gain_ref), row(bias_ref), jnp.zeros((6, model), F32)], axis=0).T
        weight_f = weight_ref[...].astype(F32)
        grad_gain = jnp.sum(weight_f * cross, axis=1, keepdims=True)
        grad_bias = jnp.sum(weight_f * total, axis=1, keepdims=True)
        lane = lax.broadcasted_iota(jnp.int32, (1, 3 * width), 1)
        made = columns[:, 0:1] * cross + columns[:, 1:2] * total
        made = jnp.where(lane == live, grad_gain, jnp.where(lane == live + 1, grad_bias, made))
        scr[...] = made.reshape(parts, count, 2, own, 3 * width)
        for r in range(parts):
            keep_ref[r] = jnp.concatenate([scr[r, k, core] for k in range(count)], axis=0)
            send_ref[r] = jnp.concatenate([scr[r, k, 1 - core] for k in range(count)], axis=0).astype(BF16)

    outs = (shape(F32, parts, count * own, 3 * width), shape(BF16, parts, count * own, 3 * width))
    scratch = (shape(BF16, count, rows, model), shape(F32, parts, count, 2, own, 3 * width))
    operands = (*units, grads, gain, bias, weight)
    return kernel(body, outs, (place,), operands, scratch, micros=4.0, name="grad_qkv")


def spread_call(place, keep, arrived):
    parts = keep.shape[0]

    def body(place_ref, keep_ref, in_ref, *outs):
        for k in range(parts):
            at = place_ref[2] ^ k
            outs[k][...] = (keep_ref[at] + in_ref[at].astype(F32)).astype(BF16)

    return kernel(body, (shape(BF16, *keep.shape[1:]),) * parts, (place,), (keep, arrived), micros=0.8, name="spread")


def halve_call(place, keep, arrived, bit):
    half = keep.shape[0] // 2

    def body(place_ref, keep_ref, in_ref, stay_ref, away_ref):
        mine = (place_ref[0] // bit) % 2
        for j in range(half):
            here, there = 2 * j + mine, 2 * j + 1 - mine
            stay_ref[j] = keep_ref[here] + in_ref[here].astype(F32)
            away_ref[j] = (keep_ref[there] + in_ref[there].astype(F32)).astype(BF16)

    rest = keep.shape[1:]
    return kernel(body, (shape(F32, half, *rest), shape(BF16, half, *rest)), (place,), (keep, arrived), micros=0.8, name="halve")


def finish_down_call(keep, arrived):
    def body(keep_ref, in_ref, out_ref):
        out_ref[...] = keep_ref[0] + in_ref[0].astype(F32)

    return kernel(body, shape(F32, *keep.shape[1:]), (), (keep, arrived), micros=0.6, name="finish_down")


def finish_up_call(place, keep, arrived, parts, own, part):
    model = keep.shape[2]

    def body(place_ref, keep_ref, in_ref, out_ref, g2, b2, g3, b3, *rest):
        msgs, scr = rest[:parts], rest[parts]
        value = keep_ref[0] + in_ref[0].astype(F32)
        out_ref[...] = value[parts * own : (parts + 1) * own]
        for at, ref in enumerate((g2, b2, g3, b3)):
            line = (parts + 1) * own + at
            ref[...] = value[line : line + 1, :own].reshape(own)
        scr[...] = value[: parts * own].reshape(parts, own, part)
        for k in range(parts):
            msgs[k][...] = scr[place_ref[2] ^ k].astype(BF16)

    outs = (shape(F32, own, model),) + (shape(F32, own),) * 4 + (shape(BF16, own, part),) * parts
    scratch = (shape(F32, parts, own, part),)
    return kernel(body, outs, (place,), (keep, arrived), scratch, micros=0.8, name="finish_up")


def place_up_call(place, pieces):
    parts = len(pieces)
    own, part = pieces[0].shape

    def body(place_ref, *refs):
        for k in range(parts):
            at = pl.multiple_of((place_ref[2] ^ k) * part, 128)
            refs[parts][:, pl.ds(at, part)] = refs[k][...].astype(F32)

    return kernel(body, shape(F32, own, parts * part), (place,), tuple(pieces), micros=0.5, name="place_up")


def share_call(place, pieces, chips):
    own = pieces[0].shape[0] // chips

    def body(place_ref, *refs):
        ins, outs, scr = refs[: len(pieces)], refs[len(pieces) : -1], refs[-1]
        total = ins[0][...].astype(F32)
        for ref in ins[1:]:
            total = total + ref[...].astype(F32)
        scr[...] = total.reshape(chips, own, total.shape[1])
        for k in range(chips):
            outs[k][...] = scr[place_ref[0] ^ k].astype(BF16)

    lanes = pieces[0].shape[1]
    outs = (shape(BF16, own, lanes),) * chips
    return kernel(body, outs, (place,), tuple(pieces), (shape(F32, chips, own, lanes),), micros=0.7, name="share")


def finish_qkv_call(place, pieces, model, live, width):
    count, own = len(pieces), pieces[0].shape[0]

    def body(place_ref, *refs):
        q_ref, k_ref, v_ref, gain_ref, bias_ref, in_ref = refs[count:]
        for k in range(count):
            in_ref[place_ref[0] ^ k] = refs[k][...].astype(F32)
        for at, ref in enumerate((q_ref, k_ref, v_ref)):
            ref[...] = jnp.concatenate(
                [in_ref[k, :, at * width : at * width + live] for k in range(count)], axis=1
            )
        total = jnp.sum(in_ref[:, :, live : live + 2], axis=0).T
        gain_ref[...] = total[0:1].reshape(own)
        bias_ref[...] = total[1:2].reshape(own)

    outs = (shape(F32, own, model),) * 3 + (shape(F32, own),) * 2
    scratch = (shape(F32, count, *pieces[0].shape),)
    return kernel(body, outs, (place,), tuple(pieces), scratch, micros=0.8, name="finish_qkv")


def input_grad_call(place, pieces, layer_in, grad_mid, gain, w_query, w_key, w_value, live):
    count = len(pieces)
    rows, model = layer_in.shape

    def body(place_ref, *refs):
        in_ref, gmid_ref, gain_ref, wq_ref, wk_ref, wv_ref, out_ref, scr = refs[count:]
        for k in range(count):
            scr[place_ref[0] ^ k] = refs[k][...]
        blocks = [unpack(scr[k], rows, 3 * live) for k in range(count)]
        grad = jnp.zeros((rows, model), F32)
        for at, w_ref in enumerate((wq_ref, wk_ref, wv_ref)):
            part = jnp.concatenate([block[:, at * live : (at + 1) * live] for block in blocks], axis=1)
            grad = grad + mm(part, w_ref[...], NT)
        unit, scale = unit_norm(in_ref[...].astype(F32))
        out_ref[...] = (gmid_ref[...] + norm_back(grad, row(gain_ref), unit, scale)).astype(BF16)

    operands = (*pieces, layer_in, grad_mid, gain, w_query, w_key, w_value)
    scratch = (shape(BF16, count, *pieces[0].shape),)
    return kernel(body, shape(BF16, rows, model), (place,), operands, scratch, micros=3.0, name="grad_inputs")


def swap_core(value):
    return lax.ppermute(value, "core", [(0, 1), (1, 0)])


def swap(value, axis, bit):
    return lax.ppermute(value, axis, [(k, k ^ bit) for k in range(lax.axis_size(axis))])


def trade(messages, axis):
    found = {k: swap(messages[k], axis, k) for k in range(len(messages) - 1, 0, -1)}
    return [messages[0]] + [found[k] for k in range(1, len(messages))]


def gather_chips(block, chips):
    found = {0: block}
    bit = chips // 2
    while bit >= 1:
        for k in sorted(found):
            found[k | bit] = swap(found[k], "chip", bit)
        bit //= 2
    return [found[k] for k in range(chips)]


def scatter_chips(place, keep, arrived, chips, bit):
    while bit < chips:
        keep, away = halve_call(place, keep, arrived, bit)
        arrived = swap(away, "chip", bit)
        bit *= 2
    return keep, arrived


def after(values, *others):
    return lax.optimization_barrier((values, others))[0]


def fast_shards(
    inputs, doc_lengths, ln1_gain, ln1_bias, w_query, w_key, w_value, ln2_gain, ln2_bias, w_out,
    ln3_gain, ln3_bias, w_up, w_down, out_grad,
):
    rows, model = inputs.shape[1:]
    chips, parts = lax.axis_size("chip"), lax.axis_size("rows")
    z_index = lax.axis_index("chip")
    heads_here = HEADS // chips
    live = heads_here * HEAD_DIM
    width = -(-live // 128) * 128
    hidden = w_up.shape[1]
    part = hidden // parts
    own = model // (parts * chips * 2)
    place = jnp.stack([z_index, lax.axis_index("core"), lax.axis_index("rows")]).astype(jnp.int32)
    scope = jax.named_scope

    def columns(weight):
        mine = lax.dynamic_slice_in_dim(weight, z_index * live, live, 1)
        return jnp.pad(mine, ((0, 0), (0, width - live)))

    place, layer_in, out_grad = lax.optimization_barrier((place, inputs[0], out_grad[0]))
    with scope("gather_in"):
        blocks = gather_chips(layer_in, chips)
    grad_out = mask_call(place, doc_lengths, out_grad)
    w_heads = jnp.concatenate([columns(w_query), columns(w_key), columns(w_value)], axis=1)
    groups = [g for g in ([0], list(range(1, chips - 1)), [chips - 1]) if g] if chips > 1 else [[0]]
    made = [qkv_call([blocks[k] for k in g], ln1_gain, ln1_bias, w_heads, width) for g in groups]
    queries, kv_own, units = ([m[at] for m in made] for at in range(3))
    with scope("core_kv"):
        kv_other = [swap_core(v) for v in kv_own]
    attn_heads, (prob, queries, kv_own, kv_other), messages = attend_call(
        place, doc_lengths, groups, queries, kv_own, kv_other, heads_here
    )
    fence = lax.optimization_barrier
    with scope("chip_attn"):
        pieces = trade(messages, "chip")
    with scope("plane_out"):
        grads_plane = trade([grad_out] * parts, "rows")
    pieces = after(pieces, grads_plane)

    vectors = (ln2_gain, ln2_bias, ln3_gain, ln3_bias)
    middle, attn, normed3 = norms_call(place, pieces, layer_in, vectors, w_out, live)
    act, slope, acts = up_call(place, normed3, w_up, parts)
    with scope("plane_act"):
        acts = trade(acts, "rows")
    output, grad_mid, back, messages = backward_call(
        place, attn, middle, act, slope, grad_out, vectors, w_out, w_up, w_down, parts, chips, live
    )
    back = after(back, acts[1:])
    with scope("chip_grad"):
        grad_heads = trade(messages, "chip")
    with scope("plane_back"):
        far = [swap(back[k], "rows", k) for k in range(3, parts)]
    grad_q, grad_kv, grad_kv_other = attend_back_call(
        place, queries, kv_own, kv_other, prob, attn_heads, grad_heads, heads_here
    )
    with scope("core_grad"):
        grad_kv_other = swap_core(grad_kv_other)
    down_keep, down_send = down_grad_call(place, after(acts, grad_q), grads_plane, chips)
    grad_kv_other, down_send, far = fence((grad_kv_other, down_send, far))
    with scope("core_down"):
        down_recv = swap_core(down_send)
    with scope("plane_back"):
        near = after(back[1:3], far)
        back = back[:1] + [swap(near[k], "rows", k + 1) for k in range(len(near))] + far
    grad_qkv, messages = join_call(place, grad_q, grad_kv, grad_kv_other, live)
    with scope("down_sum"):
        down_keep, down_away = halve_call(place, down_keep, after(down_recv, grad_qkv), 1)
        grad_qkv, down_away = fence((grad_qkv, down_away))
        down_recv = swap(down_away, "chip", 1)
    with scope("chip_qkv"):
        grad_pieces = trade(messages, "chip")
    qkv_keep, qkv_send = qkv_grad_call(
        place, groups, units, grad_qkv, ln1_gain, ln1_bias, w_heads, parts, live, width
    )
    down_recv = after(down_recv, qkv_send)
    with scope("down_sum"):
        down_keep, down_last = scatter_chips(place, down_keep, down_recv, chips, 2)
    qkv_send = after(qkv_send, (down_keep, grad_pieces[2:3]))
    with scope("core_w"):
        qkv_send = swap_core(qkv_send)
    qkv_sums = spread_call(place, qkv_keep, qkv_send)
    back = after(back, (down_keep, grad_pieces[2:3]))
    up_keep, up_send = up_grad_call(place, back, chips, part, model)
    with scope("plane_w"):
        traded = trade(qkv_sums, "rows")
    up_send = after(up_send, (down_last, grad_pieces[1:2], qkv_sums))
    with scope("core_up"):
        up_recv = swap_core(up_send)
    up_keep, up_away = halve_call(place, up_keep, up_recv, 1)
    with scope("up_sum"):
        up_recv = swap(up_away, "chip", 1)
    traded = after(traded, up_away)
    with scope("chip_w"):
        shared = share_call(place, traded, chips)
        qkv_all = trade(shared, "chip")
    grad_inputs = input_grad_call(
        place, grad_pieces, layer_in, grad_mid, ln1_gain, w_query, w_key, w_value, live
    )
    gwd = finish_down_call(down_keep, down_last)
    up_recv = after(up_recv, (grad_pieces, shared, down_last))
    with scope("up_sum"):
        up_keep, up_last = scatter_chips(place, up_keep, up_recv, chips, 2)
    up_last = after(up_last, (qkv_all, gwd, grad_inputs))
    gwo, g2, b2, g3, b3, *up_rows = finish_up_call(place, up_keep, up_last, parts, own, part)
    with scope("plane_rows"):
        up_rows = trade(up_rows, "rows")
    gwq, gwk, gwv, g1, b1 = finish_qkv_call(place, qkv_all, model, live, width)
    gwu = place_up_call(place, up_rows)
    return (
        output[None], grad_inputs[None], g1, b1, gwq, gwk, gwv, g2, b2, gwo, g3, b3, gwu, gwd,
    )


def takes_fast(mesh):
    seq, parts = mesh.shape["seq"], mesh.shape["rows"]
    chips = seq // 2
    return seq % 2 == 0 and chips & (chips - 1) == 0 and parts in (1, 2, 4) and HEADS % max(chips, 1) == 0


def solution(mesh):
    if takes_fast(mesh):
        parts, seq = mesh.shape["rows"], mesh.shape["seq"]
        split = jax.sharding.Mesh(mesh.devices.reshape(parts, seq // 2, 2), ("rows", "chip", "core"))
        return mapped(fast_shards, split, ("chip", "core"))
    return mapped(shards, mesh, "seq")
```

```python
import math

import jax
import jax.numpy as jnp
from jax import lax
from jax.experimental import pallas as pl
from jax.experimental.pallas import tpu as pltpu
from jax.sharding import PartitionSpec as P

HEADS = 12
HEAD_DIM = 64


segment_pairs = ((2048, 1), (4096, 2), (8192, 4), (16384, 6))
masked_value = -1e30


def layer_norm(vector, gain_vec, bias_vec):
    row_mean = jnp.mean(vector, axis=-1, keepdims=True)
    centered = vector - row_mean
    row_var = jnp.mean(centered * centered, axis=-1, keepdims=True)
    return centered * lax.rsqrt(row_var + 1e-05) * gain_vec + bias_vec


def doc_of(positions, doc_ends):
    return jnp.sum((positions[:, None] >= doc_ends[None, :]).astype(jnp.int32), axis=1)


def pair_terms(query_pos, key_pos, query_doc, key_doc, head_count):
    head_ids = jnp.arange(head_count, dtype=jnp.int32)
    multiplicity = jnp.zeros((head_count, query_pos.shape[0], key_pos.shape[0]), jnp.float32)
    for seg_width, dilation in segment_pairs:
        same_seg = query_pos[:, None] // seg_width == key_pos[None, :] // seg_width
        query_pick = (query_pos % seg_width % dilation)[None, :] == (head_ids % dilation)[:, None]
        key_pick = (key_pos % seg_width % dilation)[None, :] == (head_ids % dilation)[:, None]
        joined = same_seg[None] & query_pick[:, :, None] & key_pick[:, None, :]
        multiplicity = multiplicity + joined.astype(jnp.float32)
    allowed = (key_pos[None, :] <= query_pos[:, None]) & (query_doc[:, None] == key_doc[None, :])
    allowed = allowed[None] & (multiplicity > 0.0)
    return (jnp.log(jnp.maximum(multiplicity, 1.0)), allowed)


def rows_inner(left, right):
    return lax.dot_general(
        left, right, (((0,), (0,)), ((), ())), preferred_element_type=jnp.float32
    )


def cols_inner(left, right):
    return lax.dot_general(
        left, right, (((1,), (1,)), ((), ())), preferred_element_type=jnp.float32
    )


def over_blocks(state, piece, step_fn):
    total_rows = piece[0].shape[0]
    block_rows = math.gcd(total_rows, 512)
    block_total = total_rows // block_rows
    split = tuple((part.reshape((block_total, block_rows) + part.shape[1:]) for part in piece))

    def inner(carried, block_item):
        return (step_fn(carried, block_item[1], block_item[0] * block_rows), None)

    result, unused = lax.scan(inner, state, (jnp.arange(block_total, dtype=jnp.int32), split))
    return result


def add_rows(buffer, start_pos, addend):
    current = lax.dynamic_slice_in_dim(buffer, start_pos, addend.shape[0], 0)
    return lax.dynamic_update_slice_in_dim(buffer, current + addend, start_pos, 0)


def shards(
    inputs,
    doc_lengths,
    ln1_gain,
    ln1_bias,
    w_query,
    w_key,
    w_value,
    ln2_gain,
    ln2_bias,
    w_out,
    ln3_gain,
    ln3_bias,
    w_up,
    w_down,
    out_grad,
):
    tok_rows = inputs.shape[1]
    head_count = HEADS
    head_size = HEAD_DIM
    model_width = inputs.shape[2]
    row_total = tok_rows * lax.axis_size("seq")
    layer_in = inputs[0].astype(jnp.float32)
    doc_ends = jnp.cumsum(doc_lengths[0])
    first_pos = lax.axis_index("seq") * tok_rows
    query_pos = first_pos + jnp.arange(tok_rows, dtype=jnp.int32)
    query_doc = doc_of(query_pos, doc_ends)
    valid = (query_doc < doc_lengths.shape[1]).astype(jnp.float32)
    first_norm, first_back = jax.vjp(layer_norm, layer_in, ln1_gain, ln1_bias)
    normed_one = first_norm.astype(jnp.bfloat16)
    queries = jnp.dot(normed_one, w_query, preferred_element_type=jnp.float32).astype(jnp.bfloat16)
    keys_local = jnp.dot(normed_one, w_key, preferred_element_type=jnp.float32).astype(jnp.bfloat16)
    values_local = jnp.dot(normed_one, w_value, preferred_element_type=jnp.float32).astype(
        jnp.bfloat16
    )
    query_heads = queries.reshape(tok_rows, head_count, head_size)

    def key_block_terms(key_start, key_count):
        key_pos = key_start + jnp.arange(key_count, dtype=jnp.int32)
        key_doc = doc_of(key_pos, doc_ends)
        return pair_terms(query_pos, key_pos, query_doc, key_doc, head_count)

    def with_pruning(step_fn):

        def wrapped(state, parts, start_pos):
            return step_fn(state, parts, start_pos)

        return wrapped

    def forward_step(state, parts, key_start):
        run_max, run_total, run_acc = state
        key_blk = parts[0].reshape(-1, head_count, head_size)
        value_blk = parts[1].reshape(-1, head_count, head_size)
        log_mult, allowed = key_block_terms(key_start, key_blk.shape[0])
        scores = 0.125 * jnp.einsum(
            "qhd,khd->hqk", query_heads, key_blk, preferred_element_type=jnp.float32
        )
        logits = jnp.where(allowed, scores + log_mult, masked_value)
        new_max = jnp.maximum(run_max, jnp.max(logits, axis=-1))
        weights = jnp.where(allowed, jnp.exp(logits - new_max[..., None]), 0.0)
        factor = jnp.exp(run_max - new_max)
        run_total = run_total * factor + jnp.sum(weights, axis=-1)
        run_acc = run_acc * factor[..., None] + jnp.einsum(
            "hqk,khd->hqd",
            weights.astype(jnp.bfloat16),
            value_blk,
            preferred_element_type=jnp.float32,
        )
        return (new_max, run_total, run_acc)

    forward_pruned = with_pruning(forward_step)
    start_state = (
        jnp.full((head_count, tok_rows), masked_value, jnp.float32),
        jnp.zeros((head_count, tok_rows), jnp.float32),
        jnp.zeros((head_count, tok_rows, head_size), jnp.float32),
    )
    final_state = over_blocks(
        start_state,
        (
            lax.all_gather(keys_local, "seq", axis=0, tiled=True),
            lax.all_gather(values_local, "seq", axis=0, tiled=True),
        ),
        forward_pruned,
    )
    run_max, run_total, run_acc = final_state
    row_lse = run_max + jnp.log(run_total)
    attn = (run_acc / run_total[..., None]).transpose(1, 0, 2).reshape(tok_rows, model_width)
    second_norm, second_back = jax.vjp(layer_norm, attn, ln2_gain, ln2_bias)
    normed_two = second_norm.astype(jnp.bfloat16)
    middle = layer_in + jnp.dot(normed_two, w_out, preferred_element_type=jnp.float32)
    third_norm, third_back = jax.vjp(layer_norm, middle, ln3_gain, ln3_bias)
    normed_three = third_norm.astype(jnp.bfloat16)
    upper = jnp.dot(normed_three, w_up, preferred_element_type=jnp.float32)
    activated_f, gelu_back = jax.vjp(
        lambda upper_in: jax.nn.gelu(upper_in, approximate=False), upper
    )
    activated = activated_f.astype(jnp.bfloat16)
    layer_out = middle + jnp.dot(activated, w_down, preferred_element_type=jnp.float32)
    grad_out = out_grad[0].astype(jnp.float32) * valid[:, None]
    grad_branch = grad_out.astype(jnp.bfloat16)
    grad_w_down = rows_inner(activated, grad_branch)
    grad_act = cols_inner(grad_branch, w_down)
    grad_upper = gelu_back(grad_act)[0].astype(jnp.bfloat16)
    grad_w_up = rows_inner(normed_three, grad_upper)
    grad_n3 = cols_inner(grad_upper, w_up)
    grad_mid_norm, grad_ln3_gain, grad_ln3_bias = third_back(grad_n3)
    grad_middle = grad_out + grad_mid_norm
    grad_proj = grad_middle.astype(jnp.bfloat16)
    grad_w_out = rows_inner(normed_two, grad_proj)
    grad_n2 = cols_inner(grad_proj, w_out)
    grad_attn_f, grad_ln2_gain, grad_ln2_bias = second_back(grad_n2)
    grad_attn = grad_attn_f.astype(jnp.bfloat16)
    grad_heads = grad_attn.reshape(tok_rows, head_count, head_size)
    row_delta = jnp.sum(
        (grad_attn.astype(jnp.float32) * attn).reshape(tok_rows, head_count, head_size), axis=-1
    )

    def backward_step(state, parts, key_start):
        grad_q_acc, grad_k_rows, grad_v_rows = state
        key_blk = parts[0].reshape(-1, head_count, head_size)
        value_blk = parts[1].reshape(-1, head_count, head_size)
        key_count = key_blk.shape[0]
        log_mult, allowed = key_block_terms(key_start, key_count)
        scores = 0.125 * jnp.einsum(
            "qhd,khd->hqk", query_heads, key_blk, preferred_element_type=jnp.float32
        )
        logits = jnp.where(allowed, scores + log_mult, masked_value)
        weights = jnp.where(allowed, jnp.exp(logits - row_lse[..., None]), 0.0)
        grad_weights = jnp.einsum(
            "qhd,khd->hqk", grad_heads, value_blk, preferred_element_type=jnp.float32
        )
        grad_scores = (weights * (grad_weights - row_delta.T[..., None])).astype(jnp.bfloat16)
        grad_q_acc = grad_q_acc + 0.125 * jnp.einsum(
            "hqk,khd->qhd", grad_scores, key_blk, preferred_element_type=jnp.float32
        )
        value_part = jnp.einsum(
            "hqk,qhd->khd",
            weights.astype(jnp.bfloat16),
            grad_heads,
            preferred_element_type=jnp.float32,
        ).reshape(key_count, model_width)
        key_part = 0.125 * jnp.einsum(
            "hqk,qhd->khd", grad_scores, query_heads, preferred_element_type=jnp.float32
        ).reshape(key_count, model_width)
        grad_k_rows = add_rows(grad_k_rows, key_start, key_part)
        grad_v_rows = add_rows(grad_v_rows, key_start, value_part)
        return (grad_q_acc, grad_k_rows, grad_v_rows)

    backward_pruned = with_pruning(backward_step)
    zero_state = (
        jnp.zeros((tok_rows, head_count, head_size), jnp.float32),
        jnp.zeros((row_total, model_width), jnp.float32),
        jnp.zeros((row_total, model_width), jnp.float32),
    )
    back_state = over_blocks(
        zero_state,
        (
            lax.all_gather(keys_local, "seq", axis=0, tiled=True),
            lax.all_gather(values_local, "seq", axis=0, tiled=True),
        ),
        backward_pruned,
    )
    grad_q_acc, grad_k_rows, grad_v_rows = back_state
    grad_k_acc, grad_v_acc = (
        lax.psum_scatter(
            grad_k_rows.astype(jnp.bfloat16), "seq", scatter_dimension=0, tiled=True
        ).astype(jnp.float32),
        lax.psum_scatter(
            grad_v_rows.astype(jnp.bfloat16), "seq", scatter_dimension=0, tiled=True
        ).astype(jnp.float32),
    )
    grad_queries = grad_q_acc.reshape(tok_rows, model_width).astype(jnp.bfloat16)
    grad_keys = grad_k_acc.astype(jnp.bfloat16)
    grad_values = grad_v_acc.astype(jnp.bfloat16)
    grad_w_query = rows_inner(normed_one, grad_queries)
    grad_w_key = rows_inner(normed_one, grad_keys)
    grad_w_value = rows_inner(normed_one, grad_values)
    grad_n1 = (
        cols_inner(grad_queries, w_query)
        + cols_inner(grad_keys, w_key)
        + cols_inner(grad_values, w_value)
    )
    grad_in_norm, grad_ln1_gain, grad_ln1_bias = first_back(grad_n1)
    grad_inputs = (grad_middle + grad_in_norm).astype(jnp.bfloat16)
    summed = (
        lax.psum_scatter(grad_ln1_gain, ("rows", "seq"), scatter_dimension=0, tiled=True),
        lax.psum_scatter(grad_ln1_bias, ("rows", "seq"), scatter_dimension=0, tiled=True),
        lax.psum_scatter(grad_w_query, ("rows", "seq"), scatter_dimension=0, tiled=True),
        lax.psum_scatter(grad_w_key, ("rows", "seq"), scatter_dimension=0, tiled=True),
        lax.psum_scatter(grad_w_value, ("rows", "seq"), scatter_dimension=0, tiled=True),
        lax.psum_scatter(grad_ln2_gain, ("rows", "seq"), scatter_dimension=0, tiled=True),
        lax.psum_scatter(grad_ln2_bias, ("rows", "seq"), scatter_dimension=0, tiled=True),
        lax.psum_scatter(grad_w_out, ("rows", "seq"), scatter_dimension=0, tiled=True),
        lax.psum_scatter(grad_ln3_gain, ("rows", "seq"), scatter_dimension=0, tiled=True),
        lax.psum_scatter(grad_ln3_bias, ("rows", "seq"), scatter_dimension=0, tiled=True),
        lax.psum_scatter(grad_w_up, ("rows", "seq"), scatter_dimension=0, tiled=True),
        lax.psum_scatter(grad_w_down, ("rows", "seq"), scatter_dimension=0, tiled=True),
    )
    return (
        layer_out.astype(jnp.bfloat16)[None],
        grad_inputs[None],
        summed[0],
        summed[1],
        summed[2],
        summed[3],
        summed[4],
        summed[5],
        summed[6],
        summed[7],
        summed[8],
        summed[9],
        summed[10],
        summed[11],
    )


def mapped(step, mesh, seq):
    spread = P(("rows",) + (seq if isinstance(seq, tuple) else (seq,)))
    tokens, plain = P("rows", seq, None), P()
    weights = P(spread[0], None)
    return jax.shard_map(
        step,
        mesh=mesh,
        in_specs=(tokens, P("rows", None)) + (plain,) * 12 + (tokens,),
        out_specs=(tokens, tokens, spread, spread, weights, weights, weights, spread, spread, weights)
        + (spread, spread, weights, weights),
        check_vma=False,
    )


F32 = jnp.float32
PACE = 1e6
BF16 = jnp.bfloat16
NT = (((1,), (1,)), ((), ()))
TN = (((0,), (0,)), ((), ()))
NN = (((1,), (0,)), ((), ()))


def mm(left, right, dims):
    return lax.dot_general(left, right, dims, preferred_element_type=F32)


def unit_norm(vector):
    centered = vector - jnp.mean(vector, axis=-1, keepdims=True)
    scale = lax.rsqrt(jnp.mean(centered * centered, axis=-1, keepdims=True) + 1e-05)
    return centered * scale, scale


def norm_back(grad, gain, unit, scale):
    weighted = grad * gain
    mean_w = jnp.mean(weighted, axis=-1, keepdims=True)
    mean_wu = jnp.mean(weighted * unit, axis=-1, keepdims=True)
    return scale * (weighted - mean_w - unit * mean_wu)


def shape(dtype, *dims):
    return jax.ShapeDtypeStruct(dims, dtype)


def row(ref):
    return ref[...].reshape(1, ref.shape[0])


def size_of(item):
    total = jnp.dtype(item.dtype).itemsize
    for dim in item.shape:
        total *= dim
    return total


def kernel(body, outs, scalars, operands, scratch=(), micros=2.0, name=None):
    single = not isinstance(outs, (tuple, list))
    listed = (outs,) if single else tuple(outs)
    vmem = pl.BlockSpec(memory_space=pltpu.VMEM)
    smem = pl.BlockSpec(memory_space=pltpu.SMEM)
    moved = sum(size_of(v) for v in (*operands, *listed))
    held = sum(size_of(v) for v in scratch)
    return pl.pallas_call(
        body,
        out_shape=outs if single else listed,
        in_specs=[smem] * len(scalars) + [vmem] * len(operands),
        out_specs=vmem if single else (vmem,) * len(listed),
        scratch_shapes=[pltpu.VMEM(v.shape, v.dtype) for v in scratch],
        compiler_params=pltpu.CompilerParams(vmem_limit_bytes=min(60 << 20, (moved + held) * 5 // 4 + (6 << 20))),
        cost_estimate=pl.CostEstimate(flops=int(micros * PACE), bytes_accessed=int(micros * PACE / 1e3), transcendentals=0),
        name=name,
    )(*scalars, *operands)


def packed_rows(rows, live):
    return rows * live // 128


def pack(block):
    rows, live = block.shape
    whole = live // 128
    pieces = [block[:, 128 * j : 128 * (j + 1)] for j in range(whole)]
    if live % 128:
        rest = block[:, 128 * whole :]
        pieces.append(jnp.concatenate([rest[: rows // 2], rest[rows // 2 :]], axis=1))
    return jnp.concatenate(pieces, axis=0)


def unpack(block, rows, live):
    whole = live // 128
    pieces = [block[rows * j : rows * (j + 1)] for j in range(whole)]
    if live % 128:
        rest = block[rows * whole :]
        pieces.append(jnp.concatenate([rest[:, :64], rest[:, 64:]], axis=0))
    return jnp.concatenate(pieces, axis=1)


def mask_call(place, lengths, out_grad):
    rows, model = out_grad.shape

    def body(place_ref, len_ref, in_ref, out_ref):
        last = jnp.int32(0)
        for d in range(lengths.shape[1]):
            last = last + len_ref[0, d]
        pos = lax.broadcasted_iota(jnp.int32, (rows, 1), 0) + (2 * place_ref[0] + place_ref[1]) * rows
        out_ref[...] = jnp.where(pos < last, in_ref[...].astype(F32), 0.0).astype(BF16)

    return kernel(body, shape(BF16, rows, model), (place, lengths), (out_grad,), micros=0.7, name="mask_grad")


def qkv_call(blocks, gain, bias, weight, width):
    count = len(blocks)
    rows, model = blocks[0].shape

    def body(*refs):
        xs, (gain_ref, bias_ref, weight_ref, q_ref, kv_ref, unit_ref) = refs[:count], refs[count:]
        for k in range(count):
            unit, _ = unit_norm(xs[k][...].astype(F32))
            normed = (unit * row(gain_ref) + row(bias_ref)).astype(BF16)
            made = mm(normed, weight_ref[...], NN)
            q_ref[k] = (made[:, :width].astype(BF16).astype(F32) * 0.125).astype(BF16)
            kv_ref[k] = made[:, width:].astype(BF16)
            unit_ref[k] = unit.astype(BF16)

    outs = (
        shape(BF16, count, rows, width),
        shape(BF16, count, rows, 2 * width),
        shape(BF16, count, rows, model),
    )
    return kernel(body, outs, (), (*blocks, gain, bias, weight), micros=1.2 * count, name="qkv_heads")


def lane_head(lanes):
    return lax.broadcasted_iota(jnp.int32, (1, lanes), 1) // HEAD_DIM


def residue(pos_f, modulus):
    return pos_f - modulus * jnp.floor((pos_f + 0.5) * (1.0 / modulus))


def stack_heads(block, heads_here):
    head_of = lane_head(block.shape[1])
    return jnp.concatenate(
        [jnp.where(head_of == h, block, jnp.zeros_like(block)) for h in range(heads_here)], axis=0
    )


def fold_heads(stacked, rows, heads_here):
    head_of = lane_head(stacked.shape[1])
    total = jnp.zeros((rows, stacked.shape[1]), stacked.dtype)
    for h in range(heads_here):
        total = jnp.where(head_of == h, stacked[h * rows : (h + 1) * rows], total)
    return total


def attend_call(place, lengths, groups, queries, kv_own, kv_other, heads_here):
    count = sum(len(g) for g in groups)
    rows, width = queries[0].shape[1:]
    tall, wide = heads_here * rows, count * rows
    docs = lengths.shape[1]
    step = 16
    n = len(groups)

    def body(place_ref, len_ref, *refs):
        q_in, own_in, oth_in = refs[:n], refs[n : 2 * n], refs[2 * n : 3 * n]
        out_ref, prob_ref, q_ref, own_ref, oth_ref = refs[3 * n : 3 * n + 5]
        msgs, (s_scr, m_scr, hot_scr, send_scr) = refs[3 * n + 5 : 3 * n + 5 + count], refs[3 * n + 5 + count :]
        z_index, core = place_ref[0], place_ref[1]
        for g, ks in enumerate(groups):
            for j, k in enumerate(ks):
                q_ref[z_index ^ k] = q_in[g][j]
                own_ref[z_index ^ k] = own_in[g][j]
                oth_ref[z_index ^ k] = oth_in[g][j]
        sides = (own_ref, oth_ref)
        cores = (core, 1 - core)
        lane = lax.broadcasted_iota(jnp.int32, (rows, 128), 1).astype(F32)
        for side in range(2):
            for b in range(count):
                pos = lax.broadcasted_iota(jnp.int32, (rows, 1), 0) + (2 * b + cores[side]) * rows
                hot = (residue(pos.astype(F32), 12.0) == lane).astype(F32)
                hot_scr[side, b * rows : (b + 1) * rows, :] = hot.astype(BF16)
        for i in range(count):
            keys = (i + 1) * rows
            pos = lax.broadcasted_iota(jnp.int32, (rows, 1), 0) + (2 * i + core) * rows
            pos_f = pos.astype(F32)
            begin = jnp.zeros_like(pos)
            run = jnp.int32(0)
            for d in range(docs):
                run = run + len_ref[0, d]
                begin = jnp.where(pos >= run, run, begin)
            tables = []
            for h in range(heads_here):
                head = (z_index * heads_here + h).astype(F32)
                table = jnp.ones((rows, 128), F32)
                for r in (2.0, 4.0, 6.0):
                    mine = residue(head, r)
                    pick_q = (residue(pos_f, r) == mine).astype(F32)
                    pick_k = (residue(lane, r) == mine).astype(F32)
                    table = table + pick_q * pick_k
                tables.append(jnp.where(lane < 12.0, table, 0.0))
            table = jnp.concatenate(tables, axis=0).astype(BF16)
            stacked = stack_heads(q_ref[i], heads_here)
            for side in range(2):
                key = sides[side][:, :, :width].reshape(wide, width)[:keys]
                s_scr[side, :, :keys] = mm(stacked, key, NT)
                m_scr[side, :, :keys] = mm(table, hot_scr[side, :keys], NT)
            key_pos = [
                jnp.concatenate(
                    [
                        lax.broadcasted_iota(jnp.int32, (1, rows), 1) + (2 * b + cores[side]) * rows
                        for b in range(i + 1)
                    ],
                    axis=1,
                )
                for side in range(2)
            ]
            for h in range(heads_here):
                for at in range(0, rows, step):
                    lo = h * rows + at
                    pos_c, begin_c = pos[at : at + step], begin[at : at + step]
                    masked = []
                    for side in range(2):
                        ok = (key_pos[side] <= pos_c) & (key_pos[side] >= begin_c)
                        masked.append(jnp.where(ok, s_scr[side, lo : lo + step, :keys], masked_value))
                    top = jnp.maximum(
                        jnp.max(masked[0], axis=1, keepdims=True), jnp.max(masked[1], axis=1, keepdims=True)
                    )
                    parts = [
                        jnp.exp(masked[side] - top) * m_scr[side, lo : lo + step, :keys] for side in range(2)
                    ]
                    total = jnp.sum(parts[0], axis=1, keepdims=True) + jnp.sum(parts[1], axis=1, keepdims=True)
                    inverse = 1.0 / total
                    for side in range(2):
                        prob_ref[i, side, lo : lo + step, :keys] = (parts[side] * inverse).astype(BF16)
            mixed = jnp.zeros((tall, width), F32)
            for side in range(2):
                value = sides[side][:, :, width:].reshape(wide, width)[:keys]
                mixed = mixed + mm(prob_ref[i, side, :, :keys], value, NN)
            result = fold_heads(mixed, rows, heads_here)
            out_ref[i] = result
            send_scr[i] = pack(result.astype(BF16)[:, :live])
        for k in range(count):
            msgs[k][...] = send_scr[z_index ^ k]

    live = heads_here * HEAD_DIM
    outs = (
        shape(F32, count, rows, width),
        shape(BF16, count, 2, tall, wide),
        shape(BF16, count, rows, width),
        shape(BF16, count, rows, 2 * width),
        shape(BF16, count, rows, 2 * width),
    ) + (shape(BF16, packed_rows(rows, live), 128),) * count
    scratch = (
        shape(F32, 2, tall, wide),
        shape(F32, 2, tall, wide),
        shape(BF16, 2, wide, 128),
        shape(BF16, count, packed_rows(rows, live), 128),
    )
    operands = (*queries, *kv_own, *kv_other)
    found = kernel(
        body, outs, (place, lengths), operands, scratch, micros=6.0, name="attend"
    )
    return found[0], found[1:5], list(found[5:])


def attend_back_call(place, queries, kv_own, kv_other, prob, attn, grads, heads_here):
    count, rows, width = queries.shape
    tall, wide = heads_here * rows, count * rows
    step = 16

    live = heads_here * HEAD_DIM

    def body(place_ref, q_ref, own_ref, oth_ref, prob_ref, attn_ref, *refs):
        grad_refs, (dq_ref, down_ref, doth_ref, p_scr, d_scr, acc, grad_ref) = refs[:count], refs[count:]
        sides = (own_ref, oth_ref)
        acc[...] = jnp.zeros_like(acc)
        grad_ref[...] = jnp.zeros_like(grad_ref)
        for k in range(count):
            grad_ref[place_ref[0] ^ k, :, :live] = unpack(grad_refs[k][...], rows, live)
        for i in range(count):
            keys = (i + 1) * rows
            grad = grad_ref[i]
            stacked_q = stack_heads(q_ref[i], heads_here)
            stacked_g = stack_heads(grad, heads_here)
            product = grad.astype(F32) * attn_ref[i]
            head_of = lane_head(width)
            delta = [
                jnp.sum(jnp.where(head_of == h, product, 0.0), axis=1, keepdims=True) for h in range(heads_here)
            ]
            for side in range(2):
                value = sides[side][:, :, width:].reshape(wide, width)[:keys]
                p_scr[side, :, :keys] = mm(stacked_g, value, NT)
            for h in range(heads_here):
                for at in range(0, rows, step):
                    lo = h * rows + at
                    for side in range(2):
                        weights = prob_ref[i, side, lo : lo + step, :keys].astype(F32)
                        shifted = p_scr[side, lo : lo + step, :keys] - delta[h][at : at + step]
                        d_scr[side, lo : lo + step, :keys] = (weights * shifted).astype(BF16)
            grad_q = jnp.zeros((tall, width), F32)
            for side in range(2):
                key = sides[side][:, :, :width].reshape(wide, width)[:keys]
                moved = d_scr[side, :, :keys]
                grad_q = grad_q + mm(moved, key, NN)
                acc[side, :keys, :width] += mm(moved, stacked_q, TN)
                acc[side, :keys, width:] += mm(prob_ref[i, side, :, :keys], stacked_g, TN)
            dq_ref[i] = (0.125 * fold_heads(grad_q, rows, heads_here)).astype(BF16)
        down_ref[...] = acc[0].reshape(count, rows, 2 * width)
        doth_ref[...] = acc[1].reshape(count, rows, 2 * width).astype(BF16)

    outs = (
        shape(BF16, count, rows, width),
        shape(F32, count, rows, 2 * width),
        shape(BF16, count, rows, 2 * width),
    )
    scratch = (
        shape(F32, 2, tall, wide),
        shape(BF16, 2, tall, wide),
        shape(F32, 2, wide, 2 * width),
        shape(BF16, count, rows, width),
    )
    operands = (queries, kv_own, kv_other, prob, attn, *grads)
    return kernel(body, outs, (place,), operands, scratch, micros=6.0, name="attend_back")


def join_call(place, grad_q, grad_kv, arrived, live):
    count, rows, width = grad_q.shape

    def body(place_ref, q_ref, kv_ref, in_ref, out_ref, *rest):
        msgs, scr = rest[:count], rest[count]
        for b in range(count):
            both = (kv_ref[b] + in_ref[b].astype(F32)).astype(BF16)
            out_ref[b, :, :width] = q_ref[b]
            out_ref[b, :, width:] = both
            dense = [q_ref[b][:, :live], both[:, :live], both[:, width : width + live]]
            scr[b] = pack(jnp.concatenate(dense, axis=1))
        for k in range(count):
            msgs[k][...] = scr[place_ref[0] ^ k]

    message = shape(BF16, packed_rows(rows, 3 * live), 128)
    outs = (shape(BF16, count, rows, 3 * width),) + (message,) * count
    scratch = (shape(BF16, count, *message.shape),)
    joined, *msgs = kernel(body, outs, (place,), (grad_q, grad_kv, arrived), scratch, micros=0.7, name="join_grads")
    return joined, msgs


def gather_heads(place_ref, pieces, scr, rows, live):
    for k, ref in enumerate(pieces):
        scr[place_ref[0] ^ k] = ref[...]
    return jnp.concatenate([unpack(scr[k], rows, live) for k in range(len(pieces))], axis=1)


def norms_call(place, pieces, layer_in, vectors, w_out, live):
    count, rows = len(pieces), layer_in.shape[0]
    model = w_out.shape[0]

    def body(place_ref, *refs):
        in_ref, g2, b2, g3, b3, wo_ref, mid_ref, attn_ref, n3_ref, piece_scr = refs[count:]
        attn = gather_heads(place_ref, refs[:count], piece_scr, rows, live)
        attn_ref[...] = attn
        unit2, _ = unit_norm(attn.astype(F32))
        normed2 = (unit2 * row(g2) + row(b2)).astype(BF16)
        middle = in_ref[...].astype(F32) + mm(normed2, wo_ref[...], NN)
        mid_ref[...] = middle
        unit3, _ = unit_norm(middle)
        n3_ref[...] = (unit3 * row(g3) + row(b3)).astype(BF16)

    outs = (shape(F32, rows, model), shape(BF16, rows, model), shape(BF16, rows, model))
    operands = (*pieces, layer_in, *vectors, w_out)
    scratch = (shape(BF16, count, *pieces[0].shape),)
    return kernel(body, outs, (place,), operands, scratch, micros=1.5, name="norms")


def up_call(place, normed3, w_up, parts):
    rows, (model, hidden) = normed3.shape[0], w_up.shape
    part = hidden // parts

    def body(place_ref, n3_ref, wu_ref, act_ref, slope_ref, *msgs):
        normed = n3_ref[...]
        for r in range(parts):
            upper = mm(normed, wu_ref[:, r * part : (r + 1) * part], NN)
            cumulative = 0.5 * (1.0 + lax.erf(upper * 0.7071067811865476))
            density = jnp.exp(-0.5 * upper * upper) * 0.3989422804014327
            act_ref[r] = (upper * cumulative).astype(BF16)
            slope_ref[r] = (cumulative + upper * density).astype(BF16)
        for k in range(parts):
            msgs[k][...] = act_ref[place_ref[2] ^ k]

    outs = (shape(BF16, parts, rows, part),) * 2 + (shape(BF16, rows, part),) * parts
    act, slope, *msgs = kernel(body, outs, (place,), (normed3, w_up), micros=2.0, name="up_gelu")
    return act, slope, msgs


def padded_quarter(quarter):
    return -(-(quarter + 64) // 128) * 128


def backward_call(place, attn, middle, act, slope, grad_out, vectors, w_out, w_up, w_down, parts, count, live):
    rows = attn.shape[0]
    model, hidden = w_up.shape
    part, quarter = hidden // parts, model // parts
    pad_q = padded_quarter(quarter)
    message = shape(BF16, packed_rows(rows, live), 128)

    def body(
        place_ref, attn_ref, mid_ref, act_ref, slope_ref, go_ref, g2, b2, g3, b3, wo_ref, wu_ref, wd_ref,
        out_ref, gmid_ref, *rest,
    ):
        msgs, heads = rest[:parts], rest[parts : parts + count]
        up_scr, n2_scr, head_scr = rest[parts + count :]
        here = place_ref[2]
        go = go_ref[...]
        middle = mid_ref[...]
        out = middle
        grad3 = jnp.zeros((rows, model), F32)
        for r in range(parts):
            w_d = wd_ref[r * part : (r + 1) * part, :]
            out = out + mm(act_ref[r], w_d, NN)
            grad_up = (mm(go, w_d, NT) * slope_ref[r].astype(F32)).astype(BF16)
            up_scr[r] = grad_up
            grad3 = grad3 + mm(grad_up, wu_ref[:, r * part : (r + 1) * part], NT)
        out_ref[...] = out.astype(BF16)
        unit3, scale3 = unit_norm(middle)
        grad_mid = go.astype(F32) + norm_back(grad3, row(g3), unit3, scale3)
        gmid_ref[...] = grad_mid
        proj = grad_mid.astype(BF16)
        grad2 = mm(proj, wo_ref[...], NT)
        unit2, scale2 = unit_norm(attn_ref[...].astype(F32))
        grad_attn = norm_back(grad2, row(g2), unit2, scale2).astype(BF16)
        for k in range(count):
            head_scr[k] = pack(grad_attn[:, k * live : (k + 1) * live])
        for k in range(count):
            heads[k][...] = head_scr[place_ref[0] ^ k]
        sums = [
            jnp.sum(grad2 * unit2, axis=0, keepdims=True),
            jnp.sum(grad2, axis=0, keepdims=True),
            jnp.sum(grad3 * unit3, axis=0, keepdims=True),
            jnp.sum(grad3, axis=0, keepdims=True),
        ]
        table = jnp.concatenate(sums + [jnp.zeros((4, model), F32)], axis=0)
        normed2 = (unit2 * row(g2) + row(b2)).astype(BF16)
        normed3 = (unit3 * row(g3) + row(b3)).astype(BF16)
        spare, lines = pad_q - quarter, quarter // 64
        for r in range(parts):
            chunks = [table[:, r * quarter + 64 * j : r * quarter + 64 * (j + 1)] for j in range(lines)]
            side = jnp.concatenate(chunks + [jnp.zeros((rows - 8 * lines, 64), F32)], axis=0).astype(BF16)
            pieces = [normed2[:, r * quarter : (r + 1) * quarter], side]
            if spare > 64:
                pieces.append(jnp.zeros((rows, spare - 64), BF16))
            n2_scr[r] = jnp.concatenate(pieces, axis=1)
        for k in range(parts):
            msgs[k][:, :part] = up_scr[here ^ k]
            msgs[k][:, part : part + model] = proj
            msgs[k][:, part + model : part + 2 * model] = normed3
            msgs[k][:, part + 2 * model :] = n2_scr[here ^ k]

    outs = (
        shape(BF16, rows, model),
        shape(F32, rows, model),
    )
    outs += (shape(BF16, rows, part + 2 * model + pad_q),) * parts + (message,) * count
    operands = (attn, middle, act, slope, grad_out, *vectors, w_out, w_up, w_down)
    scratch = (
        shape(BF16, parts, rows, part),
        shape(BF16, parts, rows, pad_q),
        shape(BF16, count, *message.shape),
    )
    found = kernel(body, outs, (place,), operands, scratch, micros=9.0, name="token_backward")
    found = list(found)
    return found[0], found[1], found[2 : 2 + parts], found[2 + parts :]


def down_grad_call(place, acts, grads, chips):
    parts = len(acts)
    part, model = acts[0].shape[1], grads[0].shape[1]
    own = part // (2 * chips)

    def body(place_ref, *refs):
        act_refs, grad_refs, (keep_ref, send_ref, scr) = refs[:parts], refs[parts : 2 * parts], refs[2 * parts :]
        core = place_ref[1]
        act = jnp.concatenate([ref[...] for ref in act_refs], axis=0)
        grad = jnp.concatenate([ref[...] for ref in grad_refs], axis=0)
        scr[...] = mm(act, grad, TN).reshape(chips, 2, own, model)
        for k in range(chips):
            keep_ref[k] = scr[k, core]
            send_ref[k] = scr[k, 1 - core].astype(BF16)

    outs = (shape(F32, chips, own, model), shape(BF16, chips, own, model))
    scratch = (shape(F32, chips, 2, own, model),)
    return kernel(body, outs, (place,), (*acts, *grads), scratch, micros=3.0, name="grad_down")


def up_grad_call(place, back, chips, part, model):
    parts = len(back)
    quarter = model // parts
    own = model // (parts * chips * 2)
    tall = (parts + 1) * own + 8

    def body(place_ref, *refs):
        back_refs = refs[:parts]
        keep_ref, send_ref, up_scr, out_scr, vec_scr = refs[parts:]
        core = place_ref[1]
        ends = (0, part, part + model, part + 2 * model, back_refs[0].shape[1])
        grad_up, proj, normed3, normed2 = (
            jnp.concatenate([ref[:, lo:hi] for ref in back_refs], axis=0) for lo, hi in zip(ends, ends[1:])
        )
        up_scr[...] = mm(normed3, grad_up, TN).reshape(parts, chips, 2, own, part)
        out_scr[...] = mm(normed2, proj, TN)[:quarter].reshape(chips, 2, own, model)
        lines = quarter // 64
        side = jnp.zeros((8 * lines, 64), F32)
        for ref in back_refs:
            side = side + ref[:, ends[3] + quarter : ends[3] + quarter + 64].astype(F32)[: 8 * lines]
        table = jnp.concatenate([side[8 * j : 8 * (j + 1)] for j in range(lines)], axis=1)
        vec_scr[...] = jnp.zeros_like(vec_scr)
        for k in range(chips):
            for side in range(2):
                at = (2 * k + side) * own
                vec_scr[k, side, :, :own] = table[:, at : at + own]
        for k in range(chips):
            for side, ref in ((core, keep_ref), (1 - core, send_ref)):
                pieces = [up_scr[r, k, side] for r in range(parts)] + [out_scr[k, side], vec_scr[k, side]]
                ref[k] = jnp.concatenate(pieces, axis=0).astype(ref.dtype)

    outs = (shape(F32, chips, tall, model), shape(BF16, chips, tall, model))
    scratch = (
        shape(F32, parts, chips, 2, own, part),
        shape(F32, chips, 2, own, model),
        shape(F32, chips, 2, 8, model),
    )
    return kernel(body, outs, (place,), tuple(back), scratch, micros=4.0, name="grad_up_out")


def qkv_grad_call(place, groups, units, grads, gain, bias, weight, parts, live, width):
    count, rows = grads.shape[:2]
    model = weight.shape[0]
    own = model // (parts * count * 2)
    n = len(units)

    def body(place_ref, *refs):
        unit_refs = refs[:n]
        grad_ref, gain_ref, bias_ref, weight_ref, keep_ref, send_ref, unit_scr, scr = refs[n:]
        z_index, core = place_ref[0], place_ref[1]
        for g, ks in enumerate(groups):
            for j, k in enumerate(ks):
                unit_scr[z_index ^ k] = unit_refs[g][j]
        grad = grad_ref[...].reshape(count * rows, 3 * width)
        cross = mm(unit_scr[...].reshape(count * rows, model), grad, TN)
        total = jnp.sum(grad.astype(F32), axis=0, keepdims=True)
        columns = jnp.concatenate([row(gain_ref), row(bias_ref), jnp.zeros((6, model), F32)], axis=0).T
        weight_f = weight_ref[...].astype(F32)
        grad_gain = jnp.sum(weight_f * cross, axis=1, keepdims=True)
        grad_bias = jnp.sum(weight_f * total, axis=1, keepdims=True)
        lane = lax.broadcasted_iota(jnp.int32, (1, 3 * width), 1)
        made = columns[:, 0:1] * cross + columns[:, 1:2] * total
        made = jnp.where(lane == live, grad_gain, jnp.where(lane == live + 1, grad_bias, made))
        scr[...] = made.reshape(parts, count, 2, own, 3 * width)
        for r in range(parts):
            keep_ref[r] = jnp.concatenate([scr[r, k, core] for k in range(count)], axis=0)
            send_ref[r] = jnp.concatenate([scr[r, k, 1 - core] for k in range(count)], axis=0).astype(BF16)

    outs = (shape(F32, parts, count * own, 3 * width), shape(BF16, parts, count * own, 3 * width))
    scratch = (shape(BF16, count, rows, model), shape(F32, parts, count, 2, own, 3 * width))
    operands = (*units, grads, gain, bias, weight)
    return kernel(body, outs, (place,), operands, scratch, micros=4.0, name="grad_qkv")


def spread_call(place, keep, arrived):
    parts = keep.shape[0]

    def body(place_ref, keep_ref, in_ref, *outs):
        for k in range(parts):
            at = place_ref[2] ^ k
            outs[k][...] = (keep_ref[at] + in_ref[at].astype(F32)).astype(BF16)

    return kernel(body, (shape(BF16, *keep.shape[1:]),) * parts, (place,), (keep, arrived), micros=0.8, name="spread")


def halve_call(place, keep, arrived, bit):
    half = keep.shape[0] // 2

    def body(place_ref, keep_ref, in_ref, stay_ref, away_ref):
        mine = (place_ref[0] // bit) % 2
        for j in range(half):
            here, there = 2 * j + mine, 2 * j + 1 - mine
            stay_ref[j] = keep_ref[here] + in_ref[here].astype(F32)
            away_ref[j] = (keep_ref[there] + in_ref[there].astype(F32)).astype(BF16)

    rest = keep.shape[1:]
    return kernel(body, (shape(F32, half, *rest), shape(BF16, half, *rest)), (place,), (keep, arrived), micros=0.8, name="halve")


def finish_down_call(keep, arrived):
    def body(keep_ref, in_ref, out_ref):
        out_ref[...] = keep_ref[0] + in_ref[0].astype(F32)

    return kernel(body, shape(F32, *keep.shape[1:]), (), (keep, arrived), micros=0.6, name="finish_down")


def finish_up_call(place, keep, arrived, parts, own, part):
    model = keep.shape[2]

    def body(place_ref, keep_ref, in_ref, out_ref, g2, b2, g3, b3, *rest):
        msgs, scr = rest[:parts], rest[parts]
        value = keep_ref[0] + in_ref[0].astype(F32)
        out_ref[...] = value[parts * own : (parts + 1) * own]
        for at, ref in enumerate((g2, b2, g3, b3)):
            line = (parts + 1) * own + at
            ref[...] = value[line : line + 1, :own].reshape(own)
        scr[...] = value[: parts * own].reshape(parts, own, part)
        for k in range(parts):
            msgs[k][...] = scr[place_ref[2] ^ k].astype(BF16)

    outs = (shape(F32, own, model),) + (shape(F32, own),) * 4 + (shape(BF16, own, part),) * parts
    scratch = (shape(F32, parts, own, part),)
    return kernel(body, outs, (place,), (keep, arrived), scratch, micros=0.8, name="finish_up")


def place_up_call(place, pieces):
    parts = len(pieces)
    own, part = pieces[0].shape

    def body(place_ref, *refs):
        for k in range(parts):
            at = pl.multiple_of((place_ref[2] ^ k) * part, 128)
            refs[parts][:, pl.ds(at, part)] = refs[k][...].astype(F32)

    return kernel(body, shape(F32, own, parts * part), (place,), tuple(pieces), micros=0.5, name="place_up")


def share_call(place, pieces, chips):
    own = pieces[0].shape[0] // chips

    def body(place_ref, *refs):
        ins, outs, scr = refs[: len(pieces)], refs[len(pieces) : -1], refs[-1]
        total = ins[0][...].astype(F32)
        for ref in ins[1:]:
            total = total + ref[...].astype(F32)
        scr[...] = total.reshape(chips, own, total.shape[1])
        for k in range(chips):
            outs[k][...] = scr[place_ref[0] ^ k].astype(BF16)

    lanes = pieces[0].shape[1]
    outs = (shape(BF16, own, lanes),) * chips
    return kernel(body, outs, (place,), tuple(pieces), (shape(F32, chips, own, lanes),), micros=0.7, name="share")


def finish_qkv_call(place, pieces, model, live, width):
    count, own = len(pieces), pieces[0].shape[0]

    def body(place_ref, *refs):
        q_ref, k_ref, v_ref, gain_ref, bias_ref, in_ref = refs[count:]
        for k in range(count):
            in_ref[place_ref[0] ^ k] = refs[k][...].astype(F32)
        for at, ref in enumerate((q_ref, k_ref, v_ref)):
            ref[...] = jnp.concatenate(
                [in_ref[k, :, at * width : at * width + live] for k in range(count)], axis=1
            )
        total = jnp.sum(in_ref[:, :, live : live + 2], axis=0).T
        gain_ref[...] = total[0:1].reshape(own)
        bias_ref[...] = total[1:2].reshape(own)

    outs = (shape(F32, own, model),) * 3 + (shape(F32, own),) * 2
    scratch = (shape(F32, count, *pieces[0].shape),)
    return kernel(body, outs, (place,), tuple(pieces), scratch, micros=0.8, name="finish_qkv")


def input_grad_call(place, pieces, layer_in, grad_mid, gain, w_query, w_key, w_value, live):
    count = len(pieces)
    rows, model = layer_in.shape

    def body(place_ref, *refs):
        in_ref, gmid_ref, gain_ref, wq_ref, wk_ref, wv_ref, out_ref, scr = refs[count:]
        for k in range(count):
            scr[place_ref[0] ^ k] = refs[k][...]
        blocks = [unpack(scr[k], rows, 3 * live) for k in range(count)]
        grad = jnp.zeros((rows, model), F32)
        for at, w_ref in enumerate((wq_ref, wk_ref, wv_ref)):
            part = jnp.concatenate([block[:, at * live : (at + 1) * live] for block in blocks], axis=1)
            grad = grad + mm(part, w_ref[...], NT)
        unit, scale = unit_norm(in_ref[...].astype(F32))
        out_ref[...] = (gmid_ref[...] + norm_back(grad, row(gain_ref), unit, scale)).astype(BF16)

    operands = (*pieces, layer_in, grad_mid, gain, w_query, w_key, w_value)
    scratch = (shape(BF16, count, *pieces[0].shape),)
    return kernel(body, shape(BF16, rows, model), (place,), operands, scratch, micros=3.0, name="grad_inputs")


def swap_core(value):
    return lax.ppermute(value, "core", [(0, 1), (1, 0)])


def swap(value, axis, bit):
    return lax.ppermute(value, axis, [(k, k ^ bit) for k in range(lax.axis_size(axis))])


def trade(messages, axis):
    found = {k: swap(messages[k], axis, k) for k in range(len(messages) - 1, 0, -1)}
    return [messages[0]] + [found[k] for k in range(1, len(messages))]


def gather_chips(block, chips):
    found = {0: block}
    bit = chips // 2
    while bit >= 1:
        for k in sorted(found):
            found[k | bit] = swap(found[k], "chip", bit)
        bit //= 2
    return [found[k] for k in range(chips)]


def scatter_chips(place, keep, arrived, chips, bit):
    while bit < chips:
        keep, away = halve_call(place, keep, arrived, bit)
        arrived = swap(away, "chip", bit)
        bit *= 2
    return keep, arrived


def after(values, *others):
    return lax.optimization_barrier((values, others))[0]


def fast_shards(
    inputs, doc_lengths, ln1_gain, ln1_bias, w_query, w_key, w_value, ln2_gain, ln2_bias, w_out,
    ln3_gain, ln3_bias, w_up, w_down, out_grad,
):
    rows, model = inputs.shape[1:]
    chips, parts = lax.axis_size("chip"), lax.axis_size("rows")
    z_index = lax.axis_index("chip")
    heads_here = HEADS // chips
    live = heads_here * HEAD_DIM
    width = -(-live // 128) * 128
    hidden = w_up.shape[1]
    part = hidden // parts
    own = model // (parts * chips * 2)
    place = jnp.stack([z_index, lax.axis_index("core"), lax.axis_index("rows")]).astype(jnp.int32)
    scope = jax.named_scope

    def columns(weight):
        mine = lax.dynamic_slice_in_dim(weight, z_index * live, live, 1)
        return jnp.pad(mine, ((0, 0), (0, width - live)))

    place, layer_in, out_grad = lax.optimization_barrier((place, inputs[0], out_grad[0]))
    with scope("gather_in"):
        blocks = gather_chips(layer_in, chips)
    grad_out = mask_call(place, doc_lengths, out_grad)
    w_heads = jnp.concatenate([columns(w_query), columns(w_key), columns(w_value)], axis=1)
    groups = [g for g in ([0], list(range(1, chips - 1)), [chips - 1]) if g] if chips > 1 else [[0]]
    made = [qkv_call([blocks[k] for k in g], ln1_gain, ln1_bias, w_heads, width) for g in groups]
    queries, kv_own, units = ([m[at] for m in made] for at in range(3))
    with scope("core_kv"):
        kv_other = [swap_core(v) for v in kv_own]
    attn_heads, (prob, queries, kv_own, kv_other), messages = attend_call(
        place, doc_lengths, groups, queries, kv_own, kv_other, heads_here
    )
    fence = lax.optimization_barrier
    with scope("chip_attn"):
        pieces = trade(messages, "chip")
    with scope("plane_out"):
        grads_plane = trade([grad_out] * parts, "rows")
    pieces = after(pieces, grads_plane)

    vectors = (ln2_gain, ln2_bias, ln3_gain, ln3_bias)
    middle, attn, normed3 = norms_call(place, pieces, layer_in, vectors, w_out, live)
    act, slope, acts = up_call(place, normed3, w_up, parts)
    with scope("plane_act"):
        acts = trade(acts, "rows")
    output, grad_mid, back, messages = backward_call(
        place, attn, middle, act, slope, grad_out, vectors, w_out, w_up, w_down, parts, chips, live
    )
    back = after(back, acts[1:])
    with scope("chip_grad"):
        grad_heads = trade(messages, "chip")
    with scope("plane_back"):
        far = [swap(back[k], "rows", k) for k in range(3, parts)]
    grad_q, grad_kv, grad_kv_other = attend_back_call(
        place, queries, kv_own, kv_other, prob, attn_heads, grad_heads, heads_here
    )
    with scope("core_grad"):
        grad_kv_other = swap_core(grad_kv_other)
    down_keep, down_send = down_grad_call(place, after(acts, grad_q), grads_plane, chips)
    grad_kv_other, down_send, far = fence((grad_kv_other, down_send, far))
    with scope("core_down"):
        down_recv = swap_core(down_send)
    with scope("plane_back"):
        near = after(back[1:3], far)
        back = back[:1] + [swap(near[k], "rows", k + 1) for k in range(len(near))] + far
    grad_qkv, messages = join_call(place, grad_q, grad_kv, grad_kv_other, live)
    with scope("down_sum"):
        down_keep, down_away = halve_call(place, down_keep, after(down_recv, grad_qkv), 1)
        grad_qkv, down_away = fence((grad_qkv, down_away))
        down_recv = swap(down_away, "chip", 1)
    with scope("chip_qkv"):
        grad_pieces = trade(messages, "chip")
    qkv_keep, qkv_send = qkv_grad_call(
        place, groups, units, grad_qkv, ln1_gain, ln1_bias, w_heads, parts, live, width
    )
    down_recv = after(down_recv, qkv_send)
    with scope("down_sum"):
        down_keep, down_last = scatter_chips(place, down_keep, down_recv, chips, 2)
    qkv_send = after(qkv_send, (down_keep, grad_pieces[2:]))
    with scope("core_w"):
        qkv_send = swap_core(qkv_send)
    qkv_sums = spread_call(place, qkv_keep, qkv_send)
    back = after(back, (down_keep, grad_pieces[2:]))
    up_keep, up_send = up_grad_call(place, back, chips, part, model)
    with scope("plane_w"):
        traded = trade(qkv_sums, "rows")
    up_send = after(up_send, (down_last, grad_pieces[1:2], qkv_sums))
    with scope("core_up"):
        up_recv = swap_core(up_send)
    up_keep, up_away = halve_call(place, up_keep, up_recv, 1)
    with scope("up_sum"):
        up_recv = swap(up_away, "chip", 1)
    traded = after(traded, up_away)
    with scope("chip_w"):
        shared = share_call(place, traded, chips)
        qkv_all = trade(shared, "chip")
    grad_inputs = input_grad_call(
        place, grad_pieces, layer_in, grad_mid, ln1_gain, w_query, w_key, w_value, live
    )
    gwd = finish_down_call(down_keep, down_last)
    up_recv = after(up_recv, (grad_pieces, shared, down_last))
    with scope("up_sum"):
        up_keep, up_last = scatter_chips(place, up_keep, up_recv, chips, 2)
    up_last = after(up_last, (qkv_all, gwd, grad_inputs))
    gwo, g2, b2, g3, b3, *up_rows = finish_up_call(place, up_keep, up_last, parts, own, part)
    with scope("plane_rows"):
        up_rows = trade(up_rows, "rows")
    gwq, gwk, gwv, g1, b1 = finish_qkv_call(place, qkv_all, model, live, width)
    gwu = place_up_call(place, up_rows)
    return (
        output[None], grad_inputs[None], g1, b1, gwq, gwk, gwv, g2, b2, gwo, g3, b3, gwu, gwd,
    )


def takes_fast(mesh):
    seq, parts = mesh.shape["seq"], mesh.shape["rows"]
    chips = seq // 2
    return seq % 2 == 0 and chips & (chips - 1) == 0 and parts in (1, 2, 4) and HEADS % max(chips, 1) == 0


def solution(mesh):
    if takes_fast(mesh):
        parts, seq = mesh.shape["rows"], mesh.shape["seq"]
        split = jax.sharding.Mesh(mesh.devices.reshape(parts, seq // 2, 2), ("rows", "chip", "core"))
        return mapped(fast_shards, split, ("chip", "core"))
    return mapped(shards, mesh, "seq")
```

```python
import math

import jax
import jax.numpy as jnp
from jax import lax
from jax.experimental import pallas as pl
from jax.experimental.pallas import tpu as pltpu
from jax.sharding import PartitionSpec as P

HEADS = 12
HEAD_DIM = 64


segment_pairs = ((2048, 1), (4096, 2), (8192, 4), (16384, 6))
masked_value = -1e30


def layer_norm(vector, gain_vec, bias_vec):
    row_mean = jnp.mean(vector, axis=-1, keepdims=True)
    centered = vector - row_mean
    row_var = jnp.mean(centered * centered, axis=-1, keepdims=True)
    return centered * lax.rsqrt(row_var + 1e-05) * gain_vec + bias_vec


def doc_of(positions, doc_ends):
    return jnp.sum((positions[:, None] >= doc_ends[None, :]).astype(jnp.int32), axis=1)


def pair_terms(query_pos, key_pos, query_doc, key_doc, head_count):
    head_ids = jnp.arange(head_count, dtype=jnp.int32)
    multiplicity = jnp.zeros((head_count, query_pos.shape[0], key_pos.shape[0]), jnp.float32)
    for seg_width, dilation in segment_pairs:
        same_seg = query_pos[:, None] // seg_width == key_pos[None, :] // seg_width
        query_pick = (query_pos % seg_width % dilation)[None, :] == (head_ids % dilation)[:, None]
        key_pick = (key_pos % seg_width % dilation)[None, :] == (head_ids % dilation)[:, None]
        joined = same_seg[None] & query_pick[:, :, None] & key_pick[:, None, :]
        multiplicity = multiplicity + joined.astype(jnp.float32)
    allowed = (key_pos[None, :] <= query_pos[:, None]) & (query_doc[:, None] == key_doc[None, :])
    allowed = allowed[None] & (multiplicity > 0.0)
    return (jnp.log(jnp.maximum(multiplicity, 1.0)), allowed)


def rows_inner(left, right):
    return lax.dot_general(
        left, right, (((0,), (0,)), ((), ())), preferred_element_type=jnp.float32
    )


def cols_inner(left, right):
    return lax.dot_general(
        left, right, (((1,), (1,)), ((), ())), preferred_element_type=jnp.float32
    )


def over_blocks(state, piece, step_fn):
    total_rows = piece[0].shape[0]
    block_rows = math.gcd(total_rows, 512)
    block_total = total_rows // block_rows
    split = tuple((part.reshape((block_total, block_rows) + part.shape[1:]) for part in piece))

    def inner(carried, block_item):
        return (step_fn(carried, block_item[1], block_item[0] * block_rows), None)

    result, unused = lax.scan(inner, state, (jnp.arange(block_total, dtype=jnp.int32), split))
    return result


def add_rows(buffer, start_pos, addend):
    current = lax.dynamic_slice_in_dim(buffer, start_pos, addend.shape[0], 0)
    return lax.dynamic_update_slice_in_dim(buffer, current + addend, start_pos, 0)


def shards(
    inputs,
    doc_lengths,
    ln1_gain,
    ln1_bias,
    w_query,
    w_key,
    w_value,
    ln2_gain,
    ln2_bias,
    w_out,
    ln3_gain,
    ln3_bias,
    w_up,
    w_down,
    out_grad,
):
    tok_rows = inputs.shape[1]
    head_count = HEADS
    head_size = HEAD_DIM
    model_width = inputs.shape[2]
    row_total = tok_rows * lax.axis_size("seq")
    layer_in = inputs[0].astype(jnp.float32)
    doc_ends = jnp.cumsum(doc_lengths[0])
    first_pos = lax.axis_index("seq") * tok_rows
    query_pos = first_pos + jnp.arange(tok_rows, dtype=jnp.int32)
    query_doc = doc_of(query_pos, doc_ends)
    valid = (query_doc < doc_lengths.shape[1]).astype(jnp.float32)
    first_norm, first_back = jax.vjp(layer_norm, layer_in, ln1_gain, ln1_bias)
    normed_one = first_norm.astype(jnp.bfloat16)
    queries = jnp.dot(normed_one, w_query, preferred_element_type=jnp.float32).astype(jnp.bfloat16)
    keys_local = jnp.dot(normed_one, w_key, preferred_element_type=jnp.float32).astype(jnp.bfloat16)
    values_local = jnp.dot(normed_one, w_value, preferred_element_type=jnp.float32).astype(
        jnp.bfloat16
    )
    query_heads = queries.reshape(tok_rows, head_count, head_size)

    def key_block_terms(key_start, key_count):
        key_pos = key_start + jnp.arange(key_count, dtype=jnp.int32)
        key_doc = doc_of(key_pos, doc_ends)
        return pair_terms(query_pos, key_pos, query_doc, key_doc, head_count)

    def with_pruning(step_fn):

        def wrapped(state, parts, start_pos):
            return step_fn(state, parts, start_pos)

        return wrapped

    def forward_step(state, parts, key_start):
        run_max, run_total, run_acc = state
        key_blk = parts[0].reshape(-1, head_count, head_size)
        value_blk = parts[1].reshape(-1, head_count, head_size)
        log_mult, allowed = key_block_terms(key_start, key_blk.shape[0])
        scores = 0.125 * jnp.einsum(
            "qhd,khd->hqk", query_heads, key_blk, preferred_element_type=jnp.float32
        )
        logits = jnp.where(allowed, scores + log_mult, masked_value)
        new_max = jnp.maximum(run_max, jnp.max(logits, axis=-1))
        weights = jnp.where(allowed, jnp.exp(logits - new_max[..., None]), 0.0)
        factor = jnp.exp(run_max - new_max)
        run_total = run_total * factor + jnp.sum(weights, axis=-1)
        run_acc = run_acc * factor[..., None] + jnp.einsum(
            "hqk,khd->hqd",
            weights.astype(jnp.bfloat16),
            value_blk,
            preferred_element_type=jnp.float32,
        )
        return (new_max, run_total, run_acc)

    forward_pruned = with_pruning(forward_step)
    start_state = (
        jnp.full((head_count, tok_rows), masked_value, jnp.float32),
        jnp.zeros((head_count, tok_rows), jnp.float32),
        jnp.zeros((head_count, tok_rows, head_size), jnp.float32),
    )
    final_state = over_blocks(
        start_state,
        (
            lax.all_gather(keys_local, "seq", axis=0, tiled=True),
            lax.all_gather(values_local, "seq", axis=0, tiled=True),
        ),
        forward_pruned,
    )
    run_max, run_total, run_acc = final_state
    row_lse = run_max + jnp.log(run_total)
    attn = (run_acc / run_total[..., None]).transpose(1, 0, 2).reshape(tok_rows, model_width)
    second_norm, second_back = jax.vjp(layer_norm, attn, ln2_gain, ln2_bias)
    normed_two = second_norm.astype(jnp.bfloat16)
    middle = layer_in + jnp.dot(normed_two, w_out, preferred_element_type=jnp.float32)
    third_norm, third_back = jax.vjp(layer_norm, middle, ln3_gain, ln3_bias)
    normed_three = third_norm.astype(jnp.bfloat16)
    upper = jnp.dot(normed_three, w_up, preferred_element_type=jnp.float32)
    activated_f, gelu_back = jax.vjp(
        lambda upper_in: jax.nn.gelu(upper_in, approximate=False), upper
    )
    activated = activated_f.astype(jnp.bfloat16)
    layer_out = middle + jnp.dot(activated, w_down, preferred_element_type=jnp.float32)
    grad_out = out_grad[0].astype(jnp.float32) * valid[:, None]
    grad_branch = grad_out.astype(jnp.bfloat16)
    grad_w_down = rows_inner(activated, grad_branch)
    grad_act = cols_inner(grad_branch, w_down)
    grad_upper = gelu_back(grad_act)[0].astype(jnp.bfloat16)
    grad_w_up = rows_inner(normed_three, grad_upper)
    grad_n3 = cols_inner(grad_upper, w_up)
    grad_mid_norm, grad_ln3_gain, grad_ln3_bias = third_back(grad_n3)
    grad_middle = grad_out + grad_mid_norm
    grad_proj = grad_middle.astype(jnp.bfloat16)
    grad_w_out = rows_inner(normed_two, grad_proj)
    grad_n2 = cols_inner(grad_proj, w_out)
    grad_attn_f, grad_ln2_gain, grad_ln2_bias = second_back(grad_n2)
    grad_attn = grad_attn_f.astype(jnp.bfloat16)
    grad_heads = grad_attn.reshape(tok_rows, head_count, head_size)
    row_delta = jnp.sum(
        (grad_attn.astype(jnp.float32) * attn).reshape(tok_rows, head_count, head_size), axis=-1
    )

    def backward_step(state, parts, key_start):
        grad_q_acc, grad_k_rows, grad_v_rows = state
        key_blk = parts[0].reshape(-1, head_count, head_size)
        value_blk = parts[1].reshape(-1, head_count, head_size)
        key_count = key_blk.shape[0]
        log_mult, allowed = key_block_terms(key_start, key_count)
        scores = 0.125 * jnp.einsum(
            "qhd,khd->hqk", query_heads, key_blk, preferred_element_type=jnp.float32
        )
        logits = jnp.where(allowed, scores + log_mult, masked_value)
        weights = jnp.where(allowed, jnp.exp(logits - row_lse[..., None]), 0.0)
        grad_weights = jnp.einsum(
            "qhd,khd->hqk", grad_heads, value_blk, preferred_element_type=jnp.float32
        )
        grad_scores = (weights * (grad_weights - row_delta.T[..., None])).astype(jnp.bfloat16)
        grad_q_acc = grad_q_acc + 0.125 * jnp.einsum(
            "hqk,khd->qhd", grad_scores, key_blk, preferred_element_type=jnp.float32
        )
        value_part = jnp.einsum(
            "hqk,qhd->khd",
            weights.astype(jnp.bfloat16),
            grad_heads,
            preferred_element_type=jnp.float32,
        ).reshape(key_count, model_width)
        key_part = 0.125 * jnp.einsum(
            "hqk,qhd->khd", grad_scores, query_heads, preferred_element_type=jnp.float32
        ).reshape(key_count, model_width)
        grad_k_rows = add_rows(grad_k_rows, key_start, key_part)
        grad_v_rows = add_rows(grad_v_rows, key_start, value_part)
        return (grad_q_acc, grad_k_rows, grad_v_rows)

    backward_pruned = with_pruning(backward_step)
    zero_state = (
        jnp.zeros((tok_rows, head_count, head_size), jnp.float32),
        jnp.zeros((row_total, model_width), jnp.float32),
        jnp.zeros((row_total, model_width), jnp.float32),
    )
    back_state = over_blocks(
        zero_state,
        (
            lax.all_gather(keys_local, "seq", axis=0, tiled=True),
            lax.all_gather(values_local, "seq", axis=0, tiled=True),
        ),
        backward_pruned,
    )
    grad_q_acc, grad_k_rows, grad_v_rows = back_state
    grad_k_acc, grad_v_acc = (
        lax.psum_scatter(
            grad_k_rows.astype(jnp.bfloat16), "seq", scatter_dimension=0, tiled=True
        ).astype(jnp.float32),
        lax.psum_scatter(
            grad_v_rows.astype(jnp.bfloat16), "seq", scatter_dimension=0, tiled=True
        ).astype(jnp.float32),
    )
    grad_queries = grad_q_acc.reshape(tok_rows, model_width).astype(jnp.bfloat16)
    grad_keys = grad_k_acc.astype(jnp.bfloat16)
    grad_values = grad_v_acc.astype(jnp.bfloat16)
    grad_w_query = rows_inner(normed_one, grad_queries)
    grad_w_key = rows_inner(normed_one, grad_keys)
    grad_w_value = rows_inner(normed_one, grad_values)
    grad_n1 = (
        cols_inner(grad_queries, w_query)
        + cols_inner(grad_keys, w_key)
        + cols_inner(grad_values, w_value)
    )
    grad_in_norm, grad_ln1_gain, grad_ln1_bias = first_back(grad_n1)
    grad_inputs = (grad_middle + grad_in_norm).astype(jnp.bfloat16)
    summed = (
        lax.psum_scatter(grad_ln1_gain, ("rows", "seq"), scatter_dimension=0, tiled=True),
        lax.psum_scatter(grad_ln1_bias, ("rows", "seq"), scatter_dimension=0, tiled=True),
        lax.psum_scatter(grad_w_query, ("rows", "seq"), scatter_dimension=0, tiled=True),
        lax.psum_scatter(grad_w_key, ("rows", "seq"), scatter_dimension=0, tiled=True),
        lax.psum_scatter(grad_w_value, ("rows", "seq"), scatter_dimension=0, tiled=True),
        lax.psum_scatter(grad_ln2_gain, ("rows", "seq"), scatter_dimension=0, tiled=True),
        lax.psum_scatter(grad_ln2_bias, ("rows", "seq"), scatter_dimension=0, tiled=True),
        lax.psum_scatter(grad_w_out, ("rows", "seq"), scatter_dimension=0, tiled=True),
        lax.psum_scatter(grad_ln3_gain, ("rows", "seq"), scatter_dimension=0, tiled=True),
        lax.psum_scatter(grad_ln3_bias, ("rows", "seq"), scatter_dimension=0, tiled=True),
        lax.psum_scatter(grad_w_up, ("rows", "seq"), scatter_dimension=0, tiled=True),
        lax.psum_scatter(grad_w_down, ("rows", "seq"), scatter_dimension=0, tiled=True),
    )
    return (
        layer_out.astype(jnp.bfloat16)[None],
        grad_inputs[None],
        summed[0],
        summed[1],
        summed[2],
        summed[3],
        summed[4],
        summed[5],
        summed[6],
        summed[7],
        summed[8],
        summed[9],
        summed[10],
        summed[11],
    )


def mapped(step, mesh, seq):
    spread = P(("rows",) + (seq if isinstance(seq, tuple) else (seq,)))
    tokens, plain = P("rows", seq, None), P()
    weights = P(spread[0], None)
    return jax.shard_map(
        step,
        mesh=mesh,
        in_specs=(tokens, P("rows", None)) + (plain,) * 12 + (tokens,),
        out_specs=(tokens, tokens, spread, spread, weights, weights, weights, spread, spread, weights)
        + (spread, spread, weights, weights),
        check_vma=False,
    )


F32 = jnp.float32
PACE = 1e6
BF16 = jnp.bfloat16
NT = (((1,), (1,)), ((), ()))
TN = (((0,), (0,)), ((), ()))
NN = (((1,), (0,)), ((), ()))


def mm(left, right, dims):
    return lax.dot_general(left, right, dims, preferred_element_type=F32)


def unit_norm(vector):
    centered = vector - jnp.mean(vector, axis=-1, keepdims=True)
    scale = lax.rsqrt(jnp.mean(centered * centered, axis=-1, keepdims=True) + 1e-05)
    return centered * scale, scale


def norm_back(grad, gain, unit, scale):
    weighted = grad * gain
    mean_w = jnp.mean(weighted, axis=-1, keepdims=True)
    mean_wu = jnp.mean(weighted * unit, axis=-1, keepdims=True)
    return scale * (weighted - mean_w - unit * mean_wu)


def shape(dtype, *dims):
    return jax.ShapeDtypeStruct(dims, dtype)


def row(ref):
    return ref[...].reshape(1, ref.shape[0])


def size_of(item):
    total = jnp.dtype(item.dtype).itemsize
    for dim in item.shape:
        total *= dim
    return total


def kernel(body, outs, scalars, operands, scratch=(), micros=2.0, name=None):
    single = not isinstance(outs, (tuple, list))
    listed = (outs,) if single else tuple(outs)
    vmem = pl.BlockSpec(memory_space=pltpu.VMEM)
    smem = pl.BlockSpec(memory_space=pltpu.SMEM)
    moved = sum(size_of(v) for v in (*operands, *listed))
    held = sum(size_of(v) for v in scratch)
    return pl.pallas_call(
        body,
        out_shape=outs if single else listed,
        in_specs=[smem] * len(scalars) + [vmem] * len(operands),
        out_specs=vmem if single else (vmem,) * len(listed),
        scratch_shapes=[pltpu.VMEM(v.shape, v.dtype) for v in scratch],
        compiler_params=pltpu.CompilerParams(vmem_limit_bytes=min(60 << 20, (moved + held) * 5 // 4 + (6 << 20))),
        cost_estimate=pl.CostEstimate(flops=int(micros * PACE), bytes_accessed=int(micros * PACE / 1e3), transcendentals=0),
        name=name,
    )(*scalars, *operands)


def packed_rows(rows, live):
    return rows * live // 128


def pack(block):
    rows, live = block.shape
    whole = live // 128
    pieces = [block[:, 128 * j : 128 * (j + 1)] for j in range(whole)]
    if live % 128:
        rest = block[:, 128 * whole :]
        pieces.append(jnp.concatenate([rest[: rows // 2], rest[rows // 2 :]], axis=1))
    return jnp.concatenate(pieces, axis=0)


def unpack(block, rows, live):
    whole = live // 128
    pieces = [block[rows * j : rows * (j + 1)] for j in range(whole)]
    if live % 128:
        rest = block[rows * whole :]
        pieces.append(jnp.concatenate([rest[:, :64], rest[:, 64:]], axis=0))
    return jnp.concatenate(pieces, axis=1)


def mask_call(place, lengths, out_grad):
    rows, model = out_grad.shape

    def body(place_ref, len_ref, in_ref, out_ref):
        last = jnp.int32(0)
        for d in range(lengths.shape[1]):
            last = last + len_ref[0, d]
        pos = lax.broadcasted_iota(jnp.int32, (rows, 1), 0) + (2 * place_ref[0] + place_ref[1]) * rows
        out_ref[...] = jnp.where(pos < last, in_ref[...].astype(F32), 0.0).astype(BF16)

    return kernel(body, shape(BF16, rows, model), (place, lengths), (out_grad,), micros=0.7, name="mask_grad")


def qkv_call(blocks, gain, bias, weight, width):
    count = len(blocks)
    rows, model = blocks[0].shape

    def body(*refs):
        xs, (gain_ref, bias_ref, weight_ref, q_ref, kv_ref, unit_ref) = refs[:count], refs[count:]
        for k in range(count):
            unit, _ = unit_norm(xs[k][...].astype(F32))
            normed = (unit * row(gain_ref) + row(bias_ref)).astype(BF16)
            made = mm(normed, weight_ref[...], NN)
            q_ref[k] = (made[:, :width].astype(BF16).astype(F32) * 0.125).astype(BF16)
            kv_ref[k] = made[:, width:].astype(BF16)
            unit_ref[k] = unit.astype(BF16)

    outs = (
        shape(BF16, count, rows, width),
        shape(BF16, count, rows, 2 * width),
        shape(BF16, count, rows, model),
    )
    return kernel(body, outs, (), (*blocks, gain, bias, weight), micros=1.2 * count, name="qkv_heads")


def lane_head(lanes):
    return lax.broadcasted_iota(jnp.int32, (1, lanes), 1) // HEAD_DIM


def residue(pos_f, modulus):
    return pos_f - modulus * jnp.floor((pos_f + 0.5) * (1.0 / modulus))


def stack_heads(block, heads_here):
    head_of = lane_head(block.shape[1])
    return jnp.concatenate(
        [jnp.where(head_of == h, block, jnp.zeros_like(block)) for h in range(heads_here)], axis=0
    )


def fold_heads(stacked, rows, heads_here):
    head_of = lane_head(stacked.shape[1])
    total = jnp.zeros((rows, stacked.shape[1]), stacked.dtype)
    for h in range(heads_here):
        total = jnp.where(head_of == h, stacked[h * rows : (h + 1) * rows], total)
    return total


def attend_call(place, lengths, groups, queries, kv_own, kv_other, heads_here):
    count = sum(len(g) for g in groups)
    rows, width = queries[0].shape[1:]
    tall, wide = heads_here * rows, count * rows
    docs = lengths.shape[1]
    step = 16
    n = len(groups)

    def body(place_ref, len_ref, *refs):
        q_in, own_in, oth_in = refs[:n], refs[n : 2 * n], refs[2 * n : 3 * n]
        out_ref, prob_ref, q_ref, own_ref, oth_ref = refs[3 * n : 3 * n + 5]
        msgs, (s_scr, m_scr, hot_scr, send_scr) = refs[3 * n + 5 : 3 * n + 5 + count], refs[3 * n + 5 + count :]
        z_index, core = place_ref[0], place_ref[1]
        for g, ks in enumerate(groups):
            for j, k in enumerate(ks):
                q_ref[z_index ^ k] = q_in[g][j]
                own_ref[z_index ^ k] = own_in[g][j]
                oth_ref[z_index ^ k] = oth_in[g][j]
        sides = (own_ref, oth_ref)
        cores = (core, 1 - core)
        lane = lax.broadcasted_iota(jnp.int32, (rows, 128), 1).astype(F32)
        for side in range(2):
            for b in range(count):
                pos = lax.broadcasted_iota(jnp.int32, (rows, 1), 0) + (2 * b + cores[side]) * rows
                hot = (residue(pos.astype(F32), 12.0) == lane).astype(F32)
                hot_scr[side, b * rows : (b + 1) * rows, :] = hot.astype(BF16)
        for i in range(count):
            keys = (i + 1) * rows
            pos = lax.broadcasted_iota(jnp.int32, (rows, 1), 0) + (2 * i + core) * rows
            pos_f = pos.astype(F32)
            begin = jnp.zeros_like(pos)
            run = jnp.int32(0)
            for d in range(docs):
                run = run + len_ref[0, d]
                begin = jnp.where(pos >= run, run, begin)
            tables = []
            for h in range(heads_here):
                head = (z_index * heads_here + h).astype(F32)
                table = jnp.ones((rows, 128), F32)
                for r in (2.0, 4.0, 6.0):
                    mine = residue(head, r)
                    pick_q = (residue(pos_f, r) == mine).astype(F32)
                    pick_k = (residue(lane, r) == mine).astype(F32)
                    table = table + pick_q * pick_k
                tables.append(jnp.where(lane < 12.0, table, 0.0))
            table = jnp.concatenate(tables, axis=0).astype(BF16)
            stacked = stack_heads(q_ref[i], heads_here)
            for side in range(2):
                key = sides[side][:, :, :width].reshape(wide, width)[:keys]
                s_scr[side, :, :keys] = mm(stacked, key, NT)
                m_scr[side, :, :keys] = mm(table, hot_scr[side, :keys], NT)
            key_pos = [
                jnp.concatenate(
                    [
                        lax.broadcasted_iota(jnp.int32, (1, rows), 1) + (2 * b + cores[side]) * rows
                        for b in range(i + 1)
                    ],
                    axis=1,
                )
                for side in range(2)
            ]
            for h in range(heads_here):
                for at in range(0, rows, step):
                    lo = h * rows + at
                    pos_c, begin_c = pos[at : at + step], begin[at : at + step]
                    masked = []
                    for side in range(2):
                        ok = (key_pos[side] <= pos_c) & (key_pos[side] >= begin_c)
                        masked.append(jnp.where(ok, s_scr[side, lo : lo + step, :keys], masked_value))
                    top = jnp.maximum(
                        jnp.max(masked[0], axis=1, keepdims=True), jnp.max(masked[1], axis=1, keepdims=True)
                    )
                    parts = [
                        jnp.exp(masked[side] - top) * m_scr[side, lo : lo + step, :keys] for side in range(2)
                    ]
                    total = jnp.sum(parts[0], axis=1, keepdims=True) + jnp.sum(parts[1], axis=1, keepdims=True)
                    inverse = 1.0 / total
                    for side in range(2):
                        prob_ref[i, side, lo : lo + step, :keys] = (parts[side] * inverse).astype(BF16)
            mixed = jnp.zeros((tall, width), F32)
            for side in range(2):
                value = sides[side][:, :, width:].reshape(wide, width)[:keys]
                mixed = mixed + mm(prob_ref[i, side, :, :keys], value, NN)
            result = fold_heads(mixed, rows, heads_here)
            out_ref[i] = result
            send_scr[i] = pack(result.astype(BF16)[:, :live])
        for k in range(count):
            msgs[k][...] = send_scr[z_index ^ k]

    live = heads_here * HEAD_DIM
    outs = (
        shape(F32, count, rows, width),
        shape(BF16, count, 2, tall, wide),
        shape(BF16, count, rows, width),
        shape(BF16, count, rows, 2 * width),
        shape(BF16, count, rows, 2 * width),
    ) + (shape(BF16, packed_rows(rows, live), 128),) * count
    scratch = (
        shape(F32, 2, tall, wide),
        shape(F32, 2, tall, wide),
        shape(BF16, 2, wide, 128),
        shape(BF16, count, packed_rows(rows, live), 128),
    )
    operands = (*queries, *kv_own, *kv_other)
    found = kernel(
        body, outs, (place, lengths), operands, scratch, micros=6.0, name="attend"
    )
    return found[0], found[1:5], list(found[5:])


def attend_back_call(place, queries, kv_own, kv_other, prob, attn, grads, heads_here):
    count, rows, width = queries.shape
    tall, wide = heads_here * rows, count * rows
    step = 16

    live = heads_here * HEAD_DIM

    def body(place_ref, q_ref, own_ref, oth_ref, prob_ref, attn_ref, *refs):
        grad_refs, (dq_ref, down_ref, doth_ref, p_scr, d_scr, acc, grad_ref) = refs[:count], refs[count:]
        sides = (own_ref, oth_ref)
        acc[...] = jnp.zeros_like(acc)
        grad_ref[...] = jnp.zeros_like(grad_ref)
        for k in range(count):
            grad_ref[place_ref[0] ^ k, :, :live] = unpack(grad_refs[k][...], rows, live)
        for i in range(count):
            keys = (i + 1) * rows
            grad = grad_ref[i]
            stacked_q = stack_heads(q_ref[i], heads_here)
            stacked_g = stack_heads(grad, heads_here)
            product = grad.astype(F32) * attn_ref[i]
            head_of = lane_head(width)
            delta = [
                jnp.sum(jnp.where(head_of == h, product, 0.0), axis=1, keepdims=True) for h in range(heads_here)
            ]
            for side in range(2):
                value = sides[side][:, :, width:].reshape(wide, width)[:keys]
                p_scr[side, :, :keys] = mm(stacked_g, value, NT)
            for h in range(heads_here):
                for at in range(0, rows, step):
                    lo = h * rows + at
                    for side in range(2):
                        weights = prob_ref[i, side, lo : lo + step, :keys].astype(F32)
                        shifted = p_scr[side, lo : lo + step, :keys] - delta[h][at : at + step]
                        d_scr[side, lo : lo + step, :keys] = (weights * shifted).astype(BF16)
            grad_q = jnp.zeros((tall, width), F32)
            for side in range(2):
                key = sides[side][:, :, :width].reshape(wide, width)[:keys]
                moved = d_scr[side, :, :keys]
                grad_q = grad_q + mm(moved, key, NN)
                acc[side, :keys, :width] += mm(moved, stacked_q, TN)
                acc[side, :keys, width:] += mm(prob_ref[i, side, :, :keys], stacked_g, TN)
            dq_ref[i] = (0.125 * fold_heads(grad_q, rows, heads_here)).astype(BF16)
        down_ref[...] = acc[0].reshape(count, rows, 2 * width)
        doth_ref[...] = acc[1].reshape(count, rows, 2 * width).astype(BF16)

    outs = (
        shape(BF16, count, rows, width),
        shape(F32, count, rows, 2 * width),
        shape(BF16, count, rows, 2 * width),
    )
    scratch = (
        shape(F32, 2, tall, wide),
        shape(BF16, 2, tall, wide),
        shape(F32, 2, wide, 2 * width),
        shape(BF16, count, rows, width),
    )
    operands = (queries, kv_own, kv_other, prob, attn, *grads)
    return kernel(body, outs, (place,), operands, scratch, micros=6.0, name="attend_back")


def join_call(place, grad_q, grad_kv, arrived, live):
    count, rows, width = grad_q.shape

    def body(place_ref, q_ref, kv_ref, in_ref, out_ref, *rest):
        msgs, scr = rest[:count], rest[count]
        for b in range(count):
            both = (kv_ref[b] + in_ref[b].astype(F32)).astype(BF16)
            out_ref[b, :, :width] = q_ref[b]
            out_ref[b, :, width:] = both
            dense = [q_ref[b][:, :live], both[:, :live], both[:, width : width + live]]
            scr[b] = pack(jnp.concatenate(dense, axis=1))
        for k in range(count):
            msgs[k][...] = scr[place_ref[0] ^ k]

    message = shape(BF16, packed_rows(rows, 3 * live), 128)
    outs = (shape(BF16, count, rows, 3 * width),) + (message,) * count
    scratch = (shape(BF16, count, *message.shape),)
    joined, *msgs = kernel(body, outs, (place,), (grad_q, grad_kv, arrived), scratch, micros=0.7, name="join_grads")
    return joined, msgs


def gather_heads(place_ref, pieces, scr, rows, live):
    for k, ref in enumerate(pieces):
        scr[place_ref[0] ^ k] = ref[...]
    return jnp.concatenate([unpack(scr[k], rows, live) for k in range(len(pieces))], axis=1)


def norms_call(place, pieces, layer_in, vectors, w_out, live):
    count, rows = len(pieces), layer_in.shape[0]
    model = w_out.shape[0]

    def body(place_ref, *refs):
        in_ref, g2, b2, g3, b3, wo_ref, mid_ref, attn_ref, n3_ref, piece_scr = refs[count:]
        attn = gather_heads(place_ref, refs[:count], piece_scr, rows, live)
        attn_ref[...] = attn
        unit2, _ = unit_norm(attn.astype(F32))
        normed2 = (unit2 * row(g2) + row(b2)).astype(BF16)
        middle = in_ref[...].astype(F32) + mm(normed2, wo_ref[...], NN)
        mid_ref[...] = middle
        unit3, _ = unit_norm(middle)
        n3_ref[...] = (unit3 * row(g3) + row(b3)).astype(BF16)

    outs = (shape(F32, rows, model), shape(BF16, rows, model), shape(BF16, rows, model))
    operands = (*pieces, layer_in, *vectors, w_out)
    scratch = (shape(BF16, count, *pieces[0].shape),)
    return kernel(body, outs, (place,), operands, scratch, micros=1.5, name="norms")


def up_call(place, normed3, w_up, parts):
    rows, (model, hidden) = normed3.shape[0], w_up.shape
    part = hidden // parts

    def body(place_ref, n3_ref, wu_ref, act_ref, slope_ref, *msgs):
        normed = n3_ref[...]
        for r in range(parts):
            upper = mm(normed, wu_ref[:, r * part : (r + 1) * part], NN)
            cumulative = 0.5 * (1.0 + lax.erf(upper * 0.7071067811865476))
            density = jnp.exp(-0.5 * upper * upper) * 0.3989422804014327
            act_ref[r] = (upper * cumulative).astype(BF16)
            slope_ref[r] = (cumulative + upper * density).astype(BF16)
        for k in range(parts):
            msgs[k][...] = act_ref[place_ref[2] ^ k]

    outs = (shape(BF16, parts, rows, part),) * 2 + (shape(BF16, rows, part),) * parts
    act, slope, *msgs = kernel(body, outs, (place,), (normed3, w_up), micros=2.0, name="up_gelu")
    return act, slope, msgs


def padded_quarter(quarter):
    return -(-(quarter + 64) // 128) * 128


def backward_call(place, attn, middle, act, slope, grad_out, vectors, w_out, w_up, w_down, parts, count, live):
    rows = attn.shape[0]
    model, hidden = w_up.shape
    part, quarter = hidden // parts, model // parts
    pad_q = padded_quarter(quarter)
    message = shape(BF16, packed_rows(rows, live), 128)

    def body(
        place_ref, attn_ref, mid_ref, act_ref, slope_ref, go_ref, g2, b2, g3, b3, wo_ref, wu_ref, wd_ref,
        out_ref, gmid_ref, *rest,
    ):
        msgs, heads = rest[:parts], rest[parts : parts + count]
        up_scr, n2_scr, head_scr = rest[parts + count :]
        here = place_ref[2]
        go = go_ref[...]
        middle = mid_ref[...]
        out = middle
        grad3 = jnp.zeros((rows, model), F32)
        for r in range(parts):
            w_d = wd_ref[r * part : (r + 1) * part, :]
            out = out + mm(act_ref[r], w_d, NN)
            grad_up = (mm(go, w_d, NT) * slope_ref[r].astype(F32)).astype(BF16)
            up_scr[r] = grad_up
            grad3 = grad3 + mm(grad_up, wu_ref[:, r * part : (r + 1) * part], NT)
        out_ref[...] = out.astype(BF16)
        unit3, scale3 = unit_norm(middle)
        grad_mid = go.astype(F32) + norm_back(grad3, row(g3), unit3, scale3)
        gmid_ref[...] = grad_mid
        proj = grad_mid.astype(BF16)
        grad2 = mm(proj, wo_ref[...], NT)
        unit2, scale2 = unit_norm(attn_ref[...].astype(F32))
        grad_attn = norm_back(grad2, row(g2), unit2, scale2).astype(BF16)
        for k in range(count):
            head_scr[k] = pack(grad_attn[:, k * live : (k + 1) * live])
        for k in range(count):
            heads[k][...] = head_scr[place_ref[0] ^ k]
        sums = [
            jnp.sum(grad2 * unit2, axis=0, keepdims=True),
            jnp.sum(grad2, axis=0, keepdims=True),
            jnp.sum(grad3 * unit3, axis=0, keepdims=True),
            jnp.sum(grad3, axis=0, keepdims=True),
        ]
        table = jnp.concatenate(sums + [jnp.zeros((4, model), F32)], axis=0)
        normed2 = (unit2 * row(g2) + row(b2)).astype(BF16)
        normed3 = (unit3 * row(g3) + row(b3)).astype(BF16)
        spare, lines = pad_q - quarter, quarter // 64
        for r in range(parts):
            chunks = [table[:, r * quarter + 64 * j : r * quarter + 64 * (j + 1)] for j in range(lines)]
            side = jnp.concatenate(chunks + [jnp.zeros((rows - 8 * lines, 64), F32)], axis=0).astype(BF16)
            pieces = [normed2[:, r * quarter : (r + 1) * quarter], side]
            if spare > 64:
                pieces.append(jnp.zeros((rows, spare - 64), BF16))
            n2_scr[r] = jnp.concatenate(pieces, axis=1)
        for k in range(parts):
            msgs[k][:, :part] = up_scr[here ^ k]
            msgs[k][:, part : part + model] = proj
            msgs[k][:, part + model : part + 2 * model] = normed3
            msgs[k][:, part + 2 * model :] = n2_scr[here ^ k]

    outs = (
        shape(BF16, rows, model),
        shape(F32, rows, model),
    )
    outs += (shape(BF16, rows, part + 2 * model + pad_q),) * parts + (message,) * count
    operands = (attn, middle, act, slope, grad_out, *vectors, w_out, w_up, w_down)
    scratch = (
        shape(BF16, parts, rows, part),
        shape(BF16, parts, rows, pad_q),
        shape(BF16, count, *message.shape),
    )
    found = kernel(body, outs, (place,), operands, scratch, micros=9.0, name="token_backward")
    found = list(found)
    return found[0], found[1], found[2 : 2 + parts], found[2 + parts :]


def down_grad_call(place, acts, grads, chips):
    parts = len(acts)
    part, model = acts[0].shape[1], grads[0].shape[1]
    own = part // (2 * chips)

    def body(place_ref, *refs):
        act_refs, grad_refs, (keep_ref, send_ref, scr) = refs[:parts], refs[parts : 2 * parts], refs[2 * parts :]
        core = place_ref[1]
        act = jnp.concatenate([ref[...] for ref in act_refs], axis=0)
        grad = jnp.concatenate([ref[...] for ref in grad_refs], axis=0)
        scr[...] = mm(act, grad, TN).reshape(chips, 2, own, model)
        for k in range(chips):
            keep_ref[k] = scr[k, core]
            send_ref[k] = scr[k, 1 - core].astype(BF16)

    outs = (shape(F32, chips, own, model), shape(BF16, chips, own, model))
    scratch = (shape(F32, chips, 2, own, model),)
    return kernel(body, outs, (place,), (*acts, *grads), scratch, micros=3.0, name="grad_down")


def up_grad_call(place, back, chips, part, model):
    parts = len(back)
    quarter = model // parts
    own = model // (parts * chips * 2)
    tall = (parts + 1) * own + 8

    def body(place_ref, *refs):
        back_refs = refs[:parts]
        keep_ref, send_ref, up_scr, out_scr, vec_scr = refs[parts:]
        core = place_ref[1]
        ends = (0, part, part + model, part + 2 * model, back_refs[0].shape[1])
        grad_up, proj, normed3, normed2 = (
            jnp.concatenate([ref[:, lo:hi] for ref in back_refs], axis=0) for lo, hi in zip(ends, ends[1:])
        )
        up_scr[...] = mm(normed3, grad_up, TN).reshape(parts, chips, 2, own, part)
        out_scr[...] = mm(normed2, proj, TN)[:quarter].reshape(chips, 2, own, model)
        lines = quarter // 64
        side = jnp.zeros((8 * lines, 64), F32)
        for ref in back_refs:
            side = side + ref[:, ends[3] + quarter : ends[3] + quarter + 64].astype(F32)[: 8 * lines]
        table = jnp.concatenate([side[8 * j : 8 * (j + 1)] for j in range(lines)], axis=1)
        vec_scr[...] = jnp.zeros_like(vec_scr)
        for k in range(chips):
            for side in range(2):
                at = (2 * k + side) * own
                vec_scr[k, side, :, :own] = table[:, at : at + own]
        for k in range(chips):
            for side, ref in ((core, keep_ref), (1 - core, send_ref)):
                pieces = [up_scr[r, k, side] for r in range(parts)] + [out_scr[k, side], vec_scr[k, side]]
                ref[k] = jnp.concatenate(pieces, axis=0).astype(ref.dtype)

    outs = (shape(F32, chips, tall, model), shape(BF16, chips, tall, model))
    scratch = (
        shape(F32, parts, chips, 2, own, part),
        shape(F32, chips, 2, own, model),
        shape(F32, chips, 2, 8, model),
    )
    return kernel(body, outs, (place,), tuple(back), scratch, micros=4.0, name="grad_up_out")


def qkv_grad_call(place, groups, units, grads, gain, bias, weight, parts, live, width):
    count, rows = grads.shape[:2]
    model = weight.shape[0]
    own = model // (parts * count * 2)
    lanes = -(-(3 * live + 2) // 128) * 128
    n = len(units)

    def body(place_ref, *refs):
        unit_refs = refs[:n]
        grad_ref, gain_ref, bias_ref, weight_ref, keep_ref, send_ref, unit_scr, scr = refs[n:]
        z_index, core = place_ref[0], place_ref[1]
        for g, ks in enumerate(groups):
            for j, k in enumerate(ks):
                unit_scr[z_index ^ k] = unit_refs[g][j]
        grad = grad_ref[...].reshape(count * rows, 3 * width)
        cross = mm(unit_scr[...].reshape(count * rows, model), grad, TN)
        total = jnp.sum(grad.astype(F32), axis=0, keepdims=True)
        columns = jnp.concatenate([row(gain_ref), row(bias_ref), jnp.zeros((6, model), F32)], axis=0).T
        weight_f = weight_ref[...].astype(F32)
        grad_gain = jnp.sum(weight_f * cross, axis=1, keepdims=True)
        grad_bias = jnp.sum(weight_f * total, axis=1, keepdims=True)
        lane = lax.broadcasted_iota(jnp.int32, (1, lanes - 3 * live), 1)
        made = columns[:, 0:1] * cross + columns[:, 1:2] * total
        spare = jnp.where(lane == 0, grad_gain, jnp.where(lane == 1, grad_bias, 0.0))
        pieces = [made[:, at * width : at * width + live] for at in range(3)] + [spare]
        scr[...] = jnp.concatenate(pieces, axis=1).reshape(parts, count, 2, own, lanes)
        for r in range(parts):
            keep_ref[r] = jnp.concatenate([scr[r, k, core] for k in range(count)], axis=0)
            send_ref[r] = jnp.concatenate([scr[r, k, 1 - core] for k in range(count)], axis=0).astype(BF16)

    outs = (shape(F32, parts, count * own, lanes), shape(BF16, parts, count * own, lanes))
    scratch = (shape(BF16, count, rows, model), shape(F32, parts, count, 2, own, lanes))
    operands = (*units, grads, gain, bias, weight)
    return kernel(body, outs, (place,), operands, scratch, micros=4.0, name="grad_qkv")


def spread_call(place, keep, arrived):
    parts = keep.shape[0]

    def body(place_ref, keep_ref, in_ref, *outs):
        for k in range(parts):
            at = place_ref[2] ^ k
            outs[k][...] = (keep_ref[at] + in_ref[at].astype(F32)).astype(BF16)

    return kernel(body, (shape(BF16, *keep.shape[1:]),) * parts, (place,), (keep, arrived), micros=0.8, name="spread")


def halve_call(place, keep, arrived, bit):
    half = keep.shape[0] // 2

    def body(place_ref, keep_ref, in_ref, stay_ref, away_ref):
        mine = (place_ref[0] // bit) % 2
        for j in range(half):
            here, there = 2 * j + mine, 2 * j + 1 - mine
            stay_ref[j] = keep_ref[here] + in_ref[here].astype(F32)
            away_ref[j] = (keep_ref[there] + in_ref[there].astype(F32)).astype(BF16)

    rest = keep.shape[1:]
    return kernel(body, (shape(F32, half, *rest), shape(BF16, half, *rest)), (place,), (keep, arrived), micros=0.8, name="halve")


def finish_down_call(keep, arrived):
    def body(keep_ref, in_ref, out_ref):
        out_ref[...] = keep_ref[0] + in_ref[0].astype(F32)

    return kernel(body, shape(F32, *keep.shape[1:]), (), (keep, arrived), micros=0.6, name="finish_down")


def finish_up_call(place, keep, arrived, parts, own, part):
    model = keep.shape[2]

    def body(place_ref, keep_ref, in_ref, out_ref, g2, b2, g3, b3, *rest):
        msgs, scr = rest[:parts], rest[parts]
        value = keep_ref[0] + in_ref[0].astype(F32)
        out_ref[...] = value[parts * own : (parts + 1) * own]
        for at, ref in enumerate((g2, b2, g3, b3)):
            line = (parts + 1) * own + at
            ref[...] = value[line : line + 1, :own].reshape(own)
        scr[...] = value[: parts * own].reshape(parts, own, part)
        for k in range(parts):
            msgs[k][...] = scr[place_ref[2] ^ k].astype(BF16)

    outs = (shape(F32, own, model),) + (shape(F32, own),) * 4 + (shape(BF16, own, part),) * parts
    scratch = (shape(F32, parts, own, part),)
    return kernel(body, outs, (place,), (keep, arrived), scratch, micros=0.8, name="finish_up")


def place_up_call(place, pieces):
    parts = len(pieces)
    own, part = pieces[0].shape

    def body(place_ref, *refs):
        for k in range(parts):
            at = pl.multiple_of((place_ref[2] ^ k) * part, 128)
            refs[parts][:, pl.ds(at, part)] = refs[k][...].astype(F32)

    return kernel(body, shape(F32, own, parts * part), (place,), tuple(pieces), micros=0.5, name="place_up")


def share_call(place, pieces, chips):
    own = pieces[0].shape[0] // chips

    def body(place_ref, *refs):
        ins, outs, scr = refs[: len(pieces)], refs[len(pieces) : -1], refs[-1]
        total = ins[0][...].astype(F32)
        for ref in ins[1:]:
            total = total + ref[...].astype(F32)
        scr[...] = total.reshape(chips, own, total.shape[1])
        for k in range(chips):
            outs[k][...] = scr[place_ref[0] ^ k].astype(BF16)

    lanes = pieces[0].shape[1]
    outs = (shape(BF16, own, lanes),) * chips
    return kernel(body, outs, (place,), tuple(pieces), (shape(F32, chips, own, lanes),), micros=0.7, name="share")


def finish_qkv_call(place, pieces, model, live):
    count, own = len(pieces), pieces[0].shape[0]

    def body(place_ref, *refs):
        q_ref, k_ref, v_ref, gain_ref, bias_ref, in_ref = refs[count:]
        for k in range(count):
            in_ref[place_ref[0] ^ k] = refs[k][...].astype(F32)
        for at, ref in enumerate((q_ref, k_ref, v_ref)):
            ref[...] = jnp.concatenate(
                [in_ref[k, :, at * live : (at + 1) * live] for k in range(count)], axis=1
            )
        total = jnp.sum(in_ref[:, :, 3 * live : 3 * live + 2], axis=0).T
        gain_ref[...] = total[0:1].reshape(own)
        bias_ref[...] = total[1:2].reshape(own)

    outs = (shape(F32, own, model),) * 3 + (shape(F32, own),) * 2
    scratch = (shape(F32, count, *pieces[0].shape),)
    return kernel(body, outs, (place,), tuple(pieces), scratch, micros=0.8, name="finish_qkv")


def input_grad_call(place, pieces, layer_in, grad_mid, gain, w_query, w_key, w_value, live):
    count = len(pieces)
    rows, model = layer_in.shape

    def body(place_ref, *refs):
        in_ref, gmid_ref, gain_ref, wq_ref, wk_ref, wv_ref, out_ref, scr = refs[count:]
        for k in range(count):
            scr[place_ref[0] ^ k] = refs[k][...]
        blocks = [unpack(scr[k], rows, 3 * live) for k in range(count)]
        grad = jnp.zeros((rows, model), F32)
        for at, w_ref in enumerate((wq_ref, wk_ref, wv_ref)):
            part = jnp.concatenate([block[:, at * live : (at + 1) * live] for block in blocks], axis=1)
            grad = grad + mm(part, w_ref[...], NT)
        unit, scale = unit_norm(in_ref[...].astype(F32))
        out_ref[...] = (gmid_ref[...] + norm_back(grad, row(gain_ref), unit, scale)).astype(BF16)

    operands = (*pieces, layer_in, grad_mid, gain, w_query, w_key, w_value)
    scratch = (shape(BF16, count, *pieces[0].shape),)
    return kernel(body, shape(BF16, rows, model), (place,), operands, scratch, micros=3.0, name="grad_inputs")


def swap_core(value):
    return lax.ppermute(value, "core", [(0, 1), (1, 0)])


def swap(value, axis, bit):
    return lax.ppermute(value, axis, [(k, k ^ bit) for k in range(lax.axis_size(axis))])


def trade(messages, axis):
    found = {k: swap(messages[k], axis, k) for k in range(len(messages) - 1, 0, -1)}
    return [messages[0]] + [found[k] for k in range(1, len(messages))]


def gather_chips(block, chips):
    found = {0: block}
    bit = chips // 2
    while bit >= 1:
        for k in sorted(found):
            found[k | bit] = swap(found[k], "chip", bit)
        bit //= 2
    return [found[k] for k in range(chips)]


def scatter_chips(place, keep, arrived, chips, bit):
    while bit < chips:
        keep, away = halve_call(place, keep, arrived, bit)
        arrived = swap(away, "chip", bit)
        bit *= 2
    return keep, arrived


def after(values, *others):
    return lax.optimization_barrier((values, others))[0]


def fast_shards(
    inputs, doc_lengths, ln1_gain, ln1_bias, w_query, w_key, w_value, ln2_gain, ln2_bias, w_out,
    ln3_gain, ln3_bias, w_up, w_down, out_grad,
):
    rows, model = inputs.shape[1:]
    chips, parts = lax.axis_size("chip"), lax.axis_size("rows")
    z_index = lax.axis_index("chip")
    heads_here = HEADS // chips
    live = heads_here * HEAD_DIM
    width = -(-live // 128) * 128
    hidden = w_up.shape[1]
    part = hidden // parts
    own = model // (parts * chips * 2)
    place = jnp.stack([z_index, lax.axis_index("core"), lax.axis_index("rows")]).astype(jnp.int32)
    scope = jax.named_scope

    def columns(weight):
        mine = lax.dynamic_slice_in_dim(weight, z_index * live, live, 1)
        return jnp.pad(mine, ((0, 0), (0, width - live)))

    place, layer_in, out_grad = lax.optimization_barrier((place, inputs[0], out_grad[0]))
    with scope("gather_in"):
        blocks = gather_chips(layer_in, chips)
    grad_out = mask_call(place, doc_lengths, out_grad)
    w_heads = jnp.concatenate([columns(w_query), columns(w_key), columns(w_value)], axis=1)
    groups = [g for g in ([0], list(range(1, chips - 1)), [chips - 1]) if g] if chips > 1 else [[0]]
    made = [qkv_call([blocks[k] for k in g], ln1_gain, ln1_bias, w_heads, width) for g in groups]
    queries, kv_own, units = ([m[at] for m in made] for at in range(3))
    with scope("core_kv"):
        kv_other = [swap_core(v) for v in kv_own]
    attn_heads, (prob, queries, kv_own, kv_other), messages = attend_call(
        place, doc_lengths, groups, queries, kv_own, kv_other, heads_here
    )
    fence = lax.optimization_barrier
    with scope("chip_attn"):
        pieces = trade(messages, "chip")
    with scope("plane_out"):
        grads_plane = trade([grad_out] * parts, "rows")
    pieces = after(pieces, grads_plane)

    vectors = (ln2_gain, ln2_bias, ln3_gain, ln3_bias)
    middle, attn, normed3 = norms_call(place, pieces, layer_in, vectors, w_out, live)
    act, slope, acts = up_call(place, normed3, w_up, parts)
    with scope("plane_act"):
        acts = trade(acts, "rows")
    output, grad_mid, back, messages = backward_call(
        place, attn, middle, act, slope, grad_out, vectors, w_out, w_up, w_down, parts, chips, live
    )
    back = after(back, acts[1:])
    with scope("chip_grad"):
        grad_heads = trade(messages, "chip")
    with scope("plane_back"):
        far = [swap(back[k], "rows", k) for k in range(3, parts)]
    grad_q, grad_kv, grad_kv_other = attend_back_call(
        place, queries, kv_own, kv_other, prob, attn_heads, grad_heads, heads_here
    )
    with scope("core_grad"):
        grad_kv_other = swap_core(grad_kv_other)
    down_keep, down_send = down_grad_call(place, after(acts, grad_q), grads_plane, chips)
    grad_kv_other, down_send, far = fence((grad_kv_other, down_send, far))
    with scope("core_down"):
        down_recv = swap_core(down_send)
    with scope("plane_back"):
        near = after(back[1:3], far)
        back = back[:1] + [swap(near[k], "rows", k + 1) for k in range(len(near))] + far
    grad_qkv, messages = join_call(place, grad_q, grad_kv, grad_kv_other, live)
    with scope("down_sum"):
        down_keep, down_away = halve_call(place, down_keep, after(down_recv, grad_qkv), 1)
        grad_qkv, down_away = fence((grad_qkv, down_away))
        down_recv = swap(down_away, "chip", 1)
    with scope("chip_qkv"):
        grad_pieces = trade(messages, "chip")
    qkv_keep, qkv_send = qkv_grad_call(
        place, groups, units, grad_qkv, ln1_gain, ln1_bias, w_heads, parts, live, width
    )
    down_recv = after(down_recv, qkv_send)
    with scope("core_w"):
        qkv_send = swap_core(qkv_send)
    qkv_sums = spread_call(place, qkv_keep, qkv_send)
    with scope("down_sum"):
        down_keep, down_last = scatter_chips(place, down_keep, down_recv, chips, 2)
    back = after(back, (down_keep, grad_pieces[2:]))
    up_keep, up_send = up_grad_call(place, back, chips, part, model)
    with scope("plane_w"):
        traded = trade(qkv_sums, "rows")
    up_send = after(up_send, (down_last, grad_pieces[1:2]))
    with scope("core_up"):
        up_recv = swap_core(up_send)
    up_keep, up_away = halve_call(place, up_keep, up_recv, 1)
    with scope("up_sum"):
        up_recv = swap(up_away, "chip", 1)
    traded = after(traded, up_away)
    with scope("chip_w"):
        shared = share_call(place, traded, chips)
        qkv_all = trade(shared, "chip")
    grad_inputs = input_grad_call(
        place, grad_pieces, layer_in, grad_mid, ln1_gain, w_query, w_key, w_value, live
    )
    gwd = finish_down_call(down_keep, down_last)
    up_recv = after(up_recv, (grad_pieces, shared, down_last))
    with scope("up_sum"):
        up_keep, up_last = scatter_chips(place, up_keep, up_recv, chips, 2)
    up_last = after(up_last, (qkv_all, gwd, grad_inputs))
    gwo, g2, b2, g3, b3, *up_rows = finish_up_call(place, up_keep, up_last, parts, own, part)
    with scope("plane_rows"):
        up_rows = trade(up_rows, "rows")
    gwq, gwk, gwv, g1, b1 = finish_qkv_call(place, qkv_all, model, live)
    gwu = place_up_call(place, up_rows)
    return (
        output[None], grad_inputs[None], g1, b1, gwq, gwk, gwv, g2, b2, gwo, g3, b3, gwu, gwd,
    )


def takes_fast(mesh):
    seq, parts = mesh.shape["seq"], mesh.shape["rows"]
    chips = seq // 2
    return seq % 2 == 0 and chips & (chips - 1) == 0 and parts in (1, 2, 4) and HEADS % max(chips, 1) == 0


def solution(mesh):
    if takes_fast(mesh):
        parts, seq = mesh.shape["rows"], mesh.shape["seq"]
        split = jax.sharding.Mesh(mesh.devices.reshape(parts, seq // 2, 2), ("rows", "chip", "core"))
        return mapped(fast_shards, split, ("chip", "core"))
    return mapped(shards, mesh, "seq")
```
